32 devices in a mesh: rep: 8 (over z, core), shard: 4 (over y, x).
Axes of the slice: x: 2, y: 2, z: 4, core: 2. Of those that a mesh axis runs over, the one named last changes fastest.
Arguments:
- block_input: bfloat16 [2, 8192, 960], P(None, ('rep', 'shard')), may hold values from -6 to 6
- parent_ids: int32 [2, 8, 8], P(None, 'rep'), may hold values from 0 to 6, as said below
- w_query: bfloat16 [960, 960], P('shard'), may hold values from -0.1875 to 0.1875
- key_weight: bfloat16 [960, 320], P('shard'), may hold values from -0.1875 to 0.1875
- value_weight: bfloat16 [960, 320], P('shard'), may hold values from -0.1875 to 0.1875
- w_output: bfloat16 [960, 960], P('shard'), may hold values from -3.5 to 3.5
- w_gate: bfloat16 [960, 2560], P('shard'), may hold values from -0.1875 to 0.1875
- w_up: bfloat16 [960, 2560], P('shard'), may hold values from -0.1875 to 0.1875
- w_down: bfloat16 [2560, 960], P('shard'), may hold values from -0.125 to 0.125
- norm_first: bfloat16 [960], P('shard'), may hold values from 0.25 to 1.75
- norm_second: bfloat16 [960], P('shard'), may hold values from 0.25 to 1.75
- out_cotangent: bfloat16 [2, 8192, 960], P(None, ('rep', 'shard')), may hold values from -6 to 6
Outputs:
- block_output: bfloat16 [2, 8192, 960], P(None, ('rep', 'shard'))
- input_grad: bfloat16 [2, 8192, 960], P(None, ('rep', 'shard'))
- grad_query: float32 [960, 960], P('shard')
- grad_key: float32 [960, 320], P('shard')
- grad_value: float32 [960, 320], P('shard')
- grad_output: float32 [960, 960], P('shard')
- grad_gate: float32 [960, 2560], P('shard')
- grad_upper: float32 [960, 2560], P('shard')
- grad_down: float32 [2560, 960], P('shard')
- grad_norm_first: float32 [960], P('shard')
- grad_norm_second: float32 [960], P('shard')
The draws below stay inside these ranges and needn't reach their ends.
Inputs may be any that keep to these rules, and one draw needn't show every extreme that they name: `parent_ids`: segment 0 of every tree is its own parent; every odd segment's parent is the segment just before it; every even segment after 0 has as parent one of the two segments just before it.
All inputs are finite; a program needn't handle non-finite values.
Results may differ from the reference program's by a relative error of at most 0.022.
Values may be sent and summed in bfloat16 or wider, within the bound.
No kernel may reach another device: no remote copies, remote signals or barrier semaphores. Data moves between devices by JAX's collectives and lax.ppermute only.
A program may use at most 192 MiB of HBM per device.

```python
import math
import jax
import jax.numpy as jnp
from jax import lax

MODEL_WIDTH = 960
FF = 2560
QUERY_HEADS = 15
KEY_VALUE_HEADS = 5
HEAD_SIZE = 64
SEG = 128
MB = 2
TREE_TOKENS = 1024
NSEG = 8
TREES = 8
TOKENS = 8192


def draw_parent_ids(key, part):
    segment = jnp.arange(NSEG, dtype=jnp.int32)
    offset = jax.random.randint(key, (MB, TREES, NSEG), 0, 2).astype(jnp.int32)
    odd_parent = jnp.broadcast_to(segment - 1, (MB, TREES, NSEG)).astype(jnp.int32)
    even_parent = (segment[None, None, :] - 2 + offset).astype(jnp.int32)
    odd_mask = (segment % 2 == 1)[None, None, :]
    root_mask = (segment == 0)[None, None, :]
    chosen = jnp.where(odd_mask, odd_parent, even_parent)
    return jnp.where(root_mask, jnp.int32(0), chosen).astype(jnp.int32)


def shard_levels(key, shape, pieces, low, largest):
    factor_of, own = 1.0, jax.random.fold_in(key, 6)
    for position, blocks in pieces:
        draws = jnp.exp(jax.random.uniform(jax.random.fold_in(own, position), (blocks,), jnp.float32, low / len(pieces), largest / len(pieces)))
        factor_of = factor_of * jnp.repeat(draws, shape[position] // blocks).reshape([-1 if axis == position else 1 for axis in range(len(shape))])
    return factor_of


def bell_draw(own_key, dims, width, most, cuts=(), kind=jnp.bfloat16):
    array = width * jax.random.normal(own_key, dims, jnp.float32)
    if cuts:
        array = array * shard_levels(own_key, dims, cuts, -0.22, 0.18)
    return jnp.clip(array, -most, most).astype(kind)


def setup_inputs(seed: int = 0) -> dict:
    key_of = jax.random.split(jax.random.key(seed), 13)
    return {
        "block_input": bell_draw(key_of[0], (MB, TOKENS, MODEL_WIDTH), 1.0, 6.0, ((1, 32),)),
        "parent_ids": draw_parent_ids(jax.random.fold_in(key_of[12], 71), 0),
        "w_query": bell_draw(key_of[2], (MODEL_WIDTH, QUERY_HEADS * HEAD_SIZE), MODEL_WIDTH ** -0.5, 0.1875, ((0, 4),)),
        "key_weight": bell_draw(key_of[3], (MODEL_WIDTH, KEY_VALUE_HEADS * HEAD_SIZE), MODEL_WIDTH ** -0.5, 0.1875, ((0, 4),)),
        "value_weight": bell_draw(key_of[4], (MODEL_WIDTH, KEY_VALUE_HEADS * HEAD_SIZE), MODEL_WIDTH ** -0.5, 0.1875, ((0, 4),)),
        "w_output": bell_draw(key_of[5], (QUERY_HEADS * HEAD_SIZE, MODEL_WIDTH), (max(1, 4 * MODEL_WIDTH // TREE_TOKENS)) ** -0.5, 3.5, ((0, 4),)),
        "w_gate": bell_draw(key_of[6], (MODEL_WIDTH, FF), MODEL_WIDTH ** -0.5, 0.1875, ((0, 4),)),
        "w_up": bell_draw(key_of[7], (MODEL_WIDTH, FF), MODEL_WIDTH ** -0.5, 0.1875, ((0, 4),)),
        "w_down": bell_draw(key_of[8], (FF, MODEL_WIDTH), FF ** -0.5, 0.125, ((0, 4),)),
        "norm_first": jnp.clip(1.0 + 0.15 * jax.random.normal(key_of[9], (MODEL_WIDTH,), jnp.float32), 0.25, 1.75).astype(jnp.bfloat16),
        "norm_second": jnp.clip(1.0 + 0.15 * jax.random.normal(key_of[10], (MODEL_WIDTH,), jnp.float32), 0.25, 1.75).astype(jnp.bfloat16),
        "out_cotangent": bell_draw(key_of[11], (MB, TOKENS, MODEL_WIDTH), 1.0, 6.0, ((1, 32),)),
    }


EPS = 1e-05
HIGH = lax.Precision.HIGHEST

@jax.custom_vjp
def lower_half(v):
    return lax.optimization_barrier(v.astype(jnp.bfloat16)).astype(jnp.float32)

@jax.custom_vjp
def lower_half_backward(v):
    return v

def low_keep(v):
    return (lower_half(v), None)

def low_pass(kept, grad):
    return (grad,)

def back_keep(v):
    return (v, None)

def back_low(kept, grad):
    return (lower_half(grad),)
lower_half.defvjp(low_keep, low_pass)
lower_half_backward.defvjp(back_keep, back_low)

def ancestry(parents_row):
    identity = jnp.eye(NSEG, dtype=jnp.float32)
    selector = (parents_row[:, None] == jnp.arange(NSEG, dtype=jnp.int32)[None, :]).astype(jnp.float32)

    def extend(counter, table):
        return jnp.maximum(identity, jnp.dot(selector, table, precision=HIGH))
    return lax.fori_loop(0, NSEG, extend, identity)

def rotation_tables(positions):
    freqs = jnp.exp(-math.log(10000.0) * jnp.arange(HEAD_SIZE // 2, dtype=jnp.float32) * (2.0 / HEAD_SIZE))
    angles = positions[:, None] * freqs[None, :]
    return (jnp.cos(angles)[:, None, :], jnp.sin(angles)[:, None, :])

def apply_rotation(vectors, cosine_table, sine_table, heads):
    shaped = vectors.reshape(vectors.shape[0], heads, HEAD_SIZE)
    first_half = shaped[..., :HEAD_SIZE // 2]
    second_half = shaped[..., HEAD_SIZE // 2:]
    turned = jnp.concatenate([first_half * cosine_table - second_half * sine_table, second_half * cosine_table + first_half * sine_table], axis=-1)
    return turned.reshape(vectors.shape[0], heads * HEAD_SIZE)

def tree_layer(inputs, parents_row, weights):
    w_query, key_weight, value_weight, w_output, w_gate, w_up, w_down, norm_first, norm_second = weights
    table = ancestry(parents_row)
    rows_all = jnp.arange(TREE_TOKENS, dtype=jnp.int32)
    segment = rows_all // SEG
    depth = lax.optimization_barrier(jnp.sum(table, axis=1)) - 1.0
    positions = depth[segment] * SEG + (rows_all % SEG).astype(jnp.float32)
    allowed = (table[segment][:, segment] > 0.5) & (rows_all[None, :] <= rows_all[:, None])
    cosine_table, sine_table = rotation_tables(positions)
    inv_first = lax.rsqrt(lax.optimization_barrier(jnp.mean(inputs * inputs, axis=-1, keepdims=True)) + EPS)
    act_first = lower_half(inputs * inv_first * norm_first)
    query_lin = jnp.dot(act_first, w_query, precision=HIGH)
    key_linear = jnp.dot(act_first, key_weight, precision=HIGH)
    value_linear = jnp.dot(act_first, value_weight, precision=HIGH)
    queries = lower_half(apply_rotation(lower_half_backward(query_lin), cosine_table, sine_table, QUERY_HEADS)).reshape(TREE_TOKENS, QUERY_HEADS, HEAD_SIZE)
    key_matrix = lower_half(apply_rotation(lower_half_backward(key_linear), cosine_table, sine_table, KEY_VALUE_HEADS)).reshape(TREE_TOKENS, KEY_VALUE_HEADS, HEAD_SIZE)
    value_matrix = lower_half(lower_half_backward(value_linear)).reshape(TREE_TOKENS, KEY_VALUE_HEADS, HEAD_SIZE)
    key_matrix_every = jnp.repeat(key_matrix, QUERY_HEADS // KEY_VALUE_HEADS, axis=1)
    value_matrix_every = jnp.repeat(value_matrix, QUERY_HEADS // KEY_VALUE_HEADS, axis=1)
    block = min(512, TREE_TOKENS)
    scale = HEAD_SIZE ** (-0.5)

    def attend(start):
        query_block = lax.dynamic_slice_in_dim(queries, start, block, 0)
        mask_block = lax.dynamic_slice_in_dim(allowed, start, block, 0)
        raw = jnp.einsum('thd,nhd->htn', query_block, key_matrix_every, precision=HIGH)
        scores = jnp.where(mask_block[None], lower_half_backward(raw) * scale, -1e+30)
        probs = jax.nn.softmax(scores, axis=-1)
        return jnp.einsum('htn,nhd->thd', lower_half(probs), value_matrix_every, precision=HIGH)
    starts = jnp.arange(TREE_TOKENS // block, dtype=jnp.int32) * block
    mixed = lax.map(jax.checkpoint(attend), starts).reshape(TREE_TOKENS, QUERY_HEADS * HEAD_SIZE)
    attn_low = lower_half(lower_half_backward(mixed))
    resid = inputs + lower_half_backward(jnp.dot(attn_low, w_output, precision=HIGH))
    inv_second = lax.rsqrt(lax.optimization_barrier(jnp.mean(resid * resid, axis=-1, keepdims=True)) + EPS)
    act_second = lower_half(resid * inv_second * norm_second)
    gate = lower_half_backward(jnp.dot(act_second, w_gate, precision=HIGH))
    upper = lower_half_backward(jnp.dot(act_second, w_up, precision=HIGH))
    inner = lower_half(jax.nn.silu(gate) * upper)
    return resid + jnp.dot(inner, w_down, precision=HIGH)

def reference(block_input, parent_ids, w_query, key_weight, value_weight, w_output, w_gate, w_up, w_down, norm_first, norm_second, out_cotangent):
    weights = tuple((weight.astype(jnp.float32) for weight in (w_query, key_weight, value_weight, w_output, w_gate, w_up, w_down, norm_first, norm_second)))
    inputs = block_input.astype(jnp.float32).reshape(MB * TREES, TREE_TOKENS, MODEL_WIDTH)
    parents = parent_ids.reshape(MB * TREES, NSEG)
    layer = jax.checkpoint(tree_layer)

    def forward(inputs_all, weights_all):

        def single_tree(operands):
            return layer(operands[0], operands[1], weights_all)
        return lax.map(single_tree, (inputs_all, parents))
    outputs, pullback = jax.vjp(forward, inputs, weights)
    input_grad, weight_grads = pullback(out_cotangent.astype(jnp.float32).reshape(MB * TREES, TREE_TOKENS, MODEL_WIDTH))
    return (outputs.reshape(MB, TOKENS, MODEL_WIDTH).astype(jnp.bfloat16), input_grad.reshape(MB, TOKENS, MODEL_WIDTH).astype(jnp.bfloat16), weight_grads[0], weight_grads[1], weight_grads[2], weight_grads[3], weight_grads[4], weight_grads[5], weight_grads[6], weight_grads[7], weight_grads[8])
```

```python
import math

import jax
import jax.numpy as jnp
from jax import lax
from jax.sharding import PartitionSpec as P

QUERY_HEADS = 15
KEY_VALUE_HEADS = 5
HEAD_SIZE = 64
GROUP = QUERY_HEADS // KEY_VALUE_HEADS
EPS = 1e-05
AXES = ("rep", "shard")
BF = jnp.bfloat16
F32 = jnp.float32


def rms_inverse(x):
    return lax.rsqrt(jnp.mean(x * x, axis=-1, keepdims=True) + EPS)


def dot(a, b, dims):
    return lax.dot_general(a, b, (dims, ((), ())), preferred_element_type=F32)


def nn(a, b):
    return dot(a, b, ((1,), (0,)))


def nt(a, b):
    return dot(a, b, ((1,), (1,)))


def tn(a, b):
    return dot(a, b, ((0,), (0,)))


class Links:
    def __init__(self, reps, shards):
        self.reps, self.shards = reps, shards
        self.core = lax.axis_index("rep") % 2
        self.shard = lax.axis_index("shard")
        self.bits = shards.bit_length() - 1
        even = [1 << i for i in range(self.bits)]
        odd = even[:2][::-1] + even[2:]
        self.steps = list(zip(even, odd))
        self.hops = []
        for piece in range(shards):
            sums = [0, 0]
            for i, step in enumerate(self.steps):
                if piece >> i & 1:
                    sums = [sums[0] ^ step[0], sums[1] ^ step[1]]
            self.hops.append(jnp.where(self.core == 0, sums[0], sums[1]))

    def move(self, value, target):
        pairs = []
        for r in range(self.reps):
            for s in range(self.shards):
                goal = target(r, s)
                if goal is not None:
                    pairs.append((r * self.shards + s, goal[0] * self.shards + goal[1]))
        return lax.ppermute(value, AXES, pairs)

    def step(self, value, i):
        return self.move(value, lambda r, s: (r, s ^ self.steps[i][r % 2]))

    def swap(self, value):
        return self.move(value, lambda r, s: (r ^ 1, s))

    def chain(self, value):
        chips = self.reps // 2
        place = lax.axis_index("rep") // 2
        span = 1
        if chips % 4 == 0:
            inward, outward, middle = {0: 1, 3: 2}, {1: 0, 2: 3}, {1: 2, 2: 1}

            def along(value, table):
                def target(r, s):
                    chip = r // 2
                    if chip % 4 not in table:
                        return None
                    return ((chip - chip % 4 + table[chip % 4]) * 2 + r % 2, s)

                return self.move(value, target)

            value = add(value, along(value, inward))
            value = add(value, along(value, middle))
            back = along(value, outward)
            inner = (place % 4 == 1) | (place % 4 == 2)
            value = jnp.where(inner, value, back)
            span = 4
        while span < chips:
            value = add(value, self.move(value, lambda r, s: (r ^ (2 * span), s)))
            span *= 2
        return value

    def spread(self, value):
        pieces = [value]
        for i in range(self.bits):
            pieces = pieces + [self.step(piece, i) for piece in pieces]
        return pieces

    def collect(self, pieces):
        for i in reversed(range(self.bits)):
            keep = 1 << i
            pieces = [add(pieces[t], self.step(pieces[t + keep], i)) for t in range(keep)]
        return pieces[0]

    def half_rows(self, rows):
        return -(-rows // 16) * 8

    def gather(self, shard_value):
        rows, cols = shard_value.shape
        half = self.half_rows(rows)
        first = self.core * (rows - half)
        second = (1 - self.core) * (rows - half)
        mine = lax.dynamic_slice_in_dim(shard_value, first, half, 0)
        pieces = self.spread(mine)[1:]
        others = [self.swap(piece) for piece in pieces]
        whole = jnp.zeros((rows * self.shards, cols), shard_value.dtype)
        whole = lax.dynamic_update_slice(whole, shard_value, (self.shard * rows, 0))
        for piece, other, hop in zip(pieces, others, self.hops[1:]):
            whole = lax.dynamic_update_slice(whole, piece, ((self.shard ^ hop) * rows + first, 0))
        for t, other in enumerate(others, 1):
            hop = self.hops[self.twin(t)]
            whole = lax.dynamic_update_slice(whole, other, ((self.shard ^ hop) * rows + second, 0))
        return whole

    def twin(self, piece):
        return piece if self.bits < 2 else piece >> 2 << 2 | (piece & 1) << 1 | (piece >> 1 & 1)

    def gather_small(self, value):
        pieces = jnp.stack(
            [value if hop == 0 else self.move(value, lambda r, s, hop=hop: (r, s ^ hop))
                for hop in range(self.shards)
            ]
        )
        order = self.shard ^ jnp.arange(self.shards)
        hit = (order[:, None] == jnp.arange(self.shards)[None, :])[:, :, None, None]
        pieces = jnp.sum(jnp.where(hit, pieces[None], 0), axis=1, dtype=value.dtype)
        return jnp.concatenate([pieces[j] for j in range(self.shards)], axis=-1)

    def reduce_weight(self, grad):
        rows = grad.shape[0] // self.shards
        half = self.half_rows(rows)
        first = self.core * (rows - half)
        second = (1 - self.core) * (rows - half)
        parts = grad.astype(BF).reshape(self.shards, rows, grad.shape[1])
        kept = lax.dynamic_slice_in_dim(parts, first, half, 1)
        given = lax.dynamic_slice_in_dim(parts, second, half, 1)
        summed = add(kept, self.swap(given))
        owned = self.collect(
            [lax.dynamic_index_in_dim(summed, self.shard ^ hop, 0, keepdims=False) for hop in self.hops]
        )
        owned = self.chain(owned)
        other = self.swap(owned)
        low = jnp.where(self.core == 0, owned, other)
        high = jnp.where(self.core == 0, other, owned)
        return jnp.concatenate([low[: rows - half], high], axis=0).astype(F32)

    def reduce_small(self, value):
        summed = add(value, self.swap(value))
        for i in range(self.bits):
            summed = add(summed, self.step(summed, i))
        summed = self.chain(summed)
        width = value.shape[1] // self.shards
        return lax.dynamic_slice_in_dim(summed, self.shard * width, width, 1)


def add(left, right):
    return (left.astype(F32) + right.astype(F32)).astype(left.dtype)


def rotate(vectors, cosine, sine, heads, inverse):
    shaped = vectors.reshape(vectors.shape[0], heads, HEAD_SIZE)
    first = shaped[..., : HEAD_SIZE // 2]
    second = shaped[..., HEAD_SIZE // 2 :]
    cosine, sine = cosine[:, None, :], sine[:, None, :]
    if inverse:
        sine = -sine
    turned = jnp.concatenate(
        [first * cosine - second * sine, second * cosine + first * sine], axis=-1
    )
    return turned.reshape(vectors.shape[0], heads * HEAD_SIZE)


def local(
    block_input,
    parent_ids,
    w_query,
    key_weight,
    value_weight,
    w_output,
    w_gate,
    w_up,
    w_down,
    norm_first,
    norm_second,
    out_cotangent,
):
    micro, rows, width = block_input.shape
    shards = lax.axis_size("shard")
    links = Links(lax.axis_size("rep"), shards)
    tree = rows * shards
    segs = parent_ids.shape[2]
    seg_rows = tree // segs
    kv_width = KEY_VALUE_HEADS * HEAD_SIZE
    scale = HEAD_SIZE ** (-0.5)
    tokens = micro * rows

    gains = links.gather_small(jnp.stack([norm_first, norm_second])).astype(F32)
    gain_one, gain_two = gains[0:1], gains[1:2]
    full_qkv = links.gather(jnp.concatenate([w_query, key_weight, value_weight], axis=1))
    full_output = links.gather(w_output)
    full_gate = links.gather(w_gate)
    full_upper = links.gather(w_up)
    full_down = links.gather(w_down)

    parents = parent_ids[:, 0]
    seg = jnp.arange(segs)
    after = jnp.concatenate([parents[:, 1:], jnp.full((micro, 1), -1, parents.dtype)], axis=1)
    on_path = (seg % 2 == 0)[None] | (after == seg[None])
    depth = jnp.sum(jnp.where((seg[None, :] < seg[:, None])[None], on_path.astype(F32)[:, None, :], 0.0), axis=-1)

    def row_numbers(hop):
        return (links.shard ^ hop) * rows + jnp.arange(rows)

    def pick(table, numbers):
        hit = (numbers // seg_rows)[:, None] == seg[None]
        return jnp.sum(jnp.where(hit[None], table[:, None, :], 0), axis=-1)

    my_rows = row_numbers(0)
    positions = pick(depth, my_rows) * seg_rows + (my_rows % seg_rows).astype(F32)
    freqs = jnp.exp(-math.log(10000.0) * jnp.arange(HEAD_SIZE // 2, dtype=F32) * (2.0 / HEAD_SIZE))
    angles = positions.reshape(tokens)[:, None] * freqs[None, :]
    cosine, sine = jnp.cos(angles), jnp.sin(angles)
    key_rows = jnp.concatenate([row_numbers(hop) for hop in links.hops])
    key_on_path = pick(on_path.astype(F32), key_rows) > 0.5
    key_seg, my_seg = key_rows // seg_rows, my_rows // seg_rows
    allowed = ((key_seg[None, :] < my_seg[:, None])[None] & key_on_path[:, None, :]) | (
        (key_seg[None, :] == my_seg[:, None]) & (key_rows[None, :] <= my_rows[:, None])
    )[None]

    inputs = block_input.reshape(tokens, width).astype(F32)
    cotangent = out_cotangent.reshape(tokens, width)
    inv_first = rms_inverse(inputs)
    normed_first = inputs * inv_first
    act_first = (normed_first * gain_one).astype(BF)
    linear = nn(act_first, full_qkv)
    queries = rotate(linear[:, :width], cosine, sine, QUERY_HEADS, False).astype(BF)
    keys = rotate(linear[:, width : width + kv_width], cosine, sine, KEY_VALUE_HEADS, False)
    kv = jnp.concatenate([keys, linear[:, width + kv_width :]], axis=1).astype(BF)
    kv_all = jnp.concatenate(
        [piece.reshape(micro, rows, 2 * kv_width) for piece in links.spread(kv)], axis=1
    )

    def by_head(value, length):
        return value.reshape(micro, length, KEY_VALUE_HEADS, -1, HEAD_SIZE).transpose(0, 2, 3, 1, 4)

    query_heads = by_head(queries, rows)
    key_heads = by_head(kv_all[:, :, :kv_width], tree)[:, :, 0]
    value_heads = by_head(kv_all[:, :, kv_width:], tree)[:, :, 0]

    def forward(allowed, operands):
        query_part, key_part, value_part = operands
        raw = jnp.einsum("gtd,nd->gtn", query_part, key_part, preferred_element_type=F32) * scale
        masked = jnp.where(allowed[None], raw, -1e30)
        peak = jnp.max(masked, axis=-1, keepdims=True)
        expo = jnp.where(allowed[None], jnp.exp(masked - peak), 0.0)
        total = jnp.sum(expo, axis=-1, keepdims=True)
        mixed = jnp.einsum(
            "gtn,nd->gtd", (expo / total).astype(BF), value_part, preferred_element_type=F32
        )
        return mixed, peak + jnp.log(total)

    mixed, log_totals = [], []
    for m in range(micro):
        out, logs = lax.map(
            lambda ops, m=m: forward(allowed[m], ops), (query_heads[m], key_heads[m], value_heads[m])
        )
        mixed.append(out.transpose(2, 0, 1, 3).reshape(rows, width))
        log_totals.append(logs)
    attn = jnp.concatenate(mixed, axis=0).astype(BF)
    resid = inputs + nn(attn, full_output)
    inv_second = rms_inverse(resid)
    normed_second = resid * inv_second
    act_second = (normed_second * gain_two).astype(BF)
    gate = nn(act_second, full_gate)
    upper = nn(act_second, full_upper)
    sigmoid = jax.nn.sigmoid(gate)
    silu = gate * sigmoid
    inner = (silu * upper).astype(BF)
    block_out = (resid + nn(inner, full_down)).astype(BF)

    grad_down = links.reduce_weight(tn(inner, cotangent))
    d_inner = nt(cotangent, full_down)
    d_gate = (d_inner * upper * sigmoid * (1.0 + gate * (1.0 - sigmoid))).astype(BF)
    d_upper = (d_inner * silu).astype(BF)
    grad_gate = links.reduce_weight(tn(act_second, d_gate))
    grad_upper = links.reduce_weight(tn(act_second, d_upper))
    d_act_second = nt(d_gate, full_gate) + nt(d_upper, full_upper)
    gain_two_sum = jnp.sum(d_act_second * normed_second, axis=0)
    d_normed = d_act_second * gain_two
    d_resid = cotangent.astype(F32) + inv_second * (
        d_normed - normed_second * jnp.mean(d_normed * normed_second, axis=-1, keepdims=True)
    )
    d_resid_low = d_resid.astype(BF)
    grad_output = links.reduce_weight(tn(attn, d_resid_low))
    d_attn = nt(d_resid_low, full_output).astype(BF)
    d_attn_heads = by_head(d_attn, rows)

    def backward(allowed, operands):
        query_part, key_part, value_part, d_out, logs = operands
        raw = jnp.einsum("gtd,nd->gtn", query_part, key_part, preferred_element_type=F32) * scale
        probs = jnp.exp(jnp.where(allowed[None], raw, -1e30) - logs)
        d_probs = jnp.einsum("gtd,nd->gtn", d_out, value_part, preferred_element_type=F32)
        centre = jnp.sum(probs * d_probs, axis=-1, keepdims=True)
        d_scores = (probs * (d_probs - centre) * scale).astype(BF)
        d_query = jnp.einsum("gtn,nd->gtd", d_scores, key_part, preferred_element_type=F32)
        d_key = jnp.einsum("gtn,gtd->nd", d_scores, query_part, preferred_element_type=F32)
        d_value = jnp.einsum("gtn,gtd->nd", probs.astype(BF), d_out, preferred_element_type=F32)
        return d_query, d_key, d_value

    d_queries, d_kv = [], []
    for m in range(micro):
        d_query, d_key, d_value = lax.map(
            lambda ops, m=m: backward(allowed[m], ops),
            (query_heads[m], key_heads[m], value_heads[m], d_attn_heads[m], log_totals[m]),
        )
        d_queries.append(d_query.transpose(2, 0, 1, 3).reshape(rows, width))
        flat = [part.transpose(1, 0, 2).reshape(tree, kv_width) for part in (d_key, d_value)]
        d_kv.append(jnp.concatenate(flat, axis=1).astype(BF).reshape(shards, rows, 2 * kv_width))
    d_kv = jnp.stack(d_kv, axis=1).reshape(shards, tokens, 2 * kv_width)
    d_kv_sum = links.collect(list(d_kv)).astype(F32)
    d_query_low = rotate(jnp.concatenate(d_queries, axis=0), cosine, sine, QUERY_HEADS, True).astype(BF)
    d_key_low = rotate(d_kv_sum[:, :kv_width], cosine, sine, KEY_VALUE_HEADS, True).astype(BF)
    d_low = jnp.concatenate([d_query_low, d_key_low, d_kv_sum[:, kv_width:].astype(BF)], axis=1)
    grad_qkv = links.reduce_weight(tn(act_first, d_low))
    d_act_first = nt(d_low, full_qkv)
    gain_one_sum = jnp.sum(d_act_first * normed_first, axis=0)
    d_normed = d_act_first * gain_one
    d_input = d_resid + inv_first * (
        d_normed - normed_first * jnp.mean(d_normed * normed_first, axis=-1, keepdims=True)
    )
    gain_sums = links.reduce_small(jnp.stack([gain_one_sum, gain_two_sum]))
    return (
        block_out.reshape(micro, rows, width),
        d_input.astype(BF).reshape(micro, rows, width),
        grad_qkv[:, :width],
        grad_qkv[:, width : width + kv_width],
        grad_qkv[:, width + kv_width :],
        grad_output,
        grad_gate,
        grad_upper,
        grad_down,
        gain_sums[0],
        gain_sums[1],
    )


def solution(mesh):
    rows = P(None, AXES, None)
    weight, gain = P("shard", None), P("shard")
    return jax.shard_map(
        local,
        mesh=mesh,
        in_specs=(rows, P(None, "rep", None)) + (weight,) * 7 + (gain, gain, rows),
        out_specs=(rows, rows) + (weight,) * 7 + (gain, gain),
        check_vma=False,
    )
```

```python
import functools
import math

import jax
import jax.numpy as jnp
from jax import lax
from jax.experimental import pallas as pl
from jax.experimental.pallas import tpu as pltpu
from jax.sharding import PartitionSpec as P

QUERY_HEADS = 15
KEY_VALUE_HEADS = 5
HEAD_SIZE = 64
HALF_HEAD = HEAD_SIZE // 2
GROUP = QUERY_HEADS // KEY_VALUE_HEADS
KV_WIDTH = KEY_VALUE_HEADS * HEAD_SIZE
SCALE = HEAD_SIZE ** (-0.5)
EPS = 1e-05
AXES = ("rep", "shard")
BF = jnp.bfloat16
F32 = jnp.float32
CLOSED = -1e30
VMEM_LIMIT = 48 << 20


def dot(a, b, dims):
    return lax.dot_general(a, b, (dims, ((), ())), preferred_element_type=F32)


def nn(a, b):
    return dot(a, b, ((1,), (0,)))


def nt(a, b):
    return dot(a, b, ((1,), (1,)))


def tn(a, b):
    return dot(a, b, ((0,), (0,)))


def add(left, right):
    return (left.astype(F32) + right.astype(F32)).astype(left.dtype)


def after(value, *earlier):
    return lax.optimization_barrier((value, earlier))[0]


def rms_inverse(x):
    return lax.rsqrt(jnp.mean(x * x, axis=-1, keepdims=True) + EPS)


def cost(flops, exps, *arrays):
    size = sum(a.size * a.dtype.itemsize for a in arrays)
    return pl.CostEstimate(flops=flops, transcendentals=exps, bytes_accessed=size)


class Links:
    def __init__(self, reps, shards):
        self.reps, self.shards = reps, shards
        self.core = lax.axis_index("rep") % 2
        self.shard = lax.axis_index("shard")
        self.bits = shards.bit_length() - 1
        even = [1 << i for i in range(self.bits)]
        odd = even[:2][::-1] + even[2:]
        self.steps = list(zip(even, odd))
        self.hops = []
        for piece in range(shards):
            sums = [0, 0]
            for i, step in enumerate(self.steps):
                if piece >> i & 1:
                    sums = [sums[0] ^ step[0], sums[1] ^ step[1]]
            self.hops.append(jnp.where(self.core == 0, sums[0], sums[1]))

    def move(self, value, target):
        pairs = []
        for r in range(self.reps):
            for s in range(self.shards):
                goal = target(r, s)
                if goal is not None:
                    pairs.append((r * self.shards + s, goal[0] * self.shards + goal[1]))
        return lax.ppermute(value, AXES, pairs)

    def step(self, value, i):
        return self.move(value, lambda r, s: (r, s ^ self.steps[i][r % 2]))

    def swap(self, value):
        return self.move(value, lambda r, s: (r ^ 1, s))

    def chain(self, value):
        chips = self.reps // 2
        place = lax.axis_index("rep") // 2
        span = 1
        if chips % 4 == 0:
            inward, outward, middle = {0: 1, 3: 2}, {1: 0, 2: 3}, {1: 2, 2: 1}

            def along(value, table):
                def target(r, s):
                    chip = r // 2
                    if chip % 4 not in table:
                        return None
                    return ((chip - chip % 4 + table[chip % 4]) * 2 + r % 2, s)

                return self.move(value, target)

            value = add(value, along(value, inward))
            value = add(value, along(value, middle))
            back = along(value, outward)
            inner = (place % 4 == 1) | (place % 4 == 2)
            value = jnp.where(inner, value, back)
            span = 4
        while span < chips:
            value = add(value, self.move(value, lambda r, s: (r ^ (2 * span), s)))
            span *= 2
        return value

    def spread(self, value):
        pieces = [value]
        for i in range(self.bits):
            pieces = pieces + [self.step(piece, i) for piece in pieces]
        return pieces

    def collect(self, pieces):
        for i in reversed(range(self.bits)):
            keep = 1 << i
            pieces = [add(pieces[t], self.step(pieces[t + keep], i)) for t in range(keep)]
        return pieces[0]

    def twin(self, piece):
        return piece if self.bits < 2 else piece >> 2 << 2 | (piece & 1) << 1 | (piece >> 1 & 1)

    def half_rows(self, rows):
        half = -(-rows // 32) * 16
        return half, self.core * (rows - half), (1 - self.core) * (rows - half)

    def gather_rows(self, shard_value):
        rows = shard_value.shape[0]
        half, first, second = self.half_rows(rows)
        mine = lax.dynamic_slice_in_dim(shard_value, first, half, 0)
        pieces = self.spread(mine)[1:]
        others = [self.swap(piece) for piece in pieces]
        starts = [self.shard * rows]
        starts += [(self.shard ^ hop) * rows + first for hop in self.hops[1:]]
        starts += [
            (self.shard ^ self.hops[self.twin(t)]) * rows + second for t in range(1, self.shards)
        ]
        return pieces, (shard_value, *pieces, *others), starts, rows * self.shards

    def gather_pair(self, left, right):
        rows = left.shape[0]
        mine = jnp.where(self.core == 0, left, right)
        pieces = self.spread(mine)[1:]
        others = [self.swap(piece) for piece in pieces]
        whole = rows * self.shards
        first, second = self.core * whole, (1 - self.core) * whole
        starts = [self.shard * rows, whole + self.shard * rows]
        starts += [(self.shard ^ hop) * rows + first for hop in self.hops[1:]]
        starts += [
            (self.shard ^ self.hops[self.twin(t)]) * rows + second for t in range(1, self.shards)
        ]
        return pieces, (left, right, *pieces, *others), starts, 2 * whole

    def gather_small(self, value):
        pieces = jnp.stack(
            [
                value if hop == 0 else self.move(value, lambda r, s, hop=hop: (r, s ^ hop))
                for hop in range(self.shards)
            ]
        )
        order = self.shard ^ jnp.arange(self.shards)
        hit = (order[:, None] == jnp.arange(self.shards)[None, :])[:, :, None, None]
        pieces = jnp.sum(jnp.where(hit, pieces[None], 0), axis=1, dtype=value.dtype)
        return jnp.concatenate([pieces[j] for j in range(self.shards)], axis=-1)

    def reduce_owned(self, kept, given):
        received = self.swap(given)
        pieces = []
        for hop in self.hops:
            mine, theirs = (
                lax.dynamic_index_in_dim(part, self.shard ^ hop, 0, keepdims=False)
                for part in (kept, received)
            )
            pieces.append(add(mine, theirs))
        return self.collect(pieces)

    def reduce_rows(self, grad):
        rows = grad.shape[0] // self.shards
        half, first, second = self.half_rows(rows)
        parts = grad.astype(BF).reshape(self.shards, rows, grad.shape[1])
        kept = lax.dynamic_slice_in_dim(parts, first, half, 1)
        given = lax.dynamic_slice_in_dim(parts, second, half, 1)
        return self.reduce_owned(kept, given), rows

    def finish_rows(self, owned, rows):
        owned = self.chain(owned)
        other = self.swap(owned)
        low = jnp.where(self.core == 0, owned, other)
        high = jnp.where(self.core == 0, other, owned)
        half = owned.shape[0]
        return jnp.concatenate([low[: rows - half], high], axis=0).astype(F32)

    def finish_pair(self, owned):
        owned = self.chain(owned)
        other = self.swap(owned)
        left = jnp.where(self.core == 0, owned, other)
        right = jnp.where(self.core == 0, other, owned)
        return left.astype(F32), right.astype(F32)

    def reduce_small(self, value):
        summed = add(value, self.swap(value))
        for i in range(self.bits):
            summed = add(summed, self.step(summed, i))
        summed = self.chain(summed)
        width = value.shape[1] // self.shards
        return lax.dynamic_slice_in_dim(summed, self.shard * width, width, 1)


def assemble_kernel(at_once, starts_ref, *refs):
    count = (len(refs) - 2)
    pieces, whole, sems = refs[:count], refs[count], refs[count + 1]
    copies = []
    for i, piece in enumerate(pieces):
        start = pl.multiple_of(starts_ref[i], 16)
        copies.append(
            pltpu.make_async_copy(piece, whole.at[pl.ds(start, piece.shape[0]), :], sems.at[i])
        )
    if at_once:
        for copy in copies:
            copy.start()
        for copy in copies:
            copy.wait()
    else:
        for copy in copies:
            copy.start()
            copy.wait()


def assemble(gathered):
    _, pieces, starts, rows = gathered
    columns = pieces[0].shape[1]
    if any(piece.shape[0] % 16 for piece in pieces):
        whole = jnp.zeros((rows, columns), pieces[0].dtype)
        for piece, start in zip(pieces, starts):
            whole = lax.dynamic_update_slice(whole, piece, (start, 0))
        return whole
    out = jax.ShapeDtypeStruct((rows, columns), pieces[0].dtype)
    return pl.pallas_call(
        functools.partial(assemble_kernel, sum(p.shape[0] for p in pieces) == rows),
        grid_spec=pltpu.PrefetchScalarGridSpec(
            num_scalar_prefetch=1,
            grid=(1,),
            in_specs=[pl.BlockSpec(memory_space=pl.ANY)] * len(pieces),
            out_specs=pl.BlockSpec(memory_space=pl.ANY),
            scratch_shapes=[pltpu.SemaphoreType.DMA((len(pieces),))],
        ),
        out_shape=out,
        name="assemble",
        cost_estimate=cost(0, 0, out, out),
    )(jnp.stack([jnp.int32(start) for start in starts]), *pieces)


def head(ref, h):
    return ref[:, h * HEAD_SIZE : (h + 1) * HEAD_SIZE]


def widen(value, columns):
    n = value.shape[0]
    lane = lax.broadcasted_iota(jnp.int32, (n, HEAD_SIZE), 1)
    tail = jnp.zeros((n, HEAD_SIZE), F32)
    for c, column in enumerate(columns):
        tail = jnp.where(lane == c, column, tail)
    return jnp.concatenate([value, tail.astype(BF)], axis=1)


def split(column):
    high = column.astype(BF).astype(F32)
    middle = (column - high).astype(BF).astype(F32)
    return [high, middle, column - high - middle]


def attend_kernel(shards, seg_rows, q_ref, *refs):
    kv = refs[:shards]
    bias_ref = refs[shards]
    o_ref, lse_ref = refs[-2:]
    rows = q_ref.shape[0]
    i = lax.broadcasted_iota(jnp.int32, (rows, rows), 0)
    j = lax.broadcasted_iota(jnp.int32, (rows, rows), 1)
    same = (i // seg_rows) == (j // seg_rows)
    own = jnp.where(j > i, CLOSED, jnp.where(same, 0.0, bias_ref[0:1, :]))
    one = jnp.ones((rows, 1), F32)
    bias_columns = jnp.transpose(bias_ref[...])
    lse = jnp.zeros((rows, 128), F32)
    lane = lax.broadcasted_iota(jnp.int32, (rows, 128), 1)
    for g in range(KEY_VALUE_HEADS):
        keys, values = [], []
        for t in range(shards):
            keys.append(widen(head(kv[t], g), [bias_columns[:, t : t + 1]] if t else []))
            values.append(widen(head(kv[t], KEY_VALUE_HEADS + g), [one]))
        for h in range(g * GROUP, g * GROUP + GROUP):
            q = widen(head(q_ref, h), [one])
            scores = [nt(q, k) for k in keys]
            scores[0] = scores[0] + own
            peak = functools.reduce(jnp.maximum, scores)
            peak = jnp.max(peak, axis=1, keepdims=True)
            terms = [nn(jnp.exp(s - peak).astype(BF), v) for s, v in zip(scores, values)]
            mixed = sum(terms[1:], terms[0])
            total = mixed[:, HEAD_SIZE : HEAD_SIZE + 1]
            o_ref[:, h * HEAD_SIZE : (h + 1) * HEAD_SIZE] = (mixed[:, :HEAD_SIZE] / total).astype(BF)
            lse = jnp.where(lane == h, peak + jnp.log(total), lse)
    lse_ref[...] = lse


def attend_back_kernel(shards, seg_rows, q_ref, *refs):
    kv = refs[:shards]
    bias_ref, o_ref, do_ref, lse_ref, cos_ref, sin_ref = refs[shards : shards + 6]
    dq_ref = refs[-1 - shards]
    dkv = refs[-shards:]
    rows = q_ref.shape[0]
    i = lax.broadcasted_iota(jnp.int32, (rows, rows), 1)
    j = lax.broadcasted_iota(jnp.int32, (rows, rows), 0)
    bias_columns = jnp.transpose(bias_ref[...])
    same = (i // seg_rows) == (j // seg_rows)
    own_column = jnp.broadcast_to(bias_columns[:, 0:1], (rows, rows))
    own = jnp.where(j > i, CLOSED, jnp.where(same, 0.0, own_column))
    one, zero = jnp.ones((rows, 1), F32), jnp.zeros((rows, 1), F32)
    cosine, sine = cos_ref[...], sin_ref[...]
    for g in range(KEY_VALUE_HEADS):
        keys, values, turned = [], [], []
        for t in range(shards):
            k = head(kv[t], g)
            turned.append(jnp.transpose(k))
            keys.append(widen(k, [bias_columns[:, t : t + 1] if t else zero, one, one, one]))
            values.append(widen(head(kv[t], KEY_VALUE_HEADS + g), [one, one, one]))
        dk, dv = [None] * shards, [None] * shards
        for h in range(g * GROUP, g * GROUP + GROUP):
            q, do = head(q_ref, h), head(do_ref, h)
            centre = jnp.sum(head(o_ref, h).astype(F32) * do.astype(F32), axis=1, keepdims=True)
            q_wide = widen(q, [one] + split(-lse_ref[:, h : h + 1]))
            do_wide = widen(do, split(-centre))
            dq = None
            for t in range(shards):
                scores = nt(keys[t], q_wide)
                if t == 0:
                    scores = scores + own
                probs = jnp.exp(scores)
                ds = (probs * nt(values[t], do_wide)).astype(BF)
                v_term = nn(probs.astype(BF), do)
                k_term = nn(ds, q)
                q_term = nn(turned[t], ds)
                dv[t] = v_term if dv[t] is None else dv[t] + v_term
                dk[t] = k_term if dk[t] is None else dk[t] + k_term
                dq = q_term if dq is None else dq + q_term
            dq = dq * SCALE
            first, second = dq[:HALF_HEAD], dq[HALF_HEAD:]
            back = jnp.concatenate(
                [first * cosine + second * sine, second * cosine - first * sine], axis=0
            )
            dq_ref[:, h * HEAD_SIZE : (h + 1) * HEAD_SIZE] = jnp.transpose(back).astype(BF)
        for t in range(shards):
            dkv[t][:, g * HEAD_SIZE : (g + 1) * HEAD_SIZE] = dk[t].astype(BF)
            g_value = KEY_VALUE_HEADS + g
            dkv[t][:, g_value * HEAD_SIZE : (g_value + 1) * HEAD_SIZE] = dv[t].astype(BF)


def attend(m, rows, seg_rows, q, kv, bias, earlier):
    shards, tokens, width = len(kv), q.shape[0], q.shape[1]
    here = lambda w: pl.BlockSpec((rows, w), lambda i: (m, 0))
    whole = pl.BlockSpec((rows, 2 * KV_WIDTH), lambda i: (0, 0))
    outs = (jax.ShapeDtypeStruct((tokens, width), BF), jax.ShapeDtypeStruct((tokens, 128), F32))
    pairs = rows * rows * shards * QUERY_HEADS
    args = (q, *kv, bias, *earlier)
    return pl.pallas_call(
        functools.partial(attend_kernel, shards, seg_rows),
        grid=(1,),
        name="attend",
        in_specs=[here(width)]
        + [whole] * shards
        + [pl.BlockSpec((None,) + bias.shape[1:], lambda i: (m, 0, 0))]
        + [pl.BlockSpec(memory_space=pl.ANY)] * len(earlier),
        out_specs=(here(width), here(128)),
        out_shape=outs,
        input_output_aliases={shards + 2 + i: i for i in range(len(earlier))},
        cost_estimate=cost(16 * HEAD_SIZE * pairs, pairs, q),
        compiler_params=pltpu.CompilerParams(vmem_limit_bytes=VMEM_LIMIT),
    )(*args)


def attend_back(m, rows, seg_rows, q, kv, bias, o, do, lse, cosine, sine, earlier):
    shards, tokens, width = len(kv), q.shape[0], q.shape[1]
    here = lambda w: pl.BlockSpec((rows, w), lambda i: (m, 0))
    turned = pl.BlockSpec((HALF_HEAD, rows), lambda i: (0, m))
    whole = pl.BlockSpec((rows, 2 * KV_WIDTH), lambda i: (0, 0))
    outs = (jax.ShapeDtypeStruct((tokens, width), BF),)
    outs += (jax.ShapeDtypeStruct((rows, 2 * KV_WIDTH), BF),) * shards
    pairs = rows * rows * shards * QUERY_HEADS
    args = (q, *kv, bias, o, do, lse, cosine, sine, *earlier)
    return pl.pallas_call(
        functools.partial(attend_back_kernel, shards, seg_rows),
        grid=(1,),
        name="attend_back",
        in_specs=[here(width)]
        + [whole] * shards
        + [pl.BlockSpec((None,) + bias.shape[1:], lambda i: (m, 0, 0))]
        + [here(width), here(width), here(128), turned, turned]
        + [pl.BlockSpec(memory_space=pl.ANY)] * len(earlier),
        out_specs=(here(width),) + (whole,) * shards,
        out_shape=outs,
        input_output_aliases={shards + 7 + i: i for i in range(len(earlier))},
        cost_estimate=cost(40 * HEAD_SIZE * pairs, pairs, q),
        compiler_params=pltpu.CompilerParams(vmem_limit_bytes=VMEM_LIMIT),
    )(*args)


def rotate(vectors, cosine, sine, heads, inverse):
    shaped = vectors.reshape(vectors.shape[0], heads, HEAD_SIZE)
    first = shaped[..., :HALF_HEAD]
    second = shaped[..., HALF_HEAD:]
    cosine, sine = cosine[:, None, :], sine[:, None, :]
    if inverse:
        sine = -sine
    turned = jnp.concatenate(
        [first * cosine - second * sine, second * cosine + first * sine], axis=-1
    )
    return turned.reshape(vectors.shape[0], heads * HEAD_SIZE)


def local(
    block_input,
    parent_ids,
    w_query,
    key_weight,
    value_weight,
    w_output,
    w_gate,
    w_up,
    w_down,
    norm_first,
    norm_second,
    out_cotangent,
):
    micro, rows, width = block_input.shape
    shards = lax.axis_size("shard")
    links = Links(lax.axis_size("rep"), shards)
    tree = rows * shards
    segs = parent_ids.shape[2]
    seg_rows = tree // segs
    tokens = micro * rows
    hidden = w_gate.shape[1]

    gains = links.gather_small(jnp.stack([norm_first, norm_second])).astype(F32)
    gain_one, gain_two = gains[0:1], gains[1:2]
    attention_got = links.gather_pair(
        jnp.concatenate([w_query, key_weight], axis=1),
        jnp.concatenate([w_output, value_weight], axis=1),
    )
    attention_whole = assemble(attention_got)
    full_qk, full_output, full_value = (
        attention_whole[:width],
        attention_whole[width:, :width],
        attention_whole[width:, width:],
    )
    pair_got = links.gather_pair(*after((w_gate, w_up), attention_got[0]))
    down_got = links.gather_rows(after(w_down, pair_got[0]))

    parents = parent_ids[:, 0]
    seg = jnp.arange(segs)
    after_parent = jnp.concatenate([parents[:, 1:], jnp.full((micro, 1), -1, parents.dtype)], axis=1)
    on_path = (seg % 2 == 0)[None] | (after_parent == seg[None])
    below = (seg[None, :] < seg[:, None])[None]
    depth = jnp.sum(jnp.where(below, on_path.astype(F32)[:, None, :], 0.0), axis=-1)

    def row_numbers(hop):
        return (links.shard ^ hop) * rows + jnp.arange(rows)

    def pick(table, numbers):
        hit = (numbers // seg_rows)[..., None] == seg
        return jnp.sum(jnp.where(hit[None], table.reshape(micro, *(1,) * numbers.ndim, segs), 0), axis=-1)

    my_rows = row_numbers(0)
    positions = pick(depth, my_rows) * seg_rows + (my_rows % seg_rows).astype(F32)
    freqs = jnp.exp(-math.log(10000.0) * jnp.arange(HALF_HEAD, dtype=F32) * (2.0 / HEAD_SIZE))
    angles = freqs[:, None] * positions.reshape(tokens)[None, :]
    cosine_t, sine_t = jnp.cos(angles), jnp.sin(angles)
    cosine, sine = cosine_t.T, sine_t.T
    key_rows = jnp.stack([row_numbers(hop) for hop in links.hops])
    open_key = (pick(on_path.astype(F32), key_rows) > 0.5) & (
        (key_rows < links.shard * rows) | (jnp.arange(shards) == 0)[:, None]
    )
    bias = jnp.where(open_key, 0.0, CLOSED)
    bias = jnp.pad(bias, ((0, 0), (0, 8 - shards), (0, 0)))

    inputs = block_input.reshape(tokens, width).astype(F32)
    cotangent = out_cotangent.reshape(tokens, width)
    inv_first = rms_inverse(inputs)
    normed_first = inputs * inv_first
    act_first = (normed_first * gain_one).astype(BF)
    linear = nn(act_first, full_qk)
    keys = rotate(linear[:, width:], cosine, sine, KEY_VALUE_HEADS, False)
    kv = jnp.concatenate([keys, nn(act_first, full_value)], axis=1).astype(BF)
    kv_all = [links.spread(kv[m * rows : (m + 1) * rows]) for m in range(micro)]
    queries = (rotate(linear[:, :width], cosine, sine, QUERY_HEADS, False) * SCALE).astype(BF)
    attended = ()
    for m in range(micro):
        attended = attend(m, rows, seg_rows, queries, kv_all[m], bias, attended)
    attn, lse = attended

    resid = inputs + nn(attn, full_output)
    inv_second = rms_inverse(resid)
    normed_second = resid * inv_second
    act_second = (normed_second * gain_two).astype(BF)
    pair_whole = assemble(pair_got)
    full_gate, full_upper = pair_whole[:width], pair_whole[width:]
    full_down = assemble(down_got)
    gate = nn(act_second, full_gate)
    upper = nn(act_second, full_upper)
    sigmoid = jax.nn.sigmoid(gate)
    silu = gate * sigmoid
    inner = (silu * upper).astype(BF)
    block_out = (resid + nn(inner, full_down)).astype(BF)

    down_owned, down_rows = links.reduce_rows(tn(inner, cotangent))
    d_inner = nt(cotangent, full_down)
    d_gate = (d_inner * upper * sigmoid * (1.0 + gate * (1.0 - sigmoid))).astype(BF)
    d_upper = (d_inner * silu).astype(BF)
    even = links.core == 0
    kept, given = (
        tn(act_second, part).astype(BF).reshape(shards, width // shards, hidden)
        for part in (jnp.where(even, d_gate, d_upper), jnp.where(even, d_upper, d_gate))
    )
    pair_owned = links.reduce_owned(kept, given)
    d_act_second = nt(d_gate, full_gate) + nt(d_upper, full_upper)
    gain_two_sum = jnp.sum(d_act_second * normed_second, axis=0)
    d_normed = d_act_second * gain_two
    d_resid = cotangent.astype(F32) + inv_second * (
        d_normed - normed_second * jnp.mean(d_normed * normed_second, axis=-1, keepdims=True)
    )
    d_resid_low = d_resid.astype(BF)
    output_owned, output_rows = links.reduce_rows(tn(attn, d_resid_low))
    d_attn = nt(d_resid_low, full_output).astype(BF)

    d_queries, d_kv = (), []
    for m in range(micro):
        d_queries, *pieces = attend_back(
            m, rows, seg_rows, queries, kv_all[m], bias, attn, d_attn, lse, cosine_t, sine_t, d_queries
        )
        d_queries = (d_queries,)
        d_kv.append(links.collect(pieces))
    d_kv = jnp.concatenate(d_kv, axis=0).astype(F32)
    d_key_low = rotate(d_kv[:, :KV_WIDTH], cosine, sine, KEY_VALUE_HEADS, True).astype(BF)
    d_qk_low = jnp.concatenate([d_queries[0], d_key_low], axis=1)
    d_value_low = d_kv[:, KV_WIDTH:].astype(BF)
    qkv_owned, qkv_rows = links.reduce_rows(
        tn(act_first, jnp.concatenate([d_qk_low, d_value_low], axis=1))
    )
    d_act_first = nt(d_qk_low, full_qk) + nt(d_value_low, full_value)
    gain_one_sum = jnp.sum(d_act_first * normed_first, axis=0)
    d_normed = d_act_first * gain_one
    d_input = d_resid + inv_first * (
        d_normed - normed_first * jnp.mean(d_normed * normed_first, axis=-1, keepdims=True)
    )
    gain_sums = links.reduce_small(jnp.stack([gain_one_sum, gain_two_sum]))
    grad_down = links.finish_rows(down_owned, down_rows)
    grad_gate, grad_upper = links.finish_pair(pair_owned)
    grad_output = links.finish_rows(output_owned, output_rows)
    grad_qkv = links.finish_rows(qkv_owned, qkv_rows)
    return (
        block_out.reshape(micro, rows, width),
        d_input.astype(BF).reshape(micro, rows, width),
        grad_qkv[:, :width],
        grad_qkv[:, width : width + KV_WIDTH],
        grad_qkv[:, width + KV_WIDTH :],
        grad_output,
        grad_gate,
        grad_upper,
        grad_down,
        gain_sums[0],
        gain_sums[1],
    )


def solution(mesh):
    rows = P(None, AXES, None)
    weight, gain = P("shard", None), P("shard")
    return jax.shard_map(
        local,
        mesh=mesh,
        in_specs=(rows, P(None, "rep", None)) + (weight,) * 7 + (gain, gain, rows),
        out_specs=(rows, rows) + (weight,) * 7 + (gain, gain),
        check_vma=False,
    )
```

```python
import functools
import math

import jax
import jax.numpy as jnp
from jax import lax
from jax.experimental import pallas as pl
from jax.experimental.pallas import tpu as pltpu
from jax.sharding import PartitionSpec as P

QUERY_HEADS = 15
KEY_VALUE_HEADS = 5
HEAD_SIZE = 64
HALF_HEAD = HEAD_SIZE // 2
GROUP = QUERY_HEADS // KEY_VALUE_HEADS
KV_WIDTH = KEY_VALUE_HEADS * HEAD_SIZE
SCALE = HEAD_SIZE ** (-0.5)
EPS = 1e-05
AXES = ("rep", "shard")
BF = jnp.bfloat16
F32 = jnp.float32
CLOSED = -1e30
VMEM_LIMIT = 48 << 20
VMEM_MOST = 60 << 20


def dot(a, b, dims):
    return lax.dot_general(a, b, (dims, ((), ())), preferred_element_type=F32)


def nn(a, b):
    return dot(a, b, ((1,), (0,)))


def nt(a, b):
    return dot(a, b, ((1,), (1,)))


def tn(a, b):
    return dot(a, b, ((0,), (0,)))


def add(left, right):
    return (left.astype(F32) + right.astype(F32)).astype(left.dtype)


def after(value, *earlier):
    return lax.optimization_barrier((value, earlier))[0]


def rms_inverse(x):
    return lax.rsqrt(jnp.mean(x * x, axis=-1, keepdims=True) + EPS)


def cost(flops, exps, *arrays):
    size = sum(a.size * a.dtype.itemsize for a in arrays)
    return pl.CostEstimate(flops=flops, transcendentals=exps, bytes_accessed=size)


class Links:
    def __init__(self, reps, shards):
        self.reps, self.shards = reps, shards
        self.core = lax.axis_index("rep") % 2
        self.shard = lax.axis_index("shard")
        self.bits = shards.bit_length() - 1
        even = [1 << i for i in range(self.bits)]
        odd = even[:2][::-1] + even[2:]
        self.steps = list(zip(even, odd))
        self.hops = []
        for piece in range(shards):
            sums = [0, 0]
            for i, step in enumerate(self.steps):
                if piece >> i & 1:
                    sums = [sums[0] ^ step[0], sums[1] ^ step[1]]
            self.hops.append(jnp.where(self.core == 0, sums[0], sums[1]))

    def move(self, value, target):
        pairs = []
        for r in range(self.reps):
            for s in range(self.shards):
                goal = target(r, s)
                if goal is not None:
                    pairs.append((r * self.shards + s, goal[0] * self.shards + goal[1]))
        return lax.ppermute(value, AXES, pairs)

    def step(self, value, i):
        return self.move(value, lambda r, s: (r, s ^ self.steps[i][r % 2]))

    def swap(self, value):
        return self.move(value, lambda r, s: (r ^ 1, s))

    def chain(self, value):
        chips = self.reps // 2
        place = lax.axis_index("rep") // 2
        span = 1
        if chips % 4 == 0:
            inward, outward, middle = {0: 1, 3: 2}, {1: 0, 2: 3}, {1: 2, 2: 1}

            def along(value, table):
                def target(r, s):
                    chip = r // 2
                    if chip % 4 not in table:
                        return None
                    return ((chip - chip % 4 + table[chip % 4]) * 2 + r % 2, s)

                return self.move(value, target)

            value = add(value, along(value, inward))
            value = add(value, along(value, middle))
            back = along(value, outward)
            inner = (place % 4 == 1) | (place % 4 == 2)
            value = jnp.where(inner, value, back)
            span = 4
        while span < chips:
            value = add(value, self.move(value, lambda r, s: (r ^ (2 * span), s)))
            span *= 2
        return value

    def spread(self, value):
        pieces = [value]
        for i in range(self.bits):
            pieces = pieces + [self.step(piece, i) for piece in pieces]
        return pieces

    def collect(self, pieces):
        for i in reversed(range(self.bits)):
            keep = 1 << i
            pieces = [add(pieces[t], self.step(pieces[t + keep], i)) for t in range(keep)]
        return pieces[0]

    def twin(self, piece):
        return piece if self.bits < 2 else piece >> 2 << 2 | (piece & 1) << 1 | (piece >> 1 & 1)

    def gather_rows(self, shard_value):
        rows = shard_value.shape[0]
        half = rows // 2
        mine = lax.dynamic_slice_in_dim(shard_value, self.core * half, half, 0)
        direct = self.spread(mine)[1:]
        starts = [self.shard * rows]
        starts += [(self.shard ^ hop) * rows + self.core * half for hop in self.hops[1:]]
        starts += [
            (self.shard ^ self.hops[self.twin(t)]) * rows + (1 - self.core) * half
            for t in range(1, self.shards)
        ]
        return direct, *joined((shard_value, *direct, *map(self.swap, direct)), starts)

    def gather_pair(self, left, right):
        rows = left.shape[0]
        mine = jnp.where(self.core == 0, left, right)
        direct = self.spread(mine)[1:]
        whole = rows * self.shards
        first, second = self.core * whole, (1 - self.core) * whole
        starts = [self.shard * rows, whole + self.shard * rows]
        starts += [(self.shard ^ hop) * rows + first for hop in self.hops[1:]]
        starts += [
            (self.shard ^ self.hops[self.twin(t)]) * rows + second for t in range(1, self.shards)
        ]
        return direct, *joined((left, right, *direct, *map(self.swap, direct)), starts)

    def gather_small(self, value):
        pieces = jnp.stack(
            [
                value if hop == 0 else self.move(value, lambda r, s, hop=hop: (r, s ^ hop))
                for hop in range(self.shards)
            ]
        )
        order = self.shard ^ jnp.arange(self.shards)
        hit = (order[:, None] == jnp.arange(self.shards)[None, :])[:, :, None, None]
        pieces = jnp.sum(jnp.where(hit, pieces[None], 0), axis=1, dtype=value.dtype)
        return jnp.concatenate([pieces[j] for j in range(self.shards)], axis=-1)

    def half_rows(self, rows):
        half = -(-rows // 32) * 16
        return half, self.core * (rows - half), (1 - self.core) * (rows - half)

    def order(self, scale, mine, theirs):
        kept = [(self.shard ^ hop) * scale + mine for hop in self.hops]
        given = [(self.shard ^ self.hops[self.twin(t)]) * scale + theirs for t in range(self.shards)]
        return kept, given

    def reduce_owned(self, kept, received):
        block = kept.shape[0] // self.shards
        cut = lambda value, t: value[t * block : (t + 1) * block]
        return self.collect([add(cut(kept, t), cut(received, t)) for t in range(self.shards)])

    def finish_rows(self, owned, other, rows):
        low = jnp.where(self.core == 0, owned, other)
        high = jnp.where(self.core == 0, other, owned)
        return jnp.concatenate([low[: rows - owned.shape[0]], high], axis=0).astype(F32)

    def finish_pair(self, owned, other):
        left = jnp.where(self.core == 0, owned, other)
        right = jnp.where(self.core == 0, other, owned)
        return left.astype(F32), right.astype(F32)

    def reduce_small(self, value):
        summed = add(value, self.swap(value))
        for i in range(self.bits):
            summed = add(summed, self.step(summed, i))
        summed = self.chain(summed)
        width = value.shape[1] // self.shards
        return lax.dynamic_slice_in_dim(summed, self.shard * width, width, 1)


def joined(pieces, starts):
    if any(piece.shape[0] % 16 for piece in pieces):
        rows = sum(piece.shape[0] for piece in pieces)
        whole = jnp.zeros((rows, pieces[0].shape[1]), pieces[0].dtype)
        for piece, start in zip(pieces, starts):
            whole = lax.dynamic_update_slice(whole, piece, (start, 0))
        pieces, starts = (whole,), [0]
    return pieces, numbers(starts)


def numbers(values):
    return jnp.stack([jnp.asarray(value, jnp.int32) for value in values])


def joined_shape(pieces):
    return sum(piece.shape[0] for piece in pieces), pieces[0].shape[1]


def load(pieces, starts_ref, whole, sems):
    copies = []
    for i, piece in enumerate(pieces):
        start = pl.multiple_of(starts_ref[i], 16)
        copies.append(
            pltpu.make_async_copy(piece, whole.at[pl.ds(start, piece.shape[0]), :], sems.at[i])
        )
        copies[-1].start()
    return copies


def wait(copies):
    for copy in copies:
        copy.wait()


IN_VMEM = pl.BlockSpec(memory_space=pltpu.VMEM)
IN_SMEM = pl.BlockSpec(memory_space=pltpu.SMEM)
ANYWHERE = pl.BlockSpec(memory_space=pl.ANY)


def turn(chunk, cosine, sine):
    lane = lax.broadcasted_iota(jnp.int32, chunk.shape, 1)
    partner = jnp.where(
        lane % HEAD_SIZE < HALF_HEAD,
        pltpu.roll(chunk, 128 - HALF_HEAD, 1),
        pltpu.roll(chunk, HALF_HEAD, 1),
    )
    return chunk * cosine + partner * sine


def project_kernel(count, starts_ref, x_ref, gains_ref, cos_ref, sin_ref, *refs):
    pieces = refs[:count]
    q_ref, kv_ref, act_ref, whole, sems = refs[count:]
    copies = load(pieces, starts_ref, whole, sems)
    x = x_ref[...].astype(F32)
    width = x.shape[1]
    act_ref[...] = (x * rms_inverse(x) * gains_ref[0:1, :]).astype(BF)
    wait(copies)
    act = act_ref[...]
    cosine, sine = cos_ref[...], sin_ref[...]
    for first in range(0, width + KV_WIDTH, 256):
        linear = nn(act, whole[:width, first : first + 256])
        for at in range(first, first + 256, 128):
            chunk = turn(linear[:, at - first : at - first + 128], cosine, sine)
            if at + 128 <= width:
                q_ref[:, at : at + 128] = (chunk * SCALE).astype(BF)
            elif at < width:
                q_ref[:, at:width] = (chunk[:, : width - at] * SCALE).astype(BF)
                kv_ref[:, : at + 128 - width] = chunk[:, width - at :].astype(BF)
            else:
                kv_ref[:, at - width : at - width + 128] = chunk.astype(BF)
    kv_ref[:, KV_WIDTH:] = nn(act, whole[width:, width:]).astype(BF)


def project(x, gains, cosine, sine, pieces, starts):
    tokens, width = x.shape
    outs = (
        jax.ShapeDtypeStruct((tokens, width), BF),
        jax.ShapeDtypeStruct((tokens, 2 * KV_WIDTH), BF),
        jax.ShapeDtypeStruct((tokens, width), BF),
    )
    return pl.pallas_call(
        functools.partial(project_kernel, len(pieces)),
        name="project",
        in_specs=[IN_SMEM] + [IN_VMEM] * 4 + [ANYWHERE] * len(pieces),
        out_specs=(IN_VMEM,) * 3,
        out_shape=outs,
        scratch_shapes=[
            pltpu.VMEM(joined_shape(pieces), BF),
            pltpu.SemaphoreType.DMA((len(pieces),)),
        ],
        cost_estimate=cost(2 * tokens * width * (width + 2 * KV_WIDTH), 0, x, *outs, *pieces),
        compiler_params=pltpu.CompilerParams(vmem_limit_bytes=VMEM_LIMIT),
    )(starts, x, gains, cosine, sine, *pieces)


def feed_kernel(counts, s0_ref, s1_ref, s2_ref, x_ref, attn_ref, dy_ref, gains_ref, *refs):
    total = sum(counts)
    attention_pieces = refs[: counts[0]]
    pair_pieces = refs[counts[0] : counts[0] + counts[1]]
    down_pieces = refs[counts[0] + counts[1] : total]
    out_ref, inner_ref, slopes_ref, act_ref, dres_ref, low_ref, dattn_ref, gain_ref = refs[total : total + 8]
    w_attn, w_pair, w_down, resid_ref, dact_ref, sems0, sems1, sems2 = refs[total + 8 :]
    attention_copies = load(attention_pieces, s0_ref, w_attn, sems0)
    pair_copies = load(pair_pieces, s1_ref, w_pair, sems1)
    down_copies = load(down_pieces, s2_ref, w_down, sems2)
    tokens, width = x_ref.shape
    hidden = w_pair.shape[1]
    tile = hidden // 5
    gain = gains_ref[1:2, :]
    wait(attention_copies)
    w_output = w_attn[width:, :width]
    resid = x_ref[...].astype(F32) + nn(attn_ref[...], w_output)
    resid_ref[...] = resid
    dres_ref[...] = resid
    root = rms_inverse(resid)
    act_ref[...] = (resid * root * gain).astype(BF)
    wait(pair_copies)
    wait(down_copies)
    act, dy = act_ref[...], dy_ref[...]
    for first in range(0, hidden, tile):
        here = slice(first, first + tile)
        gate = nn(act, w_pair[:width, here])
        upper = nn(act, w_pair[width:, here])
        d_inner = nt(dy, w_down[here, :])
        sigmoid = 1.0 / (1.0 + jnp.exp(-gate))
        silu = gate * sigmoid
        inner = (silu * upper).astype(BF)
        inner_ref[:, here] = inner
        d_gate = (d_inner * upper * sigmoid * (1.0 + gate * (1.0 - sigmoid))).astype(BF)
        d_upper = (d_inner * silu).astype(BF)
        slopes_ref[0, :, here] = d_gate
        slopes_ref[1, :, here] = d_upper
        out = nn(inner, w_down[here, :])
        d_act = nt(d_gate, w_pair[:width, here]) + nt(d_upper, w_pair[width:, here])
        resid_ref[...] += out
        if first == 0:
            dact_ref[...] = d_act
        else:
            dact_ref[...] += d_act
    out_ref[...] = resid_ref[...].astype(BF)
    normed = dres_ref[...] * root
    d_act = dact_ref[...]
    gain_ref[...] = jnp.broadcast_to(jnp.sum(d_act * normed, axis=0, keepdims=True), gain_ref.shape)
    d_normed = d_act * gain
    d_resid = dy.astype(F32) + root * (
        d_normed - normed * jnp.mean(d_normed * normed, axis=-1, keepdims=True)
    )
    dres_ref[...] = d_resid
    low = d_resid.astype(BF)
    low_ref[...] = low
    dattn_ref[...] = nt(low, w_output).astype(BF)


def feed(x, attn, dy, gains, attention_got, pair_got, down_got):
    tokens, width = x.shape
    groups = [attention_got, pair_got, down_got]
    counts = [len(pieces) for pieces, _ in groups]
    shapes = [joined_shape(pieces) for pieces, _ in groups]
    hidden = shapes[1][1]
    outs = (
        jax.ShapeDtypeStruct((tokens, width), BF),
        jax.ShapeDtypeStruct((tokens, hidden), BF),
        jax.ShapeDtypeStruct((2, tokens, hidden), BF),
        jax.ShapeDtypeStruct((tokens, width), BF),
        jax.ShapeDtypeStruct((tokens, width), F32),
        jax.ShapeDtypeStruct((tokens, width), BF),
        jax.ShapeDtypeStruct((tokens, width), BF),
        jax.ShapeDtypeStruct((8, width), F32),
    )
    every = [piece for pieces, _ in groups for piece in pieces]
    return pl.pallas_call(
        functools.partial(feed_kernel, counts),
        name="feed",
        in_specs=[IN_SMEM] * 3 + [IN_VMEM] * 4 + [ANYWHERE] * len(every),
        out_specs=(IN_VMEM,) * 8,
        out_shape=outs,
        scratch_shapes=[pltpu.VMEM(shape, BF) for shape in shapes]
        + [pltpu.VMEM((tokens, width), F32)] * 2
        + [pltpu.SemaphoreType.DMA((count,)) for count in counts],
        cost_estimate=cost(
            2 * tokens * width * (6 * hidden + 3 * width), tokens * hidden, x, x, x, *outs, *every
        ),
        compiler_params=pltpu.CompilerParams(vmem_limit_bytes=VMEM_MOST),
    )(*(starts for _, starts in groups), x, attn, dy, gains, *every)


def weight_grad_kernel(parts, block, starts_ref, *refs):
    operands = refs[: 2 * len(parts)]
    out_ref = refs[2 * len(parts)]
    turned = refs[2 * len(parts) + 1 :]
    step = pl.program_id(0)

    @pl.when(step == 0)
    def _():
        for i in range(len(parts)):
            turned[i][...] = jnp.transpose(operands[2 * i][...])

    at = 0
    for i, rows in enumerate(parts):
        start = pl.multiple_of(starts_ref[1 + i * pl.num_programs(0) + step], 16)
        left = turned[i][pl.ds(start, rows), :]
        out_ref[at : at + rows, :] = nn(left, operands[2 * i + 1][...]).astype(BF)
        at += rows


def weight_grad(terms, column=0, columns=None, choice=0):
    count = len(terms[0][3])
    parts = [term[2] for term in terms]
    block = sum(parts)
    tokens = terms[0][0].shape[0]
    columns = columns or terms[0][1].shape[-1]
    if any(rows % 16 for rows in parts) or any(term[0].shape[1] // count % 16 for term in terms):
        made = []
        for left, right, rows, starts in terms:
            right = right if right.ndim == 2 else lax.dynamic_index_in_dim(right, choice, 0, keepdims=False)
            grad = tn(left, right[:, column * columns : (column + 1) * columns]).astype(BF)
            made.append([lax.dynamic_slice_in_dim(grad, start, rows, 0) for start in starts])
        return jnp.concatenate([part for group in zip(*made) for part in group], axis=0)
    in_specs, args, flops = [], [], 0
    for left, right, rows, starts in terms:
        in_specs.append(pl.BlockSpec(left.shape, lambda t, info: (0, 0)))
        if right.ndim == 2:
            in_specs.append(pl.BlockSpec((tokens, columns), lambda t, info: (0, column)))
        else:
            in_specs.append(pl.BlockSpec((None, tokens, columns), lambda t, info: (info[0], 0, column)))
        args += [left, right]
        flops += 2 * tokens * rows * count * columns
    out = jax.ShapeDtypeStruct((count * block, columns), BF)
    info = numbers([choice] + [start for term in terms for start in term[3]])
    return pl.pallas_call(
        functools.partial(weight_grad_kernel, parts, block),
        grid_spec=pltpu.PrefetchScalarGridSpec(
            num_scalar_prefetch=1,
            grid=(count,),
            in_specs=in_specs,
            out_specs=pl.BlockSpec((block, columns), lambda t, info: (t, 0)),
            scratch_shapes=[pltpu.VMEM((term[0].shape[1], tokens), BF) for term in terms],
        ),
        out_shape=out,
        name="weight_grad",
        cost_estimate=cost(flops, 0, out, *args),
        compiler_params=pltpu.CompilerParams(vmem_limit_bytes=VMEM_LIMIT),
    )(info, *args)


def finish_kernel(count, starts_ref, x_ref, low_ref, kv_ref, dres_ref, gains_ref, *refs):
    pieces = refs[:count]
    dx_ref, gain_ref, whole, sems = refs[count:]
    copies = load(pieces, starts_ref, whole, sems)
    x = x_ref[...].astype(F32)
    width = x.shape[1]
    root = rms_inverse(x)
    normed = x * root
    wait(copies)
    d_act = nt(low_ref[...], whole[:width, :width])
    d_act += nt(kv_ref[:, :KV_WIDTH], whole[:width, width:])
    d_act += nt(kv_ref[:, KV_WIDTH:], whole[width:, width:])
    gain_ref[...] = jnp.broadcast_to(jnp.sum(d_act * normed, axis=0, keepdims=True), gain_ref.shape)
    d_normed = d_act * gains_ref[0:1, :]
    dx_ref[...] = (
        dres_ref[...]
        + root * (d_normed - normed * jnp.mean(d_normed * normed, axis=-1, keepdims=True))
    ).astype(BF)


def finish(x, low, kv, dres, gains, pieces, starts):
    tokens, width = x.shape
    outs = (jax.ShapeDtypeStruct((tokens, width), BF), jax.ShapeDtypeStruct((8, width), F32))
    return pl.pallas_call(
        functools.partial(finish_kernel, len(pieces)),
        name="finish",
        in_specs=[IN_SMEM] + [IN_VMEM] * 5 + [ANYWHERE] * len(pieces),
        out_specs=(IN_VMEM,) * 2,
        out_shape=outs,
        scratch_shapes=[
            pltpu.VMEM(joined_shape(pieces), BF),
            pltpu.SemaphoreType.DMA((len(pieces),)),
        ],
        cost_estimate=cost(2 * tokens * width * (width + 2 * KV_WIDTH), 0, x, low, dres, *pieces),
        compiler_params=pltpu.CompilerParams(vmem_limit_bytes=VMEM_LIMIT),
    )(starts, x, low, kv, dres, gains, *pieces)


def turn_back_kernel(*refs):
    parts = refs[:-3]
    cos_ref, sin_ref, out_ref = refs[-3:]
    at = 0
    for part in parts:
        here = slice(at, at + part.shape[0])
        for first in range(0, KV_WIDTH, 128):
            chunk = part[:, first : first + 128].astype(F32)
            chunk = turn(chunk, cos_ref[here, :], -sin_ref[here, :]).astype(BF)
            last = min(first + 128, KV_WIDTH)
            out_ref[here, first:last] = chunk[:, : last - first]
        out_ref[here, KV_WIDTH:] = part[:, KV_WIDTH:]
        at += part.shape[0]


def turn_back(parts, cosine, sine):
    out = jax.ShapeDtypeStruct((sum(part.shape[0] for part in parts), 2 * KV_WIDTH), BF)
    return pl.pallas_call(
        turn_back_kernel,
        name="turn_back",
        in_specs=[IN_VMEM] * (len(parts) + 2),
        out_specs=IN_VMEM,
        out_shape=out,
        cost_estimate=cost(0, 0, out, out),
        compiler_params=pltpu.CompilerParams(vmem_limit_bytes=VMEM_LIMIT),
    )(*parts, cosine, sine)


def head(ref, h):
    return ref[:, h * HEAD_SIZE : (h + 1) * HEAD_SIZE]


def widen(value, columns):
    n = value.shape[0]
    lane = lax.broadcasted_iota(jnp.int32, (n, HEAD_SIZE), 1)
    tail = jnp.zeros((n, HEAD_SIZE), F32)
    for c, column in enumerate(columns):
        tail = jnp.where(lane == c, column, tail)
    return jnp.concatenate([value, tail.astype(BF)], axis=1)


def split(column):
    high = column.astype(BF).astype(F32)
    middle = (column - high).astype(BF).astype(F32)
    return [high, middle, column - high - middle]


def attend_kernel(shards, seg_rows, q_ref, *refs):
    kv = refs[:shards]
    bias_ref = refs[shards]
    o_ref, lse_ref = refs[-2:]
    rows = q_ref.shape[0]
    i = lax.broadcasted_iota(jnp.int32, (rows, rows), 0)
    j = lax.broadcasted_iota(jnp.int32, (rows, rows), 1)
    same = (i // seg_rows) == (j // seg_rows)
    own = jnp.where(j > i, CLOSED, jnp.where(same, 0.0, bias_ref[0:1, :]))
    one = jnp.ones((rows, 1), F32)
    bias_columns = jnp.transpose(bias_ref[...])
    lse = jnp.zeros((rows, 128), F32)
    lane = lax.broadcasted_iota(jnp.int32, (rows, 128), 1)
    for g in range(KEY_VALUE_HEADS):
        keys, values = [], []
        for t in range(shards):
            keys.append(widen(head(kv[t], g), [bias_columns[:, t : t + 1]] if t else []))
            values.append(widen(head(kv[t], KEY_VALUE_HEADS + g), [one]))
        for h in range(g * GROUP, g * GROUP + GROUP):
            q = widen(head(q_ref, h), [one])
            scores = [nt(q, k) for k in keys]
            scores[0] = scores[0] + own
            peak = functools.reduce(jnp.maximum, scores)
            peak = jnp.max(peak, axis=1, keepdims=True)
            terms = [nn(jnp.exp(s - peak).astype(BF), v) for s, v in zip(scores, values)]
            mixed = sum(terms[1:], terms[0])
            total = mixed[:, HEAD_SIZE : HEAD_SIZE + 1]
            o_ref[:, h * HEAD_SIZE : (h + 1) * HEAD_SIZE] = (mixed[:, :HEAD_SIZE] / total).astype(BF)
            lse = jnp.where(lane == h, peak + jnp.log(total), lse)
    lse_ref[...] = lse


def attend_back_kernel(shards, seg_rows, q_ref, *refs):
    kv = refs[:shards]
    bias_ref, o_ref, do_ref, lse_ref, cos_ref, sin_ref = refs[shards : shards + 6]
    dq_ref = refs[-1 - shards]
    dkv = refs[-shards:]
    rows = q_ref.shape[0]
    i = lax.broadcasted_iota(jnp.int32, (rows, rows), 1)
    j = lax.broadcasted_iota(jnp.int32, (rows, rows), 0)
    bias_columns = jnp.transpose(bias_ref[...])
    same = (i // seg_rows) == (j // seg_rows)
    own_column = jnp.broadcast_to(bias_columns[:, 0:1], (rows, rows))
    own = jnp.where(j > i, CLOSED, jnp.where(same, 0.0, own_column))
    one, zero = jnp.ones((rows, 1), F32), jnp.zeros((rows, 1), F32)
    cosine, sine = cos_ref[...], sin_ref[...]
    for g in range(KEY_VALUE_HEADS):
        keys, values, turned = [], [], []
        for t in range(shards):
            k = head(kv[t], g)
            turned.append(jnp.transpose(k))
            keys.append(widen(k, [bias_columns[:, t : t + 1] if t else zero, one, one, one]))
            values.append(widen(head(kv[t], KEY_VALUE_HEADS + g), [one, one, one]))
        dk, dv = [None] * shards, [None] * shards
        for h in range(g * GROUP, g * GROUP + GROUP):
            q, do = head(q_ref, h), head(do_ref, h)
            centre = jnp.sum(head(o_ref, h).astype(F32) * do.astype(F32), axis=1, keepdims=True)
            q_wide = widen(q, [one] + split(-lse_ref[:, h : h + 1]))
            do_wide = widen(do, split(-centre))
            dq = None
            for t in range(shards):
                scores = nt(keys[t], q_wide)
                if t == 0:
                    scores = scores + own
                probs = jnp.exp(scores)
                ds = (probs * nt(values[t], do_wide)).astype(BF)
                v_term = nn(probs.astype(BF), do)
                k_term = nn(ds, q)
                q_term = nn(turned[t], ds)
                dv[t] = v_term if dv[t] is None else dv[t] + v_term
                dk[t] = k_term if dk[t] is None else dk[t] + k_term
                dq = q_term if dq is None else dq + q_term
            dq = dq * SCALE
            first, second = dq[:HALF_HEAD], dq[HALF_HEAD:]
            back = jnp.concatenate(
                [first * cosine + second * sine, second * cosine - first * sine], axis=0
            )
            dq_ref[:, h * HEAD_SIZE : (h + 1) * HEAD_SIZE] = jnp.transpose(back).astype(BF)
        for t in range(shards):
            dkv[t][:, g * HEAD_SIZE : (g + 1) * HEAD_SIZE] = dk[t].astype(BF)
            g_value = KEY_VALUE_HEADS + g
            dkv[t][:, g_value * HEAD_SIZE : (g_value + 1) * HEAD_SIZE] = dv[t].astype(BF)


def attend(m, rows, seg_rows, q, kv, bias, earlier):
    shards, tokens, width = len(kv), q.shape[0], q.shape[1]
    here = lambda w: pl.BlockSpec((rows, w), lambda i: (m, 0))
    whole = pl.BlockSpec((rows, 2 * KV_WIDTH), lambda i: (0, 0))
    outs = (jax.ShapeDtypeStruct((tokens, width), BF), jax.ShapeDtypeStruct((tokens, 128), F32))
    pairs = rows * rows * shards * QUERY_HEADS
    args = (q, *kv, bias, *earlier)
    return pl.pallas_call(
        functools.partial(attend_kernel, shards, seg_rows),
        grid=(1,),
        name="attend",
        in_specs=[here(width)]
        + [whole] * shards
        + [pl.BlockSpec((None,) + bias.shape[1:], lambda i: (m, 0, 0))]
        + [pl.BlockSpec(memory_space=pl.ANY)] * len(earlier),
        out_specs=(here(width), here(128)),
        out_shape=outs,
        input_output_aliases={shards + 2 + i: i for i in range(len(earlier))},
        cost_estimate=cost(16 * HEAD_SIZE * pairs, pairs, q),
        compiler_params=pltpu.CompilerParams(vmem_limit_bytes=VMEM_LIMIT),
    )(*args)


def attend_back(m, rows, seg_rows, q, kv, bias, o, do, lse, cosine, sine, earlier):
    shards, tokens, width = len(kv), q.shape[0], q.shape[1]
    here = lambda w: pl.BlockSpec((rows, w), lambda i: (m, 0))
    turned = pl.BlockSpec((HALF_HEAD, rows), lambda i: (0, m))
    whole = pl.BlockSpec((rows, 2 * KV_WIDTH), lambda i: (0, 0))
    outs = (jax.ShapeDtypeStruct((tokens, width), BF),)
    outs += (jax.ShapeDtypeStruct((rows, 2 * KV_WIDTH), BF),) * shards
    pairs = rows * rows * shards * QUERY_HEADS
    args = (q, *kv, bias, o, do, lse, cosine, sine, *earlier)
    return pl.pallas_call(
        functools.partial(attend_back_kernel, shards, seg_rows),
        grid=(1,),
        name="attend_back",
        in_specs=[here(width)]
        + [whole] * shards
        + [pl.BlockSpec((None,) + bias.shape[1:], lambda i: (m, 0, 0))]
        + [here(width), here(width), here(128), turned, turned]
        + [pl.BlockSpec(memory_space=pl.ANY)] * len(earlier),
        out_specs=(here(width),) + (whole,) * shards,
        out_shape=outs,
        input_output_aliases={shards + 7 + i: i for i in range(len(earlier))},
        cost_estimate=cost(40 * HEAD_SIZE * pairs, pairs, q),
        compiler_params=pltpu.CompilerParams(vmem_limit_bytes=VMEM_LIMIT),
    )(*args)


def local(
    block_input,
    parent_ids,
    w_query,
    key_weight,
    value_weight,
    w_output,
    w_gate,
    w_up,
    w_down,
    norm_first,
    norm_second,
    out_cotangent,
):
    micro, rows, width = block_input.shape
    shards = lax.axis_size("shard")
    links = Links(lax.axis_size("rep"), shards)
    tree = rows * shards
    segs = parent_ids.shape[2]
    seg_rows = tree // segs
    tokens = micro * rows
    hidden = w_gate.shape[1]

    gains = links.gather_small(jnp.stack([norm_first, norm_second])).astype(F32)
    direct, *attention_got = links.gather_pair(
        jnp.concatenate([w_query, key_weight], axis=1),
        jnp.concatenate([w_output, value_weight], axis=1),
    )
    direct, *pair_got = links.gather_pair(*after((w_gate, w_up), direct))
    direct, *down_got = links.gather_rows(after(w_down, direct))

    parents = parent_ids[:, 0]
    seg = jnp.arange(segs)
    after_parent = jnp.concatenate([parents[:, 1:], jnp.full((micro, 1), -1, parents.dtype)], axis=1)
    on_path = (seg % 2 == 0)[None] | (after_parent == seg[None])
    below = (seg[None, :] < seg[:, None])[None]
    depth = jnp.sum(jnp.where(below, on_path.astype(F32)[:, None, :], 0.0), axis=-1)

    def row_numbers(hop):
        return (links.shard ^ hop) * rows + jnp.arange(rows)

    def pick(table, numbers):
        hit = (numbers // seg_rows)[..., None] == seg
        return jnp.sum(jnp.where(hit[None], table.reshape(micro, *(1,) * numbers.ndim, segs), 0), axis=-1)

    my_rows = row_numbers(0)
    positions = pick(depth, my_rows) * seg_rows + (my_rows % seg_rows).astype(F32)
    freqs = jnp.exp(-math.log(10000.0) * jnp.arange(HALF_HEAD, dtype=F32) * (2.0 / HEAD_SIZE))
    angles = freqs[:, None] * positions.reshape(tokens)[None, :]
    cosine_t, sine_t = jnp.cos(angles), jnp.sin(angles)
    cosine = jnp.tile(cosine_t.T, (1, 4))
    sine = jnp.tile(jnp.concatenate([-sine_t.T, sine_t.T], axis=1), (1, 2))
    key_rows = jnp.stack([row_numbers(hop) for hop in links.hops])
    open_key = (pick(on_path.astype(F32), key_rows) > 0.5) & (
        (key_rows < links.shard * rows) | (jnp.arange(shards) == 0)[:, None]
    )
    bias = jnp.where(open_key, 0.0, CLOSED)
    bias = jnp.pad(bias, ((0, 0), (0, 8 - shards), (0, 0)))

    inputs = block_input.reshape(tokens, width)
    cotangent = out_cotangent.reshape(tokens, width)
    queries, kv, act_first = project(inputs, gains, cosine, sine, *attention_got)
    kv_all = [links.spread(kv[m * rows : (m + 1) * rows]) for m in range(micro)]
    attended = ()
    for m in range(micro):
        attended = attend(m, rows, seg_rows, queries, kv_all[m], bias, attended)
    attn, lse = attended

    block_out, inner, slopes, act_second, d_resid, d_resid_low, d_attn, gain_two_sum = feed(
        inputs, attn, cotangent, gains, attention_got, pair_got, down_got
    )
    down_rows, output_rows, wide_rows = hidden // shards, width // shards, width // shards
    down_half, output_half = down_rows // 2, links.half_rows(output_rows)
    down_kept, down_given = links.order(
        down_rows, links.core * down_half, (1 - links.core) * down_half
    )
    output_kept, output_given = links.order(output_rows, *output_half[1:])
    rows_grads = lambda down, output: weight_grad(
        (
            (inner, cotangent, down_half, down),
            (attn, d_resid_low, output_half[0], output),
        )
    )
    rows_received = links.swap(rows_grads(down_given, output_given))
    rows_kept = rows_grads(down_kept, output_kept)
    rows_owned = links.reduce_owned(rows_kept, rows_received)
    wide_kept, wide_given = links.order(wide_rows, 0, 0)
    chunks = 2
    wide_owned = []
    wide_received = []
    for c in range(chunks):
        given, kept = (
            weight_grad(((act_second, slopes, wide_rows, starts),), c, hidden // chunks, choice)
            for starts, choice in ((wide_given, 1 - links.core), (wide_kept, links.core))
        )
        wide_received.append(links.swap(given))
        wide_owned.append(links.reduce_owned(kept, wide_received[c]))

    d_queries, d_kv = (), []
    d_attn = after(d_attn, rows_received, *wide_received)
    for m in range(micro):
        d_queries, *pieces = attend_back(
            m, rows, seg_rows, queries, kv_all[m], bias, attn, d_attn, lse, cosine_t, sine_t, d_queries
        )
        d_queries = (d_queries,)
        d_kv.append(links.collect(pieces))
    d_queries = d_queries[0]
    d_kv = turn_back(d_kv, cosine, sine)
    half, mine, theirs = links.half_rows(width // shards)
    qkv_kept, qkv_given = links.order(width // shards, mine, theirs)
    q_received = links.swap(weight_grad(((act_first, d_queries, half, qkv_given),)))
    q_owned = links.reduce_owned(weight_grad(((act_first, d_queries, half, qkv_kept),)), q_received)
    kv_received = links.swap(weight_grad(((act_first, d_kv, half, qkv_given),)))
    kv_owned = links.reduce_owned(weight_grad(((act_first, d_kv, half, qkv_kept),)), kv_received)
    d_input, gain_one_sum = finish(inputs, d_queries, d_kv, d_resid, gains, *attention_got)
    gain_sums = links.reduce_small(jnp.concatenate([gain_one_sum[:1], gain_two_sum[:1]]))

    def whole_sum(owned):
        owned = links.chain(owned)
        return owned, links.swap(owned)

    rows_owned, rows_other = whole_sum(rows_owned)
    grad_down = links.finish_rows(rows_owned[:down_half], rows_other[:down_half], down_rows)
    grad_output = links.finish_rows(rows_owned[down_half:], rows_other[down_half:], output_rows)
    wide = [links.finish_pair(*whole_sum(owned)) for owned in wide_owned]
    grad_gate, grad_upper = (jnp.concatenate(parts, axis=1) for parts in zip(*wide))
    grad_query = links.finish_rows(*whole_sum(q_owned), width // shards)
    grad_kv = links.finish_rows(*whole_sum(kv_owned), width // shards)
    return (
        block_out.reshape(micro, rows, width),
        d_input.reshape(micro, rows, width),
        grad_query,
        grad_kv[:, :KV_WIDTH],
        grad_kv[:, KV_WIDTH:],
        grad_output,
        grad_gate,
        grad_upper,
        grad_down,
        gain_sums[0],
        gain_sums[1],
    )


def solution(mesh):
    rows = P(None, AXES, None)
    weight, gain = P("shard", None), P("shard")
    return jax.shard_map(
        local,
        mesh=mesh,
        in_specs=(rows, P(None, "rep", None)) + (weight,) * 7 + (gain, gain, rows),
        out_specs=(rows, rows) + (weight,) * 7 + (gain, gain),
        check_vma=False,
    )
```

```python
import functools
import math

import jax
import jax.numpy as jnp
from jax import lax
from jax.experimental import pallas as pl
from jax.experimental.pallas import tpu as pltpu
from jax.sharding import PartitionSpec as P

QUERY_HEADS = 15
KEY_VALUE_HEADS = 5
HEAD_SIZE = 64
HALF_HEAD = HEAD_SIZE // 2
GROUP = QUERY_HEADS // KEY_VALUE_HEADS
KV_WIDTH = KEY_VALUE_HEADS * HEAD_SIZE
SCALE = HEAD_SIZE ** (-0.5)
EPS = 1e-05
AXES = ("rep", "shard")
BF = jnp.bfloat16
F32 = jnp.float32
CLOSED = -1e30
VMEM_LIMIT = 48 << 20
VMEM_MOST = 60 << 20


def dot(a, b, dims):
    return lax.dot_general(a, b, (dims, ((), ())), preferred_element_type=F32)


def nn(a, b):
    return dot(a, b, ((1,), (0,)))


def nt(a, b):
    return dot(a, b, ((1,), (1,)))


def tn(a, b):
    return dot(a, b, ((0,), (0,)))


def add(left, right):
    return (left.astype(F32) + right.astype(F32)).astype(left.dtype)


def after(value, *earlier):
    return lax.optimization_barrier((value, earlier))[0]


def rms_inverse(x):
    return lax.rsqrt(jnp.mean(x * x, axis=-1, keepdims=True) + EPS)


def cost(flops, exps, *arrays):
    size = sum(a.size * a.dtype.itemsize for a in arrays)
    return pl.CostEstimate(flops=flops, transcendentals=exps, bytes_accessed=size)


class Links:
    def __init__(self, reps, shards):
        self.reps, self.shards = reps, shards
        self.core = lax.axis_index("rep") % 2
        self.shard = lax.axis_index("shard")
        self.bits = shards.bit_length() - 1
        even = [1 << i for i in range(self.bits)]
        odd = even[:2][::-1] + even[2:]
        self.steps = list(zip(even, odd))
        self.hops = []
        for piece in range(shards):
            sums = [0, 0]
            for i, step in enumerate(self.steps):
                if piece >> i & 1:
                    sums = [sums[0] ^ step[0], sums[1] ^ step[1]]
            self.hops.append(jnp.where(self.core == 0, sums[0], sums[1]))

    def move(self, value, target):
        pairs = []
        for r in range(self.reps):
            for s in range(self.shards):
                goal = target(r, s)
                if goal is not None:
                    pairs.append((r * self.shards + s, goal[0] * self.shards + goal[1]))
        return lax.ppermute(value, AXES, pairs)

    def step(self, value, i):
        return self.move(value, lambda r, s: (r, s ^ self.steps[i][r % 2]))

    def swap(self, value):
        return self.move(value, lambda r, s: (r ^ 1, s))

    def chain(self, value, streams):
        chips = self.reps // 2
        place = lax.axis_index("rep") // 2
        span = 1
        if chips % 4 == 0:
            inward, outward, middle = {0: 1, 3: 2}, {1: 0, 2: 3}, {1: 2, 2: 1}

            def along(value, table, stream):
                def target(r, s):
                    chip = r // 2
                    if chip % 4 not in table:
                        return None
                    return ((chip - chip % 4 + table[chip % 4]) * 2 + r % 2, s)

                return stream(value, lambda v: self.move(v, target))

            value = add(value, along(value, inward, streams[0]))
            value = add(value, along(value, middle, streams[1]))
            back = along(value, outward, streams[2])
            inner = (place % 4 == 1) | (place % 4 == 2)
            value = jnp.where(inner, value, back)
            span = 4
        while span < chips:
            value = add(value, self.move(value, lambda r, s: (r ^ (2 * span), s)))
            span *= 2
        return value

    def beside(self, value):
        return self.move(value, lambda r, s: (r ^ 2, s))

    def near(self, value):
        return {1 << i: self.step(value, i) for i in range(self.bits)}

    def far(self, value, near):
        pieces = [value]
        for t in range(1, self.shards):
            top = t.bit_length() - 1
            pieces.append(near[t] if t in near else self.step(pieces[t - (1 << top)], top))
        return pieces

    def collect(self, pieces, stream):
        for i in reversed(range(self.bits)):
            keep = 1 << i
            got = [stream(pieces[t + keep], lambda v: self.step(v, i)) for t in range(keep)]
            pieces = [add(pieces[t], got[t]) for t in range(keep)]
        return pieces[0]

    def twin(self, piece):
        return piece if self.bits < 2 else piece >> 2 << 2 | (piece & 1) << 1 | (piece >> 1 & 1)

    def small_pieces(self, value):
        return [
            value if hop == 0 else self.move(value, lambda r, s, hop=hop: (r, s ^ hop))
            for hop in range(self.shards)
        ]

    def in_order(self, pieces):
        pieces = jnp.stack(pieces)
        value = pieces
        order = self.shard ^ jnp.arange(self.shards)
        hit = (order[:, None] == jnp.arange(self.shards)[None, :])[:, :, None, None]
        pieces = jnp.sum(jnp.where(hit, pieces[None], 0), axis=1, dtype=value.dtype)
        return jnp.concatenate([pieces[j] for j in range(self.shards)], axis=-1)

    def half_rows(self, rows):
        half = -(-rows // 32) * 16
        return half, self.core * (rows - half), (1 - self.core) * (rows - half)

    def order(self, scale, mine, theirs):
        kept = [(self.shard ^ hop) * scale + mine for hop in self.hops]
        given = [(self.shard ^ self.hops[self.twin(t)]) * scale + theirs for t in range(self.shards)]
        return kept, given

    def reduce_owned(self, kept, received, stream):
        block = kept.shape[0] // self.shards
        cut = lambda value, t: value[t * block : (t + 1) * block]
        pieces = [add(cut(kept, t), cut(received, t)) for t in range(self.shards)]
        return self.collect(pieces, stream)

    def finish_rows(self, owned, other, rows):
        low = jnp.where(self.core == 0, owned, other)
        high = jnp.where(self.core == 0, other, owned)
        return jnp.concatenate([low[: rows - owned.shape[0]], high], axis=0).astype(F32)

    def finish_pair(self, owned, other):
        left = jnp.where(self.core == 0, owned, other)
        right = jnp.where(self.core == 0, other, owned)
        return left.astype(F32), right.astype(F32)

    def reduce_small(self, value):
        summed = add(value, self.swap(value))
        for i in range(self.bits):
            summed = add(summed, self.step(summed, i))
        summed = self.chain(summed, [direct] * 3)
        width = value.shape[1] // self.shards
        return lax.dynamic_slice_in_dim(summed, self.shard * width, width, 1)


def direct(value, move):
    return move(value)


def in_turn(depth):
    done = []

    def stream(value, move):
        if len(done) >= depth:
            value = after(value, done[-depth])
        done.append(move(value))
        return done[-1]

    return stream


def meet(*values):
    return lax.optimization_barrier(values)


def joined(pieces, starts, shape):
    if any(piece.shape[0] % 16 or piece.shape[1] % 128 and piece.shape[1] < shape[1] for piece in pieces):
        whole = jnp.zeros(shape, pieces[0].dtype)
        for piece, start in zip(pieces, starts):
            whole = lax.dynamic_update_slice(whole, piece, start)
        pieces, starts = (whole,), [(0, 0)]
    return tuple(pieces), numbers([at for start in starts for at in start]), shape


def numbers(values):
    return jnp.stack([jnp.asarray(value, jnp.int32) for value in values])


def load(pieces, starts_ref, whole, sems):
    copies = []
    for i, piece in enumerate(pieces):
        rows = pl.ds(pl.multiple_of(starts_ref[2 * i], 16), piece.shape[0])
        if piece.shape[1] == whole.shape[1]:
            place = whole.at[rows, :]
        else:
            columns = pl.ds(pl.multiple_of(starts_ref[2 * i + 1], 128), piece.shape[1])
            place = whole.at[rows, columns]
        copies.append(pltpu.make_async_copy(piece, place, sems.at[i]))
        copies[-1].start()
    return copies


def wait(copies):
    for copy in copies:
        copy.wait()


IN_VMEM = pl.BlockSpec(memory_space=pltpu.VMEM)
IN_SMEM = pl.BlockSpec(memory_space=pltpu.SMEM)
ANYWHERE = pl.BlockSpec(memory_space=pl.ANY)


def turn(chunk, cosine, sine):
    lane = lax.broadcasted_iota(jnp.int32, chunk.shape, 1)
    partner = jnp.where(
        lane % HEAD_SIZE < HALF_HEAD,
        pltpu.roll(chunk, 128 - HALF_HEAD, 1),
        pltpu.roll(chunk, HALF_HEAD, 1),
    )
    return chunk * cosine + partner * sine


def project_kernel(count, starts_ref, x_ref, gains_ref, cos_ref, sin_ref, *refs):
    pieces = refs[:count]
    q_ref, kv_ref, act_ref, whole, sems = refs[count:]
    copies = load(pieces, starts_ref, whole, sems)
    x = x_ref[...].astype(F32)
    width = x.shape[1]
    act_ref[...] = (x * rms_inverse(x) * gains_ref[0:1, :]).astype(BF)
    wait(copies)
    act = act_ref[...]
    cosine, sine = cos_ref[...], sin_ref[...]
    for first in range(0, width + KV_WIDTH, 256):
        linear = nn(act, whole[:width, first : first + 256])
        for at in range(first, first + 256, 128):
            chunk = turn(linear[:, at - first : at - first + 128], cosine, sine)
            if at + 128 <= width:
                q_ref[:, at : at + 128] = (chunk * SCALE).astype(BF)
            elif at < width:
                q_ref[:, at:width] = (chunk[:, : width - at] * SCALE).astype(BF)
                kv_ref[:, : at + 128 - width] = chunk[:, width - at :].astype(BF)
            else:
                kv_ref[:, at - width : at - width + 128] = chunk.astype(BF)
    kv_ref[:, KV_WIDTH:] = nn(act, whole[width:, width:]).astype(BF)


def project(x, gains, cosine, sine, pieces, starts, shape):
    tokens, width = x.shape
    outs = (
        jax.ShapeDtypeStruct((tokens, width), BF),
        jax.ShapeDtypeStruct((tokens, 2 * KV_WIDTH), BF),
        jax.ShapeDtypeStruct((tokens, width), BF),
    )
    return pl.pallas_call(
        functools.partial(project_kernel, len(pieces)),
        name="project",
        in_specs=[IN_SMEM] + [IN_VMEM] * 4 + [ANYWHERE] * len(pieces),
        out_specs=(IN_VMEM,) * 3,
        out_shape=outs,
        scratch_shapes=[
            pltpu.VMEM(shape, BF),
            pltpu.SemaphoreType.DMA((len(pieces),)),
        ],
        cost_estimate=cost(2 * tokens * width * (width + 2 * KV_WIDTH), 0, x, *outs, *pieces),
        compiler_params=pltpu.CompilerParams(vmem_limit_bytes=VMEM_LIMIT),
    )(starts, x, gains, cosine, sine, *pieces)


def feed_kernel(counts, s0_ref, s1_ref, s2_ref, x_ref, attn_ref, dy_ref, gains_ref, *refs):
    total = sum(counts)
    attention_pieces = refs[: counts[0]]
    pair_pieces = refs[counts[0] : counts[0] + counts[1]]
    down_pieces = refs[counts[0] + counts[1] : total]
    out_ref, inner_ref, slopes_ref, act_ref, dres_ref, low_ref, dattn_ref, gain_ref = refs[total : total + 8]
    w_attn, w_pair, w_down, resid_ref, dact_ref, sems0, sems1, sems2 = refs[total + 8 :]
    attention_copies = load(attention_pieces, s0_ref, w_attn, sems0)
    pair_copies = load(pair_pieces, s1_ref, w_pair, sems1)
    down_copies = load(down_pieces, s2_ref, w_down, sems2)
    tokens, width = x_ref.shape
    hidden = w_pair.shape[1]
    tile = hidden // 5
    gain = gains_ref[1:2, :]
    wait(attention_copies)
    w_output = w_attn[width:, :width]
    resid = x_ref[...].astype(F32) + nn(attn_ref[...], w_output)
    resid_ref[...] = resid
    dres_ref[...] = resid
    root = rms_inverse(resid)
    act_ref[...] = (resid * root * gain).astype(BF)
    wait(pair_copies)
    wait(down_copies)
    act, dy = act_ref[...], dy_ref[...]
    for first in range(0, hidden, tile):
        here = slice(first, first + tile)
        gate = nn(act, w_pair[:width, here])
        upper = nn(act, w_pair[width:, here])
        d_inner = nt(dy, w_down[here, :])
        sigmoid = 1.0 / (1.0 + jnp.exp(-gate))
        silu = gate * sigmoid
        inner = (silu * upper).astype(BF)
        inner_ref[:, here] = inner
        d_gate = (d_inner * upper * sigmoid * (1.0 + gate * (1.0 - sigmoid))).astype(BF)
        d_upper = (d_inner * silu).astype(BF)
        slopes_ref[0, :, here] = d_gate
        slopes_ref[1, :, here] = d_upper
        out = nn(inner, w_down[here, :])
        d_act = nt(d_gate, w_pair[:width, here]) + nt(d_upper, w_pair[width:, here])
        resid_ref[...] += out
        if first == 0:
            dact_ref[...] = d_act
        else:
            dact_ref[...] += d_act
    out_ref[...] = resid_ref[...].astype(BF)
    normed = dres_ref[...] * root
    d_act = dact_ref[...]
    gain_ref[...] = jnp.broadcast_to(jnp.sum(d_act * normed, axis=0, keepdims=True), gain_ref.shape)
    d_normed = d_act * gain
    d_resid = dy.astype(F32) + root * (
        d_normed - normed * jnp.mean(d_normed * normed, axis=-1, keepdims=True)
    )
    dres_ref[...] = d_resid
    low = d_resid.astype(BF)
    low_ref[...] = low
    dattn_ref[...] = nt(low, w_output).astype(BF)


def feed(x, attn, dy, gains, attention_got, pair_got, down_got):
    tokens, width = x.shape
    groups = [attention_got, pair_got, down_got]
    counts = [len(pieces) for pieces, _, _ in groups]
    shapes = [shape for _, _, shape in groups]
    hidden = shapes[1][1]
    outs = (
        jax.ShapeDtypeStruct((tokens, width), BF),
        jax.ShapeDtypeStruct((tokens, hidden), BF),
        jax.ShapeDtypeStruct((2, tokens, hidden), BF),
        jax.ShapeDtypeStruct((tokens, width), BF),
        jax.ShapeDtypeStruct((tokens, width), F32),
        jax.ShapeDtypeStruct((tokens, width), BF),
        jax.ShapeDtypeStruct((tokens, width), BF),
        jax.ShapeDtypeStruct((8, width), F32),
    )
    every = [piece for pieces, _, _ in groups for piece in pieces]
    return pl.pallas_call(
        functools.partial(feed_kernel, counts),
        name="feed",
        in_specs=[IN_SMEM] * 3 + [IN_VMEM] * 4 + [ANYWHERE] * len(every),
        out_specs=(IN_VMEM,) * 8,
        out_shape=outs,
        scratch_shapes=[pltpu.VMEM(shape, BF) for shape in shapes]
        + [pltpu.VMEM((tokens, width), F32)] * 2
        + [pltpu.SemaphoreType.DMA((count,)) for count in counts],
        cost_estimate=cost(
            2 * tokens * width * (6 * hidden + 3 * width), tokens * hidden, x, x, x, *outs, *every
        ),
        compiler_params=pltpu.CompilerParams(vmem_limit_bytes=VMEM_MOST),
    )(*(starts for _, starts, _ in groups), x, attn, dy, gains, *every)


def weight_grad_kernel(parts, count, starts_ref, *refs):
    operands = refs[: 2 * len(parts)]
    out_ref = refs[2 * len(parts)]
    turned = refs[2 * len(parts) + 1 : 3 * len(parts) + 1]
    ordered = refs[3 * len(parts) + 1 :]
    block = sum(parts)

    @pl.when(pl.program_id(0) == 0)
    def _():
        for i, rows in enumerate(parts):
            turned[i][...] = jnp.transpose(operands[2 * i][...])
            for t in range(count):
                start = pl.multiple_of(starts_ref[1 + i * count + t], 16)
                ordered[i][t * rows : (t + 1) * rows, :] = turned[i][pl.ds(start, rows), :]

    at = 0
    for i, rows in enumerate(parts):
        made = nn(ordered[i][...], operands[2 * i + 1][...]).astype(BF)
        for t in range(count):
            out_ref[t * block + at : t * block + at + rows, :] = made[t * rows : (t + 1) * rows]
        at += rows


def weight_grad(terms, column=0, columns=None, choice=0):
    count = len(terms[0][3])
    parts = [term[2] for term in terms]
    block = sum(parts)
    tokens = terms[0][0].shape[0]
    columns = columns or terms[0][1].shape[-1]
    if any(rows % 16 for rows in parts) or any(term[0].shape[1] // count % 16 for term in terms):
        made = []
        for left, right, rows, starts in terms:
            right = right if right.ndim == 2 else lax.dynamic_index_in_dim(right, choice, 0, keepdims=False)
            grad = tn(left, right[:, column * columns : (column + 1) * columns]).astype(BF)
            made.append([lax.dynamic_slice_in_dim(grad, start, rows, 0) for start in starts])
        return jnp.concatenate([part for group in zip(*made) for part in group], axis=0)
    in_specs, args, flops = [], [], 0
    tile = next((size for size in (256, 320) if columns % size == 0 and size % 128 == 0), columns)
    skip = column * (columns // tile)
    for left, right, rows, starts in terms:
        in_specs.append(pl.BlockSpec(left.shape, lambda n, info: (0, 0)))
        if right.ndim == 2:
            in_specs.append(pl.BlockSpec((tokens, tile), lambda n, info: (0, skip + n)))
        else:
            in_specs.append(pl.BlockSpec((None, tokens, tile), lambda n, info: (info[0], 0, skip + n)))
        args += [left, right]
        flops += 2 * tokens * rows * count * columns
    out = jax.ShapeDtypeStruct((count * block, columns), BF)
    info = numbers([choice] + [start for term in terms for start in term[3]])
    return pl.pallas_call(
        functools.partial(weight_grad_kernel, parts, count),
        grid_spec=pltpu.PrefetchScalarGridSpec(
            num_scalar_prefetch=1,
            grid=(columns // tile,),
            in_specs=in_specs,
            out_specs=pl.BlockSpec((count * block, tile), lambda n, info: (0, n)),
            scratch_shapes=[pltpu.VMEM((term[0].shape[1], tokens), BF) for term in terms]
            + [pltpu.VMEM((count * rows, tokens), BF) for rows in parts],
        ),
        out_shape=out,
        name="weight_grad",
        cost_estimate=cost(flops, 0, out, *args),
        compiler_params=pltpu.CompilerParams(vmem_limit_bytes=VMEM_LIMIT),
    )(info, *args)


def finish_kernel(count, starts_ref, x_ref, low_ref, kv_ref, dres_ref, gains_ref, *refs):
    pieces = refs[:count]
    dx_ref, gain_ref, whole, sems = refs[count:]
    copies = load(pieces, starts_ref, whole, sems)
    x = x_ref[...].astype(F32)
    width = x.shape[1]
    root = rms_inverse(x)
    normed = x * root
    wait(copies)
    d_act = nt(low_ref[...], whole[:width, :width])
    d_act += nt(kv_ref[:, :KV_WIDTH], whole[:width, width:])
    d_act += nt(kv_ref[:, KV_WIDTH:], whole[width:, width:])
    gain_ref[...] = jnp.broadcast_to(jnp.sum(d_act * normed, axis=0, keepdims=True), gain_ref.shape)
    d_normed = d_act * gains_ref[0:1, :]
    dx_ref[...] = (
        dres_ref[...]
        + root * (d_normed - normed * jnp.mean(d_normed * normed, axis=-1, keepdims=True))
    ).astype(BF)


def finish(x, low, kv, dres, gains, pieces, starts, shape):
    tokens, width = x.shape
    outs = (jax.ShapeDtypeStruct((tokens, width), BF), jax.ShapeDtypeStruct((8, width), F32))
    return pl.pallas_call(
        functools.partial(finish_kernel, len(pieces)),
        name="finish",
        in_specs=[IN_SMEM] + [IN_VMEM] * 5 + [ANYWHERE] * len(pieces),
        out_specs=(IN_VMEM,) * 2,
        out_shape=outs,
        scratch_shapes=[
            pltpu.VMEM(shape, BF),
            pltpu.SemaphoreType.DMA((len(pieces),)),
        ],
        cost_estimate=cost(2 * tokens * width * (width + 2 * KV_WIDTH), 0, x, low, dres, *pieces),
        compiler_params=pltpu.CompilerParams(vmem_limit_bytes=VMEM_LIMIT),
    )(starts, x, low, kv, dres, gains, *pieces)


def turn_back_kernel(*refs):
    parts = refs[:-3]
    cos_ref, sin_ref, out_ref = refs[-3:]
    at = 0
    for part in parts:
        here = slice(at, at + part.shape[0])
        for first in range(0, KV_WIDTH, 128):
            chunk = part[:, first : first + 128].astype(F32)
            chunk = turn(chunk, cos_ref[here, :], -sin_ref[here, :]).astype(BF)
            last = min(first + 128, KV_WIDTH)
            out_ref[here, first:last] = chunk[:, : last - first]
        out_ref[here, KV_WIDTH:] = part[:, KV_WIDTH:]
        at += part.shape[0]


def turn_back(parts, cosine, sine):
    out = jax.ShapeDtypeStruct((sum(part.shape[0] for part in parts), 2 * KV_WIDTH), BF)
    return pl.pallas_call(
        turn_back_kernel,
        name="turn_back",
        in_specs=[IN_VMEM] * (len(parts) + 2),
        out_specs=IN_VMEM,
        out_shape=out,
        cost_estimate=cost(0, 0, out, out),
        compiler_params=pltpu.CompilerParams(vmem_limit_bytes=VMEM_LIMIT),
    )(*parts, cosine, sine)


def head(ref, h):
    return ref[:, h * HEAD_SIZE : (h + 1) * HEAD_SIZE]


def widen(value, columns):
    n = value.shape[0]
    lane = lax.broadcasted_iota(jnp.int32, (n, HEAD_SIZE), 1)
    tail = jnp.zeros((n, HEAD_SIZE), F32)
    for c, column in enumerate(columns):
        tail = jnp.where(lane == c, column, tail)
    return jnp.concatenate([value, tail.astype(BF)], axis=1)


def split(column):
    high = column.astype(BF).astype(F32)
    middle = (column - high).astype(BF).astype(F32)
    return [high, middle, column - high - middle]


def attend_kernel(shards, seg_rows, q_ref, *refs):
    kv = refs[:shards]
    bias_ref = refs[shards]
    o_ref, lse_ref = refs[-2:]
    rows = q_ref.shape[0]
    i = lax.broadcasted_iota(jnp.int32, (rows, rows), 0)
    j = lax.broadcasted_iota(jnp.int32, (rows, rows), 1)
    same = (i // seg_rows) == (j // seg_rows)
    own = jnp.where(j > i, CLOSED, jnp.where(same, 0.0, bias_ref[0:1, :]))
    one = jnp.ones((rows, 1), F32)
    bias_columns = jnp.transpose(bias_ref[...])
    lse = jnp.zeros((rows, 128), F32)
    lane = lax.broadcasted_iota(jnp.int32, (rows, 128), 1)
    for g in range(KEY_VALUE_HEADS):
        keys, values = [], []
        for t in range(shards):
            keys.append(widen(head(kv[t], g), [bias_columns[:, t : t + 1]] if t else []))
            values.append(widen(head(kv[t], KEY_VALUE_HEADS + g), [one]))
        for h in range(g * GROUP, g * GROUP + GROUP):
            q = widen(head(q_ref, h), [one])
            scores = [nt(q, k) for k in keys]
            scores[0] = scores[0] + own
            peak = functools.reduce(jnp.maximum, scores)
            peak = jnp.max(peak, axis=1, keepdims=True)
            terms = [nn(jnp.exp(s - peak).astype(BF), v) for s, v in zip(scores, values)]
            mixed = sum(terms[1:], terms[0])
            total = mixed[:, HEAD_SIZE : HEAD_SIZE + 1]
            o_ref[:, h * HEAD_SIZE : (h + 1) * HEAD_SIZE] = (mixed[:, :HEAD_SIZE] / total).astype(BF)
            lse = jnp.where(lane == h, peak + jnp.log(total), lse)
    lse_ref[...] = lse


def attend_back_kernel(shards, seg_rows, q_ref, *refs):
    kv = refs[:shards]
    bias_ref, o_ref, do_ref, lse_ref, cos_ref, sin_ref = refs[shards : shards + 6]
    dq_ref = refs[-1 - shards]
    dkv = refs[-shards:]
    rows = q_ref.shape[0]
    i = lax.broadcasted_iota(jnp.int32, (rows, rows), 1)
    j = lax.broadcasted_iota(jnp.int32, (rows, rows), 0)
    bias_columns = jnp.transpose(bias_ref[...])
    same = (i // seg_rows) == (j // seg_rows)
    own_column = jnp.broadcast_to(bias_columns[:, 0:1], (rows, rows))
    own = jnp.where(j > i, CLOSED, jnp.where(same, 0.0, own_column))
    one, zero = jnp.ones((rows, 1), F32), jnp.zeros((rows, 1), F32)
    cosine, sine = cos_ref[...], sin_ref[...]
    for g in range(KEY_VALUE_HEADS):
        keys, values, turned = [], [], []
        for t in range(shards):
            k = head(kv[t], g)
            turned.append(jnp.transpose(k))
            keys.append(widen(k, [bias_columns[:, t : t + 1] if t else zero, one, one, one]))
            values.append(widen(head(kv[t], KEY_VALUE_HEADS + g), [one, one, one]))
        dk, dv = [None] * shards, [None] * shards
        for h in range(g * GROUP, g * GROUP + GROUP):
            q, do = head(q_ref, h), head(do_ref, h)
            centre = jnp.sum(head(o_ref, h).astype(F32) * do.astype(F32), axis=1, keepdims=True)
            q_wide = widen(q, [one] + split(-lse_ref[:, h : h + 1]))
            do_wide = widen(do, split(-centre))
            dq = None
            for t in range(shards):
                scores = nt(keys[t], q_wide)
                if t == 0:
                    scores = scores + own
                probs = jnp.exp(scores)
                ds = (probs * nt(values[t], do_wide)).astype(BF)
                v_term = nn(probs.astype(BF), do)
                k_term = nn(ds, q)
                q_term = nn(turned[t], ds)
                dv[t] = v_term if dv[t] is None else dv[t] + v_term
                dk[t] = k_term if dk[t] is None else dk[t] + k_term
                dq = q_term if dq is None else dq + q_term
            dq = dq * SCALE
            first, second = dq[:HALF_HEAD], dq[HALF_HEAD:]
            back = jnp.concatenate(
                [first * cosine + second * sine, second * cosine - first * sine], axis=0
            )
            dq_ref[:, h * HEAD_SIZE : (h + 1) * HEAD_SIZE] = jnp.transpose(back).astype(BF)
        for t in range(shards):
            dkv[t][:, g * HEAD_SIZE : (g + 1) * HEAD_SIZE] = dk[t].astype(BF)
            g_value = KEY_VALUE_HEADS + g
            dkv[t][:, g_value * HEAD_SIZE : (g_value + 1) * HEAD_SIZE] = dv[t].astype(BF)


def attend(m, rows, seg_rows, q, kv, bias, earlier):
    shards, tokens, width = len(kv), q.shape[0], q.shape[1]
    here = lambda w: pl.BlockSpec((rows, w), lambda i: (m, 0))
    whole = pl.BlockSpec((rows, 2 * KV_WIDTH), lambda i: (0, 0))
    outs = (jax.ShapeDtypeStruct((tokens, width), BF), jax.ShapeDtypeStruct((tokens, 128), F32))
    pairs = rows * rows * shards * QUERY_HEADS
    args = (q, *kv, bias, *earlier)
    return pl.pallas_call(
        functools.partial(attend_kernel, shards, seg_rows),
        grid=(1,),
        name="attend",
        in_specs=[here(width)]
        + [whole] * shards
        + [pl.BlockSpec((None,) + bias.shape[1:], lambda i: (m, 0, 0))]
        + [pl.BlockSpec(memory_space=pl.ANY)] * len(earlier),
        out_specs=(here(width), here(128)),
        out_shape=outs,
        input_output_aliases={shards + 2 + i: i for i in range(len(earlier))},
        cost_estimate=cost(16 * HEAD_SIZE * pairs, pairs, q),
        compiler_params=pltpu.CompilerParams(vmem_limit_bytes=VMEM_LIMIT),
    )(*args)


def attend_back(m, rows, seg_rows, q, kv, bias, o, do, lse, cosine, sine, earlier):
    shards, tokens, width = len(kv), q.shape[0], q.shape[1]
    here = lambda w: pl.BlockSpec((rows, w), lambda i: (m, 0))
    turned = pl.BlockSpec((HALF_HEAD, rows), lambda i: (0, m))
    whole = pl.BlockSpec((rows, 2 * KV_WIDTH), lambda i: (0, 0))
    outs = (jax.ShapeDtypeStruct((tokens, width), BF),)
    outs += (jax.ShapeDtypeStruct((rows, 2 * KV_WIDTH), BF),) * shards
    pairs = rows * rows * shards * QUERY_HEADS
    args = (q, *kv, bias, o, do, lse, cosine, sine, *earlier)
    return pl.pallas_call(
        functools.partial(attend_back_kernel, shards, seg_rows),
        grid=(1,),
        name="attend_back",
        in_specs=[here(width)]
        + [whole] * shards
        + [pl.BlockSpec((None,) + bias.shape[1:], lambda i: (m, 0, 0))]
        + [here(width), here(width), here(128), turned, turned]
        + [pl.BlockSpec(memory_space=pl.ANY)] * len(earlier),
        out_specs=(here(width),) + (whole,) * shards,
        out_shape=outs,
        input_output_aliases={shards + 7 + i: i for i in range(len(earlier))},
        cost_estimate=cost(40 * HEAD_SIZE * pairs, pairs, q),
        compiler_params=pltpu.CompilerParams(vmem_limit_bytes=VMEM_LIMIT),
    )(*args)


def local(
    block_input,
    parent_ids,
    w_query,
    key_weight,
    value_weight,
    w_output,
    w_gate,
    w_up,
    w_down,
    norm_first,
    norm_second,
    out_cotangent,
):
    micro, rows, width = block_input.shape
    shards = lax.axis_size("shard")
    links = Links(lax.axis_size("rep"), shards)
    tree = rows * shards
    segs = parent_ids.shape[2]
    seg_rows = tree // segs
    tokens = micro * rows
    hidden = w_gate.shape[1]

    even = links.core == 0
    side = lax.axis_index("rep") // 2 % 2
    left = jnp.concatenate([w_query, key_weight], axis=1)
    right = jnp.concatenate([w_output, value_weight], axis=1)
    attn_mine = jnp.where(even, left, right)
    pair_cut = hidden // 2
    pair_mine = lax.dynamic_slice_in_dim(jnp.where(even, w_gate, w_up), side * pair_cut, pair_cut, 1)
    down_cut = w_down.shape[0] // 4
    down_mine = lax.dynamic_slice_in_dim(w_down, (links.core * 2 + side) * down_cut, down_cut, 0)
    attn_near = links.near(attn_mine)
    gain_pieces = links.small_pieces(jnp.stack([norm_first, norm_second]))
    attn_mine, attn_near, gain_pieces, pair_mine, down_mine = meet(
        attn_mine, attn_near, gain_pieces, pair_mine, down_mine
    )
    gains = links.in_order(gain_pieces).astype(F32)
    attn_all = links.far(attn_mine, attn_near)
    attn_swapped = {t: links.swap(attn_near[t]) for t in attn_near}
    pair_near = {1: links.step(pair_mine, 0)}
    attn_all, attn_swapped, pair_mine, pair_near, gains = meet(
        attn_all, attn_swapped, pair_mine, pair_near, gains
    )
    attn_swapped = [attn_swapped.get(t, None) for t in range(shards)]
    attn_swapped = [links.swap(attn_all[t]) if t and v is None else v for t, v in enumerate(attn_swapped)]
    deep, shard_rows = width, width // shards

    def attention_weights():
        pieces, starts = [left, right], [(links.shard * shard_rows, 0), (deep + links.shard * shard_rows, 0)]
        for t in range(1, shards):
            twin = links.hops[links.twin(t)]
            pieces += [attn_all[t], attn_swapped[t]]
            starts += [
                (links.core * deep + (links.shard ^ links.hops[t]) * shard_rows, 0),
                ((1 - links.core) * deep + (links.shard ^ twin) * shard_rows, 0),
            ]
        return joined(pieces, starts, (2 * deep, left.shape[1]))

    attention_got = attention_weights()

    parents = parent_ids[:, 0]
    seg = jnp.arange(segs)
    after_parent = jnp.concatenate([parents[:, 1:], jnp.full((micro, 1), -1, parents.dtype)], axis=1)
    on_path = (seg % 2 == 0)[None] | (after_parent == seg[None])
    below = (seg[None, :] < seg[:, None])[None]
    depth = jnp.sum(jnp.where(below, on_path.astype(F32)[:, None, :], 0.0), axis=-1)

    def row_numbers(hop):
        return (links.shard ^ hop) * rows + jnp.arange(rows)

    def pick(table, numbers):
        hit = (numbers // seg_rows)[..., None] == seg
        return jnp.sum(jnp.where(hit[None], table.reshape(micro, *(1,) * numbers.ndim, segs), 0), axis=-1)

    my_rows = row_numbers(0)
    positions = pick(depth, my_rows) * seg_rows + (my_rows % seg_rows).astype(F32)
    freqs = jnp.exp(-math.log(10000.0) * jnp.arange(HALF_HEAD, dtype=F32) * (2.0 / HEAD_SIZE))
    angles = freqs[:, None] * positions.reshape(tokens)[None, :]
    cosine_t, sine_t = jnp.cos(angles), jnp.sin(angles)
    cosine = jnp.tile(cosine_t.T, (1, 4))
    sine = jnp.tile(jnp.concatenate([-sine_t.T, sine_t.T], axis=1), (1, 2))
    key_rows = jnp.stack([row_numbers(hop) for hop in links.hops])
    open_key = (pick(on_path.astype(F32), key_rows) > 0.5) & (
        (key_rows < links.shard * rows) | (jnp.arange(shards) == 0)[:, None]
    )
    bias = jnp.where(open_key, 0.0, CLOSED)
    bias = jnp.pad(bias, ((0, 0), (0, 8 - shards), (0, 0)))

    inputs = block_input.reshape(tokens, width)
    cotangent = out_cotangent.reshape(tokens, width)
    pair_near |= {1 << i: links.step(pair_mine, i) for i in range(1, links.bits)}
    pair_beside = {1: links.beside(pair_near[1])}
    queries, kv, act_first = project(inputs, gains, cosine, sine, *attention_got)
    kv_own = [kv[m * rows : (m + 1) * rows] for m in range(micro)]
    queries, act_first, kv_own, pair_mine, pair_near, pair_beside = meet(
        queries, act_first, kv_own, pair_mine, pair_near, pair_beside
    )

    kv_near = [None] * micro
    kv_all = [None] * micro
    kv_near[0] = links.near(kv_own[0])
    pair_all = links.far(pair_mine, pair_near)
    pair_beside[2] = links.beside(pair_near[2])
    kv_near, pair_all, pair_beside, down_mine = meet(kv_near, pair_all, pair_beside, down_mine)

    kv_all[0] = links.far(kv_own[0], kv_near[0])
    for m in range(1, micro):
        kv_near[m] = links.near(kv_own[m])
    pair_beside |= {t: links.beside(pair_all[t]) for t in range(3, shards)}
    pair_swapped = [None] + [links.swap(pair_all[t]) for t in range(1, shards)]
    pair_beside_swapped = [None] + [links.swap(pair_beside[t]) for t in range(1, 3)]
    kv_all, kv_near, kv_own, pair_beside, queries, down_mine, pair_swapped, pair_beside_swapped = meet(
        kv_all, kv_near, kv_own, pair_beside, queries, down_mine, pair_swapped, pair_beside_swapped
    )

    for m in range(1, micro):
        kv_all[m] = links.far(kv_own[m], kv_near[m])
    down_near = links.near(down_mine)
    pair_beside_swapped += [links.swap(pair_beside[t]) for t in range(3, shards)]
    attended = attend(0, rows, seg_rows, queries, kv_all[0], bias, ())
    kv_all, down_mine, down_near, attended, queries, pair_beside_swapped = meet(
        kv_all, down_mine, down_near, attended, queries, pair_beside_swapped
    )

    down_all = links.far(down_mine, down_near)
    down_beside = {t: links.beside(down_near[t]) for t in down_near}
    down_swapped = {t: links.swap(down_near[t]) for t in down_near}
    for m in range(1, micro):
        attended = attend(m, rows, seg_rows, queries, kv_all[m], bias, attended)
    attended, down_all, down_beside, down_swapped = meet(attended, down_all, down_beside, down_swapped)
    attn, lse = attended
    down_beside = [down_beside[t] if t in down_beside else links.beside(down_all[t]) for t in range(1, shards)]
    down_swapped = [down_swapped[t] if t in down_swapped else links.swap(down_all[t]) for t in range(1, shards)]
    down_beside_swapped = [links.swap(piece) for piece in down_beside]

    def pair_weights():
        pieces, starts = [w_gate, w_up], [(links.shard * shard_rows, 0), (deep + links.shard * shard_rows, 0)]
        for t in range(1, shards):
            twin = links.hops[links.twin(t)]
            row = links.core * deep + (links.shard ^ links.hops[t]) * shard_rows
            far_row = (1 - links.core) * deep + (links.shard ^ twin) * shard_rows
            pieces += [pair_all[t], pair_beside[t], pair_swapped[t], pair_beside_swapped[t]]
            starts += [(at, turn * pair_cut) for at in (row, far_row) for turn in (side, 1 - side)]
        return joined(pieces, starts, (2 * deep, hidden))

    def down_weights():
        own = w_down.shape[0]
        pieces, starts = [w_down], [(links.shard * own, 0)]
        for t in range(1, shards):
            twin = links.hops[links.twin(t)]
            row = (links.shard ^ links.hops[t]) * own + links.core * 2 * down_cut
            far_row = (links.shard ^ twin) * own + (1 - links.core) * 2 * down_cut
            pieces += [down_all[t], down_beside[t - 1], down_swapped[t - 1], down_beside_swapped[t - 1]]
            starts += [(at + turn * down_cut, 0) for at in (row, far_row) for turn in (side, 1 - side)]
        return joined(pieces, starts, (own * shards, width))

    block_out, inner, slopes, act_second, d_resid, d_resid_low, d_attn, gain_two_sum = feed(
        inputs, attn, cotangent, gains, attention_got, pair_weights(), down_weights()
    )
    down_rows, output_rows, wide_rows = hidden // shards, width // shards, width // shards
    down_half, output_half = down_rows // 2, links.half_rows(output_rows)
    down_kept, down_given = links.order(
        down_rows, links.core * down_half, (1 - links.core) * down_half
    )
    output_kept, output_given = links.order(output_rows, *output_half[1:])
    rows_grads = lambda down, output: weight_grad(
        (
            (inner, cotangent, down_half, down),
            (attn, d_resid_low, output_half[0], output),
        )
    )
    around = in_turn(2)
    along = [in_turn(1) for _ in range(3)]
    wide_kept, wide_given = links.order(wide_rows, 0, 0)
    chunks = 2
    wide_grads = lambda c, starts, choice: weight_grad(
        ((act_second, slopes, wide_rows, starts),), c, hidden // chunks, choice
    )

    def whole_sum(kept, received):
        owned = links.chain(links.reduce_owned(kept, received, around), along)
        return owned, links.swap(owned)

    rows_received = links.swap(rows_grads(down_given, output_given))
    rows_kept = rows_grads(down_kept, output_kept)
    wide_received = [links.swap(wide_grads(c, wide_given, 1 - links.core)) for c in range(chunks)]
    wide_parts = [wide_grads(c, wide_kept, links.core) for c in range(chunks)]
    d_attn, rows_received, rows_kept, wide_received, wide_parts = meet(
        d_attn, rows_received, rows_kept, wide_received, wide_parts
    )

    d_queries, d_kv = (), []
    rows_sum = whole_sum(rows_kept, rows_received)
    wide_sums = []
    for m in range(micro):
        d_queries, *pieces = attend_back(
            m, rows, seg_rows, queries, kv_all[m], bias, attn, d_attn, lse, cosine_t, sine_t, d_queries
        )
        d_queries = (d_queries,)
        d_kv.append(links.collect(pieces, around))
        if m < chunks:
            wide_sums.append(whole_sum(wide_parts[m], wide_received[m]))
    for m in range(micro, chunks):
        wide_sums.append(whole_sum(wide_parts[m], wide_received[m]))
    d_queries = d_queries[0]
    d_kv = turn_back(d_kv, cosine, sine)
    half, mine, theirs = links.half_rows(width // shards)
    qkv_kept, qkv_given = links.order(width // shards, mine, theirs)
    q_received = links.swap(weight_grad(((act_first, d_queries, half, qkv_given),)))
    q_sum = whole_sum(weight_grad(((act_first, d_queries, half, qkv_kept),)), q_received)
    kv_received = links.swap(weight_grad(((act_first, d_kv, half, qkv_given),)))
    kv_sum = whole_sum(weight_grad(((act_first, d_kv, half, qkv_kept),)), kv_received)
    d_input, gain_one_sum = finish(inputs, d_queries, d_kv, d_resid, gains, *attention_got)
    gain_sums = links.reduce_small(jnp.concatenate([gain_one_sum[:1], gain_two_sum[:1]]))

    rows_owned, rows_other = rows_sum
    grad_down = links.finish_rows(rows_owned[:down_half], rows_other[:down_half], down_rows)
    grad_output = links.finish_rows(rows_owned[down_half:], rows_other[down_half:], output_rows)
    grad_gate, grad_upper = (
        jnp.concatenate(parts, axis=1) for parts in zip(*(links.finish_pair(*pair) for pair in wide_sums))
    )
    grad_query = links.finish_rows(*q_sum, width // shards)
    grad_kv = links.finish_rows(*kv_sum, width // shards)
    return (
        block_out.reshape(micro, rows, width),
        d_input.reshape(micro, rows, width),
        grad_query,
        grad_kv[:, :KV_WIDTH],
        grad_kv[:, KV_WIDTH:],
        grad_output,
        grad_gate,
        grad_upper,
        grad_down,
        gain_sums[0],
        gain_sums[1],
    )


def solution(mesh):
    rows = P(None, AXES, None)
    weight, gain = P("shard", None), P("shard")
    return jax.shard_map(
        local,
        mesh=mesh,
        in_specs=(rows, P(None, "rep", None)) + (weight,) * 7 + (gain, gain, rows),
        out_specs=(rows, rows) + (weight,) * 7 + (gain, gain),
        check_vma=False,
    )
```

```python
import functools
import math

import jax
import jax.numpy as jnp
from jax import lax
from jax.experimental import pallas as pl
from jax.experimental.pallas import tpu as pltpu
from jax.sharding import PartitionSpec as P

QUERY_HEADS = 15
KEY_VALUE_HEADS = 5
HEAD_SIZE = 64
HALF_HEAD = HEAD_SIZE // 2
GROUP = QUERY_HEADS // KEY_VALUE_HEADS
KV_WIDTH = KEY_VALUE_HEADS * HEAD_SIZE
SCALE = HEAD_SIZE ** (-0.5)
EPS = 1e-05
AXES = ("rep", "shard")
BF = jnp.bfloat16
F32 = jnp.float32
CLOSED = -1e30
VMEM_LIMIT = 48 << 20
VMEM_MOST = 60 << 20


def dot(a, b, dims):
    return lax.dot_general(a, b, (dims, ((), ())), preferred_element_type=F32)


def nn(a, b):
    return dot(a, b, ((1,), (0,)))


def nt(a, b):
    return dot(a, b, ((1,), (1,)))


def tn(a, b):
    return dot(a, b, ((0,), (0,)))


def total(parts):
    return sum(part.astype(F32) for part in parts).astype(parts[0].dtype)


def meet(*values):
    return lax.optimization_barrier(values)


def rounded_up(columns):
    return -(-columns // 128) * 128


def rms_inverse(x):
    return lax.rsqrt(jnp.mean(x * x, axis=-1, keepdims=True) + EPS)


def cost(flops, exps, *arrays):
    size = sum(a.size * a.dtype.itemsize for a in arrays)
    return pl.CostEstimate(flops=flops, transcendentals=exps, bytes_accessed=size)


class Links:
    def __init__(self, reps, shards):
        self.reps, self.shards = reps, shards
        self.core = lax.axis_index("rep") % 2
        self.shard = lax.axis_index("shard")
        self.bits = shards.bit_length() - 1
        even = [1 << i for i in range(self.bits)]
        odd = even[:2][::-1] + even[2:]
        self.steps = list(zip(even, odd))
        self.hops = []
        for piece in range(shards):
            sums = [0, 0]
            for i, step in enumerate(self.steps):
                if piece >> i & 1:
                    sums = [sums[0] ^ step[0], sums[1] ^ step[1]]
            self.hops.append(jnp.where(self.core == 0, sums[0], sums[1]))

    def move(self, value, target):
        pairs = []
        for r in range(self.reps):
            for s in range(self.shards):
                goal = target(r, s)
                if goal is not None:
                    pairs.append((r * self.shards + s, goal[0] * self.shards + goal[1]))
        return lax.ppermute(value, AXES, pairs)

    def step(self, value, i):
        return self.move(value, lambda r, s: (r, s ^ self.steps[i][r % 2]))

    def swap(self, value):
        return self.move(value, lambda r, s: (r ^ 1, s))

    def reduce(self, plan, name):
        got = yield self.swap(plan.have[name + ".given"])
        sums = [plan.have.pop(name + ".kept"), got]
        del plan.have[name + ".given"]
        for i in reversed(range(self.bits)):
            block = sums[0].shape[0] // 2
            got = yield self.step(total([part[block:] for part in sums]), i)
            sums = [part[:block] for part in sums] + [got]
        value = total(sums)
        chips = self.reps // 2
        place = lax.axis_index("rep") // 2
        span = 1
        if chips % 4 == 0:
            inward, outward, middle = {0: 1, 3: 2}, {1: 0, 2: 3}, {1: 2, 2: 1}

            def along(value, table):
                def target(r, s):
                    chip = r // 2
                    if chip % 4 not in table:
                        return None
                    return ((chip - chip % 4 + table[chip % 4]) * 2 + r % 2, s)

                return self.move(value, target)

            value = total([value, (yield along(value, inward))])
            value = total([value, (yield along(value, middle))])
            back = yield along(value, outward)
            inner = (place % 4 == 1) | (place % 4 == 2)
            value = jnp.where(inner, value, back)
            span = 4
        while span < chips:
            value = total([value, self.move(value, lambda r, s: (r ^ (2 * span), s))])
            span *= 2
        other = yield self.swap(value)
        plan.have[name] = (value, other)

    def collect(self, plan, name):
        pieces = plan.have[name + ".pieces"]
        for i in reversed(range(self.bits)):
            keep = 1 << i
            got = yield [self.step(pieces[t + keep], i) for t in range(keep)]
            pieces = [total([pieces[t], got[t]]) for t in range(keep)]
        plan.have[name] = pieces[0]

    def beside(self, value):
        return self.move(value, lambda r, s: (r ^ 2, s))

    def near(self, value):
        return {1 << i: self.step(value, i) for i in range(self.bits)}

    def far(self, value, near):
        pieces = [value]
        for t in range(1, self.shards):
            top = t.bit_length() - 1
            pieces.append(near[t] if t in near else self.step(pieces[t - (1 << top)], top))
        return pieces

    def twin(self, piece):
        return piece if self.bits < 2 else piece >> 2 << 2 | (piece & 1) << 1 | (piece >> 1 & 1)

    def small_pieces(self, value):
        return [
            value if hop == 0 else self.move(value, lambda r, s, hop=hop: (r, s ^ hop))
            for hop in range(self.shards)
        ]

    def in_order(self, pieces):
        pieces = jnp.stack(pieces)
        value = pieces
        order = self.shard ^ jnp.arange(self.shards)
        hit = (order[:, None] == jnp.arange(self.shards)[None, :])[:, :, None, None]
        pieces = jnp.sum(jnp.where(hit, pieces[None], 0), axis=1, dtype=value.dtype)
        return jnp.concatenate([pieces[j] for j in range(self.shards)], axis=-1)

    def half_rows(self, rows):
        half = -(-rows // 32) * 16
        return half, self.core * (rows - half), (1 - self.core) * (rows - half)

    def order(self, scale, mine, theirs):
        kept = [(self.shard ^ hop) * scale + mine for hop in self.hops]
        given = [(self.shard ^ self.hops[self.twin(t)]) * scale + theirs for t in range(self.shards)]
        return kept, given

    def finish_rows(self, owned, other, rows):
        low = jnp.where(self.core == 0, owned, other)
        high = jnp.where(self.core == 0, other, owned)
        return jnp.concatenate([low[: rows - owned.shape[0]], high], axis=0).astype(F32)

    def finish_pair(self, owned, other):
        left = jnp.where(self.core == 0, owned, other)
        right = jnp.where(self.core == 0, other, owned)
        return left.astype(F32), right.astype(F32)


class Plan:
    def __init__(self):
        self.have, self.tasks, self.made = {}, {}, {}

    def start(self, name, task):
        self.tasks[name] = task
        self.made[name] = None

    def advance(self, *names):
        for name in names:
            if name in self.tasks:
                try:
                    self.made[name] = self.tasks[name].send(self.made[name])
                except StopIteration:
                    del self.tasks[name], self.made[name]

    def close(self):
        self.have, self.made = lax.optimization_barrier((self.have, self.made))


def joined(pieces, starts, shape):
    if any(piece.shape[0] % 16 or piece.shape[1] % 128 and piece.shape[1] < shape[1] for piece in pieces):
        whole = jnp.zeros(shape, pieces[0].dtype)
        for piece, start in zip(pieces, starts):
            whole = lax.dynamic_update_slice(whole, piece, start)
        pieces, starts = (whole,), [(0, 0)]
    return tuple(pieces), numbers([at for start in starts for at in start]), shape


def numbers(values):
    return jnp.stack([jnp.asarray(value, jnp.int32) for value in values])


def load(pieces, starts_ref, whole, sems):
    copies = []
    for i, piece in enumerate(pieces):
        rows = pl.ds(pl.multiple_of(starts_ref[2 * i], 16), piece.shape[0])
        if piece.shape[1] == whole.shape[1]:
            place = whole.at[rows, :]
        else:
            columns = pl.ds(pl.multiple_of(starts_ref[2 * i + 1], 128), piece.shape[1])
            place = whole.at[rows, columns]
        copies.append(pltpu.make_async_copy(piece, place, sems.at[i]))
        copies[-1].start()
    return copies


def wait(copies):
    for copy in copies:
        copy.wait()


IN_VMEM = pl.BlockSpec(memory_space=pltpu.VMEM)
IN_SMEM = pl.BlockSpec(memory_space=pltpu.SMEM)
ANYWHERE = pl.BlockSpec(memory_space=pl.ANY)


def upright(ref):
    return jnp.concatenate([jnp.transpose(ref[m]) for m in range(ref.shape[0])], axis=0)


def lay_down(value, ref):
    rows = ref.shape[2]
    for m in range(ref.shape[0]):
        ref[m] = jnp.transpose(value[m * rows : (m + 1) * rows])


def turn(chunk, cosine, sine):
    lane = lax.broadcasted_iota(jnp.int32, chunk.shape, 1)
    partner = jnp.where(
        lane % HEAD_SIZE < HALF_HEAD,
        pltpu.roll(chunk, 128 - HALF_HEAD, 1),
        pltpu.roll(chunk, HALF_HEAD, 1),
    )
    return chunk * cosine + partner * sine


def project_kernel(count, starts_ref, x_ref, gains_ref, cos_ref, sin_ref, *refs):
    pieces = refs[:count]
    q_ref, kv_ref, whole, sems = refs[count:]
    copies = load(pieces, starts_ref, whole, sems)
    x = upright(x_ref).astype(F32)
    width = x.shape[1]
    act = (x * rms_inverse(x) * gains_ref[0:1, :]).astype(BF)
    wait(copies)
    cosine, sine = cos_ref[...], sin_ref[...]
    for first in range(0, width + KV_WIDTH, 256):
        linear = nn(act, whole[:width, first : first + 256])
        for at in range(first, first + 256, 128):
            chunk = turn(linear[:, at - first : at - first + 128], cosine, sine)
            if at + 128 <= width:
                q_ref[:, at : at + 128] = (chunk * SCALE).astype(BF)
            elif at < width:
                q_ref[:, at:width] = (chunk[:, : width - at] * SCALE).astype(BF)
                kv_ref[:, : at + 128 - width] = chunk[:, width - at :].astype(BF)
            else:
                kv_ref[:, at - width : at - width + 128] = chunk.astype(BF)
    kv_ref[:, KV_WIDTH:] = nn(act, whole[width:, width:]).astype(BF)


def project(x, gains, cosine, sine, pieces, starts, shape):
    micro, width, rows = x.shape
    tokens = micro * rows
    outs = (
        jax.ShapeDtypeStruct((tokens, width), BF),
        jax.ShapeDtypeStruct((tokens, 2 * KV_WIDTH), BF),
    )
    table = pl.BlockSpec((tokens, 128), lambda i: (0, 0))
    return pl.pallas_call(
        functools.partial(project_kernel, len(pieces)),
        grid=(1,),
        name="project",
        in_specs=[IN_SMEM] + [IN_VMEM] * 2 + [table] * 2 + [ANYWHERE] * len(pieces),
        out_specs=(IN_VMEM,) * 2,
        out_shape=outs,
        scratch_shapes=[pltpu.VMEM(shape, BF), pltpu.SemaphoreType.DMA((len(pieces),))],
        cost_estimate=cost(2 * tokens * width * (width + 2 * KV_WIDTH), 0, x, *outs, *pieces),
        compiler_params=pltpu.CompilerParams(vmem_limit_bytes=VMEM_LIMIT),
    )(starts, x, gains, cosine, sine, *pieces)


def feed_kernel(counts, s0_ref, s1_ref, s2_ref, x_ref, attn_ref, cot_ref, gains_ref, *refs):
    total = sum(counts)
    attention_pieces = refs[: counts[0]]
    pair_pieces = refs[counts[0] : counts[0] + counts[1]]
    down_pieces = refs[counts[0] + counts[1] : total]
    out_ref, inner_ref, slopes_ref, act_t_ref, attn_t_ref, dy_ref, dres_ref, low_ref, dattn_ref = refs[
        total : total + 9
    ]
    w_attn, w_pair, w_down, resid_ref, dact_ref, sems0, sems1, sems2 = refs[total + 9 :]
    attention_copies = load(attention_pieces, s0_ref, w_attn, sems0)
    pair_copies = load(pair_pieces, s1_ref, w_pair, sems1)
    down_copies = load(down_pieces, s2_ref, w_down, sems2)
    width = x_ref.shape[1]
    hidden = w_pair.shape[1]
    tile = hidden // 5
    gain = gains_ref[1:2, :]
    x = upright(x_ref).astype(F32)
    dy_ref[...] = upright(cot_ref)
    attn_t_ref[...] = jnp.transpose(attn_ref[...])
    wait(attention_copies)
    w_output = w_attn[width:, :width]
    resid = x + nn(attn_ref[...], w_output)
    resid_ref[...] = resid
    dres_ref[...] = resid
    root = rms_inverse(resid)
    act = (resid * root * gain).astype(BF)
    act_t_ref[...] = jnp.transpose(act)
    wait(pair_copies)
    wait(down_copies)
    dy = dy_ref[...]
    for first in range(0, hidden, tile):
        here = slice(first, first + tile)
        gate = nn(act, w_pair[:width, here])
        upper = nn(act, w_pair[width:, here])
        d_inner = nt(dy, w_down[here, :])
        sigmoid = 1.0 / (1.0 + jnp.exp(-gate))
        silu = gate * sigmoid
        inner = (silu * upper).astype(BF)
        inner_ref[here, :] = jnp.transpose(inner)
        d_gate = (d_inner * upper * sigmoid * (1.0 + gate * (1.0 - sigmoid))).astype(BF)
        d_upper = (d_inner * silu).astype(BF)
        slopes_ref[0, :, here] = d_gate
        slopes_ref[1, :, here] = d_upper
        out = nn(inner, w_down[here, :])
        d_act = nt(d_gate, w_pair[:width, here]) + nt(d_upper, w_pair[width:, here])
        resid_ref[...] += out
        if first == 0:
            dact_ref[...] = d_act
        else:
            dact_ref[...] += d_act
    lay_down(resid_ref[...].astype(BF), out_ref)
    normed = dres_ref[...] * root
    d_act = dact_ref[...]
    d_normed = d_act * gain
    d_resid = dy.astype(F32) + root * (
        d_normed - normed * jnp.mean(d_normed * normed, axis=-1, keepdims=True)
    )
    dres_ref[...] = d_resid
    low = d_resid.astype(BF)
    low_ref[...] = low
    dattn_ref[...] = nt(low, w_output).astype(BF)


def feed(x, attn, dy, gains, attention_got, pair_got, down_got):
    micro, width, rows = x.shape
    tokens = micro * rows
    groups = [attention_got, pair_got, down_got]
    counts = [len(pieces) for pieces, _, _ in groups]
    shapes = [shape for _, _, shape in groups]
    hidden = shapes[1][1]
    outs = (
        jax.ShapeDtypeStruct(x.shape, BF),
        jax.ShapeDtypeStruct((hidden, tokens), BF),
        jax.ShapeDtypeStruct((2, tokens, hidden), BF),
        jax.ShapeDtypeStruct((width, tokens), BF),
        jax.ShapeDtypeStruct((width, tokens), BF),
        jax.ShapeDtypeStruct((tokens, width), BF),
        jax.ShapeDtypeStruct((tokens, width), F32),
        jax.ShapeDtypeStruct((tokens, width), BF),
        jax.ShapeDtypeStruct((tokens, width), BF),
    )
    every = [piece for pieces, _, _ in groups for piece in pieces]
    return pl.pallas_call(
        functools.partial(feed_kernel, counts),
        name="feed",
        in_specs=[IN_SMEM] * 3 + [IN_VMEM] * 4 + [ANYWHERE] * len(every),
        out_specs=(IN_VMEM,) * 9,
        out_shape=outs,
        scratch_shapes=[pltpu.VMEM(shape, BF) for shape in shapes]
        + [pltpu.VMEM((tokens, width), F32)] * 2
        + [pltpu.SemaphoreType.DMA((count,)) for count in counts],
        cost_estimate=cost(
            2 * tokens * width * (6 * hidden + 3 * width), tokens * hidden, x, x, x, *outs, *every
        ),
        compiler_params=pltpu.CompilerParams(vmem_limit_bytes=VMEM_MOST),
    )(*(starts for _, starts, _ in groups), x, attn, dy, gains, *every)


def pick_rows(source, starts_ref, base, rows, count, target):
    for t in range(count):
        start = pl.multiple_of(starts_ref[base + t], 16)
        target[t * rows : (t + 1) * rows, :] = source[pl.ds(start, rows), :]


def weight_grad_kernel(parts, count, starts_ref, *refs):
    operands = refs[: 2 * len(parts)]
    out_ref = refs[2 * len(parts)]
    ordered = refs[2 * len(parts) + 1 :]
    block = sum(parts)

    @pl.when(pl.program_id(0) == 0)
    def _():
        for i, rows in enumerate(parts):
            pick_rows(operands[2 * i], starts_ref, 1 + i * count, rows, count, ordered[i])

    at = 0
    for i, rows in enumerate(parts):
        made = nn(ordered[i][...], operands[2 * i + 1][...]).astype(BF)
        columns = made.shape[1]
        for t in range(count):
            place = slice(t * block + at, t * block + at + rows)
            out_ref[place, :columns] = made[t * rows : (t + 1) * rows]
            if columns < out_ref.shape[1]:
                out_ref[place, columns:] = jnp.zeros((rows, out_ref.shape[1] - columns), BF)
        at += rows


def weight_grad(terms, column=0, columns=None, choice=0):
    count = len(terms[0][3])
    parts = [term[2] for term in terms]
    block = sum(parts)
    tokens = terms[0][0].shape[1]
    columns = columns or terms[0][1].shape[-1]
    wide = rounded_up(columns)
    if any(rows % 16 for rows in parts) or any(term[0].shape[0] // count % 16 for term in terms):
        made = []
        for left, right, rows, starts in terms:
            right = right if right.ndim == 2 else lax.dynamic_index_in_dim(right, choice, 0, keepdims=False)
            grad = nn(left, right[:, column * columns : (column + 1) * columns]).astype(BF)
            grad = jnp.pad(grad, ((0, 0), (0, wide - columns)))
            made.append([lax.dynamic_slice_in_dim(grad, start, rows, 0) for start in starts])
        return jnp.concatenate([part for group in zip(*made) for part in group], axis=0)
    in_specs, args, flops = [], [], 0
    tile = 256 if columns % 256 == 0 else columns
    skip = column * (columns // tile)
    for left, right, rows, starts in terms:
        in_specs.append(pl.BlockSpec(left.shape, lambda n, info: (0, 0)))
        if right.ndim == 2:
            in_specs.append(pl.BlockSpec((tokens, tile), lambda n, info: (0, skip + n)))
        else:
            in_specs.append(pl.BlockSpec((None, tokens, tile), lambda n, info: (info[0], 0, skip + n)))
        args += [left, right]
        flops += 2 * tokens * rows * count * columns
    out = jax.ShapeDtypeStruct((count * block, wide), BF)
    info = numbers([choice] + [start for term in terms for start in term[3]])
    return pl.pallas_call(
        functools.partial(weight_grad_kernel, parts, count),
        grid_spec=pltpu.PrefetchScalarGridSpec(
            num_scalar_prefetch=1,
            grid=(columns // tile,),
            in_specs=in_specs,
            out_specs=pl.BlockSpec((count * block, rounded_up(tile)), lambda n, info: (0, n)),
            scratch_shapes=[pltpu.VMEM((count * rows, tokens), BF) for rows in parts],
        ),
        out_shape=out,
        name="weight_grad",
        cost_estimate=cost(flops, 0, out, *args),
        compiler_params=pltpu.CompilerParams(vmem_limit_bytes=VMEM_LIMIT),
    )(info, *args)


def turn_keys(source, target, at, cosine, sine):
    rows = source.shape[0]
    for first in range(0, KV_WIDTH, 128):
        chunk = turn(source[:, first : first + 128].astype(F32), cosine, -sine).astype(BF)
        last = min(first + 128, KV_WIDTH)
        target[at : at + rows, first:last] = chunk[:, : last - first]
    target[at : at + rows, KV_WIDTH:] = source[:, KV_WIDTH:]


def attention_grad_kernel(shards, half, starts_ref, gain_ref, cos_ref, sin_ref, dq_ref, *refs):
    xs, dkvs = refs[:shards], refs[shards : 2 * shards]
    outs, (act, dkv, ordered) = refs[2 * shards : 2 * shards + 2], refs[2 * shards + 2 :]
    micro, width, rows = xs[0].shape
    tokens = micro * rows
    for t in range(shards):
        here = slice(t * tokens, (t + 1) * tokens)
        turn_keys(dkvs[t], dkv, t * tokens, cos_ref[here, :], sin_ref[here, :])
        for m in range(micro):
            x = xs[t][m].astype(F32)
            root = lax.rsqrt(jnp.mean(x * x, axis=0, keepdims=True) + EPS)
            first = t * tokens + m * rows
            act[:, first : first + rows] = (x * root * gain_ref[...]).astype(BF)
    for i, out_ref in enumerate(outs):
        pick_rows(act, starts_ref, i * shards, half, shards, ordered)
        out_ref[:, :width] = nn(ordered[:, :tokens], dq_ref[...]).astype(BF)
        start = rounded_up(width)
        if start > width:
            out_ref[:, width:start] = jnp.zeros((out_ref.shape[0], start - width), BF)
        out_ref[:, start:] = nn(ordered[...], dkv[...]).astype(BF)


def attention_grad(x_all, gain, cosine, sine, dq, dkv_all, half, given, kept):
    shards = len(x_all)
    micro, width, rows = x_all[0].shape
    every = shards * micro * rows
    columns = rounded_up(width) + 2 * KV_WIDTH
    out = jax.ShapeDtypeStruct((shards * half, columns), BF)
    if half % 16 or width // shards % 16:
        xs = jnp.concatenate([x[m] for x in x_all for m in range(micro)], axis=1).astype(F32)
        act = xs * lax.rsqrt(jnp.mean(xs * xs, axis=0, keepdims=True) + EPS) * gain
        act = act.astype(BF)
        dkv = jnp.concatenate(dkv_all, axis=0)
        keys = dkv[:, :KV_WIDTH].astype(F32).reshape(every, -1, 2, HALF_HEAD)
        c, s = cosine[:, None, :HALF_HEAD], sine[:, None, HALF_HEAD:HEAD_SIZE]
        first, second = keys[:, :, 0], keys[:, :, 1]
        keys = jnp.stack([first * c + second * s, second * c - first * s], axis=2)
        dkv = jnp.concatenate([keys.reshape(every, KV_WIDTH).astype(BF), dkv[:, KV_WIDTH:]], axis=1)
        q = jnp.pad(nn(act[:, : micro * rows], dq), ((0, 0), (0, rounded_up(width) - width)))
        grad = jnp.concatenate([q, nn(act, dkv)], axis=1).astype(BF)
        return [
            jnp.concatenate([lax.dynamic_slice_in_dim(grad, start, half, 0) for start in starts])
            for starts in (given, kept)
        ]
    return pl.pallas_call(
        functools.partial(attention_grad_kernel, shards, half),
        name="attention_grad",
        in_specs=[IN_SMEM] + [IN_VMEM] * (4 + 2 * shards),
        out_specs=(IN_VMEM,) * 2,
        out_shape=(out, out),
        scratch_shapes=[
            pltpu.VMEM((width, every), BF),
            pltpu.VMEM((every, 2 * KV_WIDTH), BF),
            pltpu.VMEM((shards * half, every), BF),
        ],
        cost_estimate=cost(
            4 * shards * half * (every * 2 * KV_WIDTH + micro * rows * width), 0, *x_all, *dkv_all, out, out
        ),
        compiler_params=pltpu.CompilerParams(vmem_limit_bytes=VMEM_MOST),
    )(numbers(given + kept), gain, cosine, sine, dq, *x_all, *dkv_all)


def finish_kernel(count, starts_ref, x_ref, low_ref, kv_ref, dres_ref, gains_ref, cos_ref, sin_ref, *refs):
    pieces = refs[:count]
    dx_ref, whole, kv_turned, sems = refs[count:]
    copies = load(pieces, starts_ref, whole, sems)
    turn_keys(kv_ref, kv_turned, 0, cos_ref[...], sin_ref[...])
    x = upright(x_ref).astype(F32)
    width = x.shape[1]
    root = rms_inverse(x)
    normed = x * root
    wait(copies)
    d_act = nt(low_ref[...], whole[:width, :width])
    d_act += nt(kv_turned[:, :KV_WIDTH], whole[:width, width:])
    d_act += nt(kv_turned[:, KV_WIDTH:], whole[width:, width:])
    d_normed = d_act * gains_ref[0:1, :]
    d_x = dres_ref[...] + root * (d_normed - normed * jnp.mean(d_normed * normed, axis=-1, keepdims=True))
    lay_down(d_x.astype(BF), dx_ref)


def finish(x, low, kv, dres, gains, cosine, sine, pieces, starts, shape):
    micro, width, rows = x.shape
    tokens = micro * rows
    table = pl.BlockSpec((tokens, 128), lambda i: (0, 0))
    return pl.pallas_call(
        functools.partial(finish_kernel, len(pieces)),
        grid=(1,),
        name="finish",
        in_specs=[IN_SMEM] + [IN_VMEM] * 5 + [table] * 2 + [ANYWHERE] * len(pieces),
        out_specs=IN_VMEM,
        out_shape=jax.ShapeDtypeStruct(x.shape, BF),
        scratch_shapes=[
            pltpu.VMEM(shape, BF),
            pltpu.VMEM((tokens, 2 * KV_WIDTH), BF),
            pltpu.SemaphoreType.DMA((len(pieces),)),
        ],
        cost_estimate=cost(2 * tokens * width * (width + 2 * KV_WIDTH), 0, x, low, dres, *pieces),
        compiler_params=pltpu.CompilerParams(vmem_limit_bytes=VMEM_LIMIT),
    )(starts, x, low, kv, dres, gains, cosine, sine, *pieces)


def head(ref, h):
    return ref[:, h * HEAD_SIZE : (h + 1) * HEAD_SIZE]


def widen(value, columns):
    n = value.shape[0]
    lane = lax.broadcasted_iota(jnp.int32, (n, HEAD_SIZE), 1)
    tail = jnp.zeros((n, HEAD_SIZE), F32)
    for c, column in enumerate(columns):
        tail = jnp.where(lane == c, column, tail)
    return jnp.concatenate([value, tail.astype(BF)], axis=1)


def split(column):
    high = column.astype(BF).astype(F32)
    middle = (column - high).astype(BF).astype(F32)
    return [high, middle, column - high - middle]


def attend_kernel(shards, seg_rows, q_ref, *refs):
    kv = refs[:shards]
    bias_ref = refs[shards]
    o_ref, lse_ref = refs[-2:]
    rows = q_ref.shape[0]
    i = lax.broadcasted_iota(jnp.int32, (rows, rows), 0)
    j = lax.broadcasted_iota(jnp.int32, (rows, rows), 1)
    same = (i // seg_rows) == (j // seg_rows)
    own = jnp.where(j > i, CLOSED, jnp.where(same, 0.0, bias_ref[0:1, :]))
    one = jnp.ones((rows, 1), F32)
    bias_columns = jnp.transpose(bias_ref[...])
    lse = jnp.zeros((rows, 128), F32)
    lane = lax.broadcasted_iota(jnp.int32, (rows, 128), 1)
    for g in range(KEY_VALUE_HEADS):
        keys, values = [], []
        for t in range(shards):
            keys.append(widen(head(kv[t], g), [bias_columns[:, t : t + 1]] if t else []))
            values.append(widen(head(kv[t], KEY_VALUE_HEADS + g), [one]))
        for h in range(g * GROUP, g * GROUP + GROUP):
            q = widen(head(q_ref, h), [one])
            scores = [nt(q, k) for k in keys]
            scores[0] = scores[0] + own
            peak = functools.reduce(jnp.maximum, scores)
            peak = jnp.max(peak, axis=1, keepdims=True)
            terms = [nn(jnp.exp(s - peak).astype(BF), v) for s, v in zip(scores, values)]
            mixed = sum(terms[1:], terms[0])
            total = mixed[:, HEAD_SIZE : HEAD_SIZE + 1]
            o_ref[:, h * HEAD_SIZE : (h + 1) * HEAD_SIZE] = (mixed[:, :HEAD_SIZE] / total).astype(BF)
            lse = jnp.where(lane == h, peak + jnp.log(total), lse)
    lse_ref[...] = lse


def attend_back_kernel(shards, seg_rows, q_ref, *refs):
    kv = refs[:shards]
    bias_ref, o_ref, do_ref, lse_ref, cos_ref, sin_ref = refs[shards : shards + 6]
    dq_ref = refs[-1 - shards]
    dkv = refs[-shards:]
    rows = q_ref.shape[0]
    i = lax.broadcasted_iota(jnp.int32, (rows, rows), 1)
    j = lax.broadcasted_iota(jnp.int32, (rows, rows), 0)
    bias_columns = jnp.transpose(bias_ref[...])
    same = (i // seg_rows) == (j // seg_rows)
    own_column = jnp.broadcast_to(bias_columns[:, 0:1], (rows, rows))
    own = jnp.where(j > i, CLOSED, jnp.where(same, 0.0, own_column))
    one, zero = jnp.ones((rows, 1), F32), jnp.zeros((rows, 1), F32)
    cosine, sine = cos_ref[...], sin_ref[...]
    for g in range(KEY_VALUE_HEADS):
        keys, values, turned = [], [], []
        for t in range(shards):
            k = head(kv[t], g)
            turned.append(jnp.transpose(k))
            keys.append(widen(k, [bias_columns[:, t : t + 1] if t else zero, one, one, one]))
            values.append(widen(head(kv[t], KEY_VALUE_HEADS + g), [one, one, one]))
        dk, dv = [None] * shards, [None] * shards
        for h in range(g * GROUP, g * GROUP + GROUP):
            q, do = head(q_ref, h), head(do_ref, h)
            centre = jnp.sum(head(o_ref, h).astype(F32) * do.astype(F32), axis=1, keepdims=True)
            q_wide = widen(q, [one] + split(-lse_ref[:, h : h + 1]))
            do_wide = widen(do, split(-centre))
            dq = None
            for t in range(shards):
                scores = nt(keys[t], q_wide)
                if t == 0:
                    scores = scores + own
                probs = jnp.exp(scores)
                ds = (probs * nt(values[t], do_wide)).astype(BF)
                v_term = nn(probs.astype(BF), do)
                k_term = nn(ds, q)
                q_term = nn(turned[t], ds)
                dv[t] = v_term if dv[t] is None else dv[t] + v_term
                dk[t] = k_term if dk[t] is None else dk[t] + k_term
                dq = q_term if dq is None else dq + q_term
            dq = dq * SCALE
            first, second = dq[:HALF_HEAD], dq[HALF_HEAD:]
            back = jnp.concatenate(
                [first * cosine + second * sine, second * cosine - first * sine], axis=0
            )
            dq_ref[:, h * HEAD_SIZE : (h + 1) * HEAD_SIZE] = jnp.transpose(back).astype(BF)
        for t in range(shards):
            dkv[t][:, g * HEAD_SIZE : (g + 1) * HEAD_SIZE] = dk[t].astype(BF)
            g_value = KEY_VALUE_HEADS + g
            dkv[t][:, g_value * HEAD_SIZE : (g_value + 1) * HEAD_SIZE] = dv[t].astype(BF)


def attend(micro, seg_rows, q, kv, bias):
    shards, tokens, width = len(kv), q.shape[0], q.shape[1]
    rows = tokens // micro
    here = lambda w: pl.BlockSpec((rows, w), lambda m: (m, 0))
    outs = (jax.ShapeDtypeStruct((tokens, width), BF), jax.ShapeDtypeStruct((tokens, 128), F32))
    pairs = tokens * rows * shards * QUERY_HEADS
    return pl.pallas_call(
        functools.partial(attend_kernel, shards, seg_rows),
        grid=(micro,),
        name="attend",
        in_specs=[here(width)]
        + [here(2 * KV_WIDTH)] * shards
        + [pl.BlockSpec((None,) + bias.shape[1:], lambda m: (m, 0, 0))],
        out_specs=(here(width), here(128)),
        out_shape=outs,
        cost_estimate=cost(16 * HEAD_SIZE * pairs, pairs, q),
        compiler_params=pltpu.CompilerParams(vmem_limit_bytes=VMEM_LIMIT),
    )(q, *kv, bias)


def attend_back(m, rows, seg_rows, q, kv, bias, o, do, lse, cosine, sine, earlier):
    shards, tokens, width = len(kv), q.shape[0], q.shape[1]
    here = lambda w: pl.BlockSpec((rows, w), lambda i: (m, 0))
    turned = pl.BlockSpec((HALF_HEAD, rows), lambda i: (0, m))
    outs = (jax.ShapeDtypeStruct((tokens, width), BF),)
    outs += (jax.ShapeDtypeStruct((tokens, 2 * KV_WIDTH), BF),) * shards
    pairs = rows * rows * shards * QUERY_HEADS
    return pl.pallas_call(
        functools.partial(attend_back_kernel, shards, seg_rows),
        grid=(1,),
        name="attend_back",
        in_specs=[here(width)]
        + [here(2 * KV_WIDTH)] * shards
        + [pl.BlockSpec((None,) + bias.shape[1:], lambda i: (m, 0, 0))]
        + [here(width), here(width), here(128), turned, turned]
        + [pl.BlockSpec(memory_space=pl.ANY)] * len(earlier),
        out_specs=(here(width),) + (here(2 * KV_WIDTH),) * shards,
        out_shape=outs,
        input_output_aliases={shards + 7 + i: i for i in range(len(earlier))},
        cost_estimate=cost(40 * HEAD_SIZE * pairs, pairs, q),
        compiler_params=pltpu.CompilerParams(vmem_limit_bytes=VMEM_LIMIT),
    )(q, *kv, bias, o, do, lse, cosine, sine, *earlier)


def local(
    block_input,
    parent_ids,
    w_query,
    key_weight,
    value_weight,
    w_output,
    w_gate,
    w_up,
    w_down,
    norm_first,
    norm_second,
    out_cotangent,
):
    micro, rows, width = block_input.shape
    shards = lax.axis_size("shard")
    links = Links(lax.axis_size("rep"), shards)
    tree = rows * shards
    segs = parent_ids.shape[2]
    seg_rows = tree // segs
    tokens = micro * rows
    hidden = w_gate.shape[1]

    inputs = block_input.swapaxes(1, 2)
    cotangent = out_cotangent.swapaxes(1, 2)

    even = links.core == 0
    side = lax.axis_index("rep") // 2 % 2
    left = jnp.concatenate([w_query, key_weight], axis=1)
    right = jnp.concatenate([w_output, value_weight], axis=1)
    attn_mine = jnp.where(even, left, right)
    pair_cut = hidden // 2
    pair_mine = lax.dynamic_slice_in_dim(jnp.where(even, w_gate, w_up), side * pair_cut, pair_cut, 1)
    down_cut = w_down.shape[0] // 2
    down_mine = lax.dynamic_slice_in_dim(w_down, links.core * down_cut, down_cut, 0)

    attn_near = links.near(attn_mine)
    gain_pieces = links.small_pieces(jnp.stack([norm_first, norm_second]))
    attn_mine, attn_near, gain_pieces, pair_mine, down_mine = meet(
        attn_mine, attn_near, gain_pieces, pair_mine, down_mine
    )

    gains = links.in_order(gain_pieces).astype(F32)
    attn_all = links.far(attn_mine, attn_near)
    attn_swapped = {t: links.swap(attn_near[t]) for t in attn_near}
    pair_near = {1: links.step(pair_mine, 0)}
    parents = parent_ids[:, 0]
    seg = jnp.arange(segs)
    after_parent = jnp.concatenate([parents[:, 1:], jnp.full((micro, 1), -1, parents.dtype)], axis=1)
    on_path = (seg % 2 == 0)[None] | (after_parent == seg[None])
    below = (seg[None, :] < seg[:, None])[None]
    depth = jnp.sum(jnp.where(below, on_path.astype(F32)[:, None, :], 0.0), axis=-1)

    def row_numbers(hop):
        return (links.shard ^ hop) * rows + jnp.arange(rows)

    def pick(table, numbers):
        hit = (numbers // seg_rows)[..., None] == seg
        return jnp.sum(jnp.where(hit[None], table.reshape(micro, *(1,) * numbers.ndim, segs), 0), axis=-1)

    key_rows = jnp.stack([row_numbers(hop) for hop in links.hops])
    positions = pick(depth, key_rows) * seg_rows + (key_rows % seg_rows).astype(F32)
    freqs = jnp.exp(-math.log(10000.0) * jnp.arange(HALF_HEAD, dtype=F32) * (2.0 / HEAD_SIZE))
    angles = freqs[:, None] * positions.swapaxes(0, 1).reshape(1, shards * tokens)
    cosine_t, sine_t = jnp.cos(angles), jnp.sin(angles)
    cosine = jnp.tile(cosine_t.T, (1, 4))
    sine = jnp.tile(jnp.concatenate([-sine_t.T, sine_t.T], axis=1), (1, 2))
    open_key = (pick(on_path.astype(F32), key_rows) > 0.5) & (
        (key_rows < links.shard * rows) | (jnp.arange(shards) == 0)[:, None]
    )
    bias = jnp.where(open_key, 0.0, CLOSED)
    bias = jnp.pad(bias, ((0, 0), (0, 8 - shards), (0, 0)))

    attn_all, attn_swapped, pair_mine, pair_near, gains, cosine, sine, bias, down_mine = meet(
        attn_all, attn_swapped, pair_mine, pair_near, gains, cosine, sine, bias, down_mine
    )

    for t in range(1, shards):
        if t not in attn_swapped:
            attn_swapped[t] = links.swap(attn_all[t])
    shard_rows = width // shards

    def pair_place(weight, hop):
        return weight * width + (links.shard ^ hop) * shard_rows

    pieces, starts = [left, right], [(pair_place(0, 0), 0), (pair_place(1, 0), 0)]
    for t in range(1, shards):
        pieces += [attn_all[t], attn_swapped[t]]
        starts += [
            (pair_place(links.core, links.hops[t]), 0),
            (pair_place(1 - links.core, links.hops[links.twin(t)]), 0),
        ]
    attention_got = joined(pieces, starts, (2 * width, left.shape[1]))
    pair_near |= {1 << i: links.step(pair_mine, i) for i in range(1, links.bits)}
    pair_beside = {1: links.beside(pair_near[1])}
    down_near = {1: links.step(down_mine, 0)}
    queries, kv = project(inputs, gains, cosine, sine, *attention_got)
    queries, kv, pair_mine, pair_near, pair_beside, down_mine, down_near = meet(
        queries, kv, pair_mine, pair_near, pair_beside, down_mine, down_near
    )

    kv_near = links.near(kv)
    pair_beside |= {t: links.beside(pair_near[t]) for t in pair_near if t > 1}
    kv_near, kv, pair_beside, pair_near, pair_mine = meet(kv_near, kv, pair_beside, pair_near, pair_mine)

    kv_all = links.far(kv, kv_near)
    pair_all = links.far(pair_mine, pair_near)
    pair_swapped = {t: links.swap(pair_near[t]) for t in pair_near}
    pair_crossed = {t: links.swap(pair_beside[t]) for t in pair_beside}
    kv_all, pair_all, pair_swapped, pair_crossed, pair_beside, down_mine, down_near = meet(
        kv_all, pair_all, pair_swapped, pair_crossed, pair_beside, down_mine, down_near
    )

    down_near |= {1 << i: links.step(down_mine, i) for i in range(1, links.bits)}
    down_all = links.far(down_mine, down_near)
    pair_beside |= {t: links.beside(pair_all[t]) for t in range(1, shards) if t not in pair_beside}
    attn, lse = attend(micro, seg_rows, queries, kv_all, bias)
    pair_swapped |= {t: links.swap(pair_all[t]) for t in range(1, shards) if t not in pair_swapped}
    attn, lse, down_all, pair_beside, pair_all, pair_swapped = meet(
        attn, lse, down_all, pair_beside, pair_all, pair_swapped
    )

    pair_crossed |= {t: links.swap(pair_beside[t]) for t in range(1, shards) if t not in pair_crossed}
    down_swapped = [None] + [links.swap(down_all[t]) for t in range(1, shards)]
    pieces, starts = [w_gate, w_up], [(pair_place(0, 0), 0), (pair_place(1, 0), 0)]
    for t in range(1, shards):
        pieces += [pair_all[t], pair_beside[t], pair_swapped[t], pair_crossed[t]]
        for row in (
            pair_place(links.core, links.hops[t]),
            pair_place(1 - links.core, links.hops[links.twin(t)]),
        ):
            starts += [(row, side * pair_cut), (row, (1 - side) * pair_cut)]
    pair_got = joined(pieces, starts, (2 * width, hidden))
    own = w_down.shape[0]
    pieces, starts = [w_down], [(links.shard * own, 0)]
    for t in range(1, shards):
        pieces += [down_all[t], down_swapped[t]]
        starts += [
            ((links.shard ^ links.hops[t]) * own + links.core * down_cut, 0),
            ((links.shard ^ links.hops[links.twin(t)]) * own + (1 - links.core) * down_cut, 0),
        ]
    down_got = joined(pieces, starts, (own * shards, width))
    attn, pair_pieces, down_pieces = meet(attn, pair_got[0], down_got[0])
    pair_got, down_got = (pair_pieces, *pair_got[1:]), (down_pieces, *down_got[1:])

    plan = Plan()
    have = lambda *names: [plan.have[name] for name in names]
    x_near = links.near(inputs)
    made = feed(inputs, attn, cotangent, gains, attention_got, pair_got, down_got)
    names = ("out", "inner", "slopes", "act", "attn_t", "dy", "d_resid", "d_resid_low", "d_attn")
    plan.have = dict(zip(names, made)) | {"x_near": x_near, "queries": queries, "kv": kv_all, "lse": lse, "attn": attn}
    plan.close()

    down_half = own // 2
    output_half, output_mine, output_theirs = links.half_rows(shard_rows)
    down_kept, down_given = links.order(own, links.core * down_half, (1 - links.core) * down_half)
    wide_kept, wide_given = links.order(shard_rows, 0, 0)
    some_kept, some_given = links.order(shard_rows, output_mine, output_theirs)

    def rows_grads(down, output):
        inner, dy, attn_t, low = have("inner", "dy", "attn_t", "d_resid_low")
        return weight_grad(((inner, dy, down_half, down), (attn_t, low, output_half, output)))

    def wide_grads(chunk, starts, choice):
        act, slopes = have("act", "slopes")
        return weight_grad(((act, slopes, shard_rows, starts),), chunk, hidden // 2, choice)

    plan.have["x_all"] = links.far(inputs, plan.have.pop("x_near"))
    plan.have["rows.given"] = rows_grads(down_given, some_given)
    plan.have["rows.kept"] = rows_grads(down_kept, some_kept)
    plan.close()

    for name in ("rows", "wide0", "wide1", "some"):
        plan.start(name, links.reduce(plan, name))
    plan.advance("rows")
    for chunk, name in enumerate(("wide0", "wide1")):
        plan.have[name + ".given"] = wide_grads(chunk, wide_given, 1 - links.core)
        plan.have[name + ".kept"] = wide_grads(chunk, wide_kept, links.core)
    plan.close()

    made = ()
    hops = [("rows", "wide0", "wide1"), ("rows", "wide0")]
    for m in range(micro):
        plan.advance(*hops[min(m, 1)])
        q, kv_now, o, do, lse_now = have("queries", "kv", "attn", "d_attn", "lse")
        made = attend_back(m, rows, seg_rows, q, kv_now, bias, o, do, lse_now, cosine_t, sine_t, made)
        plan.have["attn_grads"] = made = tuple(made)
        plan.close()
        made = plan.have["attn_grads"]

    d_queries, *d_kv = plan.have.pop("attn_grads")
    plan.have["dkv.pieces"] = d_kv
    plan.have["d_queries"] = d_queries
    plan.start("dkv", links.collect(plan, "dkv"))
    plan.advance("rows", "wide0", "wide1")
    given, kept = attention_grad(
        plan.have["x_all"], gains[0][:, None], cosine, sine, d_queries, d_kv, output_half, some_given, some_kept
    )
    plan.have["some.given"], plan.have["some.kept"] = given, kept
    plan.close()

    order = [("rows", "wide0", "wide1", "some", "dkv")] * 5 + [("wide1", "some")]
    while plan.tasks:
        plan.advance(*(order.pop(0) if order else tuple(plan.tasks)))
        if "dkv" in plan.have and "d_input" not in plan.have:
            plan.have["d_input"] = finish(
                inputs, *have("d_queries", "dkv", "d_resid"), gains, cosine, sine, *attention_got
            )
        plan.close()

    def owned(name, rows_of):
        value, other = plan.have[name]
        return links.finish_rows(value, other, rows_of)

    rows_own, rows_other = plan.have["rows"]
    grad_down = links.finish_rows(rows_own[:down_half, :width], rows_other[:down_half, :width], own)
    grad_output = links.finish_rows(rows_own[down_half:, :width], rows_other[down_half:, :width], shard_rows)
    grad_gate, grad_upper = (
        jnp.concatenate(parts, axis=1)
        for parts in zip(*(links.finish_pair(*plan.have[name]) for name in ("wide0", "wide1")))
    )
    some = owned("some", shard_rows)
    first = rounded_up(width)
    grad_query, grad_key, grad_value = (
        some[:, :width],
        some[:, first : first + KV_WIDTH],
        some[:, first + KV_WIDTH :],
    )

    def gain_grad(gain, *pairs):
        sums = sum(jnp.sum(weight.astype(F32) * grad, axis=1) for weight, grad in pairs)
        return sums / gain.astype(F32)

    return (
        plan.have["out"].swapaxes(1, 2),
        plan.have["d_input"].swapaxes(1, 2),
        grad_query,
        grad_key,
        grad_value,
        grad_output,
        grad_gate,
        grad_upper,
        grad_down,
        gain_grad(norm_first, (w_query, grad_query), (key_weight, grad_key), (value_weight, grad_value)),
        gain_grad(norm_second, (w_gate, grad_gate), (w_up, grad_upper)),
    )


def solution(mesh):
    rows = P(None, AXES, None)
    weight, gain = P("shard", None), P("shard")
    return jax.shard_map(
        local,
        mesh=mesh,
        in_specs=(rows, P(None, "rep", None)) + (weight,) * 7 + (gain, gain, rows),
        out_specs=(rows, rows) + (weight,) * 7 + (gain, gain),
        check_vma=False,
    )
```

```python
import functools
import math

import jax
import jax.numpy as jnp
from jax import lax
from jax.experimental import pallas as pl
from jax.experimental.layout import Layout, with_layout_constraint
from jax.experimental.pallas import tpu as pltpu
from jax.sharding import PartitionSpec as P

QUERY_HEADS = 15
KEY_VALUE_HEADS = 5
HEAD_SIZE = 64
HALF_HEAD = HEAD_SIZE // 2
GROUP = QUERY_HEADS // KEY_VALUE_HEADS
KV_WIDTH = KEY_VALUE_HEADS * HEAD_SIZE
SCALE = HEAD_SIZE ** (-0.5)
EPS = 1e-05
AXES = ("rep", "shard")
BF = jnp.bfloat16
F32 = jnp.float32
CLOSED = -1e30
VMEM_LIMIT = 48 << 20
VMEM_MOST = 60 << 20


def dot(a, b, dims):
    return lax.dot_general(a, b, (dims, ((), ())), preferred_element_type=F32)


def nn(a, b):
    return dot(a, b, ((1,), (0,)))


def nt(a, b):
    return dot(a, b, ((1,), (1,)))


def tn(a, b):
    return dot(a, b, ((0,), (0,)))


def total(parts):
    return sum(part.astype(F32) for part in parts).astype(parts[0].dtype)


def meet(*values):
    return lax.optimization_barrier(values)


def rounded_up(columns):
    return -(-columns // 128) * 128


def rms_inverse(x):
    return lax.rsqrt(jnp.mean(x * x, axis=-1, keepdims=True) + EPS)


def cost(flops, exps, *arrays):
    size = sum(a.size * a.dtype.itemsize for a in arrays)
    return pl.CostEstimate(flops=flops, transcendentals=exps, bytes_accessed=size)


class Links:
    def __init__(self, reps, shards):
        self.reps, self.shards = reps, shards
        self.core = lax.axis_index("rep") % 2
        self.shard = lax.axis_index("shard")
        self.bits = shards.bit_length() - 1
        even = [1 << i for i in range(self.bits)]
        odd = even[:2][::-1] + even[2:]
        self.steps = list(zip(even, odd))
        self.hops = []
        for piece in range(shards):
            sums = [0, 0]
            for i, step in enumerate(self.steps):
                if piece >> i & 1:
                    sums = [sums[0] ^ step[0], sums[1] ^ step[1]]
            self.hops.append(jnp.where(self.core == 0, sums[0], sums[1]))

    def move(self, value, target):
        pairs = []
        for r in range(self.reps):
            for s in range(self.shards):
                goal = target(r, s)
                if goal is not None:
                    pairs.append((r * self.shards + s, goal[0] * self.shards + goal[1]))
        return lax.ppermute(value, AXES, pairs)

    def step(self, value, i):
        return self.move(value, lambda r, s: (r, s ^ self.steps[i][r % 2]))

    def swap(self, value):
        return self.move(value, lambda r, s: (r ^ 1, s))

    def reduce(self, plan, name):
        got = yield self.swap(plan.have[name + ".given"])
        sums = [plan.have.pop(name + ".kept"), got]
        del plan.have[name + ".given"]
        for i in reversed(range(self.bits)):
            block = sums[0].shape[0] // 2
            got = yield self.step(total([part[block:] for part in sums]), i)
            sums = [part[:block] for part in sums] + [got]
        value = total(sums)
        chips = self.reps // 2
        place = lax.axis_index("rep") // 2
        span = 1
        if chips % 4 == 0:
            inward, outward, middle = {0: 1, 3: 2}, {1: 0, 2: 3}, {1: 2, 2: 1}

            def along(value, table):
                def target(r, s):
                    chip = r // 2
                    if chip % 4 not in table:
                        return None
                    return ((chip - chip % 4 + table[chip % 4]) * 2 + r % 2, s)

                return self.move(value, target)

            value = total([value, (yield along(value, inward))])
            value = total([value, (yield along(value, middle))])
            back = yield along(value, outward)
            inner = (place % 4 == 1) | (place % 4 == 2)
            value = jnp.where(inner, value, back)
            span = 4
        while span < chips:
            value = total([value, self.move(value, lambda r, s: (r ^ (2 * span), s))])
            span *= 2
        other = yield self.swap(value)
        plan.have[name] = (value, other)

    def collect(self, plan, name):
        low, high = plan.have[name + ".pieces"]
        got = yield self.step(high, self.bits - 1)
        sums = [low, got]
        for i in reversed(range(self.bits - 1)):
            block = sums[0].shape[0] // 2
            got = yield self.step(total([part[block:] for part in sums]), i)
            sums = [part[:block] for part in sums] + [got]
        plan.have[name] = total(sums)[0]

    def beside(self, value):
        return self.move(value, lambda r, s: (r ^ 2, s))

    def near(self, value):
        return {1 << i: self.step(value, i) for i in range(self.bits)}

    def far(self, value, near):
        pieces = [value]
        for t in range(1, self.shards):
            top = t.bit_length() - 1
            pieces.append(near[t] if t in near else self.step(pieces[t - (1 << top)], top))
        return pieces

    def twin(self, piece):
        return piece if self.bits < 2 else piece >> 2 << 2 | (piece & 1) << 1 | (piece >> 1 & 1)

    def small_pieces(self, value):
        return [
            value if hop == 0 else self.move(value, lambda r, s, hop=hop: (r, s ^ hop))
            for hop in range(self.shards)
        ]

    def in_order(self, pieces):
        pieces = jnp.stack(pieces)
        value = pieces
        order = self.shard ^ jnp.arange(self.shards)
        hit = (order[:, None] == jnp.arange(self.shards)[None, :])[:, :, None, None]
        pieces = jnp.sum(jnp.where(hit, pieces[None], 0), axis=1, dtype=value.dtype)
        return jnp.concatenate([pieces[j] for j in range(self.shards)], axis=-1)

    def half_rows(self, rows):
        half = -(-rows // 32) * 16
        return half, self.core * (rows - half), (1 - self.core) * (rows - half)

    def order(self, scale, mine, theirs):
        kept = [(self.shard ^ hop) * scale + mine for hop in self.hops]
        given = [(self.shard ^ self.hops[self.twin(t)]) * scale + theirs for t in range(self.shards)]
        return kept, given

    def finish_rows(self, owned, other, rows):
        low = jnp.where(self.core == 0, owned, other)
        high = jnp.where(self.core == 0, other, owned)
        return jnp.concatenate([low[: rows - owned.shape[0]], high], axis=0).astype(F32)

    def finish_pair(self, owned, other):
        left = jnp.where(self.core == 0, owned, other)
        right = jnp.where(self.core == 0, other, owned)
        return left.astype(F32), right.astype(F32)


class Plan:
    def __init__(self):
        self.have, self.tasks, self.made = {}, {}, {}

    def start(self, name, task):
        self.tasks[name] = task
        self.made[name] = None

    def advance(self, *names):
        for name in names:
            if name in self.tasks:
                try:
                    self.made[name] = self.tasks[name].send(self.made[name])
                except StopIteration:
                    del self.tasks[name], self.made[name]

    def close(self):
        self.have, self.made = lax.optimization_barrier((self.have, self.made))


def joined(pieces, starts, shape):
    if any(piece.shape[0] % 16 or piece.shape[1] % 128 and piece.shape[1] < shape[1] for piece in pieces):
        whole = jnp.zeros(shape, pieces[0].dtype)
        for piece, start in zip(pieces, starts):
            whole = lax.dynamic_update_slice(whole, piece, start)
        pieces, starts = (whole,), [(0, 0)]
    return tuple(pieces), numbers([at for start in starts for at in start]), shape


def numbers(values):
    return jnp.stack([jnp.asarray(value, jnp.int32) for value in values])


def load(pieces, starts_ref, whole, sems):
    copies = []
    for i, piece in enumerate(pieces):
        rows = pl.ds(pl.multiple_of(starts_ref[2 * i], 16), piece.shape[0])
        if piece.shape[1] == whole.shape[1]:
            place = whole.at[rows, :]
        else:
            columns = pl.ds(pl.multiple_of(starts_ref[2 * i + 1], 128), piece.shape[1])
            place = whole.at[rows, columns]
        copies.append(pltpu.make_async_copy(piece, place, sems.at[i]))
        copies[-1].start()
    return copies


def wait(copies):
    for copy in copies:
        copy.wait()


IN_VMEM = pl.BlockSpec(memory_space=pltpu.VMEM)
IN_SMEM = pl.BlockSpec(memory_space=pltpu.SMEM)
ANYWHERE = pl.BlockSpec(memory_space=pl.ANY)


def upright(ref):
    return jnp.concatenate([jnp.transpose(ref[m]) for m in range(ref.shape[0])], axis=0)


def lay_down(value, ref):
    rows = ref.shape[2]
    for m in range(ref.shape[0]):
        ref[m] = jnp.transpose(value[m * rows : (m + 1) * rows])


def turn(chunk, cosine, sine):
    lane = lax.broadcasted_iota(jnp.int32, chunk.shape, 1)
    partner = jnp.where(
        lane % HEAD_SIZE < HALF_HEAD,
        pltpu.roll(chunk, 128 - HALF_HEAD, 1),
        pltpu.roll(chunk, HALF_HEAD, 1),
    )
    return chunk * cosine + partner * sine


def project_kernel(count, starts_ref, x_ref, gains_ref, cos_ref, sin_ref, *refs):
    pieces = refs[:count]
    q_ref, kv_ref, whole, sems = refs[count:]
    copies = load(pieces, starts_ref, whole, sems)
    x = upright(x_ref).astype(F32)
    width = x.shape[1]
    act = (x * rms_inverse(x) * gains_ref[0:1, :]).astype(BF)
    wait(copies)
    cosine, sine = cos_ref[...], sin_ref[...]
    for first in range(0, width + KV_WIDTH, 256):
        linear = nn(act, whole[:width, first : first + 256])
        for at in range(first, first + 256, 128):
            chunk = turn(linear[:, at - first : at - first + 128], cosine, sine)
            if at + 128 <= width:
                q_ref[:, at : at + 128] = (chunk * SCALE).astype(BF)
            elif at < width:
                q_ref[:, at:width] = (chunk[:, : width - at] * SCALE).astype(BF)
                kv_ref[:, : at + 128 - width] = chunk[:, width - at :].astype(BF)
            else:
                kv_ref[:, at - width : at - width + 128] = chunk.astype(BF)
    kv_ref[:, KV_WIDTH:] = nn(act, whole[width:, width:]).astype(BF)


def project(x, gains, cosine, sine, pieces, starts, shape):
    micro, width, rows = x.shape
    tokens = micro * rows
    outs = (
        jax.ShapeDtypeStruct((tokens, width), BF),
        jax.ShapeDtypeStruct((tokens, 2 * KV_WIDTH), BF),
    )
    table = pl.BlockSpec((tokens, 128), lambda i: (0, 0))
    return pl.pallas_call(
        functools.partial(project_kernel, len(pieces)),
        grid=(1,),
        name="project",
        in_specs=[IN_SMEM] + [IN_VMEM] * 2 + [table] * 2 + [ANYWHERE] * len(pieces),
        out_specs=(IN_VMEM,) * 2,
        out_shape=outs,
        scratch_shapes=[pltpu.VMEM(shape, BF), pltpu.SemaphoreType.DMA((len(pieces),))],
        cost_estimate=cost(2 * tokens * width * (width + 2 * KV_WIDTH), 0, x, *outs, *pieces),
        compiler_params=pltpu.CompilerParams(vmem_limit_bytes=VMEM_LIMIT),
    )(starts, x, gains, cosine, sine, *pieces)


def feed_kernel(counts, s0_ref, s1_ref, s2_ref, x_ref, attn_ref, cot_ref, gains_ref, *refs):
    total = sum(counts)
    attention_pieces = refs[: counts[0]]
    pair_pieces = refs[counts[0] : counts[0] + counts[1]]
    down_pieces = refs[counts[0] + counts[1] : total]
    out_ref, inner_ref, slopes_ref, act_t_ref, attn_t_ref, dy_ref, dres_ref, low_ref, dattn_ref = refs[
        total : total + 9
    ]
    w_attn, w_pair, w_down, resid_ref, dact_ref, sems0, sems1, sems2 = refs[total + 9 :]
    attention_copies = load(attention_pieces, s0_ref, w_attn, sems0)
    pair_copies = load(pair_pieces, s1_ref, w_pair, sems1)
    down_copies = load(down_pieces, s2_ref, w_down, sems2)
    width = x_ref.shape[1]
    hidden = w_pair.shape[1]
    tile = hidden // 5
    gain = gains_ref[1:2, :]
    x = upright(x_ref).astype(F32)
    dy_ref[...] = upright(cot_ref)
    attn_t_ref[...] = jnp.transpose(attn_ref[...])
    wait(attention_copies)
    w_output = w_attn[width:, :width]
    resid = x + nn(attn_ref[...], w_output)
    resid_ref[...] = resid
    dres_ref[...] = resid
    root = rms_inverse(resid)
    act = (resid * root * gain).astype(BF)
    act_t_ref[...] = jnp.transpose(act)
    wait(pair_copies)
    wait(down_copies)
    dy = dy_ref[...]
    for first in range(0, hidden, tile):
        here = slice(first, first + tile)
        gate = nn(act, w_pair[:width, here])
        upper = nn(act, w_pair[width:, here])
        d_inner = nt(dy, w_down[here, :])
        sigmoid = 1.0 / (1.0 + jnp.exp(-gate))
        silu = gate * sigmoid
        inner = (silu * upper).astype(BF)
        inner_ref[here, :] = jnp.transpose(inner)
        d_gate = (d_inner * upper * sigmoid * (1.0 + gate * (1.0 - sigmoid))).astype(BF)
        d_upper = (d_inner * silu).astype(BF)
        slopes_ref[0, :, here] = d_gate
        slopes_ref[1, :, here] = d_upper
        out = nn(inner, w_down[here, :])
        d_act = nt(d_gate, w_pair[:width, here]) + nt(d_upper, w_pair[width:, here])
        resid_ref[...] += out
        if first == 0:
            dact_ref[...] = d_act
        else:
            dact_ref[...] += d_act
    lay_down(resid_ref[...].astype(BF), out_ref)
    normed = dres_ref[...] * root
    d_act = dact_ref[...]
    d_normed = d_act * gain
    d_resid = dy.astype(F32) + root * (
        d_normed - normed * jnp.mean(d_normed * normed, axis=-1, keepdims=True)
    )
    dres_ref[...] = d_resid
    low = d_resid.astype(BF)
    low_ref[...] = low
    dattn_ref[...] = nt(low, w_output).astype(BF)


def feed(x, attn, dy, gains, attention_got, pair_got, down_got):
    micro, width, rows = x.shape
    tokens = micro * rows
    groups = [attention_got, pair_got, down_got]
    counts = [len(pieces) for pieces, _, _ in groups]
    shapes = [shape for _, _, shape in groups]
    hidden = shapes[1][1]
    outs = (
        jax.ShapeDtypeStruct(x.shape, BF),
        jax.ShapeDtypeStruct((hidden, tokens), BF),
        jax.ShapeDtypeStruct((2, tokens, hidden), BF),
        jax.ShapeDtypeStruct((width, tokens), BF),
        jax.ShapeDtypeStruct((width, tokens), BF),
        jax.ShapeDtypeStruct((tokens, width), BF),
        jax.ShapeDtypeStruct((tokens, width), F32),
        jax.ShapeDtypeStruct((tokens, width), BF),
        jax.ShapeDtypeStruct((tokens, width), BF),
    )
    every = [piece for pieces, _, _ in groups for piece in pieces]
    return pl.pallas_call(
        functools.partial(feed_kernel, counts),
        name="feed",
        in_specs=[IN_SMEM] * 3 + [IN_VMEM] * 4 + [ANYWHERE] * len(every),
        out_specs=(IN_VMEM,) * 9,
        out_shape=outs,
        scratch_shapes=[pltpu.VMEM(shape, BF) for shape in shapes]
        + [pltpu.VMEM((tokens, width), F32)] * 2
        + [pltpu.SemaphoreType.DMA((count,)) for count in counts],
        cost_estimate=cost(
            2 * tokens * width * (6 * hidden + 3 * width), tokens * hidden, x, x, x, *outs, *every
        ),
        compiler_params=pltpu.CompilerParams(vmem_limit_bytes=VMEM_MOST),
    )(*(starts for _, starts, _ in groups), x, attn, dy, gains, *every)


def pick_rows(source, starts_ref, base, rows, count, target):
    for t in range(count):
        start = pl.multiple_of(starts_ref[base + t], 16)
        target[t * rows : (t + 1) * rows, :] = source[pl.ds(start, rows), :]


def rows_grad_kernel(parts, count, starts_ref, *refs):
    operands = refs[: 2 * len(parts)]
    outs = refs[2 * len(parts) : 2 * len(parts) + 2]
    ordered = refs[2 * len(parts) + 2 :]
    block = sum(parts)
    for o, out_ref in enumerate(outs):
        at = 0
        for i, rows in enumerate(parts):
            pick_rows(operands[2 * i], starts_ref, (o * len(parts) + i) * count, rows, count, ordered[i])
            made = nn(ordered[i][...], operands[2 * i + 1][...]).astype(BF)
            columns = made.shape[1]
            for t in range(count):
                place = slice(t * block + at, t * block + at + rows)
                out_ref[place, :columns] = made[t * rows : (t + 1) * rows]
                if columns < out_ref.shape[1]:
                    out_ref[place, columns:] = jnp.zeros((rows, out_ref.shape[1] - columns), BF)
            at += rows


def rows_grad(terms):
    count = len(terms[0][3])
    parts = [term[2] for term in terms]
    block, columns = sum(parts), terms[0][1].shape[1]
    wide = rounded_up(columns)
    if any(rows % 16 for rows in parts) or any(term[0].shape[0] // count % 16 for term in terms):
        outs = []
        for o in (3, 4):
            made = []
            for term in terms:
                grad = jnp.pad(nn(term[0], term[1]).astype(BF), ((0, 0), (0, wide - columns)))
                made.append([lax.dynamic_slice_in_dim(grad, start, term[2], 0) for start in term[o]])
            outs.append(jnp.concatenate([part for group in zip(*made) for part in group], axis=0))
        return outs
    args = [operand for term in terms for operand in term[:2]]
    out = jax.ShapeDtypeStruct((count * block, wide), BF)
    flops = sum(4 * left.shape[1] * rows * count * columns for left, _, rows, _, _ in terms)
    return pl.pallas_call(
        functools.partial(rows_grad_kernel, parts, count),
        name="rows_grad",
        in_specs=[IN_SMEM] + [IN_VMEM] * len(args),
        out_specs=(IN_VMEM,) * 2,
        out_shape=(out, out),
        scratch_shapes=[pltpu.VMEM((count * rows, terms[0][0].shape[1]), BF) for rows in parts],
        cost_estimate=cost(flops, 0, out, out, *args),
        compiler_params=pltpu.CompilerParams(vmem_limit_bytes=VMEM_LIMIT),
    )(numbers([start for o in (3, 4) for term in terms for start in term[o]]), *args)


def wide_grad_kernel(cuts, count, rows, info_ref, left_ref, given_ref, kept_ref, *refs):
    outs, ordered = refs[: 2 * len(cuts)], refs[2 * len(cuts)]

    @pl.when(pl.program_id(0) == 0)
    def _():
        at = 0
        for o in range(2):
            first = 0
            for cut in cuts:
                for t in range(count):
                    start = pl.multiple_of(info_ref[2 + o * count + t] + first, 16)
                    ordered[at : at + cut, :] = left_ref[pl.ds(start, cut), :]
                    at += cut
                first += cut

    for o, right_ref in enumerate((given_ref, kept_ref)):
        made = nn(ordered[o * count * rows : (o + 1) * count * rows, :], right_ref[...]).astype(BF)
        at = 0
        for c, cut in enumerate(cuts):
            outs[o * len(cuts) + c][...] = made[at : at + count * cut]
            at += count * cut


def wide_grad(left, rights, rows, cuts, given, kept, core):
    count, (_, tokens, columns) = len(given), rights.shape
    outs = tuple(jax.ShapeDtypeStruct((count * cut, columns), BF) for cut in cuts) * 2
    if rows % 16 or any(cut % 16 for cut in cuts):
        made = []
        for starts, choice in ((given, 1 - core), (kept, core)):
            grad = nn(left, lax.dynamic_index_in_dim(rights, choice, 0, keepdims=False)).astype(BF)
            first = 0
            for cut in cuts:
                made.append(
                    jnp.concatenate([lax.dynamic_slice_in_dim(grad, start + first, cut, 0) for start in starts])
                )
                first += cut
        return made
    tile = 512 if columns % 512 == 0 else columns
    return pl.pallas_call(
        functools.partial(wide_grad_kernel, cuts, count, rows),
        grid_spec=pltpu.PrefetchScalarGridSpec(
            num_scalar_prefetch=1,
            grid=(columns // tile,),
            in_specs=[
                pl.BlockSpec(left.shape, lambda n, info: (0, 0)),
                pl.BlockSpec((None, tokens, tile), lambda n, info: (info[0], 0, n)),
                pl.BlockSpec((None, tokens, tile), lambda n, info: (info[1], 0, n)),
            ],
            out_specs=tuple(pl.BlockSpec((out.shape[0], tile), lambda n, info: (0, n)) for out in outs),
            scratch_shapes=[pltpu.VMEM((2 * count * rows, tokens), BF)],
        ),
        out_shape=outs,
        name="wide_grad",
        cost_estimate=cost(4 * tokens * rows * count * columns, 0, left, rights, *outs),
        compiler_params=pltpu.CompilerParams(vmem_limit_bytes=VMEM_LIMIT),
    )(numbers([1 - core, core] + given + kept), left, rights, rights)


def turn_keys(source, target, at, cosine, sine):
    rows = source.shape[0]
    for first in range(0, KV_WIDTH, 128):
        chunk = turn(source[:, first : first + 128].astype(F32), cosine, -sine).astype(BF)
        last = min(first + 128, KV_WIDTH)
        target[at : at + rows, first:last] = chunk[:, : last - first]
    target[at : at + rows, KV_WIDTH:] = source[:, KV_WIDTH:]


def attention_grad_kernel(shards, half, starts_ref, gain_ref, cos_ref, sin_ref, dq_ref, *refs):
    xs, halves = refs[:shards], refs[shards : shards + 2]
    dkvs = [ref.at[t] for ref in halves for t in range(shards // 2)]
    outs, (act, dkv, ordered) = refs[shards + 2 : shards + 4], refs[shards + 4 :]
    micro, width, rows = xs[0].shape
    tokens = micro * rows
    for t in range(shards):
        here = slice(t * tokens, (t + 1) * tokens)
        turn_keys(dkvs[t], dkv, t * tokens, cos_ref[here, :], sin_ref[here, :])
        for m in range(micro):
            x = xs[t][m].astype(F32)
            root = lax.rsqrt(jnp.mean(x * x, axis=0, keepdims=True) + EPS)
            first = t * tokens + m * rows
            act[:, first : first + rows] = (x * root * gain_ref[...]).astype(BF)
    for i, out_ref in enumerate(outs):
        pick_rows(act, starts_ref, i * shards, half, shards, ordered)
        out_ref[:, :width] = nn(ordered[:, :tokens], dq_ref[...]).astype(BF)
        start = rounded_up(width)
        if start > width:
            out_ref[:, width:start] = jnp.zeros((out_ref.shape[0], start - width), BF)
        out_ref[:, start:] = nn(ordered[...], dkv[...]).astype(BF)


def attention_grad(x_all, gain, cosine, sine, dq, dkv_all, half, given, kept):
    shards = len(x_all)
    micro, width, rows = x_all[0].shape
    every = shards * micro * rows
    columns = rounded_up(width) + 2 * KV_WIDTH
    out = jax.ShapeDtypeStruct((shards * half, columns), BF)
    if half % 16 or width // shards % 16:
        xs = jnp.concatenate([x[m] for x in x_all for m in range(micro)], axis=1).astype(F32)
        act = xs * lax.rsqrt(jnp.mean(xs * xs, axis=0, keepdims=True) + EPS) * gain
        act = act.astype(BF)
        dkv = jnp.concatenate(dkv_all, axis=0).reshape(every, 2 * KV_WIDTH)
        keys = dkv[:, :KV_WIDTH].astype(F32).reshape(every, -1, 2, HALF_HEAD)
        c, s = cosine[:, None, :HALF_HEAD], sine[:, None, HALF_HEAD:HEAD_SIZE]
        first, second = keys[:, :, 0], keys[:, :, 1]
        keys = jnp.stack([first * c + second * s, second * c - first * s], axis=2)
        dkv = jnp.concatenate([keys.reshape(every, KV_WIDTH).astype(BF), dkv[:, KV_WIDTH:]], axis=1)
        q = jnp.pad(nn(act[:, : micro * rows], dq), ((0, 0), (0, rounded_up(width) - width)))
        grad = jnp.concatenate([q, nn(act, dkv)], axis=1).astype(BF)
        return [
            jnp.concatenate([lax.dynamic_slice_in_dim(grad, start, half, 0) for start in starts])
            for starts in (given, kept)
        ]
    return pl.pallas_call(
        functools.partial(attention_grad_kernel, shards, half),
        name="attention_grad",
        in_specs=[IN_SMEM] + [IN_VMEM] * (6 + shards),
        out_specs=(IN_VMEM,) * 2,
        out_shape=(out, out),
        scratch_shapes=[
            pltpu.VMEM((width, every), BF),
            pltpu.VMEM((every, 2 * KV_WIDTH), BF),
            pltpu.VMEM((shards * half, every), BF),
        ],
        cost_estimate=cost(
            4 * shards * half * (every * 2 * KV_WIDTH + micro * rows * width), 0, *x_all, *dkv_all, out, out
        ),
        compiler_params=pltpu.CompilerParams(vmem_limit_bytes=VMEM_MOST),
    )(numbers(given + kept), gain, cosine, sine, dq, *x_all, *dkv_all)


def finish_kernel(count, starts_ref, x_ref, low_ref, kv_ref, dres_ref, gains_ref, cos_ref, sin_ref, *refs):
    pieces = refs[:count]
    dx_ref, whole, kv_turned, sems = refs[count:]
    copies = load(pieces, starts_ref, whole, sems)
    turn_keys(kv_ref, kv_turned, 0, cos_ref[...], sin_ref[...])
    x = upright(x_ref).astype(F32)
    width = x.shape[1]
    root = rms_inverse(x)
    normed = x * root
    wait(copies)
    d_act = nt(low_ref[...], whole[:width, :width])
    d_act += nt(kv_turned[:, :KV_WIDTH], whole[:width, width:])
    d_act += nt(kv_turned[:, KV_WIDTH:], whole[width:, width:])
    d_normed = d_act * gains_ref[0:1, :]
    d_x = dres_ref[...] + root * (d_normed - normed * jnp.mean(d_normed * normed, axis=-1, keepdims=True))
    lay_down(d_x.astype(BF), dx_ref)


def finish(x, low, kv, dres, gains, cosine, sine, pieces, starts, shape):
    micro, width, rows = x.shape
    tokens = micro * rows
    table = pl.BlockSpec((tokens, 128), lambda i: (0, 0))
    return pl.pallas_call(
        functools.partial(finish_kernel, len(pieces)),
        grid=(1,),
        name="finish",
        in_specs=[IN_SMEM] + [IN_VMEM] * 5 + [table] * 2 + [ANYWHERE] * len(pieces),
        out_specs=IN_VMEM,
        out_shape=jax.ShapeDtypeStruct(x.shape, BF),
        scratch_shapes=[
            pltpu.VMEM(shape, BF),
            pltpu.VMEM((tokens, 2 * KV_WIDTH), BF),
            pltpu.SemaphoreType.DMA((len(pieces),)),
        ],
        cost_estimate=cost(2 * tokens * width * (width + 2 * KV_WIDTH), 0, x, low, dres, *pieces),
        compiler_params=pltpu.CompilerParams(vmem_limit_bytes=VMEM_LIMIT),
    )(starts, x, low, kv, dres, gains, cosine, sine, *pieces)


def head(ref, h):
    return ref[:, h * HEAD_SIZE : (h + 1) * HEAD_SIZE]


def widen(value, columns):
    n = value.shape[0]
    lane = lax.broadcasted_iota(jnp.int32, (n, HEAD_SIZE), 1)
    tail = jnp.zeros((n, HEAD_SIZE), F32)
    for c, column in enumerate(columns):
        tail = jnp.where(lane == c, column, tail)
    return jnp.concatenate([value, tail.astype(BF)], axis=1)


def split(column):
    high = column.astype(BF).astype(F32)
    middle = (column - high).astype(BF).astype(F32)
    return [high, middle, column - high - middle]


def attend_kernel(shards, seg_rows, q_ref, *refs):
    kv = refs[:shards]
    bias_ref = refs[shards]
    o_ref, lse_ref = refs[-2:]
    rows = q_ref.shape[0]
    i = lax.broadcasted_iota(jnp.int32, (rows, rows), 0)
    j = lax.broadcasted_iota(jnp.int32, (rows, rows), 1)
    same = (i // seg_rows) == (j // seg_rows)
    own = jnp.where(j > i, CLOSED, jnp.where(same, 0.0, bias_ref[0:1, :]))
    one = jnp.ones((rows, 1), F32)
    bias_columns = jnp.transpose(bias_ref[...])
    lse = jnp.zeros((rows, 128), F32)
    lane = lax.broadcasted_iota(jnp.int32, (rows, 128), 1)
    for g in range(KEY_VALUE_HEADS):
        keys, values = [], []
        for t in range(shards):
            keys.append(widen(head(kv[t], g), [bias_columns[:, t : t + 1]] if t else []))
            values.append(widen(head(kv[t], KEY_VALUE_HEADS + g), [one]))
        for h in range(g * GROUP, g * GROUP + GROUP):
            q = widen(head(q_ref, h), [one])
            scores = [nt(q, k) for k in keys]
            scores[0] = scores[0] + own
            peak = functools.reduce(jnp.maximum, scores)
            peak = jnp.max(peak, axis=1, keepdims=True)
            terms = [nn(jnp.exp(s - peak).astype(BF), v) for s, v in zip(scores, values)]
            mixed = sum(terms[1:], terms[0])
            total = mixed[:, HEAD_SIZE : HEAD_SIZE + 1]
            o_ref[:, h * HEAD_SIZE : (h + 1) * HEAD_SIZE] = (mixed[:, :HEAD_SIZE] / total).astype(BF)
            lse = jnp.where(lane == h, peak + jnp.log(total), lse)
    lse_ref[...] = lse


def attend_back_kernel(shards, seg_rows, q_ref, *refs):
    kv = refs[:shards]
    bias_ref, o_ref, do_ref, lse_ref, cos_ref, sin_ref = refs[shards : shards + 6]
    dq_ref, low_ref, high_ref = refs[-3:]
    dkv = [ref.at[t] for ref in (low_ref, high_ref) for t in range(shards // 2)]
    rows = q_ref.shape[0]
    i = lax.broadcasted_iota(jnp.int32, (rows, rows), 1)
    j = lax.broadcasted_iota(jnp.int32, (rows, rows), 0)
    bias_columns = jnp.transpose(bias_ref[...])
    same = (i // seg_rows) == (j // seg_rows)
    own_column = jnp.broadcast_to(bias_columns[:, 0:1], (rows, rows))
    own = jnp.where(j > i, CLOSED, jnp.where(same, 0.0, own_column))
    one, zero = jnp.ones((rows, 1), F32), jnp.zeros((rows, 1), F32)
    cosine, sine = cos_ref[...], sin_ref[...]
    for g in range(KEY_VALUE_HEADS):
        keys, values, turned = [], [], []
        for t in range(shards):
            k = head(kv[t], g)
            turned.append(jnp.transpose(k))
            keys.append(widen(k, [bias_columns[:, t : t + 1] if t else zero, one, one, one]))
            values.append(widen(head(kv[t], KEY_VALUE_HEADS + g), [one, one, one]))
        dk, dv = [None] * shards, [None] * shards
        for h in range(g * GROUP, g * GROUP + GROUP):
            q, do = head(q_ref, h), head(do_ref, h)
            centre = jnp.sum(head(o_ref, h).astype(F32) * do.astype(F32), axis=1, keepdims=True)
            q_wide = widen(q, [one] + split(-lse_ref[:, h : h + 1]))
            do_wide = widen(do, split(-centre))
            dq = None
            for t in range(shards):
                scores = nt(keys[t], q_wide)
                if t == 0:
                    scores = scores + own
                probs = jnp.exp(scores)
                ds = (probs * nt(values[t], do_wide)).astype(BF)
                v_term = nn(probs.astype(BF), do)
                k_term = nn(ds, q)
                q_term = nn(turned[t], ds)
                dv[t] = v_term if dv[t] is None else dv[t] + v_term
                dk[t] = k_term if dk[t] is None else dk[t] + k_term
                dq = q_term if dq is None else dq + q_term
            dq = dq * SCALE
            first, second = dq[:HALF_HEAD], dq[HALF_HEAD:]
            back = jnp.concatenate(
                [first * cosine + second * sine, second * cosine - first * sine], axis=0
            )
            dq_ref[:, h * HEAD_SIZE : (h + 1) * HEAD_SIZE] = jnp.transpose(back).astype(BF)
        for t in range(shards):
            dkv[t][:, g * HEAD_SIZE : (g + 1) * HEAD_SIZE] = dk[t].astype(BF)
            g_value = KEY_VALUE_HEADS + g
            dkv[t][:, g_value * HEAD_SIZE : (g_value + 1) * HEAD_SIZE] = dv[t].astype(BF)


def attend(micro, seg_rows, q, kv, bias):
    shards, tokens, width = len(kv), q.shape[0], q.shape[1]
    rows = tokens // micro
    here = lambda w: pl.BlockSpec((rows, w), lambda m: (m, 0))
    outs = (jax.ShapeDtypeStruct((tokens, width), BF), jax.ShapeDtypeStruct((tokens, 128), F32))
    pairs = tokens * rows * shards * QUERY_HEADS
    return pl.pallas_call(
        functools.partial(attend_kernel, shards, seg_rows),
        grid=(micro,),
        name="attend",
        in_specs=[here(width)]
        + [here(2 * KV_WIDTH)] * shards
        + [pl.BlockSpec((None,) + bias.shape[1:], lambda m: (m, 0, 0))],
        out_specs=(here(width), here(128)),
        out_shape=outs,
        cost_estimate=cost(16 * HEAD_SIZE * pairs, pairs, q),
        compiler_params=pltpu.CompilerParams(vmem_limit_bytes=VMEM_LIMIT),
    )(q, *kv, bias)


def attend_back(m, rows, seg_rows, q, kv, bias, o, do, lse, cosine, sine, earlier):
    shards, tokens, width = len(kv), q.shape[0], q.shape[1]
    here = lambda w: pl.BlockSpec((rows, w), lambda i: (m, 0))
    turned = pl.BlockSpec((HALF_HEAD, rows), lambda i: (0, m))
    outs = (jax.ShapeDtypeStruct((tokens, width), BF),)
    outs += (jax.ShapeDtypeStruct((shards // 2, tokens, 2 * KV_WIDTH), BF),) * 2
    pieces = pl.BlockSpec((shards // 2, rows, 2 * KV_WIDTH), lambda i: (0, m, 0))
    pairs = rows * rows * shards * QUERY_HEADS
    return pl.pallas_call(
        functools.partial(attend_back_kernel, shards, seg_rows),
        grid=(1,),
        name="attend_back",
        in_specs=[here(width)]
        + [here(2 * KV_WIDTH)] * shards
        + [pl.BlockSpec((None,) + bias.shape[1:], lambda i: (m, 0, 0))]
        + [here(width), here(width), here(128), turned, turned]
        + [pl.BlockSpec(memory_space=pl.ANY)] * len(earlier),
        out_specs=(here(width), pieces, pieces),
        out_shape=outs,
        input_output_aliases={shards + 7 + i: i for i in range(len(earlier))},
        cost_estimate=cost(40 * HEAD_SIZE * pairs, pairs, q),
        compiler_params=pltpu.CompilerParams(vmem_limit_bytes=VMEM_LIMIT),
    )(q, *kv, bias, o, do, lse, cosine, sine, *earlier)


def local(
    block_input,
    parent_ids,
    w_query,
    key_weight,
    value_weight,
    w_output,
    w_gate,
    w_up,
    w_down,
    norm_first,
    norm_second,
    out_cotangent,
):
    micro, rows, width = block_input.shape
    shards = lax.axis_size("shard")
    links = Links(lax.axis_size("rep"), shards)
    tree = rows * shards
    segs = parent_ids.shape[2]
    seg_rows = tree // segs
    tokens = micro * rows
    hidden = w_gate.shape[1]

    inputs = block_input.swapaxes(1, 2)
    cotangent = out_cotangent.swapaxes(1, 2)

    even = links.core == 0
    side = lax.axis_index("rep") // 2 % 2
    left = jnp.concatenate([w_query, key_weight], axis=1)
    right = jnp.concatenate([w_output, value_weight], axis=1)
    attn_mine = jnp.where(even, left, right)
    pair_cut = hidden // 2
    pair_mine = lax.dynamic_slice_in_dim(jnp.where(even, w_gate, w_up), side * pair_cut, pair_cut, 1)
    down_cut = w_down.shape[0] // 2
    down_mine = lax.dynamic_slice_in_dim(w_down, links.core * down_cut, down_cut, 0)

    attn_near = links.near(attn_mine)
    pair_near = {1: links.step(pair_mine, 0)}
    gain_pieces = links.small_pieces(jnp.stack([norm_first, norm_second]))
    attn_mine, attn_near, gain_pieces, pair_mine, down_mine = meet(
        attn_mine, attn_near, gain_pieces, pair_mine, down_mine
    )

    gains = links.in_order(gain_pieces).astype(F32)
    attn_all = links.far(attn_mine, attn_near)
    attn_swapped = {t: links.swap(attn_near[t]) for t in attn_near}
    pair_later = {1 << i: links.step(pair_mine, i) for i in range(1, links.bits)}
    own_down = with_layout_constraint(w_down, Layout(major_to_minor=(0, 1)))
    parents = parent_ids[:, 0]
    seg = jnp.arange(segs)
    after_parent = jnp.concatenate([parents[:, 1:], jnp.full((micro, 1), -1, parents.dtype)], axis=1)
    on_path = (seg % 2 == 0)[None] | (after_parent == seg[None])
    below = (seg[None, :] < seg[:, None])[None]
    depth = jnp.sum(jnp.where(below, on_path.astype(F32)[:, None, :], 0.0), axis=-1)

    def row_numbers(hop):
        return (links.shard ^ hop) * rows + jnp.arange(rows)

    def pick(table, numbers):
        hit = (numbers // seg_rows)[..., None] == seg
        return jnp.sum(jnp.where(hit[None], table.reshape(micro, *(1,) * numbers.ndim, segs), 0), axis=-1)

    key_rows = jnp.stack([row_numbers(hop) for hop in links.hops])
    positions = pick(depth, key_rows) * seg_rows + (key_rows % seg_rows).astype(F32)
    freqs = jnp.exp(-math.log(10000.0) * jnp.arange(HALF_HEAD, dtype=F32) * (2.0 / HEAD_SIZE))
    angles = freqs[:, None] * positions.swapaxes(0, 1).reshape(1, shards * tokens)
    cosine_t, sine_t = jnp.cos(angles), jnp.sin(angles)
    cosine = jnp.tile(cosine_t.T, (1, 4))
    sine = jnp.tile(jnp.concatenate([-sine_t.T, sine_t.T], axis=1), (1, 2))
    open_key = (pick(on_path.astype(F32), key_rows) > 0.5) & (
        (key_rows < links.shard * rows) | (jnp.arange(shards) == 0)[:, None]
    )
    bias = jnp.where(open_key, 0.0, CLOSED)
    bias = jnp.pad(bias, ((0, 0), (0, 8 - shards), (0, 0)))

    attn_all, attn_swapped, pair_mine, pair_near, gains, cosine, sine, bias, down_mine, own_down = meet(
        attn_all, attn_swapped, pair_mine, pair_near, gains, cosine, sine, bias, down_mine, own_down
    )

    for t in range(1, shards):
        if t not in attn_swapped:
            attn_swapped[t] = links.swap(attn_all[t])
    shard_rows = width // shards

    def pair_place(weight, hop):
        return weight * width + (links.shard ^ hop) * shard_rows

    pieces, starts = [left, right], [(pair_place(0, 0), 0), (pair_place(1, 0), 0)]
    for t in range(1, shards):
        pieces += [attn_all[t], attn_swapped[t]]
        starts += [
            (pair_place(links.core, links.hops[t]), 0),
            (pair_place(1 - links.core, links.hops[links.twin(t)]), 0),
        ]
    attention_got = joined(pieces, starts, (2 * width, left.shape[1]))
    pair_near |= pair_later
    pair_beside = {1: links.beside(pair_near[1])}
    down_near = {1: links.step(down_mine, 0)}
    queries, kv = project(inputs, gains, cosine, sine, *attention_got)
    queries, kv, pair_mine, pair_near = meet(queries, kv, pair_mine, pair_near)

    kv_near = links.near(kv)
    pair_all = links.far(pair_mine, pair_near)
    pair_further = {t: links.beside(pair_near[t]) for t in pair_near if t > 1}
    kv_near, kv, pair_beside, pair_near, down_near, down_mine = meet(
        kv_near, kv, pair_beside, pair_near, down_near, down_mine
    )

    kv_all = links.far(kv, kv_near)
    down_near |= {1 << i: links.step(down_mine, i) for i in range(1, links.bits)}
    pair_swapped = {t: links.swap(pair_near[t]) for t in pair_near}
    pair_crossed = {t: links.swap(pair_beside[t]) for t in pair_beside}
    pair_beside |= pair_further
    kv_all, pair_all, pair_swapped, pair_crossed, pair_beside = meet(
        kv_all, pair_all, pair_swapped, pair_crossed, pair_beside
    )

    down_all = links.far(down_mine, down_near)
    pair_beside |= {t: links.beside(pair_all[t]) for t in range(1, shards) if t not in pair_beside}
    attn, lse = attend(micro, seg_rows, queries, kv_all, bias)
    pair_swapped |= {t: links.swap(pair_all[t]) for t in range(1, shards) if t not in pair_swapped}
    attn, lse, down_all, pair_beside, pair_all, pair_swapped = meet(
        attn, lse, down_all, pair_beside, pair_all, pair_swapped
    )

    pair_crossed |= {t: links.swap(pair_beside[t]) for t in range(1, shards) if t not in pair_crossed}
    down_swapped = [None] + [links.swap(down_all[t]) for t in range(1, shards)]
    pieces, starts = [w_gate, w_up], [(pair_place(0, 0), 0), (pair_place(1, 0), 0)]
    for t in range(1, shards):
        pieces += [pair_all[t], pair_beside[t], pair_swapped[t], pair_crossed[t]]
        for row in (
            pair_place(links.core, links.hops[t]),
            pair_place(1 - links.core, links.hops[links.twin(t)]),
        ):
            starts += [(row, side * pair_cut), (row, (1 - side) * pair_cut)]
    pair_got = joined(pieces, starts, (2 * width, hidden))
    own = w_down.shape[0]
    pieces, starts = [own_down], [(links.shard * own, 0)]
    for t in range(1, shards):
        pieces += [down_all[t], down_swapped[t]]
        starts += [
            ((links.shard ^ links.hops[t]) * own + links.core * down_cut, 0),
            ((links.shard ^ links.hops[links.twin(t)]) * own + (1 - links.core) * down_cut, 0),
        ]
    down_got = joined(pieces, starts, (own * shards, width))
    attn, pair_pieces, down_pieces = meet(attn, pair_got[0], down_got[0])
    pair_got, down_got = (pair_pieces, *pair_got[1:]), (down_pieces, *down_got[1:])

    plan = Plan()
    have = lambda *names: [plan.have[name] for name in names]
    x_near = links.near(inputs)
    made = feed(inputs, attn, cotangent, gains, attention_got, pair_got, down_got)
    names = ("out", "inner", "slopes", "act", "attn_t", "dy", "d_resid", "d_resid_low", "d_attn")
    plan.have = dict(zip(names, made)) | {"x_near": x_near, "queries": queries, "kv": kv_all, "lse": lse, "attn": attn}
    plan.close()

    down_half = own // 2
    output_half, output_mine, output_theirs = links.half_rows(shard_rows)
    down_kept, down_given = links.order(own, links.core * down_half, (1 - links.core) * down_half)
    wide_kept, wide_given = links.order(shard_rows, 0, 0)
    some_kept, some_given = links.order(shard_rows, output_mine, output_theirs)

    inner, dy, attn_t, low = have("inner", "dy", "attn_t", "d_resid_low")
    plan.have["x_all"] = links.far(inputs, plan.have.pop("x_near"))
    plan.have["rows.given"], plan.have["rows.kept"] = rows_grad(
        (
            (inner, dy, down_half, down_given, down_kept),
            (attn_t, low, output_half, some_given, some_kept),
        )
    )
    plan.close()

    for name in ("rows", "wide0", "wide1", "some"):
        plan.start(name, links.reduce(plan, name))
    plan.advance("rows")
    cuts = (-(-shard_rows // 32) * 16, shard_rows - -(-shard_rows // 32) * 16)
    act, slopes = have("act", "slopes")
    made = wide_grad(act, slopes, shard_rows, cuts, wide_given, wide_kept, links.core)
    names = [name + part for part in (".given", ".kept") for name in ("wide0", "wide1")]
    plan.have |= dict(zip(names, made))
    plan.close()

    made = ()
    hops = [("rows", "wide0", "wide1"), ("rows", "wide0")]
    for m in range(micro):
        plan.advance(*hops[min(m, 1)])
        q, kv_now, o, do, lse_now = have("queries", "kv", "attn", "d_attn", "lse")
        made = attend_back(m, rows, seg_rows, q, kv_now, bias, o, do, lse_now, cosine_t, sine_t, made)
        plan.have["attn_grads"] = made = tuple(made)
        plan.close()
        made = plan.have["attn_grads"]

    d_queries, *d_kv = plan.have.pop("attn_grads")
    plan.have["dkv.pieces"] = d_kv
    plan.have["d_queries"] = d_queries
    plan.start("dkv", links.collect(plan, "dkv"))
    plan.advance("rows", "wide0", "wide1")
    given, kept = attention_grad(
        plan.have["x_all"], gains[0][:, None], cosine, sine, d_queries, d_kv, output_half, some_given, some_kept
    )
    plan.have["some.given"], plan.have["some.kept"] = given, kept
    plan.close()

    def gain_grad(gain, *pairs):
        sums = sum(jnp.sum(weight.astype(F32) * grad, axis=1) for weight, grad in pairs)
        return sums / gain.astype(F32)

    def settle():
        have, done = plan.have, plan.have.setdefault("done", {})
        if "dkv" in have and "d_input" not in done:
            done["d_input"] = finish(
                inputs, have["d_queries"], have["dkv"], have["d_resid"], gains, cosine, sine, *attention_got
            )
        if "rows" in have and "down" not in done:
            value, other = have["rows"]
            done["down"] = links.finish_rows(value[:down_half, :width], other[:down_half, :width], own)
            done["output"] = links.finish_rows(value[down_half:, :width], other[down_half:, :width], shard_rows)
        if "wide0" in have and "wide1" in have and "gate" not in done:
            halves = [links.finish_pair(*have[name]) for name in ("wide0", "wide1")]
            done["gate"], done["upper"] = (jnp.concatenate(parts, axis=0) for parts in zip(*halves))
            done["gain_two"] = gain_grad(norm_second, (w_gate, done["gate"]), (w_up, done["upper"]))
        if "some" in have and "query" not in done:
            grad = links.finish_rows(*have["some"], shard_rows)
            first = rounded_up(width)
            done["query"], done["key"] = grad[:, :width], grad[:, first : first + KV_WIDTH]
            done["value"] = grad[:, first + KV_WIDTH :]
            done["gain_one"] = gain_grad(
                norm_first,
                (w_query, done["query"]),
                (key_weight, done["key"]),
                (value_weight, done["value"]),
            )

    order = [("rows", "wide0", "wide1", "some", "dkv")] * 5 + [("wide1", "some")]
    while plan.tasks:
        plan.advance(*(order.pop(0) if order else tuple(plan.tasks)))
        settle()
        if plan.tasks:
            plan.close()

    done = plan.have["done"]
    return (
        plan.have["out"].swapaxes(1, 2),
        done["d_input"].swapaxes(1, 2),
        *(done[name] for name in ("query", "key", "value", "output", "gate", "upper", "down")),
        done["gain_one"],
        done["gain_two"],
    )


def solution(mesh):
    rows = P(None, AXES, None)
    weight, gain = P("shard", None), P("shard")
    return jax.shard_map(
        local,
        mesh=mesh,
        in_specs=(rows, P(None, "rep", None)) + (weight,) * 7 + (gain, gain, rows),
        out_specs=(rows, rows) + (weight,) * 7 + (gain, gain),
        check_vma=False,
    )
```

```python
import functools
import math

import jax
import jax.numpy as jnp
from jax import lax
from jax.experimental import pallas as pl
from jax.experimental.layout import Layout, with_layout_constraint
from jax.experimental.pallas import tpu as pltpu
from jax.sharding import PartitionSpec as P

QUERY_HEADS = 15
KEY_VALUE_HEADS = 5
HEAD_SIZE = 64
HALF_HEAD = HEAD_SIZE // 2
GROUP = QUERY_HEADS // KEY_VALUE_HEADS
KV_WIDTH = KEY_VALUE_HEADS * HEAD_SIZE
SCALE = HEAD_SIZE ** (-0.5)
EPS = 1e-05
AXES = ("rep", "shard")
BF = jnp.bfloat16
F32 = jnp.float32
CLOSED = -1e30
VMEM_LIMIT = 48 << 20
VMEM_MOST = 60 << 20


def dot(a, b, dims):
    return lax.dot_general(a, b, (dims, ((), ())), preferred_element_type=F32)


def nn(a, b):
    return dot(a, b, ((1,), (0,)))


def nt(a, b):
    return dot(a, b, ((1,), (1,)))


def tn(a, b):
    return dot(a, b, ((0,), (0,)))


def total(parts):
    return sum(part.astype(F32) for part in parts).astype(parts[0].dtype)


def meet(*values):
    return lax.optimization_barrier(values)


def rounded_up(columns):
    return -(-columns // 128) * 128


def rms_inverse(x):
    return lax.rsqrt(jnp.mean(x * x, axis=-1, keepdims=True) + EPS)


def cost(flops, exps, *arrays):
    size = sum(a.size * a.dtype.itemsize for a in arrays)
    return pl.CostEstimate(flops=flops, transcendentals=exps, bytes_accessed=size)


class Links:
    def __init__(self, reps, shards):
        self.reps, self.shards = reps, shards
        self.core = lax.axis_index("rep") % 2
        self.shard = lax.axis_index("shard")
        self.bits = shards.bit_length() - 1
        even = [1 << i for i in range(self.bits)]
        odd = even[:2][::-1] + even[2:]
        self.steps = list(zip(even, odd))
        self.hops = []
        for piece in range(shards):
            sums = [0, 0]
            for i, step in enumerate(self.steps):
                if piece >> i & 1:
                    sums = [sums[0] ^ step[0], sums[1] ^ step[1]]
            self.hops.append(jnp.where(self.core == 0, sums[0], sums[1]))

    def move(self, value, target):
        pairs = []
        for r in range(self.reps):
            for s in range(self.shards):
                goal = target(r, s)
                if goal is not None:
                    pairs.append((r * self.shards + s, goal[0] * self.shards + goal[1]))
        return lax.ppermute(value, AXES, pairs)

    def step(self, value, i):
        return self.move(value, lambda r, s: (r, s ^ self.steps[i][r % 2]))

    def swap(self, value):
        return self.move(value, lambda r, s: (r ^ 1, s))

    def reduce(self, plan, name, quick=False):
        got = yield self.swap(plan.have[name + ".given"])
        sums = [plan.have.pop(name + ".kept"), got]
        del plan.have[name + ".given"]
        for i in reversed(range(self.bits)):
            block = sums[0].shape[0] // 2
            got = yield self.step(total([part[block:] for part in sums]), i)
            sums = [part[:block] for part in sums] + [got]
        value = total(sums)
        chips = self.reps // 2
        place = lax.axis_index("rep") // 2
        span = 1
        if chips % 4 == 0 and quick and value.shape[0] % 4 == 0:
            quarter = value.shape[0] // 4
            across = lambda value, j: self.move(value, lambda r, s: (r ^ (2 * j), s))
            cut = lambda j: lax.dynamic_slice_in_dim(value, (place % 4 ^ j) * quarter, quarter, 0)
            got = yield [across(cut(j), j) for j in range(1, 4)]
            mine = total([cut(0)] + got)
            got = yield [across(mine, j) for j in range(1, 4)]
            parts = jnp.stack([mine] + got).reshape(2, 2, quarter, -1)
            parts = jnp.where(place % 4 >= 2, parts[::-1], parts)
            parts = jnp.where(place % 2 == 1, parts[:, ::-1], parts)
            value = parts.reshape(4 * quarter, -1)
            span = 4
        elif chips % 4 == 0:
            inward, outward, middle = {0: 1, 3: 2}, {1: 0, 2: 3}, {1: 2, 2: 1}

            def along(value, table):
                def target(r, s):
                    chip = r // 2
                    if chip % 4 not in table:
                        return None
                    return ((chip - chip % 4 + table[chip % 4]) * 2 + r % 2, s)

                return self.move(value, target)

            value = total([value, (yield along(value, inward))])
            value = total([value, (yield along(value, middle))])
            back = yield along(value, outward)
            inner = (place % 4 == 1) | (place % 4 == 2)
            value = jnp.where(inner, value, back)
            span = 4
        while span < chips:
            value = total([value, self.move(value, lambda r, s: (r ^ (2 * span), s))])
            span *= 2
        other = yield self.swap(value)
        plan.have[name] = (value, other)

    def collect(self, plan, name):
        low, high = plan.have[name + ".pieces"]
        got = yield self.step(high, self.bits - 1)
        sums = [low, got]
        for i in reversed(range(self.bits - 1)):
            block = sums[0].shape[0] // 2
            got = yield self.step(total([part[block:] for part in sums]), i)
            sums = [part[:block] for part in sums] + [got]
        plan.have[name] = total(sums)[0]

    def beside(self, value):
        return self.move(value, lambda r, s: (r ^ 2, s))

    def near(self, value):
        return {1 << i: self.step(value, i) for i in range(self.bits)}

    def far(self, value, near):
        pieces = [value]
        for t in range(1, self.shards):
            top = t.bit_length() - 1
            pieces.append(near[t] if t in near else self.step(pieces[t - (1 << top)], top))
        return pieces

    def twin(self, piece):
        return piece if self.bits < 2 else piece >> 2 << 2 | (piece & 1) << 1 | (piece >> 1 & 1)

    def small_pieces(self, value):
        return [
            value if hop == 0 else self.move(value, lambda r, s, hop=hop: (r, s ^ hop))
            for hop in range(self.shards)
        ]

    def in_order(self, pieces):
        pieces = jnp.stack(pieces)
        value = pieces
        order = self.shard ^ jnp.arange(self.shards)
        hit = (order[:, None] == jnp.arange(self.shards)[None, :])[:, :, None, None]
        pieces = jnp.sum(jnp.where(hit, pieces[None], 0), axis=1, dtype=value.dtype)
        return jnp.concatenate([pieces[j] for j in range(self.shards)], axis=-1)

    def half_rows(self, rows):
        half = -(-rows // 32) * 16
        return half, self.core * (rows - half), (1 - self.core) * (rows - half)

    def order(self, scale, mine, theirs):
        kept = [(self.shard ^ hop) * scale + mine for hop in self.hops]
        given = [(self.shard ^ self.hops[self.twin(t)]) * scale + theirs for t in range(self.shards)]
        return kept, given

    def finish_rows(self, owned, other, rows):
        low = jnp.where(self.core == 0, owned, other)
        high = jnp.where(self.core == 0, other, owned)
        return jnp.concatenate([low[: rows - owned.shape[0]], high], axis=0).astype(F32)

    def finish_pair(self, owned, other):
        left = jnp.where(self.core == 0, owned, other)
        right = jnp.where(self.core == 0, other, owned)
        return left.astype(F32), right.astype(F32)


class Plan:
    def __init__(self):
        self.have, self.tasks, self.made = {}, {}, {}

    def start(self, name, task):
        self.tasks[name] = task
        self.made[name] = None

    def advance(self, *names):
        for name in names:
            if name in self.tasks:
                try:
                    self.made[name] = self.tasks[name].send(self.made[name])
                except StopIteration:
                    del self.tasks[name], self.made[name]

    def close(self):
        self.have, self.made = lax.optimization_barrier((self.have, self.made))


def joined(pieces, starts, shape):
    if any(piece.shape[0] % 16 or piece.shape[1] % 128 and piece.shape[1] < shape[1] for piece in pieces):
        whole = jnp.zeros(shape, pieces[0].dtype)
        for piece, start in zip(pieces, starts):
            whole = lax.dynamic_update_slice(whole, piece, start)
        pieces, starts = (whole,), [(0, 0)]
    return tuple(pieces), numbers([at for start in starts for at in start]), shape


def numbers(values):
    return jnp.stack([jnp.asarray(value, jnp.int32) for value in values])


def load(pieces, starts_ref, whole, sems):
    copies = []
    for i, piece in enumerate(pieces):
        rows = pl.ds(pl.multiple_of(starts_ref[2 * i], 16), piece.shape[0])
        if piece.shape[1] == whole.shape[1]:
            place = whole.at[rows, :]
        else:
            columns = pl.ds(pl.multiple_of(starts_ref[2 * i + 1], 128), piece.shape[1])
            place = whole.at[rows, columns]
        copies.append(pltpu.make_async_copy(piece, place, sems.at[i]))
        copies[-1].start()
    return copies


def wait(copies):
    for copy in copies:
        copy.wait()


IN_VMEM = pl.BlockSpec(memory_space=pltpu.VMEM)
IN_SMEM = pl.BlockSpec(memory_space=pltpu.SMEM)
ANYWHERE = pl.BlockSpec(memory_space=pl.ANY)


def upright(ref):
    return jnp.concatenate([jnp.transpose(ref[m]) for m in range(ref.shape[0])], axis=0)


def lay_down(value, ref):
    rows = ref.shape[2]
    for m in range(ref.shape[0]):
        ref[m] = jnp.transpose(value[m * rows : (m + 1) * rows])


def turn(chunk, cosine, sine):
    lane = lax.broadcasted_iota(jnp.int32, chunk.shape, 1)
    partner = jnp.where(
        lane % HEAD_SIZE < HALF_HEAD,
        pltpu.roll(chunk, 128 - HALF_HEAD, 1),
        pltpu.roll(chunk, HALF_HEAD, 1),
    )
    return chunk * cosine + partner * sine


def project_kernel(count, starts_ref, x_ref, gains_ref, cos_ref, sin_ref, *refs):
    pieces = refs[:count]
    q_ref, kv_ref, whole, sems = refs[count:]
    copies = load(pieces, starts_ref, whole, sems)
    x = upright(x_ref).astype(F32)
    width = x.shape[1]
    act = (x * rms_inverse(x) * gains_ref[0:1, :]).astype(BF)
    wait(copies)
    cosine, sine = cos_ref[...], sin_ref[...]
    for first in range(0, width + KV_WIDTH, 256):
        linear = nn(act, whole[:width, first : first + 256])
        for at in range(first, first + 256, 128):
            chunk = turn(linear[:, at - first : at - first + 128], cosine, sine)
            if at + 128 <= width:
                q_ref[:, at : at + 128] = (chunk * SCALE).astype(BF)
            elif at < width:
                q_ref[:, at:width] = (chunk[:, : width - at] * SCALE).astype(BF)
                kv_ref[:, : at + 128 - width] = chunk[:, width - at :].astype(BF)
            else:
                kv_ref[:, at - width : at - width + 128] = chunk.astype(BF)
    kv_ref[:, KV_WIDTH:] = nn(act, whole[width:, width:]).astype(BF)


def project(x, gains, cosine, sine, pieces, starts, shape):
    micro, width, rows = x.shape
    tokens = micro * rows
    outs = (
        jax.ShapeDtypeStruct((tokens, width), BF),
        jax.ShapeDtypeStruct((tokens, 2 * KV_WIDTH), BF),
    )
    table = pl.BlockSpec((tokens, 128), lambda i: (0, 0))
    return pl.pallas_call(
        functools.partial(project_kernel, len(pieces)),
        grid=(1,),
        name="project",
        in_specs=[IN_SMEM] + [IN_VMEM] * 2 + [table] * 2 + [ANYWHERE] * len(pieces),
        out_specs=(IN_VMEM,) * 2,
        out_shape=outs,
        scratch_shapes=[pltpu.VMEM(shape, BF), pltpu.SemaphoreType.DMA((len(pieces),))],
        cost_estimate=cost(2 * tokens * width * (width + 2 * KV_WIDTH), 0, x, *outs, *pieces),
        compiler_params=pltpu.CompilerParams(vmem_limit_bytes=VMEM_LIMIT),
    )(starts, x, gains, cosine, sine, *pieces)


def feed_kernel(counts, s0_ref, s1_ref, s2_ref, x_ref, attn_ref, cot_ref, gains_ref, *refs):
    total_count = sum(counts)
    attention_pieces = refs[: counts[0]]
    pair_pieces = refs[counts[0] : counts[0] + counts[1]]
    down_pieces = refs[counts[0] + counts[1] : total_count]
    out_ref, inner_ref, slopes_ref, act_t_ref, attn_t_ref, dy_ref, resid_ref = refs[total_count : total_count + 7]
    w_attn, w_pair, w_down, sum_ref, sems0, sems1, sems2 = refs[total_count + 7 :]
    attention_copies = load(attention_pieces, s0_ref, w_attn, sems0)
    pair_copies = load(pair_pieces, s1_ref, w_pair, sems1)
    down_copies = load(down_pieces, s2_ref, w_down, sems2)
    width = x_ref.shape[1]
    hidden = w_pair.shape[1]
    tile = hidden // 5
    x = upright(x_ref).astype(F32)
    dy_ref[...] = upright(cot_ref)
    attn_t_ref[...] = jnp.transpose(attn_ref[...])
    wait(attention_copies)
    resid = x + nn(attn_ref[...], w_attn[width:, :width])
    resid_ref[...] = resid
    sum_ref[...] = resid
    act = (resid * rms_inverse(resid) * gains_ref[1:2, :]).astype(BF)
    act_t_ref[...] = jnp.transpose(act)
    wait(pair_copies)
    wait(down_copies)
    dy = dy_ref[...]
    for first in range(0, hidden, tile):
        here = slice(first, first + tile)
        gate = nn(act, w_pair[:width, here])
        upper = nn(act, w_pair[width:, here])
        d_inner = nt(dy, w_down[here, :])
        sigmoid = 1.0 / (1.0 + jnp.exp(-gate))
        silu = gate * sigmoid
        inner = (silu * upper).astype(BF)
        inner_ref[here, :] = jnp.transpose(inner)
        slopes_ref[0, :, here] = (d_inner * upper * sigmoid * (1.0 + gate * (1.0 - sigmoid))).astype(BF)
        slopes_ref[1, :, here] = (d_inner * silu).astype(BF)
        sum_ref[...] += nn(inner, w_down[here, :])
    lay_down(sum_ref[...].astype(BF), out_ref)


def feed(x, attn, dy, gains, attention_got, pair_got, down_got):
    micro, width, rows = x.shape
    tokens = micro * rows
    groups = [attention_got, pair_got, down_got]
    counts = [len(pieces) for pieces, _, _ in groups]
    shapes = [shape for _, _, shape in groups]
    hidden = shapes[1][1]
    outs = (
        jax.ShapeDtypeStruct(x.shape, BF),
        jax.ShapeDtypeStruct((hidden, tokens), BF),
        jax.ShapeDtypeStruct((2, tokens, hidden), BF),
        jax.ShapeDtypeStruct((width, tokens), BF),
        jax.ShapeDtypeStruct((width, tokens), BF),
        jax.ShapeDtypeStruct((tokens, width), BF),
        jax.ShapeDtypeStruct((tokens, width), F32),
    )
    every = [piece for pieces, _, _ in groups for piece in pieces]
    return pl.pallas_call(
        functools.partial(feed_kernel, counts),
        name="feed",
        in_specs=[IN_SMEM] * 3 + [IN_VMEM] * 4 + [ANYWHERE] * len(every),
        out_specs=(IN_VMEM,) * 7,
        out_shape=outs,
        scratch_shapes=[pltpu.VMEM(shape, BF) for shape in shapes]
        + [pltpu.VMEM((tokens, width), F32)]
        + [pltpu.SemaphoreType.DMA((count,)) for count in counts],
        cost_estimate=cost(
            2 * tokens * width * (4 * hidden + width), tokens * hidden, x, x, x, *outs, *every
        ),
        compiler_params=pltpu.CompilerParams(vmem_limit_bytes=VMEM_MOST),
    )(*(starts for _, starts, _ in groups), x, attn, dy, gains, *every)


def feed_back_kernel(counts, s0_ref, s1_ref, resid_ref, dy_ref, slopes_ref, gains_ref, *refs):
    total_count = sum(counts)
    dres_ref, low_ref, dattn_ref, w_attn, w_pair, sems0, sems1 = refs[total_count:]
    pair_copies = load(refs[counts[0] : total_count], s1_ref, w_pair, sems1)
    attention_copies = load(refs[: counts[0]], s0_ref, w_attn, sems0)
    width = resid_ref.shape[1]
    resid = resid_ref[...]
    root = rms_inverse(resid)
    normed = resid * root
    wait(pair_copies)
    d_act = nt(slopes_ref[0], w_pair[:width, :]) + nt(slopes_ref[1], w_pair[width:, :])
    d_normed = d_act * gains_ref[1:2, :]
    d_resid = dy_ref[...].astype(F32) + root * (
        d_normed - normed * jnp.mean(d_normed * normed, axis=-1, keepdims=True)
    )
    dres_ref[...] = d_resid
    low = d_resid.astype(BF)
    low_ref[...] = low
    wait(attention_copies)
    dattn_ref[...] = nt(low, w_attn[width:, :width]).astype(BF)


def feed_back(resid, dy, slopes, gains, attention_got, pair_got):
    tokens, width = resid.shape
    groups = [attention_got, pair_got]
    counts = [len(pieces) for pieces, _, _ in groups]
    shapes = [shape for _, _, shape in groups]
    outs = (
        jax.ShapeDtypeStruct((tokens, width), F32),
        jax.ShapeDtypeStruct((tokens, width), BF),
        jax.ShapeDtypeStruct((tokens, width), BF),
    )
    every = [piece for pieces, _, _ in groups for piece in pieces]
    return pl.pallas_call(
        functools.partial(feed_back_kernel, counts),
        name="feed_back",
        in_specs=[IN_SMEM] * 2 + [IN_VMEM] * 4 + [ANYWHERE] * len(every),
        out_specs=(IN_VMEM,) * 3,
        out_shape=outs,
        scratch_shapes=[pltpu.VMEM(shape, BF) for shape in shapes]
        + [pltpu.SemaphoreType.DMA((count,)) for count in counts],
        cost_estimate=cost(
            2 * tokens * width * (2 * shapes[1][1] + width), 0, resid, dy, slopes, *outs, *every
        ),
        compiler_params=pltpu.CompilerParams(vmem_limit_bytes=VMEM_MOST),
    )(*(starts for _, starts, _ in groups), resid, dy, slopes, gains, *every)


def pick_rows(source, starts_ref, base, rows, count, target):
    for t in range(count):
        start = pl.multiple_of(starts_ref[base + t], 16)
        target[t * rows : (t + 1) * rows, :] = source[pl.ds(start, rows), :]


def rows_grad_kernel(parts, count, starts_ref, *refs):
    operands = refs[: 2 * len(parts)]
    outs = refs[2 * len(parts) : 2 * len(parts) + 2]
    ordered = refs[2 * len(parts) + 2 :]
    block = sum(parts)
    for o, out_ref in enumerate(outs):
        at = 0
        for i, rows in enumerate(parts):
            pick_rows(operands[2 * i], starts_ref, (o * len(parts) + i) * count, rows, count, ordered[i])
            made = nn(ordered[i][...], operands[2 * i + 1][...]).astype(BF)
            columns = made.shape[1]
            for t in range(count):
                place = slice(t * block + at, t * block + at + rows)
                out_ref[place, :columns] = made[t * rows : (t + 1) * rows]
                if columns < out_ref.shape[1]:
                    out_ref[place, columns:] = jnp.zeros((rows, out_ref.shape[1] - columns), BF)
            at += rows


def rows_grad(terms):
    count = len(terms[0][3])
    parts = [term[2] for term in terms]
    block, columns = sum(parts), terms[0][1].shape[1]
    wide = rounded_up(columns)
    if any(rows % 16 for rows in parts) or any(term[0].shape[0] // count % 16 for term in terms):
        outs = []
        for o in (3, 4):
            made = []
            for term in terms:
                grad = jnp.pad(nn(term[0], term[1]).astype(BF), ((0, 0), (0, wide - columns)))
                made.append([lax.dynamic_slice_in_dim(grad, start, term[2], 0) for start in term[o]])
            outs.append(jnp.concatenate([part for group in zip(*made) for part in group], axis=0))
        return outs
    args = [operand for term in terms for operand in term[:2]]
    out = jax.ShapeDtypeStruct((count * block, wide), BF)
    flops = sum(4 * left.shape[1] * rows * count * columns for left, _, rows, _, _ in terms)
    return pl.pallas_call(
        functools.partial(rows_grad_kernel, parts, count),
        name="rows_grad",
        in_specs=[IN_SMEM] + [IN_VMEM] * len(args),
        out_specs=(IN_VMEM,) * 2,
        out_shape=(out, out),
        scratch_shapes=[pltpu.VMEM((count * rows, terms[0][0].shape[1]), BF) for rows in parts],
        cost_estimate=cost(flops, 0, out, out, *args),
        compiler_params=pltpu.CompilerParams(vmem_limit_bytes=VMEM_LIMIT),
    )(numbers([start for o in (3, 4) for term in terms for start in term[o]]), *args)


def wide_grad_kernel(cuts, count, rows, info_ref, left_ref, given_ref, kept_ref, *refs):
    outs, ordered = refs[: 2 * len(cuts)], refs[2 * len(cuts)]

    @pl.when(pl.program_id(0) == 0)
    def _():
        at = 0
        for o in range(2):
            first = 0
            for cut in cuts:
                for t in range(count):
                    start = pl.multiple_of(info_ref[2 + o * count + t] + first, 16)
                    ordered[at : at + cut, :] = left_ref[pl.ds(start, cut), :]
                    at += cut
                first += cut

    for o, right_ref in enumerate((given_ref, kept_ref)):
        made = nn(ordered[o * count * rows : (o + 1) * count * rows, :], right_ref[...]).astype(BF)
        at = 0
        for c, cut in enumerate(cuts):
            outs[o * len(cuts) + c][...] = made[at : at + count * cut]
            at += count * cut


def wide_grad(left, rights, rows, cuts, given, kept, core):
    count, (_, tokens, columns) = len(given), rights.shape
    outs = tuple(jax.ShapeDtypeStruct((count * cut, columns), BF) for cut in cuts) * 2
    if rows % 16 or any(cut % 16 for cut in cuts):
        made = []
        for starts, choice in ((given, 1 - core), (kept, core)):
            grad = nn(left, lax.dynamic_index_in_dim(rights, choice, 0, keepdims=False)).astype(BF)
            first = 0
            for cut in cuts:
                made.append(
                    jnp.concatenate([lax.dynamic_slice_in_dim(grad, start + first, cut, 0) for start in starts])
                )
                first += cut
        return made
    tile = 512 if columns % 512 == 0 else columns
    return pl.pallas_call(
        functools.partial(wide_grad_kernel, cuts, count, rows),
        grid_spec=pltpu.PrefetchScalarGridSpec(
            num_scalar_prefetch=1,
            grid=(columns // tile,),
            in_specs=[
                pl.BlockSpec(left.shape, lambda n, info: (0, 0)),
                pl.BlockSpec((None, tokens, tile), lambda n, info: (info[0], 0, n)),
                pl.BlockSpec((None, tokens, tile), lambda n, info: (info[1], 0, n)),
            ],
            out_specs=tuple(pl.BlockSpec((out.shape[0], tile), lambda n, info: (0, n)) for out in outs),
            scratch_shapes=[pltpu.VMEM((2 * count * rows, tokens), BF)],
        ),
        out_shape=outs,
        name="wide_grad",
        cost_estimate=cost(4 * tokens * rows * count * columns, 0, left, rights, *outs),
        compiler_params=pltpu.CompilerParams(vmem_limit_bytes=VMEM_LIMIT),
    )(numbers([1 - core, core] + given + kept), left, rights, rights)


def turn_keys(source, target, at, cosine, sine):
    rows = source.shape[0]
    for first in range(0, KV_WIDTH, 128):
        chunk = turn(source[:, first : first + 128].astype(F32), cosine, -sine).astype(BF)
        last = min(first + 128, KV_WIDTH)
        target[at : at + rows, first:last] = chunk[:, : last - first]
    target[at : at + rows, KV_WIDTH:] = source[:, KV_WIDTH:]


def attention_grad_kernel(shards, half, starts_ref, gain_ref, cos_ref, sin_ref, dq_ref, attn_ref, low_ref, *refs):
    xs, halves = refs[:shards], refs[shards : shards + 2]
    dkvs = [ref.at[t] for ref in halves for t in range(shards // 2)]
    outs, (act, dkv, ordered, attn_ordered) = refs[shards + 2 : shards + 4], refs[shards + 4 :]
    micro, width, rows = xs[0].shape
    tokens = micro * rows
    wide = rounded_up(width)
    for t in range(shards):
        here = slice(t * tokens, (t + 1) * tokens)
        turn_keys(dkvs[t], dkv, t * tokens, cos_ref[here, :], sin_ref[here, :])
        for m in range(micro):
            x = xs[t][m].astype(F32)
            root = lax.rsqrt(jnp.mean(x * x, axis=0, keepdims=True) + EPS)
            first = t * tokens + m * rows
            act[:, first : first + rows] = (x * root * gain_ref[...]).astype(BF)
    for i, out_ref in enumerate(outs):
        pick_rows(act, starts_ref, i * shards, half, shards, ordered)
        pick_rows(attn_ref, starts_ref, i * shards, half, shards, attn_ordered)
        for first, made in (
            (0, nn(ordered[:, :tokens], dq_ref[...])),
            (wide, nn(attn_ordered[...], low_ref[...])),
        ):
            out_ref[:, first : first + width] = made.astype(BF)
            if wide > width:
                out_ref[:, first + width : first + wide] = jnp.zeros((made.shape[0], wide - width), BF)
        out_ref[:, 2 * wide :] = nn(ordered[...], dkv[...]).astype(BF)


def attention_grad(x_all, gain, cosine, sine, dq, attn_t, low, dkv_all, half, given, kept):
    shards = len(x_all)
    micro, width, rows = x_all[0].shape
    every = shards * micro * rows
    wide = rounded_up(width)
    out = jax.ShapeDtypeStruct((shards * half, 2 * wide + 2 * KV_WIDTH), BF)
    if half % 16 or width // shards % 16:
        xs = jnp.concatenate([x[m] for x in x_all for m in range(micro)], axis=1).astype(F32)
        act = xs * lax.rsqrt(jnp.mean(xs * xs, axis=0, keepdims=True) + EPS) * gain
        act = act.astype(BF)
        dkv = jnp.concatenate(dkv_all, axis=0).reshape(every, 2 * KV_WIDTH)
        keys = dkv[:, :KV_WIDTH].astype(F32).reshape(every, -1, 2, HALF_HEAD)
        c, s = cosine[:, None, :HALF_HEAD], sine[:, None, HALF_HEAD:HEAD_SIZE]
        first, second = keys[:, :, 0], keys[:, :, 1]
        keys = jnp.stack([first * c + second * s, second * c - first * s], axis=2)
        dkv = jnp.concatenate([keys.reshape(every, KV_WIDTH).astype(BF), dkv[:, KV_WIDTH:]], axis=1)
        space = ((0, 0), (0, wide - width))
        parts = [jnp.pad(nn(act[:, : micro * rows], dq), space), jnp.pad(nn(attn_t, low), space), nn(act, dkv)]
        grad = jnp.concatenate(parts, axis=1).astype(BF)
        return [
            jnp.concatenate([lax.dynamic_slice_in_dim(grad, start, half, 0) for start in starts])
            for starts in (given, kept)
        ]
    return pl.pallas_call(
        functools.partial(attention_grad_kernel, shards, half),
        name="attention_grad",
        in_specs=[IN_SMEM] + [IN_VMEM] * (8 + shards),
        out_specs=(IN_VMEM,) * 2,
        out_shape=(out, out),
        scratch_shapes=[
            pltpu.VMEM((width, every), BF),
            pltpu.VMEM((every, 2 * KV_WIDTH), BF),
            pltpu.VMEM((shards * half, every), BF),
            pltpu.VMEM((shards * half, micro * rows), BF),
        ],
        cost_estimate=cost(
            4 * shards * half * (every * 2 * KV_WIDTH + 2 * micro * rows * width),
            0,
            *x_all,
            *dkv_all,
            out,
            out,
        ),
        compiler_params=pltpu.CompilerParams(vmem_limit_bytes=VMEM_MOST),
    )(numbers(given + kept), gain, cosine, sine, dq, attn_t, low, *x_all, *dkv_all)


def finish_kernel(count, starts_ref, x_ref, low_ref, kv_ref, dres_ref, gains_ref, cos_ref, sin_ref, *refs):
    pieces = refs[:count]
    dx_ref, whole, kv_turned, sems = refs[count:]
    copies = load(pieces, starts_ref, whole, sems)
    turn_keys(kv_ref, kv_turned, 0, cos_ref[...], sin_ref[...])
    x = upright(x_ref).astype(F32)
    width = x.shape[1]
    root = rms_inverse(x)
    normed = x * root
    wait(copies)
    d_act = nt(low_ref[...], whole[:width, :width])
    d_act += nt(kv_turned[:, :KV_WIDTH], whole[:width, width:])
    d_act += nt(kv_turned[:, KV_WIDTH:], whole[width:, width:])
    d_normed = d_act * gains_ref[0:1, :]
    d_x = dres_ref[...] + root * (d_normed - normed * jnp.mean(d_normed * normed, axis=-1, keepdims=True))
    lay_down(d_x.astype(BF), dx_ref)


def finish(x, low, kv, dres, gains, cosine, sine, pieces, starts, shape):
    micro, width, rows = x.shape
    tokens = micro * rows
    table = pl.BlockSpec((tokens, 128), lambda i: (0, 0))
    return pl.pallas_call(
        functools.partial(finish_kernel, len(pieces)),
        grid=(1,),
        name="finish",
        in_specs=[IN_SMEM] + [IN_VMEM] * 5 + [table] * 2 + [ANYWHERE] * len(pieces),
        out_specs=IN_VMEM,
        out_shape=jax.ShapeDtypeStruct(x.shape, BF),
        scratch_shapes=[
            pltpu.VMEM(shape, BF),
            pltpu.VMEM((tokens, 2 * KV_WIDTH), BF),
            pltpu.SemaphoreType.DMA((len(pieces),)),
        ],
        cost_estimate=cost(2 * tokens * width * (width + 2 * KV_WIDTH), 0, x, low, dres, *pieces),
        compiler_params=pltpu.CompilerParams(vmem_limit_bytes=VMEM_LIMIT),
    )(starts, x, low, kv, dres, gains, cosine, sine, *pieces)


def head(ref, h):
    return ref[:, h * HEAD_SIZE : (h + 1) * HEAD_SIZE]


def widen(value, columns):
    n = value.shape[0]
    lane = lax.broadcasted_iota(jnp.int32, (n, HEAD_SIZE), 1)
    tail = jnp.zeros((n, HEAD_SIZE), F32)
    for c, column in enumerate(columns):
        tail = jnp.where(lane == c, column, tail)
    return jnp.concatenate([value, tail.astype(BF)], axis=1)


def split(column):
    high = column.astype(BF).astype(F32)
    middle = (column - high).astype(BF).astype(F32)
    return [high, middle, column - high - middle]


def attend_kernel(shards, seg_rows, q_ref, *refs):
    kv = refs[:shards]
    bias_ref = refs[shards]
    o_ref, lse_ref = refs[-2:]
    rows = q_ref.shape[0]
    i = lax.broadcasted_iota(jnp.int32, (rows, rows), 0)
    j = lax.broadcasted_iota(jnp.int32, (rows, rows), 1)
    same = (i // seg_rows) == (j // seg_rows)
    own = jnp.where(j > i, CLOSED, jnp.where(same, 0.0, bias_ref[0:1, :]))
    one = jnp.ones((rows, 1), F32)
    bias_columns = jnp.transpose(bias_ref[...])
    lse = jnp.zeros((rows, 128), F32)
    lane = lax.broadcasted_iota(jnp.int32, (rows, 128), 1)
    for g in range(KEY_VALUE_HEADS):
        keys, values = [], []
        for t in range(shards):
            keys.append(widen(head(kv[t], g), [bias_columns[:, t : t + 1]] if t else []))
            values.append(widen(head(kv[t], KEY_VALUE_HEADS + g), [one]))
        for h in range(g * GROUP, g * GROUP + GROUP):
            q = widen(head(q_ref, h), [one])
            scores = [nt(q, k) for k in keys]
            scores[0] = scores[0] + own
            peak = functools.reduce(jnp.maximum, scores)
            peak = jnp.max(peak, axis=1, keepdims=True)
            terms = [nn(jnp.exp(s - peak).astype(BF), v) for s, v in zip(scores, values)]
            mixed = sum(terms[1:], terms[0])
            total = mixed[:, HEAD_SIZE : HEAD_SIZE + 1]
            o_ref[:, h * HEAD_SIZE : (h + 1) * HEAD_SIZE] = (mixed[:, :HEAD_SIZE] / total).astype(BF)
            lse = jnp.where(lane == h, peak + jnp.log(total), lse)
    lse_ref[...] = lse


def attend_back_kernel(shards, seg_rows, q_ref, *refs):
    kv = refs[:shards]
    bias_ref, o_ref, do_ref, lse_ref, cos_ref, sin_ref = refs[shards : shards + 6]
    dq_ref, low_ref, high_ref = refs[-3:]
    dkv = [ref.at[t] for ref in (low_ref, high_ref) for t in range(shards // 2)]
    rows = q_ref.shape[0]
    i = lax.broadcasted_iota(jnp.int32, (rows, rows), 1)
    j = lax.broadcasted_iota(jnp.int32, (rows, rows), 0)
    bias_columns = jnp.transpose(bias_ref[...])
    same = (i // seg_rows) == (j // seg_rows)
    own_column = jnp.broadcast_to(bias_columns[:, 0:1], (rows, rows))
    own = jnp.where(j > i, CLOSED, jnp.where(same, 0.0, own_column))
    one, zero = jnp.ones((rows, 1), F32), jnp.zeros((rows, 1), F32)
    cosine, sine = cos_ref[...], sin_ref[...]
    for g in range(KEY_VALUE_HEADS):
        keys, values, turned = [], [], []
        for t in range(shards):
            k = head(kv[t], g)
            turned.append(jnp.transpose(k))
            keys.append(widen(k, [bias_columns[:, t : t + 1] if t else zero, one, one, one]))
            values.append(widen(head(kv[t], KEY_VALUE_HEADS + g), [one, one, one]))
        dk, dv = [None] * shards, [None] * shards
        for h in range(g * GROUP, g * GROUP + GROUP):
            q, do = head(q_ref, h), head(do_ref, h)
            centre = jnp.sum(head(o_ref, h).astype(F32) * do.astype(F32), axis=1, keepdims=True)
            q_wide = widen(q, [one] + split(-lse_ref[:, h : h + 1]))
            do_wide = widen(do, split(-centre))
            dq = None
            for t in range(shards):
                scores = nt(keys[t], q_wide)
                if t == 0:
                    scores = scores + own
                probs = jnp.exp(scores)
                ds = (probs * nt(values[t], do_wide)).astype(BF)
                v_term = nn(probs.astype(BF), do)
                k_term = nn(ds, q)
                q_term = nn(turned[t], ds)
                dv[t] = v_term if dv[t] is None else dv[t] + v_term
                dk[t] = k_term if dk[t] is None else dk[t] + k_term
                dq = q_term if dq is None else dq + q_term
            dq = dq * SCALE
            first, second = dq[:HALF_HEAD], dq[HALF_HEAD:]
            back = jnp.concatenate(
                [first * cosine + second * sine, second * cosine - first * sine], axis=0
            )
            dq_ref[:, h * HEAD_SIZE : (h + 1) * HEAD_SIZE] = jnp.transpose(back).astype(BF)
        for t in range(shards):
            dkv[t][:, g * HEAD_SIZE : (g + 1) * HEAD_SIZE] = dk[t].astype(BF)
            g_value = KEY_VALUE_HEADS + g
            dkv[t][:, g_value * HEAD_SIZE : (g_value + 1) * HEAD_SIZE] = dv[t].astype(BF)


def attend(micro, seg_rows, q, kv, bias):
    shards, tokens, width = len(kv), q.shape[0], q.shape[1]
    rows = tokens // micro
    here = lambda w: pl.BlockSpec((rows, w), lambda m: (m, 0))
    outs = (jax.ShapeDtypeStruct((tokens, width), BF), jax.ShapeDtypeStruct((tokens, 128), F32))
    pairs = tokens * rows * shards * QUERY_HEADS
    return pl.pallas_call(
        functools.partial(attend_kernel, shards, seg_rows),
        grid=(micro,),
        name="attend",
        in_specs=[here(width)]
        + [here(2 * KV_WIDTH)] * shards
        + [pl.BlockSpec((None,) + bias.shape[1:], lambda m: (m, 0, 0))],
        out_specs=(here(width), here(128)),
        out_shape=outs,
        cost_estimate=cost(16 * HEAD_SIZE * pairs, pairs, q),
        compiler_params=pltpu.CompilerParams(vmem_limit_bytes=VMEM_LIMIT),
    )(q, *kv, bias)


def attend_back(m, rows, seg_rows, q, kv, bias, o, do, lse, cosine, sine, earlier):
    shards, tokens, width = len(kv), q.shape[0], q.shape[1]
    here = lambda w: pl.BlockSpec((rows, w), lambda i: (m, 0))
    turned = pl.BlockSpec((HALF_HEAD, rows), lambda i: (0, m))
    outs = (jax.ShapeDtypeStruct((tokens, width), BF),)
    outs += (jax.ShapeDtypeStruct((shards // 2, tokens, 2 * KV_WIDTH), BF),) * 2
    pieces = pl.BlockSpec((shards // 2, rows, 2 * KV_WIDTH), lambda i: (0, m, 0))
    pairs = rows * rows * shards * QUERY_HEADS
    return pl.pallas_call(
        functools.partial(attend_back_kernel, shards, seg_rows),
        grid=(1,),
        name="attend_back",
        in_specs=[here(width)]
        + [here(2 * KV_WIDTH)] * shards
        + [pl.BlockSpec((None,) + bias.shape[1:], lambda i: (m, 0, 0))]
        + [here(width), here(width), here(128), turned, turned]
        + [pl.BlockSpec(memory_space=pl.ANY)] * len(earlier),
        out_specs=(here(width), pieces, pieces),
        out_shape=outs,
        input_output_aliases={shards + 7 + i: i for i in range(len(earlier))},
        cost_estimate=cost(40 * HEAD_SIZE * pairs, pairs, q),
        compiler_params=pltpu.CompilerParams(vmem_limit_bytes=VMEM_LIMIT),
    )(q, *kv, bias, o, do, lse, cosine, sine, *earlier)


def local(
    block_input,
    parent_ids,
    w_query,
    key_weight,
    value_weight,
    w_output,
    w_gate,
    w_up,
    w_down,
    norm_first,
    norm_second,
    out_cotangent,
):
    micro, rows, width = block_input.shape
    shards = lax.axis_size("shard")
    links = Links(lax.axis_size("rep"), shards)
    tree = rows * shards
    segs = parent_ids.shape[2]
    seg_rows = tree // segs
    tokens = micro * rows
    hidden = w_gate.shape[1]

    inputs = block_input.swapaxes(1, 2)
    cotangent = out_cotangent.swapaxes(1, 2)

    even = links.core == 0
    side = lax.axis_index("rep") // 2 % 2
    left = jnp.concatenate([w_query, key_weight], axis=1)
    right = jnp.concatenate([w_output, value_weight], axis=1)
    attn_mine = jnp.where(even, left, right)
    pair_cut = hidden // 2
    pair_mine = lax.dynamic_slice_in_dim(jnp.where(even, w_gate, w_up), side * pair_cut, pair_cut, 1)
    down_cut = w_down.shape[0] // 2
    down_mine = lax.dynamic_slice_in_dim(w_down, links.core * down_cut, down_cut, 0)

    attn_near = links.near(attn_mine)
    gain_pieces = links.small_pieces(jnp.stack([norm_first, norm_second]))
    attn_mine, attn_near, gain_pieces, pair_mine, down_mine = meet(
        attn_mine, attn_near, gain_pieces, pair_mine, down_mine
    )

    gains = links.in_order(gain_pieces).astype(F32)
    attn_all = links.far(attn_mine, attn_near)
    attn_swapped = {t: links.swap(attn_near[t]) for t in attn_near}
    pair_near = {1: links.step(pair_mine, 0)}
    own_down = with_layout_constraint(w_down, Layout(major_to_minor=(0, 1)))
    parents = parent_ids[:, 0]
    seg = jnp.arange(segs)
    after_parent = jnp.concatenate([parents[:, 1:], jnp.full((micro, 1), -1, parents.dtype)], axis=1)
    on_path = (seg % 2 == 0)[None] | (after_parent == seg[None])
    below = (seg[None, :] < seg[:, None])[None]
    depth = jnp.sum(jnp.where(below, on_path.astype(F32)[:, None, :], 0.0), axis=-1)

    def row_numbers(hop):
        return (links.shard ^ hop) * rows + jnp.arange(rows)

    def pick(table, numbers):
        hit = (numbers // seg_rows)[..., None] == seg
        return jnp.sum(jnp.where(hit[None], table.reshape(micro, *(1,) * numbers.ndim, segs), 0), axis=-1)

    key_rows = jnp.stack([row_numbers(hop) for hop in links.hops])
    positions = pick(depth, key_rows) * seg_rows + (key_rows % seg_rows).astype(F32)
    freqs = jnp.exp(-math.log(10000.0) * jnp.arange(HALF_HEAD, dtype=F32) * (2.0 / HEAD_SIZE))
    angles = freqs[:, None] * positions.swapaxes(0, 1).reshape(1, shards * tokens)
    cosine_t, sine_t = jnp.cos(angles), jnp.sin(angles)
    cosine = jnp.tile(cosine_t.T, (1, 4))
    sine = jnp.tile(jnp.concatenate([-sine_t.T, sine_t.T], axis=1), (1, 2))
    open_key = (pick(on_path.astype(F32), key_rows) > 0.5) & (
        (key_rows < links.shard * rows) | (jnp.arange(shards) == 0)[:, None]
    )
    bias = jnp.where(open_key, 0.0, CLOSED)
    bias = jnp.pad(bias, ((0, 0), (0, 8 - shards), (0, 0)))

    attn_all, attn_swapped, pair_mine, pair_near, gains, cosine, sine, bias, down_mine, own_down = meet(
        attn_all, attn_swapped, pair_mine, pair_near, gains, cosine, sine, bias, down_mine, own_down
    )

    for t in range(1, shards):
        if t not in attn_swapped:
            attn_swapped[t] = links.swap(attn_all[t])
    shard_rows = width // shards

    def pair_place(weight, hop):
        return weight * width + (links.shard ^ hop) * shard_rows

    pieces, starts = [left, right], [(pair_place(0, 0), 0), (pair_place(1, 0), 0)]
    for t in range(1, shards):
        pieces += [attn_all[t], attn_swapped[t]]
        starts += [
            (pair_place(links.core, links.hops[t]), 0),
            (pair_place(1 - links.core, links.hops[links.twin(t)]), 0),
        ]
    attention_got = joined(pieces, starts, (2 * width, left.shape[1]))
    pair_near |= {1 << i: links.step(pair_mine, i) for i in range(1, links.bits)}
    pair_beside = {1: links.beside(pair_near[1])}
    down_near = {1: links.step(down_mine, 0)}
    queries, kv = project(inputs, gains, cosine, sine, *attention_got)
    queries, kv, pair_mine, pair_near, pair_beside, down_mine, down_near = meet(
        queries, kv, pair_mine, pair_near, pair_beside, down_mine, down_near
    )

    kv_near = links.near(kv)
    pair_beside |= {t: links.beside(pair_near[t]) for t in pair_near if t > 1}
    kv_near, kv, pair_beside, pair_near, pair_mine = meet(kv_near, kv, pair_beside, pair_near, pair_mine)

    kv_all = links.far(kv, kv_near)
    pair_all = links.far(pair_mine, pair_near)
    pair_swapped = {t: links.swap(pair_near[t]) for t in pair_near}
    pair_crossed = {t: links.swap(pair_beside[t]) for t in pair_beside}
    kv_all, pair_all, pair_swapped, pair_crossed, pair_beside, down_mine, down_near = meet(
        kv_all, pair_all, pair_swapped, pair_crossed, pair_beside, down_mine, down_near
    )

    down_near |= {1 << i: links.step(down_mine, i) for i in range(1, links.bits)}
    down_all = links.far(down_mine, down_near)
    pair_beside |= {t: links.beside(pair_all[t]) for t in range(1, shards) if t not in pair_beside}
    attn, lse = attend(micro, seg_rows, queries, kv_all, bias)
    pair_swapped |= {t: links.swap(pair_all[t]) for t in range(1, shards) if t not in pair_swapped}
    attn, lse, down_all, pair_beside, pair_all, pair_swapped = meet(
        attn, lse, down_all, pair_beside, pair_all, pair_swapped
    )

    pair_crossed |= {t: links.swap(pair_beside[t]) for t in range(1, shards) if t not in pair_crossed}
    down_swapped = [None] + [links.swap(down_all[t]) for t in range(1, shards)]
    pieces, starts = [w_gate, w_up], [(pair_place(0, 0), 0), (pair_place(1, 0), 0)]
    for t in range(1, shards):
        pieces += [pair_all[t], pair_beside[t], pair_swapped[t], pair_crossed[t]]
        for row in (
            pair_place(links.core, links.hops[t]),
            pair_place(1 - links.core, links.hops[links.twin(t)]),
        ):
            starts += [(row, side * pair_cut), (row, (1 - side) * pair_cut)]
    pair_got = joined(pieces, starts, (2 * width, hidden))
    own = w_down.shape[0]
    pieces, starts = [own_down], [(links.shard * own, 0)]
    for t in range(1, shards):
        pieces += [down_all[t], down_swapped[t]]
        starts += [
            ((links.shard ^ links.hops[t]) * own + links.core * down_cut, 0),
            ((links.shard ^ links.hops[links.twin(t)]) * own + (1 - links.core) * down_cut, 0),
        ]
    down_got = joined(pieces, starts, (own * shards, width))
    attn, pair_pieces, down_pieces = meet(attn, pair_got[0], down_got[0])
    pair_got, down_got = (pair_pieces, *pair_got[1:]), (down_pieces, *down_got[1:])

    plan = Plan()
    have = lambda *names: [plan.have[name] for name in names]
    x_near = links.near(inputs)
    made = feed(inputs, attn, cotangent, gains, attention_got, pair_got, down_got)
    names = ("out", "inner", "slopes", "act", "attn_t", "dy", "resid")
    plan.have = dict(zip(names, made)) | {"x_near": x_near, "queries": queries, "kv": kv_all, "lse": lse, "attn": attn}
    plan.close()

    down_half = own // 2
    output_half, output_mine, output_theirs = links.half_rows(shard_rows)
    down_kept, down_given = links.order(own, links.core * down_half, (1 - links.core) * down_half)
    wide_kept, wide_given = links.order(shard_rows, 0, 0)
    some_kept, some_given = links.order(shard_rows, output_mine, output_theirs)

    plan.have["x_all"] = links.far(inputs, plan.have.pop("x_near"))
    plan.have["rows.given"], plan.have["rows.kept"] = rows_grad(
        ((*have("inner", "dy"), down_half, down_given, down_kept),)
    )
    plan.close()

    for name in ("rows", "wide0", "wide1", "some"):
        plan.start(name, links.reduce(plan, name, name == "some"))
    plan.advance("rows")
    cuts = (-(-shard_rows // 32) * 16, shard_rows - -(-shard_rows // 32) * 16)
    act, slopes = have("act", "slopes")
    made = wide_grad(act, slopes, shard_rows, cuts, wide_given, wide_kept, links.core)
    names = [name + part for part in (".given", ".kept") for name in ("wide0", "wide1")]
    plan.have |= dict(zip(names, made))
    plan.close()

    plan.advance("rows", "wide0", "wide1")
    names = ("d_resid", "d_resid_low", "d_attn")
    made = feed_back(*have("resid", "dy", "slopes"), gains, attention_got, pair_got)
    plan.have |= dict(zip(names, made))
    plan.close()

    made = ()
    hops = [("rows", "wide0"), ("rows", "wide0", "wide1")]
    for m in range(micro):
        plan.advance(*hops[min(m, 1)])
        q, kv_now, o, do, lse_now = have("queries", "kv", "attn", "d_attn", "lse")
        made = attend_back(m, rows, seg_rows, q, kv_now, bias, o, do, lse_now, cosine_t, sine_t, made)
        plan.have["attn_grads"] = made = tuple(made)
        plan.close()
        made = plan.have["attn_grads"]

    d_queries, *d_kv = plan.have.pop("attn_grads")
    plan.have["dkv.pieces"] = d_kv
    plan.have["d_queries"] = d_queries
    plan.start("dkv", links.collect(plan, "dkv"))
    plan.advance("dkv", "wide0", "wide1", "rows")
    given, kept = attention_grad(
        plan.have["x_all"],
        gains[0][:, None],
        cosine,
        sine,
        d_queries,
        *have("attn_t", "d_resid_low"),
        d_kv,
        output_half,
        some_given,
        some_kept,
    )
    plan.have["some.given"], plan.have["some.kept"] = given, kept
    plan.close()

    def gain_grad(gain, *pairs):
        sums = sum(jnp.sum(weight.astype(F32) * grad, axis=1) for weight, grad in pairs)
        return sums / gain.astype(F32)

    def settle():
        have, done = plan.have, plan.have.setdefault("done", {})
        if "dkv" in have and "d_input" not in done:
            done["d_input"] = finish(
                inputs, have["d_queries"], have["dkv"], have["d_resid"], gains, cosine, sine, *attention_got
            )
        if "rows" in have and "down" not in done:
            value, other = have["rows"]
            done["down"] = links.finish_rows(value[:, :width], other[:, :width], own)
        if "wide0" in have and "wide1" in have and "gate" not in done:
            halves = [links.finish_pair(*have[name]) for name in ("wide0", "wide1")]
            done["gate"], done["upper"] = (jnp.concatenate(parts, axis=0) for parts in zip(*halves))
            done["gain_two"] = gain_grad(norm_second, (w_gate, done["gate"]), (w_up, done["upper"]))
        if "some" in have and "query" not in done:
            grad = links.finish_rows(*have["some"], shard_rows)
            first = rounded_up(width)
            done["query"], done["output"] = grad[:, :width], grad[:, first : first + width]
            done["key"], done["value"] = jnp.split(grad[:, 2 * first :], 2, axis=1)
            done["gain_one"] = gain_grad(
                norm_first,
                (w_query, done["query"]),
                (key_weight, done["key"]),
                (value_weight, done["value"]),
            )

    order = [("rows", "wide0", "wide1", "dkv", "some")]
    while plan.tasks:
        plan.advance(*(order.pop(0) if order else tuple(plan.tasks)))
        settle()
        if plan.tasks:
            plan.close()

    done = plan.have["done"]
    return (
        plan.have["out"].swapaxes(1, 2),
        done["d_input"].swapaxes(1, 2),
        *(done[name] for name in ("query", "key", "value", "output", "gate", "upper", "down")),
        done["gain_one"],
        done["gain_two"],
    )


def solution(mesh):
    rows = P(None, AXES, None)
    weight, gain = P("shard", None), P("shard")
    return jax.shard_map(
        local,
        mesh=mesh,
        in_specs=(rows, P(None, "rep", None)) + (weight,) * 7 + (gain, gain, rows),
        out_specs=(rows, rows) + (weight,) * 7 + (gain, gain),
        check_vma=False,
    )
```

```python
import functools
import math

import jax
import jax.numpy as jnp
from jax import lax
from jax.experimental import pallas as pl
from jax.experimental.pallas import tpu as pltpu
from jax.sharding import PartitionSpec as P

QUERY_HEADS = 15
KEY_VALUE_HEADS = 5
HEAD_SIZE = 64
HALF_HEAD = HEAD_SIZE // 2
GROUP = QUERY_HEADS // KEY_VALUE_HEADS
KV_WIDTH = KEY_VALUE_HEADS * HEAD_SIZE
SCALE = HEAD_SIZE ** (-0.5)
EPS = 1e-05
AXES = ("rep", "shard")
BF = jnp.bfloat16
F32 = jnp.float32
CLOSED = -1e30
VMEM_LIMIT = 48 << 20
VMEM_MOST = 60 << 20


def dot(a, b, dims):
    return lax.dot_general(a, b, (dims, ((), ())), preferred_element_type=F32)


def nn(a, b):
    return dot(a, b, ((1,), (0,)))


def nt(a, b):
    return dot(a, b, ((1,), (1,)))


def tn(a, b):
    return dot(a, b, ((0,), (0,)))


def total(parts):
    return sum(part.astype(F32) for part in parts).astype(parts[0].dtype)


def meet(*values):
    return lax.optimization_barrier(values)


def rounded_up(columns):
    return -(-columns // 128) * 128


def rms_inverse(x):
    return lax.rsqrt(jnp.mean(x * x, axis=-1, keepdims=True) + EPS)


def cost(flops, exps, *arrays):
    size = sum(a.size * a.dtype.itemsize for a in arrays)
    return pl.CostEstimate(flops=flops, transcendentals=exps, bytes_accessed=size)


class Links:
    def __init__(self, reps, shards):
        self.reps, self.shards = reps, shards
        self.core = lax.axis_index("rep") % 2
        self.shard = lax.axis_index("shard")
        self.bits = shards.bit_length() - 1
        even = [1 << i for i in range(self.bits)]
        odd = even[:2][::-1] + even[2:]
        self.steps = list(zip(even, odd))
        self.hops = []
        for piece in range(shards):
            sums = [0, 0]
            for i, step in enumerate(self.steps):
                if piece >> i & 1:
                    sums = [sums[0] ^ step[0], sums[1] ^ step[1]]
            self.hops.append(jnp.where(self.core == 0, sums[0], sums[1]))

    def move(self, value, target):
        pairs = []
        for r in range(self.reps):
            for s in range(self.shards):
                goal = target(r, s)
                if goal is not None:
                    pairs.append((r * self.shards + s, goal[0] * self.shards + goal[1]))
        return lax.ppermute(value, AXES, pairs)

    def step(self, value, i):
        return self.move(value, lambda r, s: (r, s ^ self.steps[i][r % 2]))

    def swap(self, value):
        return self.move(value, lambda r, s: (r ^ 1, s))

    def reduce(self, plan, name, quick=False):
        top = self.bits
        if name + ".given" in plan.have:
            got = yield self.swap(plan.have.pop(name + ".given"))
            sums = [plan.have.pop(name + ".kept"), got]
        else:
            got = yield self.step(plan.have.pop(name + ".high"), top - 1)
            sums = [plan.have.pop(name + ".low"), got]
            top -= 1
        for i in reversed(range(top)):
            block = sums[0].shape[0] // 2
            got = yield self.step(total([part[block:] for part in sums]), i)
            sums = [part[:block] for part in sums] + [got]
        value = total(sums)
        chips = self.reps // 2
        place = lax.axis_index("rep") // 2
        span = 1
        if chips % 4 == 0 and quick and value.shape[0] % 4 == 0:
            quarter = value.shape[0] // 4
            across = lambda value, j: self.move(value, lambda r, s: (r ^ (2 * j), s))
            cut = lambda j: lax.dynamic_slice_in_dim(value, (place % 4 ^ j) * quarter, quarter, 0)
            got = yield [across(cut(j), j) for j in range(1, 4)]
            mine = total([cut(0)] + got)
            got = yield [across(mine, j) for j in range(1, 4)]
            parts = jnp.stack([mine] + got).reshape(2, 2, quarter, -1)
            parts = jnp.where(place % 4 >= 2, parts[::-1], parts)
            parts = jnp.where(place % 2 == 1, parts[:, ::-1], parts)
            value = parts.reshape(4 * quarter, -1)
            span = 4
        elif chips % 4 == 0:
            inward, outward, middle = {0: 1, 3: 2}, {1: 0, 2: 3}, {1: 2, 2: 1}

            def along(value, table):
                def target(r, s):
                    chip = r // 2
                    if chip % 4 not in table:
                        return None
                    return ((chip - chip % 4 + table[chip % 4]) * 2 + r % 2, s)

                return self.move(value, target)

            value = total([value, (yield along(value, inward))])
            value = total([value, (yield along(value, middle))])
            back = yield along(value, outward)
            inner = (place % 4 == 1) | (place % 4 == 2)
            value = jnp.where(inner, value, back)
            span = 4
        while span < chips:
            value = total([value, self.move(value, lambda r, s: (r ^ (2 * span), s))])
            span *= 2
        other = yield self.swap(value)
        plan.have[name] = (value, other)

    def collect(self, plan, name):
        low, high = plan.have[name + ".pieces"]
        got = yield self.step(high, self.bits - 1)
        sums = [low, got]
        for i in reversed(range(self.bits - 1)):
            block = sums[0].shape[0] // 2
            got = yield self.step(total([part[block:] for part in sums]), i)
            sums = [part[:block] for part in sums] + [got]
        plan.have[name] = total(sums)[0]

    def beside(self, value):
        return self.move(value, lambda r, s: (r ^ 2, s))

    def near(self, value):
        return {1 << i: self.step(value, i) for i in range(self.bits)}

    def far(self, value, near):
        pieces = [value]
        for t in range(1, self.shards):
            top = t.bit_length() - 1
            pieces.append(near[t] if t in near else self.step(pieces[t - (1 << top)], top))
        return pieces

    def twin(self, piece):
        return piece if self.bits < 2 else piece >> 2 << 2 | (piece & 1) << 1 | (piece >> 1 & 1)

    def small_pieces(self, value):
        return [
            value if hop == 0 else self.move(value, lambda r, s, hop=hop: (r, s ^ hop))
            for hop in range(self.shards)
        ]

    def in_order(self, pieces):
        pieces = jnp.stack(pieces)
        value = pieces
        order = self.shard ^ jnp.arange(self.shards)
        hit = (order[:, None] == jnp.arange(self.shards)[None, :])[:, :, None, None]
        pieces = jnp.sum(jnp.where(hit, pieces[None], 0), axis=1, dtype=value.dtype)
        return jnp.concatenate([pieces[j] for j in range(self.shards)], axis=-1)

    def half_rows(self, rows):
        half = -(-rows // 32) * 16
        return half, self.core * (rows - half), (1 - self.core) * (rows - half)

    def order(self, scale, mine, theirs):
        kept = [(self.shard ^ hop) * scale + mine for hop in self.hops]
        given = [(self.shard ^ self.hops[self.twin(t)]) * scale + theirs for t in range(self.shards)]
        return kept, given

    def finish_rows(self, owned, other, rows):
        low = jnp.where(self.core == 0, owned, other)
        high = jnp.where(self.core == 0, other, owned)
        return jnp.concatenate([low[: rows - owned.shape[0]], high], axis=0).astype(F32)


class Plan:
    def __init__(self):
        self.have, self.tasks, self.made = {}, {}, {}

    def start(self, name, task):
        self.tasks[name] = task
        self.made[name] = None

    def advance(self, *names):
        for name in names:
            if name in self.tasks:
                try:
                    self.made[name] = self.tasks[name].send(self.made[name])
                except StopIteration:
                    del self.tasks[name], self.made[name]

    def close(self):
        self.have, self.made = lax.optimization_barrier((self.have, self.made))


def joined(pieces, starts, shape):
    if any(piece.shape[0] % 16 or piece.shape[1] % 128 and piece.shape[1] < shape[1] for piece in pieces):
        whole = jnp.zeros(shape, pieces[0].dtype)
        for piece, start in zip(pieces, starts):
            whole = lax.dynamic_update_slice(whole, piece, start)
        pieces, starts = (whole,), [(0, 0)]
    return tuple(pieces), numbers([at for start in starts for at in start]), shape


def numbers(values):
    return jnp.stack([jnp.asarray(value, jnp.int32) for value in values])


def load(pieces, starts_ref, whole, sems):
    copies = []
    for i, piece in enumerate(pieces):
        rows = pl.ds(pl.multiple_of(starts_ref[2 * i], 16), piece.shape[0])
        if piece.shape[1] == whole.shape[1]:
            place = whole.at[rows, :]
        else:
            columns = pl.ds(pl.multiple_of(starts_ref[2 * i + 1], 128), piece.shape[1])
            place = whole.at[rows, columns]
        copies.append(pltpu.make_async_copy(piece, place, sems.at[i]))
        copies[-1].start()
    return copies


def wait(copies):
    for copy in copies:
        copy.wait()


IN_VMEM = pl.BlockSpec(memory_space=pltpu.VMEM)
IN_SMEM = pl.BlockSpec(memory_space=pltpu.SMEM)
ANYWHERE = pl.BlockSpec(memory_space=pl.ANY)


def upright(ref):
    return jnp.concatenate([jnp.transpose(ref[m]) for m in range(ref.shape[0])], axis=0)


def turn(chunk, cosine, sine):
    lane = lax.broadcasted_iota(jnp.int32, chunk.shape, 1)
    partner = jnp.where(
        lane % HEAD_SIZE < HALF_HEAD,
        pltpu.roll(chunk, 128 - HALF_HEAD, 1),
        pltpu.roll(chunk, HALF_HEAD, 1),
    )
    return chunk * cosine + partner * sine


def project_kernel(count, starts_ref, x_ref, gains_ref, cos_ref, sin_ref, *refs):
    pieces = refs[:count]
    q_ref, kv_ref, whole, sems = refs[count:]
    copies = load(pieces, starts_ref, whole, sems)
    x = upright(x_ref).astype(F32)
    width = x.shape[1]
    act = (x * rms_inverse(x) * gains_ref[0:1, :]).astype(BF)
    wait(copies)
    cosine, sine = cos_ref[...], sin_ref[...]
    for first in range(0, width + KV_WIDTH, 256):
        linear = nn(act, whole[:width, first : first + 256])
        for at in range(first, first + 256, 128):
            chunk = turn(linear[:, at - first : at - first + 128], cosine, sine)
            if at + 128 <= width:
                q_ref[:, at : at + 128] = (chunk * SCALE).astype(BF)
            elif at < width:
                q_ref[:, at:width] = (chunk[:, : width - at] * SCALE).astype(BF)
                kv_ref[:, : at + 128 - width] = chunk[:, width - at :].astype(BF)
            else:
                kv_ref[:, at - width : at - width + 128] = chunk.astype(BF)
    start = width // 128 * 128
    kv_ref[:, KV_WIDTH:] = nn(act, whole[width:, start:])[:, width - start :].astype(BF)


def project(x, gains, cosine, sine, pieces, starts, shape):
    micro, width, rows = x.shape
    tokens = micro * rows
    outs = (
        jax.ShapeDtypeStruct((tokens, width), BF),
        jax.ShapeDtypeStruct((tokens, 2 * KV_WIDTH), BF),
    )
    table = pl.BlockSpec((tokens, 128), lambda i: (0, 0))
    return pl.pallas_call(
        functools.partial(project_kernel, len(pieces)),
        grid=(1,),
        name="project",
        in_specs=[IN_SMEM] + [IN_VMEM] * 2 + [table] * 2 + [ANYWHERE] * len(pieces),
        out_specs=(IN_VMEM,) * 2,
        out_shape=outs,
        scratch_shapes=[pltpu.VMEM(shape, BF), pltpu.SemaphoreType.DMA((len(pieces),))],
        cost_estimate=cost(2 * tokens * width * (width + 2 * KV_WIDTH), 0, x, *outs, *pieces),
        compiler_params=pltpu.CompilerParams(vmem_limit_bytes=VMEM_LIMIT),
    )(starts, x, gains, cosine, sine, *pieces)


def across(ref):
    return jnp.concatenate([ref[m] for m in range(ref.shape[0])], axis=1)


def spread_out(value, ref):
    rows = ref.shape[2]
    for m in range(ref.shape[0]):
        ref[m] = value[:, m * rows : (m + 1) * rows]


def feed_kernel(counts, core_ref, s0_ref, s1_ref, s2_ref, x_ref, attn_ref, cot_ref, gains_ref, *refs):
    total_count = sum(counts)
    attention_pieces = refs[: counts[0]]
    pair_pieces = refs[counts[0] : counts[0] + counts[1]]
    down_pieces = refs[counts[0] + counts[1] : total_count]
    out_ref, inner_ref, kept_ref, given_ref, act_t_ref, attn_t_ref, resid_ref = refs[total_count : total_count + 7]
    w_attn, w_pair, w_down, sum_ref, sems0, sems1, sems2 = refs[total_count + 7 :]
    attention_copies = load(attention_pieces, s0_ref, w_attn, sems0)
    pair_copies = load(pair_pieces, s1_ref, w_pair, sems1)
    down_copies = load(down_pieces, s2_ref, w_down, sems2)
    width = x_ref.shape[1]
    hidden = w_pair.shape[1]
    tile = hidden // 5
    even = core_ref[0] == 0
    x = upright(x_ref).astype(F32)
    dy = upright(cot_ref)
    attn_t_ref[...] = jnp.transpose(attn_ref[...])
    wait(attention_copies)
    resid = x + nn(attn_ref[...], w_attn[width:, : rounded_up(width)])[:, :width]
    resid_t = jnp.transpose(resid)
    resid_ref[...] = resid_t
    sum_ref[...] = resid_t
    act = (resid * rms_inverse(resid) * gains_ref[1:2, :]).astype(BF)
    act_t_ref[...] = jnp.transpose(act)
    wait(pair_copies)
    wait(down_copies)
    for first in range(0, hidden, tile):
        here = slice(first, first + tile)
        gate = nn(act, w_pair[:width, here])
        upper = nn(act, w_pair[width:, here])
        d_inner = nn(dy, w_down[:, here])
        sigmoid = 1.0 / (1.0 + jnp.exp(-gate))
        silu = gate * sigmoid
        inner = (silu * upper).astype(BF)
        inner_ref[:, here] = inner
        d_gate = d_inner * upper * sigmoid * (1.0 + gate * (1.0 - sigmoid))
        d_upper = d_inner * silu
        kept_ref[:, here] = jnp.where(even, d_gate, d_upper).astype(BF)
        given_ref[:, here] = jnp.where(even, d_upper, d_gate).astype(BF)
        sum_ref[...] += nn(w_down[:, here], jnp.transpose(inner))
    spread_out(sum_ref[...].astype(BF), out_ref)


def feed(core, x, attn, dy, gains, attention_got, pair_got, down_got):
    micro, width, rows = x.shape
    tokens = micro * rows
    groups = [attention_got, pair_got, down_got]
    counts = [len(pieces) for pieces, _, _ in groups]
    shapes = [shape for _, _, shape in groups]
    hidden = shapes[1][1]
    outs = (jax.ShapeDtypeStruct(x.shape, BF),)
    outs += (jax.ShapeDtypeStruct((tokens, hidden), BF),) * 3
    outs += (jax.ShapeDtypeStruct((width, tokens), BF),) * 2
    outs += (jax.ShapeDtypeStruct((width, tokens), F32),)
    every = [piece for pieces, _, _ in groups for piece in pieces]
    return pl.pallas_call(
        functools.partial(feed_kernel, counts),
        name="feed",
        in_specs=[IN_SMEM] * 4 + [IN_VMEM] * 4 + [ANYWHERE] * len(every),
        out_specs=(IN_VMEM,) * 7,
        out_shape=outs,
        scratch_shapes=[pltpu.VMEM(shape, BF) for shape in shapes]
        + [pltpu.VMEM((width, tokens), F32)]
        + [pltpu.SemaphoreType.DMA((count,)) for count in counts],
        cost_estimate=cost(
            2 * tokens * width * (4 * hidden + width), tokens * hidden, x, x, x, *outs, *every
        ),
        compiler_params=pltpu.CompilerParams(vmem_limit_bytes=VMEM_MOST),
    )(core, *(starts for _, starts, _ in groups), x, attn, dy, gains, *every)


def feed_back_kernel(counts, core_ref, s0_ref, s1_ref, resid_ref, cot_ref, kept_ref, given_ref, gain_ref, *refs):
    total_count = sum(counts)
    dres_ref, low_ref, dattn_ref, w_attn, w_pair, sems0, sems1 = refs[total_count:]
    pair_copies = load(refs[counts[0] : total_count], s1_ref, w_pair, sems1)
    attention_copies = load(refs[: counts[0]], s0_ref, w_attn, sems0)
    width = resid_ref.shape[0]
    resid = resid_ref[...]
    root = lax.rsqrt(jnp.mean(resid * resid, axis=0, keepdims=True) + EPS)
    normed = resid * root
    wait(pair_copies)
    weight = lambda i: w_pair[pl.ds(pl.multiple_of(i * width, 16), width), :]
    d_act = nt(weight(core_ref[0]), kept_ref[...]) + nt(weight(1 - core_ref[0]), given_ref[...])
    d_normed = d_act * gain_ref[...]
    d_resid = across(cot_ref).astype(F32) + root * (
        d_normed - normed * jnp.mean(d_normed * normed, axis=0, keepdims=True)
    )
    dres_ref[...] = d_resid
    low = d_resid.astype(BF)
    low_ref[:, :width] = jnp.transpose(low)
    if low_ref.shape[1] > width:
        low_ref[:, width:] = jnp.zeros((low_ref.shape[0], low_ref.shape[1] - width), BF)
    wait(attention_copies)
    dattn_ref[...] = jnp.transpose(nn(w_attn[width:, :width], low).astype(BF))


def feed_back(core, resid, dy, kept, given, gain, attention_got, pair_got):
    width, tokens = resid.shape
    groups = [attention_got, pair_got]
    counts = [len(pieces) for pieces, _, _ in groups]
    shapes = [shape for _, _, shape in groups]
    outs = (
        jax.ShapeDtypeStruct((width, tokens), F32),
        jax.ShapeDtypeStruct((tokens, rounded_up(width)), BF),
        jax.ShapeDtypeStruct((tokens, width), BF),
    )
    every = [piece for pieces, _, _ in groups for piece in pieces]
    return pl.pallas_call(
        functools.partial(feed_back_kernel, counts),
        name="feed_back",
        in_specs=[IN_SMEM] * 3 + [IN_VMEM] * 5 + [ANYWHERE] * len(every),
        out_specs=(IN_VMEM,) * 3,
        out_shape=outs,
        scratch_shapes=[pltpu.VMEM(shape, BF) for shape in shapes]
        + [pltpu.SemaphoreType.DMA((count,)) for count in counts],
        cost_estimate=cost(
            2 * tokens * width * (2 * shapes[1][1] + width), 0, resid, dy, kept, given, *outs, *every
        ),
        compiler_params=pltpu.CompilerParams(vmem_limit_bytes=VMEM_MOST),
    )(core, *(starts for _, starts, _ in groups), resid, dy, kept, given, gain, *every)


def pick_rows(source, starts_ref, base, rows, count, target):
    for t in range(count):
        start = pl.multiple_of(starts_ref[base + t], 16)
        target[t * rows : (t + 1) * rows, :] = source[pl.ds(start, rows), :]


def down_grad_kernel(shards, cut, info_ref, cot_ref, far_cot_ref, inner_ref, far_inner_ref, low_ref, high_ref, dy):
    micro, width, rows = cot_ref.shape
    tokens, part = micro * rows, low_ref.shape[0] // (shards // 2)
    first = pl.multiple_of(info_ref[0], 16)
    for i, ref in enumerate((cot_ref, far_cot_ref)):
        for m in range(micro):
            at = i * tokens + m * rows
            dy[:, at : at + rows] = ref[m, pl.ds(first, part), :]
    for t in range(shards):
        columns = pl.ds(pl.multiple_of(info_ref[1 + t], 128), cut)
        made = nn(dy[:, :tokens], inner_ref[:, columns]) + nn(dy[:, tokens:], far_inner_ref[:, columns])
        out_ref, at = (low_ref, t) if t < shards // 2 else (high_ref, t - shards // 2)
        out_ref[at * part : (at + 1) * part, :] = made.astype(BF)


def down_grad(cot, far_cot, inner, far_inner, first, starts):
    shards, (micro, width, rows), (tokens, hidden) = len(starts), cot.shape, inner.shape
    part, cut = width // 2, hidden // shards
    outs = (jax.ShapeDtypeStruct((shards // 2 * part, cut), BF),) * 2
    if part % 16 or cut % 128:
        grad = nn(jnp.concatenate(list(cot), axis=1), inner) + nn(jnp.concatenate(list(far_cot), axis=1), far_inner)
        grad = lax.dynamic_slice_in_dim(grad.astype(BF), first, part, 0)
        blocks = [lax.dynamic_slice_in_dim(grad, start, cut, 1) for start in starts]
        return [jnp.concatenate(blocks[: shards // 2]), jnp.concatenate(blocks[shards // 2 :])]
    return pl.pallas_call(
        functools.partial(down_grad_kernel, shards, cut),
        name="down_grad",
        in_specs=[IN_SMEM] + [IN_VMEM] * 4,
        out_specs=(IN_VMEM,) * 2,
        out_shape=outs,
        scratch_shapes=[pltpu.VMEM((part, 2 * tokens), BF)],
        cost_estimate=cost(4 * part * tokens * hidden, 0, cot, cot, inner, inner, *outs),
        compiler_params=pltpu.CompilerParams(vmem_limit_bytes=VMEM_LIMIT),
    )(numbers([first] + starts), cot, far_cot, inner, far_inner)


def wide_grad_kernel(cuts, count, starts_ref, left_ref, far_left_ref, right_ref, far_right_ref, *refs):
    outs, ordered = refs[: 2 * len(cuts)], refs[2 * len(cuts)]
    tokens = left_ref.shape[1]

    @pl.when(pl.program_id(0) == 0)
    def _():
        at = first = 0
        for cut in cuts:
            for t in range(count):
                start = pl.multiple_of(starts_ref[t] + first, 16)
                ordered[at : at + cut, :tokens] = left_ref[pl.ds(start, cut), :]
                ordered[at : at + cut, tokens:] = far_left_ref[pl.ds(start, cut), :]
                at += cut
            first += cut

    made = nn(ordered[:, :tokens], right_ref[...]) + nn(ordered[:, tokens:], far_right_ref[...])
    at = 0
    for i, out_ref in enumerate(outs):
        size = out_ref.shape[0]
        out_ref[...] = made[at : at + size].astype(BF)
        at += size


def wide_grad(left, far_left, right, far_right, rows, cuts, starts):
    count, (tokens, columns) = len(starts), right.shape
    outs = tuple(jax.ShapeDtypeStruct((count // 2 * cut, columns), BF) for cut in cuts for _ in range(2))
    if rows % 16 or any(cut % 16 for cut in cuts):
        grad = (nn(left, right) + nn(far_left, far_right)).astype(BF)
        made, first = [], 0
        for cut in cuts:
            blocks = [lax.dynamic_slice_in_dim(grad, start + first, cut, 0) for start in starts]
            made += [jnp.concatenate(blocks[: count // 2]), jnp.concatenate(blocks[count // 2 :])]
            first += cut
        return made
    tile = 512 if columns % 512 == 0 else columns
    part = pl.BlockSpec((tokens, tile), lambda n, starts: (0, n))
    whole = pl.BlockSpec(left.shape, lambda n, starts: (0, 0))
    return pl.pallas_call(
        functools.partial(wide_grad_kernel, cuts, count),
        grid_spec=pltpu.PrefetchScalarGridSpec(
            num_scalar_prefetch=1,
            grid=(columns // tile,),
            in_specs=[whole, whole, part, part],
            out_specs=tuple(pl.BlockSpec((out.shape[0], tile), lambda n, starts: (0, n)) for out in outs),
            scratch_shapes=[pltpu.VMEM((count * rows, 2 * tokens), BF)],
        ),
        out_shape=outs,
        name="wide_grad",
        cost_estimate=cost(4 * tokens * rows * count * columns, 0, left, left, right, right, *outs),
        compiler_params=pltpu.CompilerParams(vmem_limit_bytes=VMEM_LIMIT),
    )(numbers(starts), left, far_left, right, far_right)


def settle_wide_kernel(cuts, core_ref, gain_ref, *refs):
    sums = refs[: 2 * len(cuts)]
    w_left, w_right, left_ref, right_ref, sum_ref = refs[2 * len(cuts) :]
    even = core_ref[0] == 0
    at = 0
    for c, cut in enumerate(cuts):
        here = slice(at, at + cut)
        mine, theirs = sums[2 * c][...].astype(F32), sums[2 * c + 1][...].astype(F32)
        left, right = jnp.where(even, mine, theirs), jnp.where(even, theirs, mine)
        left_ref[here, :], right_ref[here, :] = left, right
        both = w_left[here, :].astype(F32) * left + w_right[here, :].astype(F32) * right
        sum_ref[here, :] = jnp.sum(both, axis=1, keepdims=True) / gain_ref[here, :]
        at += cut


def settle_wide(core, gain, sums, cuts, w_left, w_right):
    out = jax.ShapeDtypeStruct(w_left.shape, F32)
    column = jax.ShapeDtypeStruct((w_left.shape[0], 1), F32)
    if any(cut % 16 for cut in cuts):
        pairs = [(mine.astype(F32), theirs.astype(F32)) for mine, theirs in sums]
        left = jnp.concatenate([jnp.where(core[0] == 0, a, b) for a, b in pairs])
        right = jnp.concatenate([jnp.where(core[0] == 0, b, a) for a, b in pairs])
        both = w_left.astype(F32) * left + w_right.astype(F32) * right
        return left, right, jnp.sum(both, axis=1, keepdims=True) / gain
    args = [value for pair in sums for value in pair]
    return pl.pallas_call(
        functools.partial(settle_wide_kernel, cuts),
        name="settle",
        in_specs=[IN_SMEM] + [IN_VMEM] * (3 + len(args)),
        out_specs=(IN_VMEM,) * 3,
        out_shape=(out, out, column),
        cost_estimate=cost(4 * w_left.size, 0, out, out, *args),
        compiler_params=pltpu.CompilerParams(vmem_limit_bytes=VMEM_LIMIT),
    )(core, gain, *args, w_left, w_right)


def turn_keys(source, target, at, cosine, sine):
    rows = source.shape[0]
    for first in range(0, KV_WIDTH, 128):
        chunk = turn(source[:, first : first + 128].astype(F32), cosine, -sine).astype(BF)
        last = min(first + 128, KV_WIDTH)
        target[at : at + rows, first:last] = chunk[:, : last - first]
    target[at : at + rows, KV_WIDTH:] = source[:, KV_WIDTH:]


def attention_grad_kernel(shards, half, starts_ref, gain_ref, cos_ref, sin_ref, dq_ref, attn_ref, low_ref, *refs):
    xs, halves = refs[:shards], refs[shards : shards + 2]
    dkvs = [ref.at[t] for ref in halves for t in range(shards // 2)]
    outs, (act, dkv, ordered, attn_ordered) = refs[shards + 2 : shards + 4], refs[shards + 4 :]
    micro, width, rows = xs[0].shape
    tokens = micro * rows
    wide = rounded_up(width)
    for t in range(shards):
        here = slice(t * tokens, (t + 1) * tokens)
        turn_keys(dkvs[t], dkv, t * tokens, cos_ref[here, :], sin_ref[here, :])
        for m in range(micro):
            x = xs[t][m].astype(F32)
            root = lax.rsqrt(jnp.mean(x * x, axis=0, keepdims=True) + EPS)
            first = t * tokens + m * rows
            act[:, first : first + rows] = (x * root * gain_ref[...]).astype(BF)
    for i, out_ref in enumerate(outs):
        pick_rows(act, starts_ref, i * shards, half, shards, ordered)
        pick_rows(attn_ref, starts_ref, i * shards, half, shards, attn_ordered)
        out_ref[:, :wide] = nn(ordered[:, :tokens], dq_ref[...]).astype(BF)
        out_ref[:, wide : 2 * wide] = nn(attn_ordered[...], low_ref[...]).astype(BF)
        out_ref[:, 2 * wide :] = nn(ordered[...], dkv[...]).astype(BF)


def attention_grad(x_all, gain, cosine, sine, dq, attn_t, low, dkv_all, half, given, kept):
    shards = len(x_all)
    micro, width, rows = x_all[0].shape
    every = shards * micro * rows
    wide = rounded_up(width)
    out = jax.ShapeDtypeStruct((shards * half, 2 * wide + 2 * KV_WIDTH), BF)
    if half % 16 or width // shards % 16:
        xs = jnp.concatenate([x[m] for x in x_all for m in range(micro)], axis=1).astype(F32)
        act = xs * lax.rsqrt(jnp.mean(xs * xs, axis=0, keepdims=True) + EPS) * gain
        act = act.astype(BF)
        dkv = jnp.concatenate(dkv_all, axis=0).reshape(every, 2 * KV_WIDTH)
        keys = dkv[:, :KV_WIDTH].astype(F32).reshape(every, -1, 2, HALF_HEAD)
        c, s = cosine[:, None, :HALF_HEAD], sine[:, None, HALF_HEAD:HEAD_SIZE]
        first, second = keys[:, :, 0], keys[:, :, 1]
        keys = jnp.stack([first * c + second * s, second * c - first * s], axis=2)
        dkv = jnp.concatenate([keys.reshape(every, KV_WIDTH).astype(BF), dkv[:, KV_WIDTH:]], axis=1)
        parts = [nn(act[:, : micro * rows], dq), nn(attn_t, low), nn(act, dkv)]
        grad = jnp.concatenate(parts, axis=1).astype(BF)
        return [
            jnp.concatenate([lax.dynamic_slice_in_dim(grad, start, half, 0) for start in starts])
            for starts in (given, kept)
        ]
    return pl.pallas_call(
        functools.partial(attention_grad_kernel, shards, half),
        name="attention_grad",
        in_specs=[IN_SMEM] + [IN_VMEM] * (8 + shards),
        out_specs=(IN_VMEM,) * 2,
        out_shape=(out, out),
        scratch_shapes=[
            pltpu.VMEM((width, every), BF),
            pltpu.VMEM((every, 2 * KV_WIDTH), BF),
            pltpu.VMEM((shards * half, every), BF),
            pltpu.VMEM((shards * half, micro * rows), BF),
        ],
        cost_estimate=cost(
            4 * shards * half * (every * 2 * KV_WIDTH + 2 * micro * rows * width),
            0,
            *x_all,
            *dkv_all,
            out,
            out,
        ),
        compiler_params=pltpu.CompilerParams(vmem_limit_bytes=VMEM_MOST),
    )(numbers(given + kept), gain, cosine, sine, dq, attn_t, low, *x_all, *dkv_all)


def finish_kernel(count, starts_ref, x_ref, low_ref, kv_ref, dres_ref, gain_ref, cos_ref, sin_ref, *refs):
    pieces = refs[:count]
    dx_ref, whole, kv_turned, sems = refs[count:]
    copies = load(pieces, starts_ref, whole, sems)
    turn_keys(kv_ref, kv_turned, 0, cos_ref[...], sin_ref[...])
    x = across(x_ref).astype(F32)
    width = x.shape[0]
    root = lax.rsqrt(jnp.mean(x * x, axis=0, keepdims=True) + EPS)
    normed = x * root
    wait(copies)
    d_act = nt(whole[:width, :width], low_ref[:, :width])
    d_act += nt(whole[:width, width:], kv_turned[:, :KV_WIDTH])
    d_act += nt(whole[width:, width:], kv_turned[:, KV_WIDTH:])
    d_normed = d_act * gain_ref[...]
    d_x = dres_ref[...] + root * (d_normed - normed * jnp.mean(d_normed * normed, axis=0, keepdims=True))
    spread_out(d_x.astype(BF), dx_ref)


def finish(x, low, kv, dres, gain, cosine, sine, pieces, starts, shape):
    micro, width, rows = x.shape
    tokens = micro * rows
    table = pl.BlockSpec((tokens, 128), lambda i: (0, 0))
    return pl.pallas_call(
        functools.partial(finish_kernel, len(pieces)),
        grid=(1,),
        name="finish",
        in_specs=[IN_SMEM] + [IN_VMEM] * 5 + [table] * 2 + [ANYWHERE] * len(pieces),
        out_specs=IN_VMEM,
        out_shape=jax.ShapeDtypeStruct(x.shape, BF),
        scratch_shapes=[
            pltpu.VMEM(shape, BF),
            pltpu.VMEM((tokens, 2 * KV_WIDTH), BF),
            pltpu.SemaphoreType.DMA((len(pieces),)),
        ],
        cost_estimate=cost(2 * tokens * width * (width + 2 * KV_WIDTH), 0, x, low, dres, *pieces),
        compiler_params=pltpu.CompilerParams(vmem_limit_bytes=VMEM_LIMIT),
    )(starts, x, low, kv, dres, gain, cosine, sine, *pieces)


def head(ref, h):
    return ref[:, h * HEAD_SIZE : (h + 1) * HEAD_SIZE]


def widen(value, columns):
    n = value.shape[0]
    lane = lax.broadcasted_iota(jnp.int32, (n, HEAD_SIZE), 1)
    tail = jnp.zeros((n, HEAD_SIZE), F32)
    for c, column in enumerate(columns):
        tail = jnp.where(lane == c, column, tail)
    return jnp.concatenate([value, tail.astype(BF)], axis=1)


def split(column):
    high = column.astype(BF).astype(F32)
    middle = (column - high).astype(BF).astype(F32)
    return [high, middle, column - high - middle]


def attend_kernel(shards, seg_rows, q_ref, *refs):
    kv = refs[:shards]
    bias_ref = refs[shards]
    o_ref, lse_ref = refs[-2:]
    rows = q_ref.shape[0]
    i = lax.broadcasted_iota(jnp.int32, (rows, rows), 0)
    j = lax.broadcasted_iota(jnp.int32, (rows, rows), 1)
    same = (i // seg_rows) == (j // seg_rows)
    own = jnp.where(j > i, CLOSED, jnp.where(same, 0.0, bias_ref[0:1, :]))
    one = jnp.ones((rows, 1), F32)
    bias_columns = jnp.transpose(bias_ref[...])
    lse = jnp.zeros((rows, 128), F32)
    lane = lax.broadcasted_iota(jnp.int32, (rows, 128), 1)
    for g in range(KEY_VALUE_HEADS):
        keys, values = [], []
        for t in range(shards):
            keys.append(widen(head(kv[t], g), [bias_columns[:, t : t + 1]] if t else []))
            values.append(widen(head(kv[t], KEY_VALUE_HEADS + g), [one]))
        for h in range(g * GROUP, g * GROUP + GROUP):
            q = widen(head(q_ref, h), [one])
            scores = [nt(q, k) for k in keys]
            scores[0] = scores[0] + own
            peak = functools.reduce(jnp.maximum, scores)
            peak = jnp.max(peak, axis=1, keepdims=True)
            terms = [nn(jnp.exp(s - peak).astype(BF), v) for s, v in zip(scores, values)]
            mixed = sum(terms[1:], terms[0])
            total = mixed[:, HEAD_SIZE : HEAD_SIZE + 1]
            o_ref[:, h * HEAD_SIZE : (h + 1) * HEAD_SIZE] = (mixed[:, :HEAD_SIZE] / total).astype(BF)
            lse = jnp.where(lane == h, peak + jnp.log(total), lse)
    lse_ref[...] = lse


def attend_back_kernel(shards, seg_rows, q_ref, *refs):
    kv = refs[:shards]
    bias_ref, o_ref, do_ref, lse_ref, cos_ref, sin_ref = refs[shards : shards + 6]
    dq_ref, low_ref, high_ref = refs[-3:]
    dkv = [ref.at[t] for ref in (low_ref, high_ref) for t in range(shards // 2)]
    rows = q_ref.shape[0]
    i = lax.broadcasted_iota(jnp.int32, (rows, rows), 1)
    j = lax.broadcasted_iota(jnp.int32, (rows, rows), 0)
    bias_columns = jnp.transpose(bias_ref[...])
    same = (i // seg_rows) == (j // seg_rows)
    own_column = jnp.broadcast_to(bias_columns[:, 0:1], (rows, rows))
    own = jnp.where(j > i, CLOSED, jnp.where(same, 0.0, own_column))
    one, zero = jnp.ones((rows, 1), F32), jnp.zeros((rows, 1), F32)
    cosine, sine = cos_ref[...], sin_ref[...]
    if dq_ref.shape[1] > QUERY_HEADS * HEAD_SIZE:
        dq_ref[:, QUERY_HEADS * HEAD_SIZE :] = jnp.zeros((rows, dq_ref.shape[1] - QUERY_HEADS * HEAD_SIZE), BF)
    for g in range(KEY_VALUE_HEADS):
        keys, values, turned = [], [], []
        for t in range(shards):
            k = head(kv[t], g)
            turned.append(jnp.transpose(k))
            keys.append(widen(k, [bias_columns[:, t : t + 1] if t else zero, one, one, one]))
            values.append(widen(head(kv[t], KEY_VALUE_HEADS + g), [one, one, one]))
        dk, dv = [None] * shards, [None] * shards
        for h in range(g * GROUP, g * GROUP + GROUP):
            q, do = head(q_ref, h), head(do_ref, h)
            centre = jnp.sum(head(o_ref, h).astype(F32) * do.astype(F32), axis=1, keepdims=True)
            q_wide = widen(q, [one] + split(-lse_ref[:, h : h + 1]))
            do_wide = widen(do, split(-centre))
            dq = None
            for t in range(shards):
                scores = nt(keys[t], q_wide)
                if t == 0:
                    scores = scores + own
                probs = jnp.exp(scores)
                ds = (probs * nt(values[t], do_wide)).astype(BF)
                v_term = nn(probs.astype(BF), do)
                k_term = nn(ds, q)
                q_term = nn(turned[t], ds)
                dv[t] = v_term if dv[t] is None else dv[t] + v_term
                dk[t] = k_term if dk[t] is None else dk[t] + k_term
                dq = q_term if dq is None else dq + q_term
            dq = dq * SCALE
            first, second = dq[:HALF_HEAD], dq[HALF_HEAD:]
            back = jnp.concatenate(
                [first * cosine + second * sine, second * cosine - first * sine], axis=0
            )
            dq_ref[:, h * HEAD_SIZE : (h + 1) * HEAD_SIZE] = jnp.transpose(back.astype(BF))
        for t in range(shards):
            dkv[t][:, g * HEAD_SIZE : (g + 1) * HEAD_SIZE] = dk[t].astype(BF)
            g_value = KEY_VALUE_HEADS + g
            dkv[t][:, g_value * HEAD_SIZE : (g_value + 1) * HEAD_SIZE] = dv[t].astype(BF)


def attend(micro, seg_rows, q, kv, bias):
    shards, tokens, width = len(kv), q.shape[0], q.shape[1]
    rows = tokens // micro
    here = lambda w: pl.BlockSpec((rows, w), lambda m: (m, 0))
    outs = (jax.ShapeDtypeStruct((tokens, width), BF), jax.ShapeDtypeStruct((tokens, 128), F32))
    pairs = tokens * rows * shards * QUERY_HEADS
    return pl.pallas_call(
        functools.partial(attend_kernel, shards, seg_rows),
        grid=(micro,),
        name="attend",
        in_specs=[here(width)]
        + [here(2 * KV_WIDTH)] * shards
        + [pl.BlockSpec((None,) + bias.shape[1:], lambda m: (m, 0, 0))],
        out_specs=(here(width), here(128)),
        out_shape=outs,
        cost_estimate=cost(16 * HEAD_SIZE * pairs, pairs, q),
        compiler_params=pltpu.CompilerParams(vmem_limit_bytes=VMEM_LIMIT),
    )(q, *kv, bias)


def attend_back(m, rows, seg_rows, q, kv, bias, o, do, lse, cosine, sine, earlier):
    shards, tokens, width = len(kv), q.shape[0], q.shape[1]
    here = lambda w: pl.BlockSpec((rows, w), lambda i: (m, 0))
    turned = pl.BlockSpec((HALF_HEAD, rows), lambda i: (0, m))
    outs = (jax.ShapeDtypeStruct((tokens, rounded_up(width)), BF),)
    outs += (jax.ShapeDtypeStruct((shards // 2, tokens, 2 * KV_WIDTH), BF),) * 2
    pieces = pl.BlockSpec((shards // 2, rows, 2 * KV_WIDTH), lambda i: (0, m, 0))
    pairs = rows * rows * shards * QUERY_HEADS
    return pl.pallas_call(
        functools.partial(attend_back_kernel, shards, seg_rows),
        grid=(1,),
        name="attend_back",
        in_specs=[here(width)]
        + [here(2 * KV_WIDTH)] * shards
        + [pl.BlockSpec((None,) + bias.shape[1:], lambda i: (m, 0, 0))]
        + [here(width), here(width), here(128), turned, turned]
        + [pl.BlockSpec(memory_space=pl.ANY)] * len(earlier),
        out_specs=(here(rounded_up(width)), pieces, pieces),
        out_shape=outs,
        input_output_aliases={shards + 7 + i: i for i in range(len(earlier))},
        cost_estimate=cost(40 * HEAD_SIZE * pairs, pairs, q),
        compiler_params=pltpu.CompilerParams(vmem_limit_bytes=VMEM_LIMIT),
    )(q, *kv, bias, o, do, lse, cosine, sine, *earlier)


def local(
    block_input,
    parent_ids,
    w_query,
    key_weight,
    value_weight,
    w_output,
    w_gate,
    w_up,
    w_down,
    norm_first,
    norm_second,
    out_cotangent,
):
    micro, rows, width = block_input.shape
    shards = lax.axis_size("shard")
    links = Links(lax.axis_size("rep"), shards)
    tree = rows * shards
    segs = parent_ids.shape[2]
    seg_rows = tree // segs
    tokens = micro * rows
    hidden = w_gate.shape[1]

    inputs = block_input.swapaxes(1, 2)
    cotangent = out_cotangent.swapaxes(1, 2)

    even = links.core == 0
    side = lax.axis_index("rep") // 2 % 2
    left = jnp.concatenate([w_query, key_weight], axis=1)
    right = jnp.concatenate([w_output, value_weight], axis=1)
    attn_mine = jnp.where(even, left, right)
    pair_cut = hidden // 2
    pair_mine = lax.dynamic_slice_in_dim(jnp.where(even, w_gate, w_up), side * pair_cut, pair_cut, 1)
    down_own = w_down.T
    down_cut = width // 2
    down_mine = lax.dynamic_slice_in_dim(down_own, links.core * down_cut, down_cut, 0)
    core = numbers([links.core])

    attn_near = links.near(attn_mine)
    gain_pieces = links.small_pieces(jnp.stack([norm_first, norm_second]))
    attn_mine, attn_near, gain_pieces, pair_mine, down_mine = meet(
        attn_mine, attn_near, gain_pieces, pair_mine, down_mine
    )

    gains = links.in_order(gain_pieces).astype(F32)
    attn_all = links.far(attn_mine, attn_near)
    attn_swapped = {t: links.swap(attn_near[t]) for t in attn_near}
    pair_near = {1: links.step(pair_mine, 0)}
    parents = parent_ids[:, 0]
    seg = jnp.arange(segs)
    after_parent = jnp.concatenate([parents[:, 1:], jnp.full((micro, 1), -1, parents.dtype)], axis=1)
    on_path = (seg % 2 == 0)[None] | (after_parent == seg[None])
    below = (seg[None, :] < seg[:, None])[None]
    depth = jnp.sum(jnp.where(below, on_path.astype(F32)[:, None, :], 0.0), axis=-1)

    def row_numbers(hop):
        return (links.shard ^ hop) * rows + jnp.arange(rows)

    def pick(table, numbers):
        hit = (numbers // seg_rows)[..., None] == seg
        return jnp.sum(jnp.where(hit[None], table.reshape(micro, *(1,) * numbers.ndim, segs), 0), axis=-1)

    key_rows = jnp.stack([row_numbers(hop) for hop in links.hops])
    positions = pick(depth, key_rows) * seg_rows + (key_rows % seg_rows).astype(F32)
    freqs = jnp.exp(-math.log(10000.0) * jnp.arange(HALF_HEAD, dtype=F32) * (2.0 / HEAD_SIZE))
    angles = freqs[:, None] * positions.swapaxes(0, 1).reshape(1, shards * tokens)
    cosine_t, sine_t = jnp.cos(angles), jnp.sin(angles)
    cosine = jnp.tile(cosine_t.T, (1, 4))
    sine = jnp.tile(jnp.concatenate([-sine_t.T, sine_t.T], axis=1), (1, 2))
    open_key = (pick(on_path.astype(F32), key_rows) > 0.5) & (
        (key_rows < links.shard * rows) | (jnp.arange(shards) == 0)[:, None]
    )
    bias = jnp.where(open_key, 0.0, CLOSED)
    bias = jnp.pad(bias, ((0, 0), (0, 8 - shards), (0, 0)))

    gain_one, gain_two = gains[0][:, None], gains[1][:, None]
    tables = (cosine, sine, cosine_t, sine_t, bias, gains, gain_one, gain_two)
    attn_all, attn_swapped, pair_mine, pair_near, down_mine, tables = meet(
        attn_all, attn_swapped, pair_mine, pair_near, down_mine, tables
    )
    cosine, sine, cosine_t, sine_t, bias, gains, gain_one, gain_two = tables

    for t in range(1, shards):
        if t not in attn_swapped:
            attn_swapped[t] = links.swap(attn_all[t])
    shard_rows = width // shards

    def pair_place(weight, hop):
        return weight * width + (links.shard ^ hop) * shard_rows

    pieces, starts = [left, right], [(pair_place(0, 0), 0), (pair_place(1, 0), 0)]
    for t in range(1, shards):
        pieces += [attn_all[t], attn_swapped[t]]
        starts += [
            (pair_place(links.core, links.hops[t]), 0),
            (pair_place(1 - links.core, links.hops[links.twin(t)]), 0),
        ]
    attention_got = joined(pieces, starts, (2 * width, left.shape[1]))
    pair_near |= {1 << i: links.step(pair_mine, i) for i in range(1, links.bits)}
    pair_beside = {1: links.beside(pair_near[1])}
    down_near = {1: links.step(down_mine, 0)}
    queries, kv = project(inputs, gains, cosine, sine, *attention_got)
    queries, kv, pair_mine, pair_near, pair_beside, down_mine, down_near = meet(
        queries, kv, pair_mine, pair_near, pair_beside, down_mine, down_near
    )

    kv_near = links.near(kv)
    pair_beside |= {t: links.beside(pair_near[t]) for t in pair_near if t > 1}
    kv_near, kv, pair_beside, pair_near, pair_mine = meet(kv_near, kv, pair_beside, pair_near, pair_mine)

    kv_all = links.far(kv, kv_near)
    pair_all = links.far(pair_mine, pair_near)
    pair_swapped = {t: links.swap(pair_near[t]) for t in pair_near}
    pair_crossed = {t: links.swap(pair_beside[t]) for t in pair_beside}
    kv_all, pair_all, pair_swapped, pair_crossed, pair_beside, down_mine, down_near = meet(
        kv_all, pair_all, pair_swapped, pair_crossed, pair_beside, down_mine, down_near
    )

    down_near |= {1 << i: links.step(down_mine, i) for i in range(1, links.bits)}
    down_all = links.far(down_mine, down_near)
    pair_beside |= {t: links.beside(pair_all[t]) for t in range(1, shards) if t not in pair_beside}
    attn, lse = attend(micro, seg_rows, queries, kv_all, bias)
    pair_swapped |= {t: links.swap(pair_all[t]) for t in range(1, shards) if t not in pair_swapped}
    attn, lse, down_all, pair_beside, pair_all, pair_swapped = meet(
        attn, lse, down_all, pair_beside, pair_all, pair_swapped
    )

    pair_crossed |= {t: links.swap(pair_beside[t]) for t in range(1, shards) if t not in pair_crossed}
    down_swapped = [None] + [links.swap(down_all[t]) for t in range(1, shards)]
    pieces, starts = [w_gate, w_up], [(pair_place(0, 0), 0), (pair_place(1, 0), 0)]
    for t in range(1, shards):
        pieces += [pair_all[t], pair_beside[t], pair_swapped[t], pair_crossed[t]]
        for row in (
            pair_place(links.core, links.hops[t]),
            pair_place(1 - links.core, links.hops[links.twin(t)]),
        ):
            starts += [(row, side * pair_cut), (row, (1 - side) * pair_cut)]
    pair_got = joined(pieces, starts, (2 * width, hidden))
    own = w_down.shape[0]
    pieces, starts = [down_own], [(0, links.shard * own)]
    for t in range(1, shards):
        pieces += [down_all[t], down_swapped[t]]
        starts += [
            (links.core * down_cut, (links.shard ^ links.hops[t]) * own),
            ((1 - links.core) * down_cut, (links.shard ^ links.hops[links.twin(t)]) * own),
        ]
    down_got = joined(pieces, starts, (width, own * shards))
    attn, pair_pieces, down_pieces = meet(attn, pair_got[0], down_got[0])
    pair_got, down_got = (pair_pieces, *pair_got[1:]), (down_pieces, *down_got[1:])

    plan = Plan()
    have = lambda *names: [plan.have[name] for name in names]
    x_near = links.near(inputs)
    far_cotangent = links.swap(cotangent)
    made = feed(core, inputs, attn, cotangent, gains, attention_got, pair_got, down_got)
    names = ("out", "inner", "kept", "given", "act", "attn_t", "resid")
    plan.have = dict(zip(names, made)) | {"x_near": x_near, "far_dy": far_cotangent, "queries": queries, "kv": kv_all, "lse": lse, "attn": attn}
    plan.close()

    half, mine, theirs = links.half_rows(shard_rows)
    some_kept, some_given = links.order(shard_rows, mine, theirs)
    cuts = (-(-shard_rows // 32) * 16, shard_rows - -(-shard_rows // 32) * 16)

    plan.have["x_all"] = links.far(inputs, plan.have.pop("x_near"))
    for name in ("inner", "act", "given"):
        plan.have["far_" + name] = links.swap(plan.have[name])
    names = ("d_resid", "low", "d_attn")
    resid, kept, given = have("resid", "kept", "given")
    plan.have |= dict(zip(names, feed_back(core, resid, cotangent, kept, given, gain_two, attention_got, pair_got)))
    plan.close()

    names = ("down.low", "down.high")
    far_dy, inner, far_inner = have("far_dy", "inner", "far_inner")
    starts = [(links.shard ^ hop) * own for hop in links.hops]
    plan.have |= dict(zip(names, down_grad(cotangent, far_dy, inner, far_inner, links.core * down_cut, starts)))
    plan.close()

    for name in ("down", "wide0", "wide1", "some"):
        plan.start(name, links.reduce(plan, name, name == "some"))
    plan.advance("down")
    names = ("wide0.low", "wide0.high", "wide1.low", "wide1.high")
    act, far_act, kept, far_kept = have("act", "far_act", "kept", "far_given")
    starts = [(links.shard ^ hop) * shard_rows for hop in links.hops]
    plan.have |= dict(zip(names, wide_grad(act, far_act, kept, far_kept, shard_rows, cuts, starts)))
    plan.close()

    made = ()
    hops = [("down", "wide0"), ("down", "wide0", "wide1")]
    for m in range(micro):
        plan.advance(*hops[min(m, 1)])
        q, kv_now, o, do, lse_now = have("queries", "kv", "attn", "d_attn", "lse")
        made = attend_back(m, rows, seg_rows, q, kv_now, bias, o, do, lse_now, cosine_t, sine_t, made)
        plan.have["attn_grads"] = made = tuple(made)
        plan.close()
        made = plan.have["attn_grads"]

    d_queries, *d_kv = plan.have.pop("attn_grads")
    plan.have["dkv.pieces"] = d_kv
    plan.have["d_queries"] = d_queries
    plan.start("dkv", links.collect(plan, "dkv"))
    plan.advance("dkv", "wide0", "wide1", "down")
    given, kept = attention_grad(
        plan.have["x_all"],
        gain_one,
        cosine,
        sine,
        d_queries,
        *have("attn_t", "low"),
        d_kv,
        half,
        some_given,
        some_kept,
    )
    plan.have["some.given"], plan.have["some.kept"] = given, kept
    plan.close()

    def gain_grad(gain, *pairs):
        sums = sum(jnp.sum(weight.astype(F32) * grad, axis=1) for weight, grad in pairs)
        return sums / gain.astype(F32)

    def settle():
        have, done = plan.have, plan.have.setdefault("done", {})
        if "dkv" in have and "d_input" not in done:
            done["d_input"] = finish(
                inputs, have["d_queries"], have["dkv"], have["d_resid"], gain_one, cosine, sine, *attention_got
            )
        if "down" in have and "down" not in done:
            done["down"] = links.finish_rows(*have["down"], width).T
        if "wide0" in have and "wide1" in have and "gate" not in done:
            done["gate"], done["upper"], gain = settle_wide(
                core,
                norm_second.astype(F32)[:, None],
                (have["wide0"], have["wide1"]),
                cuts,
                w_gate,
                w_up,
            )
            done["gain_two"] = gain[:, 0]
        if "some" in have and "query" not in done:
            grad = links.finish_rows(*have["some"], shard_rows)
            first = rounded_up(width)
            done["query"], done["output"] = grad[:, :width], grad[:, first : first + width]
            done["key"], done["value"] = jnp.split(grad[:, 2 * first :], 2, axis=1)
            done["gain_one"] = gain_grad(
                norm_first,
                (w_query, done["query"]),
                (key_weight, done["key"]),
                (value_weight, done["value"]),
            )

    order = []
    while plan.tasks:
        plan.advance(*(order.pop(0) if order else tuple(plan.tasks)))
        settle()
        if plan.tasks:
            plan.close()

    done = plan.have["done"]
    return (
        plan.have["out"].swapaxes(1, 2),
        done["d_input"].swapaxes(1, 2),
        *(done[name] for name in ("query", "key", "value", "output", "gate", "upper", "down")),
        done["gain_one"],
        done["gain_two"],
    )


def solution(mesh):
    rows = P(None, AXES, None)
    weight, gain = P("shard", None), P("shard")
    return jax.shard_map(
        local,
        mesh=mesh,
        in_specs=(rows, P(None, "rep", None)) + (weight,) * 7 + (gain, gain, rows),
        out_specs=(rows, rows) + (weight,) * 7 + (gain, gain),
        check_vma=False,
    )
```

```python
import functools
import math

import jax
import jax.numpy as jnp
from jax import lax
from jax.experimental import pallas as pl
from jax.experimental.pallas import tpu as pltpu
from jax.sharding import PartitionSpec as P

QUERY_HEADS = 15
KEY_VALUE_HEADS = 5
HEAD_SIZE = 64
HALF_HEAD = HEAD_SIZE // 2
GROUP = QUERY_HEADS // KEY_VALUE_HEADS
KV_WIDTH = KEY_VALUE_HEADS * HEAD_SIZE
SCALE = HEAD_SIZE ** (-0.5)
EPS = 1e-05
AXES = ("rep", "shard")
BF = jnp.bfloat16
F32 = jnp.float32
CLOSED = -1e30
VMEM_LIMIT = 48 << 20
VMEM_MOST = 60 << 20


def dot(a, b, dims):
    return lax.dot_general(a, b, (dims, ((), ())), preferred_element_type=F32)


def nn(a, b):
    return dot(a, b, ((1,), (0,)))


def nt(a, b):
    return dot(a, b, ((1,), (1,)))


def tn(a, b):
    return dot(a, b, ((0,), (0,)))


def total(parts):
    return sum(part.astype(F32) for part in parts).astype(parts[0].dtype)


def meet(*values):
    return lax.optimization_barrier(values)


def rounded_up(columns):
    return -(-columns // 128) * 128


def rms_inverse(x):
    return lax.rsqrt(jnp.mean(x * x, axis=-1, keepdims=True) + EPS)


def cost(flops, exps, *arrays):
    size = sum(a.size * a.dtype.itemsize for a in arrays)
    return pl.CostEstimate(flops=flops, transcendentals=exps, bytes_accessed=size)


class Links:
    def __init__(self, reps, shards):
        self.reps, self.shards = reps, shards
        self.core = lax.axis_index("rep") % 2
        self.shard = lax.axis_index("shard")
        self.bits = shards.bit_length() - 1
        even = [1 << i for i in range(self.bits)]
        odd = even[:2][::-1] + even[2:]
        self.steps = list(zip(even, odd))
        self.hops = []
        for piece in range(shards):
            sums = [0, 0]
            for i, step in enumerate(self.steps):
                if piece >> i & 1:
                    sums = [sums[0] ^ step[0], sums[1] ^ step[1]]
            self.hops.append(jnp.where(self.core == 0, sums[0], sums[1]))

    def move(self, value, target):
        pairs = []
        for r in range(self.reps):
            for s in range(self.shards):
                goal = target(r, s)
                if goal is not None:
                    pairs.append((r * self.shards + s, goal[0] * self.shards + goal[1]))
        return lax.ppermute(value, AXES, pairs)

    def step(self, value, i):
        return self.move(value, lambda r, s: (r, s ^ self.steps[i][r % 2]))

    def swap(self, value):
        return self.move(value, lambda r, s: (r ^ 1, s))

    def reduce(self, plan, name, quick=False):
        top = self.bits
        if name + ".given" in plan.have:
            got = yield self.swap(plan.have.pop(name + ".given"))
            sums = [plan.have.pop(name + ".kept"), got]
        else:
            got = yield self.step(plan.have.pop(name + ".high"), top - 1)
            sums = [plan.have.pop(name + ".low"), got]
            top -= 1
        for i in reversed(range(top)):
            block = sums[0].shape[0] // 2
            got = yield self.step(total([part[block:] for part in sums]), i)
            sums = [part[:block] for part in sums] + [got]
        value = total(sums)
        chips = self.reps // 2
        place = lax.axis_index("rep") // 2
        span = 1
        if chips % 4 == 0 and quick and value.shape[0] % 4 == 0:
            quarter = value.shape[0] // 4
            across = lambda value, j: self.move(value, lambda r, s: (r ^ (2 * j), s))
            cut = lambda j: lax.dynamic_slice_in_dim(value, (place % 4 ^ j) * quarter, quarter, 0)
            got = yield [across(cut(j), j) for j in range(1, 4)]
            mine = total([cut(0)] + got)
            got = yield [across(mine, j) for j in range(1, 4)]
            parts = jnp.stack([mine] + got).reshape(2, 2, quarter, -1)
            parts = jnp.where(place % 4 >= 2, parts[::-1], parts)
            parts = jnp.where(place % 2 == 1, parts[:, ::-1], parts)
            value = parts.reshape(4 * quarter, -1)
            span = 4
        elif chips % 4 == 0:
            inward, outward, middle = {0: 1, 3: 2}, {1: 0, 2: 3}, {1: 2, 2: 1}

            def along(value, table):
                def target(r, s):
                    chip = r // 2
                    if chip % 4 not in table:
                        return None
                    return ((chip - chip % 4 + table[chip % 4]) * 2 + r % 2, s)

                return self.move(value, target)

            value = total([value, (yield along(value, inward))])
            value = total([value, (yield along(value, middle))])
            back = yield along(value, outward)
            inner = (place % 4 == 1) | (place % 4 == 2)
            value = jnp.where(inner, value, back)
            span = 4
        while span < chips:
            value = total([value, self.move(value, lambda r, s: (r ^ (2 * span), s))])
            span *= 2
        other = yield self.swap(value)
        plan.have[name] = (value, other)

    def collect(self, plan, name):
        low, high = plan.have[name + ".pieces"]
        got = yield self.step(high, self.bits - 1)
        sums = [low, got]
        for i in reversed(range(self.bits - 1)):
            block = sums[0].shape[0] // 2
            got = yield self.step(total([part[block:] for part in sums]), i)
            sums = [part[:block] for part in sums] + [got]
        plan.have[name] = total(sums)[0]

    def beside(self, value):
        return self.move(value, lambda r, s: (r ^ 2, s))

    def near(self, value):
        return {1 << i: self.step(value, i) for i in range(self.bits)}

    def far(self, value, near):
        pieces = [value]
        for t in range(1, self.shards):
            top = t.bit_length() - 1
            pieces.append(near[t] if t in near else self.step(pieces[t - (1 << top)], top))
        return pieces

    def twin(self, piece):
        return piece if self.bits < 2 else piece >> 2 << 2 | (piece & 1) << 1 | (piece >> 1 & 1)

    def small_pieces(self, value):
        return [
            value if hop == 0 else self.move(value, lambda r, s, hop=hop: (r, s ^ hop))
            for hop in range(self.shards)
        ]

    def in_order(self, pieces):
        pieces = jnp.stack(pieces)
        value = pieces
        order = self.shard ^ jnp.arange(self.shards)
        hit = (order[:, None] == jnp.arange(self.shards)[None, :])[:, :, None, None]
        pieces = jnp.sum(jnp.where(hit, pieces[None], 0), axis=1, dtype=value.dtype)
        return jnp.concatenate([pieces[j] for j in range(self.shards)], axis=-1)

    def half_rows(self, rows):
        half = -(-rows // 32) * 16
        return half, self.core * (rows - half), (1 - self.core) * (rows - half)

    def order(self, scale, mine, theirs):
        kept = [(self.shard ^ hop) * scale + mine for hop in self.hops]
        given = [(self.shard ^ self.hops[self.twin(t)]) * scale + theirs for t in range(self.shards)]
        return kept, given

    def finish_rows(self, owned, other, rows):
        low = jnp.where(self.core == 0, owned, other)
        high = jnp.where(self.core == 0, other, owned)
        return jnp.concatenate([low[: rows - owned.shape[0]], high], axis=0).astype(F32)


class Plan:
    def __init__(self):
        self.have, self.tasks, self.made = {}, {}, {}

    def start(self, name, task):
        self.tasks[name] = task
        self.made[name] = None

    def advance(self, *names):
        for name in names:
            if name in self.tasks:
                try:
                    self.made[name] = self.tasks[name].send(self.made[name])
                except StopIteration:
                    del self.tasks[name], self.made[name]

    def close(self):
        self.have, self.made = lax.optimization_barrier((self.have, self.made))


def joined(pieces, starts, shape):
    if any(piece.shape[0] % 16 or piece.shape[1] % 128 and piece.shape[1] < shape[1] for piece in pieces):
        whole = jnp.zeros(shape, pieces[0].dtype)
        for piece, start in zip(pieces, starts):
            whole = lax.dynamic_update_slice(whole, piece, start)
        pieces, starts = (whole,), [(0, 0)]
    return tuple(pieces), numbers([at for start in starts for at in start]), shape


def numbers(values):
    return jnp.stack([jnp.asarray(value, jnp.int32) for value in values])


def load(pieces, starts_ref, whole, sems):
    copies = copies_of(pieces, starts_ref, whole, sems, 0)
    for _, copy in copies:
        copy.start()
    return lambda: [copy.wait() for _, copy in copies]


def copies_of(pieces, starts_ref, whole, sems, row):
    copies = []
    for i, piece in enumerate(pieces):
        rows = pl.ds(pl.multiple_of(starts_ref[2 * i] - row, 16), piece.shape[0])
        if piece.shape[1] == whole.shape[1]:
            place = whole.at[rows, :]
        else:
            columns = pl.ds(pl.multiple_of(starts_ref[2 * i + 1], 128), piece.shape[1])
            place = whole.at[rows, columns]
        copies.append((i, pltpu.make_async_copy(piece, place, sems.at[i])))
    return copies


def load_lower(pieces, starts_ref, whole, sems, row):
    if pieces[0].shape[0] > row:
        copy = pltpu.make_async_copy(pieces[0].at[row:, :], whole, sems.at[0])
        copy.start()
        return copy.wait
    copies = copies_of(pieces, starts_ref, whole, sems, row)

    def each(act):
        for i, copy in copies:
            pl.when(starts_ref[2 * i] >= row)(functools.partial(act, copy))

    each(lambda copy: copy.start())
    return lambda: each(lambda copy: copy.wait())


def load_halves(pieces, starts_ref, whole, sems):
    half = whole.shape[1] // 2
    copies = []
    for i, piece in enumerate(pieces):
        rows = pl.ds(pl.multiple_of(starts_ref[2 * i], 16), piece.shape[0])
        for h in range(2):
            columns = slice(h * half, (h + 1) * half)
            source = piece.at[:, columns] if piece.shape[1] > half else piece
            copy = pltpu.make_async_copy(source, whole.at[rows, columns], sems.at[i, h])
            copies.append((h, None if piece.shape[1] > half else starts_ref[2 * i + 1] == h * half, copy))

    def each(h, act):
        for at, there, copy in copies:
            if at == h and there is None:
                act(copy)
            elif at == h:
                pl.when(there)(functools.partial(act, copy))

    return lambda h: each(h, lambda copy: copy.start()), lambda h: each(h, lambda copy: copy.wait())


IN_VMEM = pl.BlockSpec(memory_space=pltpu.VMEM)
IN_SMEM = pl.BlockSpec(memory_space=pltpu.SMEM)
ANYWHERE = pl.BlockSpec(memory_space=pl.ANY)


def upright(ref):
    return jnp.concatenate([jnp.transpose(ref[m]) for m in range(ref.shape[0])], axis=0)


def turn(chunk, cosine, sine):
    lane = lax.broadcasted_iota(jnp.int32, chunk.shape, 1)
    partner = jnp.where(
        lane % HEAD_SIZE < HALF_HEAD,
        pltpu.roll(chunk, 128 - HALF_HEAD, 1),
        pltpu.roll(chunk, HALF_HEAD, 1),
    )
    return chunk * cosine + partner * sine


def project_kernel(count, starts_ref, x_ref, gains_ref, cos_ref, sin_ref, *refs):
    pieces = refs[:count]
    q_ref, kv_ref, whole, sems = refs[count:]
    wait = load(pieces, starts_ref, whole, sems)
    x = upright(x_ref).astype(F32)
    width = x.shape[1]
    act = (x * rms_inverse(x) * gains_ref[0:1, :]).astype(BF)
    wait()
    cosine, sine = cos_ref[...], sin_ref[...]
    for first in range(0, width + KV_WIDTH, 256):
        linear = nn(act, whole[:width, first : first + 256])
        for at in range(first, first + 256, 128):
            chunk = turn(linear[:, at - first : at - first + 128], cosine, sine)
            if at + 128 <= width:
                q_ref[:, at : at + 128] = (chunk * SCALE).astype(BF)
            elif at < width:
                q_ref[:, at:width] = (chunk[:, : width - at] * SCALE).astype(BF)
                kv_ref[:, : at + 128 - width] = chunk[:, width - at :].astype(BF)
            else:
                kv_ref[:, at - width : at - width + 128] = chunk.astype(BF)
    start = width // 128 * 128
    kv_ref[:, KV_WIDTH:] = nn(act, whole[width:, start:])[:, width - start :].astype(BF)


def project(x, gains, cosine, sine, pieces, starts, shape):
    micro, width, rows = x.shape
    tokens = micro * rows
    outs = (
        jax.ShapeDtypeStruct((tokens, width), BF),
        jax.ShapeDtypeStruct((tokens, 2 * KV_WIDTH), BF),
    )
    table = pl.BlockSpec((tokens, 128), lambda i: (0, 0))
    return pl.pallas_call(
        functools.partial(project_kernel, len(pieces)),
        grid=(1,),
        name="project",
        in_specs=[IN_SMEM] + [IN_VMEM] * 2 + [table] * 2 + [ANYWHERE] * len(pieces),
        out_specs=(IN_VMEM,) * 2,
        out_shape=outs,
        scratch_shapes=[pltpu.VMEM(shape, BF), pltpu.SemaphoreType.DMA((len(pieces),))],
        cost_estimate=cost(2 * tokens * width * (width + 2 * KV_WIDTH), 0, x, *outs, *pieces),
        compiler_params=pltpu.CompilerParams(vmem_limit_bytes=VMEM_LIMIT),
    )(starts, x, gains, cosine, sine, *pieces)


def across(ref):
    return jnp.concatenate([ref[m] for m in range(ref.shape[0])], axis=1)


def spread_out(value, ref):
    rows = ref.shape[2]
    for m in range(ref.shape[0]):
        ref[m] = value[:, m * rows : (m + 1) * rows]


def feed_kernel(counts, core_ref, s0_ref, s1_ref, s2_ref, x_ref, attn_ref, cot_ref, gains_ref, *refs):
    total_count = sum(counts)
    attention_pieces = refs[: counts[0]]
    pair_pieces = refs[counts[0] : counts[0] + counts[1]]
    down_pieces = refs[counts[0] + counts[1] : total_count]
    out_ref, inner_ref, kept_ref, given_ref, act_t_ref, attn_t_ref, resid_ref = refs[total_count : total_count + 7]
    w_attn, w_pair, w_down, sum_ref, sems0, sems1, sems2 = refs[total_count + 7 :]
    width = x_ref.shape[1]
    hidden = w_pair.shape[1]
    tile = hidden // 4
    wait_attention = load_lower(attention_pieces, s0_ref, w_attn, sems0, width)
    start_pair, wait_pair = load_halves(pair_pieces, s1_ref, w_pair, sems1)
    start_pair(0)
    wait_down = load(down_pieces, s2_ref, w_down, sems2)
    start_pair(1)
    even = core_ref[0] == 0
    x = upright(x_ref).astype(F32)
    dy = upright(cot_ref)
    attn_t_ref[...] = jnp.transpose(attn_ref[...])
    wait_attention()
    resid = x + nn(attn_ref[...], w_attn[:, : rounded_up(width)])[:, :width]
    resid_t = jnp.transpose(resid)
    resid_ref[...] = resid_t
    sum_ref[...] = resid_t
    act = (resid * rms_inverse(resid) * gains_ref[1:2, :]).astype(BF)
    act_t_ref[...] = jnp.transpose(act)
    wait_pair(0)
    wait_down()
    for first in range(0, hidden, tile):
        if first == hidden // 2:
            wait_pair(1)
        here = slice(first, first + tile)
        gate = nn(act, w_pair[:width, here])
        upper = nn(act, w_pair[width:, here])
        d_inner = nn(dy, w_down[:, here])
        sigmoid = 1.0 / (1.0 + jnp.exp(-gate))
        silu = gate * sigmoid
        inner = (silu * upper).astype(BF)
        inner_ref[:, here] = inner
        d_gate = d_inner * upper * sigmoid * (1.0 + gate * (1.0 - sigmoid))
        d_upper = d_inner * silu
        kept_ref[:, here] = jnp.where(even, d_gate, d_upper).astype(BF)
        given_ref[:, here] = jnp.where(even, d_upper, d_gate).astype(BF)
        sum_ref[...] += nn(w_down[:, here], jnp.transpose(inner))
    spread_out(sum_ref[...].astype(BF), out_ref)


def feed(core, x, attn, dy, gains, attention_got, pair_got, down_got):
    micro, width, rows = x.shape
    tokens = micro * rows
    groups = [attention_got, pair_got, down_got]
    counts = [len(pieces) for pieces, _, _ in groups]
    shapes = [shape for _, _, shape in groups]
    hidden = shapes[1][1]
    outs = (jax.ShapeDtypeStruct(x.shape, BF),)
    outs += (jax.ShapeDtypeStruct((tokens, hidden), BF),) * 3
    outs += (jax.ShapeDtypeStruct((width, tokens), BF),) * 2
    outs += (jax.ShapeDtypeStruct((width, tokens), F32),)
    every = [piece for pieces, _, _ in groups for piece in pieces]
    return pl.pallas_call(
        functools.partial(feed_kernel, counts),
        name="feed",
        in_specs=[IN_SMEM] * 4 + [IN_VMEM] * 4 + [ANYWHERE] * len(every),
        out_specs=(IN_VMEM,) * 7,
        out_shape=outs,
        scratch_shapes=[pltpu.VMEM((width, shapes[0][1]), BF)]
        + [pltpu.VMEM(shape, BF) for shape in shapes[1:]]
        + [pltpu.VMEM((width, tokens), F32)]
        + [pltpu.SemaphoreType.DMA(size) for size in ((counts[0],), (counts[1], 2), (counts[2],))],
        cost_estimate=cost(
            2 * tokens * width * (4 * hidden + width), tokens * hidden, x, x, x, *outs, *every
        ),
        compiler_params=pltpu.CompilerParams(vmem_limit_bytes=VMEM_MOST),
    )(core, *(starts for _, starts, _ in groups), x, attn, dy, gains, *every)


def feed_back_kernel(counts, core_ref, s0_ref, s1_ref, resid_ref, cot_ref, kept_ref, given_ref, gain_ref, *refs):
    total_count = sum(counts)
    dres_ref, low_ref, dattn_ref, w_attn, w_pair, sems0, sems1 = refs[total_count:]
    width = resid_ref.shape[0]
    start_pair, wait_pair = load_halves(refs[counts[0] : total_count], s1_ref, w_pair, sems1)
    start_pair(0)
    start_pair(1)
    wait_attention = load_lower(refs[: counts[0]], s0_ref, w_attn, sems0, width)
    resid = resid_ref[...]
    root = lax.rsqrt(jnp.mean(resid * resid, axis=0, keepdims=True) + EPS)
    normed = resid * root
    half = w_pair.shape[1] // 2
    for h in range(2):
        columns = slice(h * half, (h + 1) * half)
        weight = lambda i: w_pair[pl.ds(pl.multiple_of(i * width, 16), width), columns]
        wait_pair(h)
        part = nt(weight(core_ref[0]), kept_ref[:, columns]) + nt(weight(1 - core_ref[0]), given_ref[:, columns])
        d_act = part if h == 0 else d_act + part
    d_normed = d_act * gain_ref[...]
    d_resid = across(cot_ref).astype(F32) + root * (
        d_normed - normed * jnp.mean(d_normed * normed, axis=0, keepdims=True)
    )
    dres_ref[...] = d_resid
    low = d_resid.astype(BF)
    low_ref[:, :width] = jnp.transpose(low)
    if low_ref.shape[1] > width:
        low_ref[:, width:] = jnp.zeros((low_ref.shape[0], low_ref.shape[1] - width), BF)
    wait_attention()
    dattn_ref[...] = jnp.transpose(nn(w_attn[:, :width], low).astype(BF))


def feed_back(core, resid, dy, kept, given, gain, attention_got, pair_got):
    width, tokens = resid.shape
    groups = [attention_got, pair_got]
    counts = [len(pieces) for pieces, _, _ in groups]
    shapes = [shape for _, _, shape in groups]
    outs = (
        jax.ShapeDtypeStruct((width, tokens), F32),
        jax.ShapeDtypeStruct((tokens, rounded_up(width)), BF),
        jax.ShapeDtypeStruct((tokens, width), BF),
    )
    every = [piece for pieces, _, _ in groups for piece in pieces]
    return pl.pallas_call(
        functools.partial(feed_back_kernel, counts),
        name="feed_back",
        in_specs=[IN_SMEM] * 3 + [IN_VMEM] * 5 + [ANYWHERE] * len(every),
        out_specs=(IN_VMEM,) * 3,
        out_shape=outs,
        scratch_shapes=[pltpu.VMEM((width, shapes[0][1]), BF), pltpu.VMEM(shapes[1], BF)]
        + [pltpu.SemaphoreType.DMA(size) for size in ((counts[0],), (counts[1], 2))],
        cost_estimate=cost(
            2 * tokens * width * (2 * shapes[1][1] + width), 0, resid, dy, kept, given, *outs, *every
        ),
        compiler_params=pltpu.CompilerParams(vmem_limit_bytes=VMEM_MOST),
    )(core, *(starts for _, starts, _ in groups), resid, dy, kept, given, gain, *every)


def pick_rows(source, starts_ref, base, rows, count, target):
    for t in range(count):
        start = pl.multiple_of(starts_ref[base + t], 16)
        target[t * rows : (t + 1) * rows, :] = source[pl.ds(start, rows), :]


def down_grad_kernel(shards, cut, info_ref, cot_ref, far_cot_ref, inner_ref, far_inner_ref, low_ref, high_ref, dy):
    micro, width, rows = cot_ref.shape
    tokens, part = micro * rows, low_ref.shape[0] // (shards // 2)
    first = pl.multiple_of(info_ref[0], 16)
    for i, ref in enumerate((cot_ref, far_cot_ref)):
        for m in range(micro):
            at = i * tokens + m * rows
            dy[:, at : at + rows] = ref[m, pl.ds(first, part), :]
    for t in range(shards):
        columns = pl.ds(pl.multiple_of(info_ref[1 + t], 128), cut)
        made = nn(dy[:, :tokens], inner_ref[:, columns]) + nn(dy[:, tokens:], far_inner_ref[:, columns])
        out_ref, at = (low_ref, t) if t < shards // 2 else (high_ref, t - shards // 2)
        out_ref[at * part : (at + 1) * part, :] = made.astype(BF)


def down_grad(cot, far_cot, inner, far_inner, first, starts):
    shards, (micro, width, rows), (tokens, hidden) = len(starts), cot.shape, inner.shape
    part, cut = width // 2, hidden // shards
    outs = (jax.ShapeDtypeStruct((shards // 2 * part, cut), BF),) * 2
    if part % 16 or cut % 128:
        grad = nn(jnp.concatenate(list(cot), axis=1), inner) + nn(jnp.concatenate(list(far_cot), axis=1), far_inner)
        grad = lax.dynamic_slice_in_dim(grad.astype(BF), first, part, 0)
        blocks = [lax.dynamic_slice_in_dim(grad, start, cut, 1) for start in starts]
        return [jnp.concatenate(blocks[: shards // 2]), jnp.concatenate(blocks[shards // 2 :])]
    return pl.pallas_call(
        functools.partial(down_grad_kernel, shards, cut),
        name="down_grad",
        in_specs=[IN_SMEM] + [IN_VMEM] * 4,
        out_specs=(IN_VMEM,) * 2,
        out_shape=outs,
        scratch_shapes=[pltpu.VMEM((part, 2 * tokens), BF)],
        cost_estimate=cost(4 * part * tokens * hidden, 0, cot, cot, inner, inner, *outs),
        compiler_params=pltpu.CompilerParams(vmem_limit_bytes=VMEM_LIMIT),
    )(numbers([first] + starts), cot, far_cot, inner, far_inner)


def wide_grad_kernel(cuts, count, starts_ref, left_ref, far_left_ref, right_ref, far_right_ref, *refs):
    outs, ordered = refs[: 2 * len(cuts)], refs[2 * len(cuts)]
    tokens = left_ref.shape[1]

    @pl.when(pl.program_id(0) == 0)
    def _():
        at = first = 0
        for cut in cuts:
            for t in range(count):
                start = pl.multiple_of(starts_ref[t] + first, 16)
                ordered[at : at + cut, :tokens] = left_ref[pl.ds(start, cut), :]
                ordered[at : at + cut, tokens:] = far_left_ref[pl.ds(start, cut), :]
                at += cut
            first += cut

    made = nn(ordered[:, :tokens], right_ref[...]) + nn(ordered[:, tokens:], far_right_ref[...])
    at = 0
    for i, out_ref in enumerate(outs):
        size = out_ref.shape[0]
        out_ref[...] = made[at : at + size].astype(BF)
        at += size


def wide_grad(left, far_left, right, far_right, rows, cuts, starts):
    count, (tokens, columns) = len(starts), right.shape
    outs = tuple(jax.ShapeDtypeStruct((count // 2 * cut, columns), BF) for cut in cuts for _ in range(2))
    if rows % 16 or any(cut % 16 for cut in cuts):
        grad = (nn(left, right) + nn(far_left, far_right)).astype(BF)
        made, first = [], 0
        for cut in cuts:
            blocks = [lax.dynamic_slice_in_dim(grad, start + first, cut, 0) for start in starts]
            made += [jnp.concatenate(blocks[: count // 2]), jnp.concatenate(blocks[count // 2 :])]
            first += cut
        return made
    tile = 512 if columns % 512 == 0 else columns
    part = pl.BlockSpec((tokens, tile), lambda n, starts: (0, n))
    whole = pl.BlockSpec(left.shape, lambda n, starts: (0, 0))
    return pl.pallas_call(
        functools.partial(wide_grad_kernel, cuts, count),
        grid_spec=pltpu.PrefetchScalarGridSpec(
            num_scalar_prefetch=1,
            grid=(columns // tile,),
            in_specs=[whole, whole, part, part],
            out_specs=tuple(pl.BlockSpec((out.shape[0], tile), lambda n, starts: (0, n)) for out in outs),
            scratch_shapes=[pltpu.VMEM((count * rows, 2 * tokens), BF)],
        ),
        out_shape=outs,
        name="wide_grad",
        cost_estimate=cost(4 * tokens * rows * count * columns, 0, left, left, right, right, *outs),
        compiler_params=pltpu.CompilerParams(vmem_limit_bytes=VMEM_LIMIT),
    )(numbers(starts), left, far_left, right, far_right)


def settle_wide_kernel(cuts, core_ref, gain_ref, *refs):
    sums = refs[: 2 * len(cuts)]
    w_left, w_right, left_ref, right_ref, sum_ref = refs[2 * len(cuts) :]
    even = core_ref[0] == 0
    at = 0
    for c, cut in enumerate(cuts):
        here = slice(at, at + cut)
        mine, theirs = sums[2 * c][...].astype(F32), sums[2 * c + 1][...].astype(F32)
        left, right = jnp.where(even, mine, theirs), jnp.where(even, theirs, mine)
        left_ref[here, :], right_ref[here, :] = left, right
        both = w_left[here, :].astype(F32) * left + w_right[here, :].astype(F32) * right
        sum_ref[here, :] = jnp.sum(both, axis=1, keepdims=True) / gain_ref[here, :]
        at += cut


def settle_wide(core, gain, sums, cuts, w_left, w_right):
    out = jax.ShapeDtypeStruct(w_left.shape, F32)
    column = jax.ShapeDtypeStruct((w_left.shape[0], 1), F32)
    if any(cut % 16 for cut in cuts):
        pairs = [(mine.astype(F32), theirs.astype(F32)) for mine, theirs in sums]
        left = jnp.concatenate([jnp.where(core[0] == 0, a, b) for a, b in pairs])
        right = jnp.concatenate([jnp.where(core[0] == 0, b, a) for a, b in pairs])
        both = w_left.astype(F32) * left + w_right.astype(F32) * right
        return left, right, jnp.sum(both, axis=1, keepdims=True) / gain
    args = [value for pair in sums for value in pair]
    return pl.pallas_call(
        functools.partial(settle_wide_kernel, cuts),
        name="settle",
        in_specs=[IN_SMEM] + [IN_VMEM] * (3 + len(args)),
        out_specs=(IN_VMEM,) * 3,
        out_shape=(out, out, column),
        cost_estimate=cost(4 * w_left.size, 0, out, out, *args),
        compiler_params=pltpu.CompilerParams(vmem_limit_bytes=VMEM_LIMIT),
    )(core, gain, *args, w_left, w_right)


def turn_keys(source, target, at, cosine, sine):
    rows = source.shape[0]
    for first in range(0, KV_WIDTH, 128):
        chunk = turn(source[:, first : first + 128].astype(F32), cosine, -sine).astype(BF)
        last = min(first + 128, KV_WIDTH)
        target[at : at + rows, first:last] = chunk[:, : last - first]
    target[at : at + rows, KV_WIDTH:] = source[:, KV_WIDTH:]


def attention_grad_kernel(shards, half, starts_ref, gain_ref, cos_ref, sin_ref, dq_ref, attn_ref, low_ref, *refs):
    xs, halves = refs[:shards], refs[shards : shards + 2]
    dkvs = [ref.at[t] for ref in halves for t in range(shards // 2)]
    outs, (act, dkv, ordered, attn_ordered) = refs[shards + 2 : shards + 4], refs[shards + 4 :]
    micro, width, rows = xs[0].shape
    tokens = micro * rows
    wide = rounded_up(width)
    for t in range(shards):
        here = slice(t * tokens, (t + 1) * tokens)
        turn_keys(dkvs[t], dkv, t * tokens, cos_ref[here, :], sin_ref[here, :])
        for m in range(micro):
            x = xs[t][m].astype(F32)
            root = lax.rsqrt(jnp.mean(x * x, axis=0, keepdims=True) + EPS)
            first = t * tokens + m * rows
            act[:, first : first + rows] = (x * root * gain_ref[...]).astype(BF)
    for i, out_ref in enumerate(outs):
        pick_rows(act, starts_ref, i * shards, half, shards, ordered)
        pick_rows(attn_ref, starts_ref, i * shards, half, shards, attn_ordered)
        out_ref[:, :wide] = nn(ordered[:, :tokens], dq_ref[...]).astype(BF)
        out_ref[:, wide : 2 * wide] = nn(attn_ordered[...], low_ref[...]).astype(BF)
        out_ref[:, 2 * wide :] = nn(ordered[...], dkv[...]).astype(BF)


def attention_grad(x_all, gain, cosine, sine, dq, attn_t, low, dkv_all, half, given, kept):
    shards = len(x_all)
    micro, width, rows = x_all[0].shape
    every = shards * micro * rows
    wide = rounded_up(width)
    out = jax.ShapeDtypeStruct((shards * half, 2 * wide + 2 * KV_WIDTH), BF)
    if half % 16 or width // shards % 16:
        xs = jnp.concatenate([x[m] for x in x_all for m in range(micro)], axis=1).astype(F32)
        act = xs * lax.rsqrt(jnp.mean(xs * xs, axis=0, keepdims=True) + EPS) * gain
        act = act.astype(BF)
        dkv = jnp.concatenate(dkv_all, axis=0).reshape(every, 2 * KV_WIDTH)
        keys = dkv[:, :KV_WIDTH].astype(F32).reshape(every, -1, 2, HALF_HEAD)
        c, s = cosine[:, None, :HALF_HEAD], sine[:, None, HALF_HEAD:HEAD_SIZE]
        first, second = keys[:, :, 0], keys[:, :, 1]
        keys = jnp.stack([first * c + second * s, second * c - first * s], axis=2)
        dkv = jnp.concatenate([keys.reshape(every, KV_WIDTH).astype(BF), dkv[:, KV_WIDTH:]], axis=1)
        parts = [nn(act[:, : micro * rows], dq), nn(attn_t, low), nn(act, dkv)]
        grad = jnp.concatenate(parts, axis=1).astype(BF)
        return [
            jnp.concatenate([lax.dynamic_slice_in_dim(grad, start, half, 0) for start in starts])
            for starts in (given, kept)
        ]
    return pl.pallas_call(
        functools.partial(attention_grad_kernel, shards, half),
        name="attention_grad",
        in_specs=[IN_SMEM] + [IN_VMEM] * (8 + shards),
        out_specs=(IN_VMEM,) * 2,
        out_shape=(out, out),
        scratch_shapes=[
            pltpu.VMEM((width, every), BF),
            pltpu.VMEM((every, 2 * KV_WIDTH), BF),
            pltpu.VMEM((shards * half, every), BF),
            pltpu.VMEM((shards * half, micro * rows), BF),
        ],
        cost_estimate=cost(
            4 * shards * half * (every * 2 * KV_WIDTH + 2 * micro * rows * width),
            0,
            *x_all,
            *dkv_all,
            out,
            out,
        ),
        compiler_params=pltpu.CompilerParams(vmem_limit_bytes=VMEM_MOST),
    )(numbers(given + kept), gain, cosine, sine, dq, attn_t, low, *x_all, *dkv_all)


def finish_kernel(count, starts_ref, x_ref, low_ref, kv_ref, dres_ref, gain_ref, cos_ref, sin_ref, *refs):
    pieces = refs[:count]
    dx_ref, whole, kv_turned, sems = refs[count:]
    wait = load(pieces, starts_ref, whole, sems)
    turn_keys(kv_ref, kv_turned, 0, cos_ref[...], sin_ref[...])
    x = across(x_ref).astype(F32)
    width = x.shape[0]
    root = lax.rsqrt(jnp.mean(x * x, axis=0, keepdims=True) + EPS)
    normed = x * root
    wait()
    d_act = nt(whole[:width, :width], low_ref[:, :width])
    d_act += nt(whole[:width, width:], kv_turned[:, :KV_WIDTH])
    d_act += nt(whole[width:, width:], kv_turned[:, KV_WIDTH:])
    d_normed = d_act * gain_ref[...]
    d_x = dres_ref[...] + root * (d_normed - normed * jnp.mean(d_normed * normed, axis=0, keepdims=True))
    spread_out(d_x.astype(BF), dx_ref)


def finish(x, low, kv, dres, gain, cosine, sine, pieces, starts, shape):
    micro, width, rows = x.shape
    tokens = micro * rows
    table = pl.BlockSpec((tokens, 128), lambda i: (0, 0))
    return pl.pallas_call(
        functools.partial(finish_kernel, len(pieces)),
        grid=(1,),
        name="finish",
        in_specs=[IN_SMEM] + [IN_VMEM] * 5 + [table] * 2 + [ANYWHERE] * len(pieces),
        out_specs=IN_VMEM,
        out_shape=jax.ShapeDtypeStruct(x.shape, BF),
        scratch_shapes=[
            pltpu.VMEM(shape, BF),
            pltpu.VMEM((tokens, 2 * KV_WIDTH), BF),
            pltpu.SemaphoreType.DMA((len(pieces),)),
        ],
        cost_estimate=cost(2 * tokens * width * (width + 2 * KV_WIDTH), 0, x, low, dres, *pieces),
        compiler_params=pltpu.CompilerParams(vmem_limit_bytes=VMEM_LIMIT),
    )(starts, x, low, kv, dres, gain, cosine, sine, *pieces)


def head(ref, h):
    return ref[:, h * HEAD_SIZE : (h + 1) * HEAD_SIZE]


def widen(value, columns):
    n = value.shape[0]
    lane = lax.broadcasted_iota(jnp.int32, (n, HEAD_SIZE), 1)
    tail = jnp.zeros((n, HEAD_SIZE), F32)
    for c, column in enumerate(columns):
        tail = jnp.where(lane == c, column, tail)
    return jnp.concatenate([value, tail.astype(BF)], axis=1)


def split(column):
    high = column.astype(BF).astype(F32)
    middle = (column - high).astype(BF).astype(F32)
    return [high, middle, column - high - middle]


def attend_kernel(shards, seg_rows, q_ref, *refs):
    kv = refs[:shards]
    bias_ref = refs[shards]
    o_ref, lse_ref = refs[-2:]
    rows = q_ref.shape[0]
    i = lax.broadcasted_iota(jnp.int32, (rows, rows), 0)
    j = lax.broadcasted_iota(jnp.int32, (rows, rows), 1)
    same = (i // seg_rows) == (j // seg_rows)
    own = jnp.where(j > i, CLOSED, jnp.where(same, 0.0, bias_ref[0:1, :]))
    one = jnp.ones((rows, 1), F32)
    bias_columns = jnp.transpose(bias_ref[...])
    lse = jnp.zeros((rows, 128), F32)
    lane = lax.broadcasted_iota(jnp.int32, (rows, 128), 1)
    for g in range(KEY_VALUE_HEADS):
        keys, values = [], []
        for t in range(shards):
            keys.append(widen(head(kv[t], g), [bias_columns[:, t : t + 1]] if t else []))
            values.append(widen(head(kv[t], KEY_VALUE_HEADS + g), [one]))
        for h in range(g * GROUP, g * GROUP + GROUP):
            q = widen(head(q_ref, h), [one])
            scores = [nt(q, k) for k in keys]
            scores[0] = scores[0] + own
            peak = functools.reduce(jnp.maximum, scores)
            peak = jnp.max(peak, axis=1, keepdims=True)
            terms = [nn(jnp.exp(s - peak).astype(BF), v) for s, v in zip(scores, values)]
            mixed = sum(terms[1:], terms[0])
            total = mixed[:, HEAD_SIZE : HEAD_SIZE + 1]
            o_ref[:, h * HEAD_SIZE : (h + 1) * HEAD_SIZE] = (mixed[:, :HEAD_SIZE] / total).astype(BF)
            lse = jnp.where(lane == h, peak + jnp.log(total), lse)
    lse_ref[...] = lse


def attend_back_kernel(shards, seg_rows, q_ref, *refs):
    kv = refs[:shards]
    bias_ref, o_ref, do_ref, lse_ref, cos_ref, sin_ref = refs[shards : shards + 6]
    dq_ref, low_ref, high_ref = refs[-3:]
    dkv = [ref.at[t] for ref in (low_ref, high_ref) for t in range(shards // 2)]
    rows = q_ref.shape[0]
    i = lax.broadcasted_iota(jnp.int32, (rows, rows), 1)
    j = lax.broadcasted_iota(jnp.int32, (rows, rows), 0)
    bias_columns = jnp.transpose(bias_ref[...])
    same = (i // seg_rows) == (j // seg_rows)
    own_column = jnp.broadcast_to(bias_columns[:, 0:1], (rows, rows))
    own = jnp.where(j > i, CLOSED, jnp.where(same, 0.0, own_column))
    one, zero = jnp.ones((rows, 1), F32), jnp.zeros((rows, 1), F32)
    cosine, sine = cos_ref[...], sin_ref[...]
    if dq_ref.shape[1] > QUERY_HEADS * HEAD_SIZE:
        dq_ref[:, QUERY_HEADS * HEAD_SIZE :] = jnp.zeros((rows, dq_ref.shape[1] - QUERY_HEADS * HEAD_SIZE), BF)
    for g in range(KEY_VALUE_HEADS):
        keys, values, turned = [], [], []
        for t in range(shards):
            k = head(kv[t], g)
            turned.append(jnp.transpose(k))
            keys.append(widen(k, [bias_columns[:, t : t + 1] if t else zero, one, one, one]))
            values.append(widen(head(kv[t], KEY_VALUE_HEADS + g), [one, one, one]))
        dk, dv = [None] * shards, [None] * shards
        for h in range(g * GROUP, g * GROUP + GROUP):
            q, do = head(q_ref, h), head(do_ref, h)
            centre = jnp.sum(head(o_ref, h).astype(F32) * do.astype(F32), axis=1, keepdims=True)
            q_wide = widen(q, [one] + split(-lse_ref[:, h : h + 1]))
            do_wide = widen(do, split(-centre))
            dq = None
            for t in range(shards):
                scores = nt(keys[t], q_wide)
                if t == 0:
                    scores = scores + own
                probs = jnp.exp(scores)
                ds = (probs * nt(values[t], do_wide)).astype(BF)
                v_term = nn(probs.astype(BF), do)
                k_term = nn(ds, q)
                q_term = nn(turned[t], ds)
                dv[t] = v_term if dv[t] is None else dv[t] + v_term
                dk[t] = k_term if dk[t] is None else dk[t] + k_term
                dq = q_term if dq is None else dq + q_term
            dq = dq * SCALE
            first, second = dq[:HALF_HEAD], dq[HALF_HEAD:]
            back = jnp.concatenate(
                [first * cosine + second * sine, second * cosine - first * sine], axis=0
            )
            dq_ref[:, h * HEAD_SIZE : (h + 1) * HEAD_SIZE] = jnp.transpose(back.astype(BF))
        for t in range(shards):
            dkv[t][:, g * HEAD_SIZE : (g + 1) * HEAD_SIZE] = dk[t].astype(BF)
            g_value = KEY_VALUE_HEADS + g
            dkv[t][:, g_value * HEAD_SIZE : (g_value + 1) * HEAD_SIZE] = dv[t].astype(BF)


def attend(micro, seg_rows, q, kv, bias):
    shards, tokens, width = len(kv), q.shape[0], q.shape[1]
    rows = tokens // micro
    here = lambda w: pl.BlockSpec((rows, w), lambda m: (m, 0))
    outs = (jax.ShapeDtypeStruct((tokens, width), BF), jax.ShapeDtypeStruct((tokens, 128), F32))
    pairs = tokens * rows * shards * QUERY_HEADS
    return pl.pallas_call(
        functools.partial(attend_kernel, shards, seg_rows),
        grid=(micro,),
        name="attend",
        in_specs=[here(width)]
        + [here(2 * KV_WIDTH)] * shards
        + [pl.BlockSpec((None,) + bias.shape[1:], lambda m: (m, 0, 0))],
        out_specs=(here(width), here(128)),
        out_shape=outs,
        cost_estimate=cost(16 * HEAD_SIZE * pairs, pairs, q),
        compiler_params=pltpu.CompilerParams(vmem_limit_bytes=VMEM_LIMIT),
    )(q, *kv, bias)


def attend_back(m, rows, seg_rows, q, kv, bias, o, do, lse, cosine, sine, earlier):
    shards, tokens, width = len(kv), q.shape[0], q.shape[1]
    here = lambda w: pl.BlockSpec((rows, w), lambda i: (m, 0))
    turned = pl.BlockSpec((HALF_HEAD, rows), lambda i: (0, m))
    outs = (jax.ShapeDtypeStruct((tokens, rounded_up(width)), BF),)
    outs += (jax.ShapeDtypeStruct((shards // 2, tokens, 2 * KV_WIDTH), BF),) * 2
    pieces = pl.BlockSpec((shards // 2, rows, 2 * KV_WIDTH), lambda i: (0, m, 0))
    pairs = rows * rows * shards * QUERY_HEADS
    return pl.pallas_call(
        functools.partial(attend_back_kernel, shards, seg_rows),
        grid=(1,),
        name="attend_back",
        in_specs=[here(width)]
        + [here(2 * KV_WIDTH)] * shards
        + [pl.BlockSpec((None,) + bias.shape[1:], lambda i: (m, 0, 0))]
        + [here(width), here(width), here(128), turned, turned]
        + [pl.BlockSpec(memory_space=pl.ANY)] * len(earlier),
        out_specs=(here(rounded_up(width)), pieces, pieces),
        out_shape=outs,
        input_output_aliases={shards + 7 + i: i for i in range(len(earlier))},
        cost_estimate=cost(40 * HEAD_SIZE * pairs, pairs, q),
        compiler_params=pltpu.CompilerParams(vmem_limit_bytes=VMEM_LIMIT),
    )(q, *kv, bias, o, do, lse, cosine, sine, *earlier)


def local(
    block_input,
    parent_ids,
    w_query,
    key_weight,
    value_weight,
    w_output,
    w_gate,
    w_up,
    w_down,
    norm_first,
    norm_second,
    out_cotangent,
):
    micro, rows, width = block_input.shape
    shards = lax.axis_size("shard")
    links = Links(lax.axis_size("rep"), shards)
    tree = rows * shards
    segs = parent_ids.shape[2]
    seg_rows = tree // segs
    tokens = micro * rows
    hidden = w_gate.shape[1]

    inputs = block_input.swapaxes(1, 2)
    cotangent = out_cotangent.swapaxes(1, 2)

    even = links.core == 0
    side = lax.axis_index("rep") // 2 % 2
    left = jnp.concatenate([w_query, key_weight], axis=1)
    right = jnp.concatenate([w_output, value_weight], axis=1)
    attn_mine = jnp.where(even, left, right)
    pair_cut = hidden // 2
    pair_mine = lax.dynamic_slice_in_dim(jnp.where(even, w_gate, w_up), side * pair_cut, pair_cut, 1)
    down_own = w_down.T
    down_cut = width // 2
    down_mine = lax.dynamic_slice_in_dim(down_own, links.core * down_cut, down_cut, 0)
    core = numbers([links.core])

    attn_near = links.near(attn_mine)
    gain_pieces = links.small_pieces(jnp.stack([norm_first, norm_second]))
    attn_mine, attn_near, gain_pieces, pair_mine, down_mine = meet(
        attn_mine, attn_near, gain_pieces, pair_mine, down_mine
    )

    gains = links.in_order(gain_pieces).astype(F32)
    attn_all = links.far(attn_mine, attn_near)
    attn_swapped = {t: links.swap(attn_near[t]) for t in attn_near}
    pair_near = {1: links.step(pair_mine, 0)}
    parents = parent_ids[:, 0]
    seg = jnp.arange(segs)
    after_parent = jnp.concatenate([parents[:, 1:], jnp.full((micro, 1), -1, parents.dtype)], axis=1)
    on_path = (seg % 2 == 0)[None] | (after_parent == seg[None])
    below = (seg[None, :] < seg[:, None])[None]
    depth = jnp.sum(jnp.where(below, on_path.astype(F32)[:, None, :], 0.0), axis=-1)

    def row_numbers(hop):
        return (links.shard ^ hop) * rows + jnp.arange(rows)

    def pick(table, numbers):
        hit = (numbers // seg_rows)[..., None] == seg
        return jnp.sum(jnp.where(hit[None], table.reshape(micro, *(1,) * numbers.ndim, segs), 0), axis=-1)

    key_rows = jnp.stack([row_numbers(hop) for hop in links.hops])
    positions = pick(depth, key_rows) * seg_rows + (key_rows % seg_rows).astype(F32)
    freqs = jnp.exp(-math.log(10000.0) * jnp.arange(HALF_HEAD, dtype=F32) * (2.0 / HEAD_SIZE))
    angles = freqs[:, None] * positions.swapaxes(0, 1).reshape(1, shards * tokens)
    cosine_t, sine_t = jnp.cos(angles), jnp.sin(angles)
    cosine = jnp.tile(cosine_t.T, (1, 4))
    sine = jnp.tile(jnp.concatenate([-sine_t.T, sine_t.T], axis=1), (1, 2))
    open_key = (pick(on_path.astype(F32), key_rows) > 0.5) & (
        (key_rows < links.shard * rows) | (jnp.arange(shards) == 0)[:, None]
    )
    bias = jnp.where(open_key, 0.0, CLOSED)
    bias = jnp.pad(bias, ((0, 0), (0, 8 - shards), (0, 0)))

    gain_one, gain_two = gains[0][:, None], gains[1][:, None]
    tables = (cosine, sine, cosine_t, sine_t, bias, gains, gain_one, gain_two)
    attn_all, attn_swapped, pair_mine, pair_near, down_mine, tables = meet(
        attn_all, attn_swapped, pair_mine, pair_near, down_mine, tables
    )
    cosine, sine, cosine_t, sine_t, bias, gains, gain_one, gain_two = tables

    for t in range(1, shards):
        if t not in attn_swapped:
            attn_swapped[t] = links.swap(attn_all[t])
    shard_rows = width // shards

    def pair_place(weight, hop):
        return weight * width + (links.shard ^ hop) * shard_rows

    pieces, starts = [left, right], [(pair_place(0, 0), 0), (pair_place(1, 0), 0)]
    for t in range(1, shards):
        pieces += [attn_all[t], attn_swapped[t]]
        starts += [
            (pair_place(links.core, links.hops[t]), 0),
            (pair_place(1 - links.core, links.hops[links.twin(t)]), 0),
        ]
    attention_got = joined(pieces, starts, (2 * width, left.shape[1]))
    pair_near |= {1 << i: links.step(pair_mine, i) for i in range(1, links.bits)}
    pair_beside = {1: links.beside(pair_near[1])}
    down_near = {1: links.step(down_mine, 0)}
    queries, kv = project(inputs, gains, cosine, sine, *attention_got)
    queries, kv, pair_mine, pair_near, pair_beside, down_mine, down_near = meet(
        queries, kv, pair_mine, pair_near, pair_beside, down_mine, down_near
    )

    kv_near = links.near(kv)
    pair_beside |= {t: links.beside(pair_near[t]) for t in pair_near if t > 1}
    kv_near, kv, pair_beside, pair_near, pair_mine = meet(kv_near, kv, pair_beside, pair_near, pair_mine)

    kv_all = links.far(kv, kv_near)
    pair_all = links.far(pair_mine, pair_near)
    pair_swapped = {t: links.swap(pair_near[t]) for t in pair_near}
    pair_crossed = {t: links.swap(pair_beside[t]) for t in pair_beside}
    kv_all, pair_all, pair_swapped, pair_crossed, pair_beside, down_mine, down_near = meet(
        kv_all, pair_all, pair_swapped, pair_crossed, pair_beside, down_mine, down_near
    )

    down_near |= {1 << i: links.step(down_mine, i) for i in range(1, links.bits)}
    down_all = links.far(down_mine, down_near)
    pair_beside |= {t: links.beside(pair_all[t]) for t in range(1, shards) if t not in pair_beside}
    attn, lse = attend(micro, seg_rows, queries, kv_all, bias)
    pair_swapped |= {t: links.swap(pair_all[t]) for t in range(1, shards) if t not in pair_swapped}
    attn, lse, down_all, pair_beside, pair_all, pair_swapped = meet(
        attn, lse, down_all, pair_beside, pair_all, pair_swapped
    )

    pair_crossed |= {t: links.swap(pair_beside[t]) for t in range(1, shards) if t not in pair_crossed}
    down_swapped = [None] + [links.swap(down_all[t]) for t in range(1, shards)]
    pieces, starts = [w_gate, w_up], [(pair_place(0, 0), 0), (pair_place(1, 0), 0)]
    for t in range(1, shards):
        pieces += [pair_all[t], pair_beside[t], pair_swapped[t], pair_crossed[t]]
        for row in (
            pair_place(links.core, links.hops[t]),
            pair_place(1 - links.core, links.hops[links.twin(t)]),
        ):
            starts += [(row, side * pair_cut), (row, (1 - side) * pair_cut)]
    pair_got = joined(pieces, starts, (2 * width, hidden))
    own = w_down.shape[0]
    pieces, starts = [down_own], [(0, links.shard * own)]
    for t in range(1, shards):
        pieces += [down_all[t], down_swapped[t]]
        starts += [
            (links.core * down_cut, (links.shard ^ links.hops[t]) * own),
            ((1 - links.core) * down_cut, (links.shard ^ links.hops[links.twin(t)]) * own),
        ]
    down_got = joined(pieces, starts, (width, own * shards))
    attn, pair_pieces, down_pieces = meet(attn, pair_got[0], down_got[0])
    pair_got, down_got = (pair_pieces, *pair_got[1:]), (down_pieces, *down_got[1:])

    plan = Plan()
    have = lambda *names: [plan.have[name] for name in names]
    x_near = links.near(inputs)
    far_cotangent = links.swap(cotangent)
    made = feed(core, inputs, attn, cotangent, gains, attention_got, pair_got, down_got)
    names = ("out", "inner", "kept", "given", "act", "attn_t", "resid")
    plan.have = dict(zip(names, made)) | {"x_near": x_near, "far_dy": far_cotangent, "queries": queries, "kv": kv_all, "lse": lse, "attn": attn}
    plan.close()

    half, mine, theirs = links.half_rows(shard_rows)
    some_kept, some_given = links.order(shard_rows, mine, theirs)
    cuts = (-(-shard_rows // 32) * 16, shard_rows - -(-shard_rows // 32) * 16)

    plan.have["x_all"] = links.far(inputs, plan.have.pop("x_near"))
    for name in ("inner", "act", "given"):
        plan.have["far_" + name] = links.swap(plan.have[name])
    names = ("d_resid", "low", "d_attn")
    resid, kept, given = have("resid", "kept", "given")
    plan.have |= dict(zip(names, feed_back(core, resid, cotangent, kept, given, gain_two, attention_got, pair_got)))
    plan.close()

    names = ("down.low", "down.high")
    far_dy, inner, far_inner = have("far_dy", "inner", "far_inner")
    starts = [(links.shard ^ hop) * own for hop in links.hops]
    plan.have |= dict(zip(names, down_grad(cotangent, far_dy, inner, far_inner, links.core * down_cut, starts)))
    plan.close()

    for name in ("down", "wide0", "wide1", "some"):
        plan.start(name, links.reduce(plan, name, name == "some"))
    plan.advance("down")
    names = ("wide0.low", "wide0.high", "wide1.low", "wide1.high")
    act, far_act, kept, far_kept = have("act", "far_act", "kept", "far_given")
    starts = [(links.shard ^ hop) * shard_rows for hop in links.hops]
    plan.have |= dict(zip(names, wide_grad(act, far_act, kept, far_kept, shard_rows, cuts, starts)))
    plan.close()

    made = ()
    hops = [("down", "wide0"), ("down", "wide0", "wide1")]
    for m in range(micro):
        plan.advance(*hops[min(m, 1)])
        q, kv_now, o, do, lse_now = have("queries", "kv", "attn", "d_attn", "lse")
        made = attend_back(m, rows, seg_rows, q, kv_now, bias, o, do, lse_now, cosine_t, sine_t, made)
        plan.have["attn_grads"] = made = tuple(made)
        plan.close()
        made = plan.have["attn_grads"]

    d_queries, *d_kv = plan.have.pop("attn_grads")
    plan.have["dkv.pieces"] = d_kv
    plan.have["d_queries"] = d_queries
    plan.start("dkv", links.collect(plan, "dkv"))
    plan.advance("dkv", "wide0", "wide1", "down")
    given, kept = attention_grad(
        plan.have["x_all"],
        gain_one,
        cosine,
        sine,
        d_queries,
        *have("attn_t", "low"),
        d_kv,
        half,
        some_given,
        some_kept,
    )
    plan.have["some.given"], plan.have["some.kept"] = given, kept
    plan.close()

    def gain_grad(gain, *pairs):
        sums = sum(jnp.sum(weight.astype(F32) * grad, axis=1) for weight, grad in pairs)
        return sums / gain.astype(F32)

    def settle():
        have, done = plan.have, plan.have.setdefault("done", {})
        if "dkv" in have and "d_input" not in done:
            done["d_input"] = finish(
                inputs, have["d_queries"], have["dkv"], have["d_resid"], gain_one, cosine, sine, *attention_got
            )
        if "down" in have and "down" not in done:
            done["down"] = links.finish_rows(*have["down"], width).T
        if "wide0" in have and "wide1" in have and "gate" not in done:
            done["gate"], done["upper"], gain = settle_wide(
                core,
                norm_second.astype(F32)[:, None],
                (have["wide0"], have["wide1"]),
                cuts,
                w_gate,
                w_up,
            )
            done["gain_two"] = gain[:, 0]
        if "some" in have and "query" not in done:
            grad = links.finish_rows(*have["some"], shard_rows)
            first = rounded_up(width)
            done["query"], done["output"] = grad[:, :width], grad[:, first : first + width]
            done["key"], done["value"] = jnp.split(grad[:, 2 * first :], 2, axis=1)
            done["gain_one"] = gain_grad(
                norm_first,
                (w_query, done["query"]),
                (key_weight, done["key"]),
                (value_weight, done["value"]),
            )

    order, rounds = [], 0
    while plan.tasks:
        plan.advance(*(order.pop(0) if order else tuple(plan.tasks)))
        plan.advance(*{0: ('some',), 1: ('some',)}.get(rounds, ()))
        settle()
        rounds += 1
        if rounds <= 2 and plan.tasks:
            plan.close()

    done = plan.have["done"]
    return (
        plan.have["out"].swapaxes(1, 2),
        done["d_input"].swapaxes(1, 2),
        *(done[name] for name in ("query", "key", "value", "output", "gate", "upper", "down")),
        done["gain_one"],
        done["gain_two"],
    )


def solution(mesh):
    rows = P(None, AXES, None)
    weight, gain = P("shard", None), P("shard")
    return jax.shard_map(
        local,
        mesh=mesh,
        in_specs=(rows, P(None, "rep", None)) + (weight,) * 7 + (gain, gain, rows),
        out_specs=(rows, rows) + (weight,) * 7 + (gain, gain),
        check_vma=False,
    )
```

```python
import functools
import math

import jax
import jax.numpy as jnp
from jax import lax
from jax.experimental import pallas as pl
from jax.experimental.pallas import tpu as pltpu
from jax.sharding import PartitionSpec as P

QUERY_HEADS = 15
KEY_VALUE_HEADS = 5
HEAD_SIZE = 64
HALF_HEAD = HEAD_SIZE // 2
GROUP = QUERY_HEADS // KEY_VALUE_HEADS
KV_WIDTH = KEY_VALUE_HEADS * HEAD_SIZE
SCALE = HEAD_SIZE ** (-0.5)
EPS = 1e-05
AXES = ("rep", "shard")
BF = jnp.bfloat16
F32 = jnp.float32
CLOSED = -1e30
VMEM_LIMIT = 48 << 20
VMEM_MOST = 60 << 20


def dot(a, b, dims):
    return lax.dot_general(a, b, (dims, ((), ())), preferred_element_type=F32)


def nn(a, b):
    return dot(a, b, ((1,), (0,)))


def nt(a, b):
    return dot(a, b, ((1,), (1,)))


def tn(a, b):
    return dot(a, b, ((0,), (0,)))


def total(parts):
    return sum(part.astype(F32) for part in parts).astype(parts[0].dtype)


def meet(*values):
    return lax.optimization_barrier(values)


def rounded_up(columns):
    return -(-columns // 128) * 128


def rms_inverse(x):
    return lax.rsqrt(jnp.mean(x * x, axis=-1, keepdims=True) + EPS)


def cost(flops, exps, *arrays):
    size = sum(a.size * a.dtype.itemsize for a in arrays)
    return pl.CostEstimate(flops=flops, transcendentals=exps, bytes_accessed=size)


class Links:
    def __init__(self, reps, shards):
        self.reps, self.shards = reps, shards
        self.core = lax.axis_index("rep") % 2
        self.shard = lax.axis_index("shard")
        self.bits = shards.bit_length() - 1
        even = [1 << i for i in range(self.bits)]
        odd = even[:2][::-1] + even[2:]
        self.steps = list(zip(even, odd))
        self.hops = []
        for piece in range(shards):
            sums = [0, 0]
            for i, step in enumerate(self.steps):
                if piece >> i & 1:
                    sums = [sums[0] ^ step[0], sums[1] ^ step[1]]
            self.hops.append(jnp.where(self.core == 0, sums[0], sums[1]))

    def move(self, value, target):
        pairs = []
        for r in range(self.reps):
            for s in range(self.shards):
                goal = target(r, s)
                if goal is not None:
                    pairs.append((r * self.shards + s, goal[0] * self.shards + goal[1]))
        return lax.ppermute(value, AXES, pairs)

    def step(self, value, i):
        return self.move(value, lambda r, s: (r, s ^ self.steps[i][r % 2]))

    def swap(self, value):
        return self.move(value, lambda r, s: (r ^ 1, s))

    def reduce(self, plan, name, quick=False):
        top = self.bits
        if name + ".given" in plan.have:
            got = yield self.swap(plan.have.pop(name + ".given"))
            sums = [plan.have.pop(name + ".kept"), got]
        else:
            got = yield self.step(plan.have.pop(name + ".high"), top - 1)
            sums = [plan.have.pop(name + ".low"), got]
            top -= 1
        for i in reversed(range(top)):
            block = sums[0].shape[0] // 2
            got = yield self.step(total([part[block:] for part in sums]), i)
            sums = [part[:block] for part in sums] + [got]
        value = total(sums)
        chips = self.reps // 2
        place = lax.axis_index("rep") // 2
        span = 1
        if chips % 4 == 0 and quick and value.shape[0] % 4 == 0:
            quarter = value.shape[0] // 4
            across = lambda value, j: self.move(value, lambda r, s: (r ^ (2 * j), s))
            cut = lambda j: lax.dynamic_slice_in_dim(value, (place % 4 ^ j) * quarter, quarter, 0)
            got = yield [across(cut(j), j) for j in range(1, 4)]
            mine = total([cut(0)] + got)
            got = yield [across(mine, j) for j in range(1, 4)]
            parts = jnp.stack([mine] + got).reshape(2, 2, quarter, -1)
            parts = jnp.where(place % 4 >= 2, parts[::-1], parts)
            parts = jnp.where(place % 2 == 1, parts[:, ::-1], parts)
            value = parts.reshape(4 * quarter, -1)
            span = 4
        elif chips % 4 == 0:
            inward, outward, middle = {0: 1, 3: 2}, {1: 0, 2: 3}, {1: 2, 2: 1}

            def along(value, table):
                def target(r, s):
                    chip = r // 2
                    if chip % 4 not in table:
                        return None
                    return ((chip - chip % 4 + table[chip % 4]) * 2 + r % 2, s)

                return self.move(value, target)

            value = total([value, (yield along(value, inward))])
            value = total([value, (yield along(value, middle))])
            back = yield along(value, outward)
            inner = (place % 4 == 1) | (place % 4 == 2)
            value = jnp.where(inner, value, back)
            span = 4
        while span < chips:
            value = total([value, self.move(value, lambda r, s: (r ^ (2 * span), s))])
            span *= 2
        other = yield self.swap(value)
        plan.have[name] = (value, other)

    def collect(self, plan, name):
        low, high = plan.have[name + ".pieces"]
        got = yield self.step(high, self.bits - 1)
        sums = [low, got]
        for i in reversed(range(self.bits - 1)):
            block = sums[0].shape[0] // 2
            got = yield self.step(total([part[block:] for part in sums]), i)
            sums = [part[:block] for part in sums] + [got]
        plan.have[name] = total(sums)[0]

    def beside(self, value):
        return self.move(value, lambda r, s: (r ^ 2, s))

    def near(self, value):
        return {1 << i: self.step(value, i) for i in range(self.bits)}

    def far(self, value, near):
        pieces = [value]
        for t in range(1, self.shards):
            top = t.bit_length() - 1
            pieces.append(near[t] if t in near else self.step(pieces[t - (1 << top)], top))
        return pieces

    def twin(self, piece):
        return piece if self.bits < 2 else piece >> 2 << 2 | (piece & 1) << 1 | (piece >> 1 & 1)

    def small_pieces(self, value):
        return [
            value if hop == 0 else self.move(value, lambda r, s, hop=hop: (r, s ^ hop))
            for hop in range(self.shards)
        ]

    def in_order(self, pieces):
        pieces = jnp.stack(pieces)
        value = pieces
        order = self.shard ^ jnp.arange(self.shards)
        hit = (order[:, None] == jnp.arange(self.shards)[None, :])[:, :, None, None]
        pieces = jnp.sum(jnp.where(hit, pieces[None], 0), axis=1, dtype=value.dtype)
        return jnp.concatenate([pieces[j] for j in range(self.shards)], axis=-1)

    def half_rows(self, rows):
        half = -(-rows // 32) * 16
        return half, self.core * (rows - half), (1 - self.core) * (rows - half)

    def order(self, scale, mine, theirs):
        kept = [(self.shard ^ hop) * scale + mine for hop in self.hops]
        given = [(self.shard ^ self.hops[self.twin(t)]) * scale + theirs for t in range(self.shards)]
        return kept, given

    def finish_rows(self, owned, other, rows):
        low = jnp.where(self.core == 0, owned, other)
        high = jnp.where(self.core == 0, other, owned)
        return jnp.concatenate([low[: rows - owned.shape[0]], high], axis=0).astype(F32)


class Plan:
    def __init__(self):
        self.have, self.tasks, self.made = {}, {}, {}

    def start(self, name, task):
        self.tasks[name] = task
        self.made[name] = None

    def advance(self, *names):
        for name in names:
            if name in self.tasks:
                try:
                    self.made[name] = self.tasks[name].send(self.made[name])
                except StopIteration:
                    del self.tasks[name], self.made[name]

    def close(self):
        self.have, self.made = lax.optimization_barrier((self.have, self.made))


def joined(pieces, starts, shape):
    if any(piece.shape[0] % 16 or piece.shape[1] % 128 and piece.shape[1] < shape[1] for piece in pieces):
        whole = jnp.zeros(shape, pieces[0].dtype)
        for piece, start in zip(pieces, starts):
            whole = lax.dynamic_update_slice(whole, piece, start)
        pieces, starts = (whole,), [(0, 0)]
    return tuple(pieces), numbers([at for start in starts for at in start]), shape


def numbers(values):
    return jnp.stack([jnp.asarray(value, jnp.int32) for value in values])


def load(pieces, starts_ref, whole, sems):
    copies = copies_of(pieces, starts_ref, whole, sems, 0)
    for _, copy in copies:
        copy.start()
    return lambda: [copy.wait() for _, copy in copies]


def copies_of(pieces, starts_ref, whole, sems, row):
    copies = []
    for i, piece in enumerate(pieces):
        rows = pl.ds(pl.multiple_of(starts_ref[2 * i] - row, 16), piece.shape[0])
        if piece.shape[1] == whole.shape[1]:
            place = whole.at[rows, :]
        else:
            columns = pl.ds(pl.multiple_of(starts_ref[2 * i + 1], 128), piece.shape[1])
            place = whole.at[rows, columns]
        copies.append((i, pltpu.make_async_copy(piece, place, sems.at[i])))
    return copies


def load_lower(pieces, starts_ref, whole, sems, row):
    if pieces[0].shape[0] > row:
        copy = pltpu.make_async_copy(pieces[0].at[row:, :], whole, sems.at[0])
        copy.start()
        return copy.wait
    copies = copies_of(pieces, starts_ref, whole, sems, row)

    def each(act):
        for i, copy in copies:
            pl.when(starts_ref[2 * i] >= row)(functools.partial(act, copy))

    each(lambda copy: copy.start())
    return lambda: each(lambda copy: copy.wait())


def load_halves(pieces, starts_ref, whole, sems):
    half = whole.shape[1] // 2
    copies = []
    for i, piece in enumerate(pieces):
        rows = pl.ds(pl.multiple_of(starts_ref[2 * i], 16), piece.shape[0])
        for h in range(2):
            columns = slice(h * half, (h + 1) * half)
            source = piece.at[:, columns] if piece.shape[1] > half else piece
            copy = pltpu.make_async_copy(source, whole.at[rows, columns], sems.at[i, h])
            copies.append((h, None if piece.shape[1] > half else starts_ref[2 * i + 1] == h * half, copy))

    def each(h, act):
        for at, there, copy in copies:
            if at == h and there is None:
                act(copy)
            elif at == h:
                pl.when(there)(functools.partial(act, copy))

    return lambda h: each(h, lambda copy: copy.start()), lambda h: each(h, lambda copy: copy.wait())


IN_VMEM = pl.BlockSpec(memory_space=pltpu.VMEM)
IN_SMEM = pl.BlockSpec(memory_space=pltpu.SMEM)
ANYWHERE = pl.BlockSpec(memory_space=pl.ANY)


def upright(ref):
    return jnp.concatenate([jnp.transpose(ref[m]) for m in range(ref.shape[0])], axis=0)


def turn(chunk, cosine, sine):
    lane = lax.broadcasted_iota(jnp.int32, chunk.shape, 1)
    partner = jnp.where(
        lane % HEAD_SIZE < HALF_HEAD,
        pltpu.roll(chunk, 128 - HALF_HEAD, 1),
        pltpu.roll(chunk, HALF_HEAD, 1),
    )
    return chunk * cosine + partner * sine


def project_kernel(count, starts_ref, x_ref, gains_ref, cos_ref, sin_ref, *refs):
    pieces = refs[:count]
    q_ref, kv_ref, whole, sems = refs[count:]
    wait = load(pieces, starts_ref, whole, sems)
    x = upright(x_ref).astype(F32)
    width = x.shape[1]
    act = (x * rms_inverse(x) * gains_ref[0:1, :]).astype(BF)
    wait()
    cosine, sine = cos_ref[...], sin_ref[...]
    for first in range(0, width + KV_WIDTH, 256):
        linear = nn(act, whole[:width, first : first + 256])
        for at in range(first, first + 256, 128):
            chunk = turn(linear[:, at - first : at - first + 128], cosine, sine)
            if at + 128 <= width:
                q_ref[:, at : at + 128] = (chunk * SCALE).astype(BF)
            elif at < width:
                q_ref[:, at:width] = (chunk[:, : width - at] * SCALE).astype(BF)
                kv_ref[:, : at + 128 - width] = chunk[:, width - at :].astype(BF)
            else:
                kv_ref[:, at - width : at - width + 128] = chunk.astype(BF)
    start = width // 128 * 128
    kv_ref[:, KV_WIDTH:] = nn(act, whole[width:, start:])[:, width - start :].astype(BF)


def project(x, gains, cosine, sine, pieces, starts, shape):
    micro, width, rows = x.shape
    tokens = micro * rows
    outs = (
        jax.ShapeDtypeStruct((tokens, width), BF),
        jax.ShapeDtypeStruct((tokens, 2 * KV_WIDTH), BF),
    )
    table = pl.BlockSpec((tokens, 128), lambda i: (0, 0))
    return pl.pallas_call(
        functools.partial(project_kernel, len(pieces)),
        grid=(1,),
        name="project",
        in_specs=[IN_SMEM] + [IN_VMEM] * 2 + [table] * 2 + [ANYWHERE] * len(pieces),
        out_specs=(IN_VMEM,) * 2,
        out_shape=outs,
        scratch_shapes=[pltpu.VMEM(shape, BF), pltpu.SemaphoreType.DMA((len(pieces),))],
        cost_estimate=cost(2 * tokens * width * (width + 2 * KV_WIDTH), 0, x, *outs, *pieces),
        compiler_params=pltpu.CompilerParams(vmem_limit_bytes=VMEM_LIMIT),
    )(starts, x, gains, cosine, sine, *pieces)


def across(ref):
    return jnp.concatenate([ref[m] for m in range(ref.shape[0])], axis=1)


def spread_out(value, ref):
    rows = ref.shape[2]
    for m in range(ref.shape[0]):
        ref[m] = value[:, m * rows : (m + 1) * rows]


def feed_kernel(counts, core_ref, s0_ref, s1_ref, s2_ref, x_ref, attn_ref, cot_ref, gains_ref, *refs):
    total_count = sum(counts)
    attention_pieces = refs[: counts[0]]
    pair_pieces = refs[counts[0] : counts[0] + counts[1]]
    down_pieces = refs[counts[0] + counts[1] : total_count]
    out_ref, inner_ref, kept_ref, given_ref, act_t_ref, attn_t_ref, resid_ref = refs[total_count : total_count + 7]
    w_attn, w_pair, w_down, sum_ref, sems0, sems1, sems2 = refs[total_count + 7 :]
    width = x_ref.shape[1]
    hidden = w_pair.shape[1]
    tile = hidden // 4
    wait_attention = load_lower(attention_pieces, s0_ref, w_attn, sems0, width)
    start_pair, wait_pair = load_halves(pair_pieces, s1_ref, w_pair, sems1)
    start_pair(0)
    wait_down = load(down_pieces, s2_ref, w_down, sems2)
    start_pair(1)
    even = core_ref[0] == 0
    x = upright(x_ref).astype(F32)
    dy = upright(cot_ref)
    attn_t_ref[...] = jnp.transpose(attn_ref[...])
    wait_attention()
    resid = x + nn(attn_ref[...], w_attn[:, : rounded_up(width)])[:, :width]
    resid_t = jnp.transpose(resid)
    resid_ref[...] = resid_t
    sum_ref[...] = resid_t
    act = (resid * rms_inverse(resid) * gains_ref[1:2, :]).astype(BF)
    act_t_ref[...] = jnp.transpose(act)
    wait_pair(0)
    wait_down()
    for first in range(0, hidden, tile):
        if first == hidden // 2:
            wait_pair(1)
        here = slice(first, first + tile)
        gate = nn(act, w_pair[:width, here])
        upper = nn(act, w_pair[width:, here])
        d_inner = nn(dy, w_down[:, here])
        sigmoid = 1.0 / (1.0 + jnp.exp(-gate))
        silu = gate * sigmoid
        inner = (silu * upper).astype(BF)
        inner_ref[:, here] = inner
        d_gate = d_inner * upper * sigmoid * (1.0 + gate * (1.0 - sigmoid))
        d_upper = d_inner * silu
        kept_ref[:, here] = jnp.where(even, d_gate, d_upper).astype(BF)
        given_ref[:, here] = jnp.where(even, d_upper, d_gate).astype(BF)
        sum_ref[...] += nn(w_down[:, here], jnp.transpose(inner))
    spread_out(sum_ref[...].astype(BF), out_ref)


def feed(core, x, attn, dy, gains, attention_got, pair_got, down_got):
    micro, width, rows = x.shape
    tokens = micro * rows
    groups = [attention_got, pair_got, down_got]
    counts = [len(pieces) for pieces, _, _ in groups]
    shapes = [shape for _, _, shape in groups]
    hidden = shapes[1][1]
    outs = (jax.ShapeDtypeStruct(x.shape, BF),)
    outs += (jax.ShapeDtypeStruct((tokens, hidden), BF),) * 3
    outs += (jax.ShapeDtypeStruct((width, tokens), BF),) * 2
    outs += (jax.ShapeDtypeStruct((width, tokens), F32),)
    every = [piece for pieces, _, _ in groups for piece in pieces]
    return pl.pallas_call(
        functools.partial(feed_kernel, counts),
        name="feed",
        in_specs=[IN_SMEM] * 4 + [IN_VMEM] * 4 + [ANYWHERE] * len(every),
        out_specs=(IN_VMEM,) * 7,
        out_shape=outs,
        scratch_shapes=[pltpu.VMEM((width, shapes[0][1]), BF)]
        + [pltpu.VMEM(shape, BF) for shape in shapes[1:]]
        + [pltpu.VMEM((width, tokens), F32)]
        + [pltpu.SemaphoreType.DMA(size) for size in ((counts[0],), (counts[1], 2), (counts[2],))],
        cost_estimate=cost(
            2 * tokens * width * (4 * hidden + width), tokens * hidden, x, x, x, *outs, *every
        ),
        compiler_params=pltpu.CompilerParams(vmem_limit_bytes=VMEM_MOST),
    )(core, *(starts for _, starts, _ in groups), x, attn, dy, gains, *every)


def feed_back_kernel(counts, core_ref, s0_ref, s1_ref, resid_ref, cot_ref, kept_ref, given_ref, gain_ref, *refs):
    total_count = sum(counts)
    dres_ref, low_ref, dattn_ref, w_attn, w_pair, sems0, sems1 = refs[total_count:]
    width = resid_ref.shape[0]
    start_pair, wait_pair = load_halves(refs[counts[0] : total_count], s1_ref, w_pair, sems1)
    start_pair(0)
    start_pair(1)
    wait_attention = load_lower(refs[: counts[0]], s0_ref, w_attn, sems0, width)
    resid = resid_ref[...]
    root = lax.rsqrt(jnp.mean(resid * resid, axis=0, keepdims=True) + EPS)
    normed = resid * root
    half = w_pair.shape[1] // 2
    for h in range(2):
        columns = slice(h * half, (h + 1) * half)
        weight = lambda i: w_pair[pl.ds(pl.multiple_of(i * width, 16), width), columns]
        wait_pair(h)
        part = nt(weight(core_ref[0]), kept_ref[:, columns]) + nt(weight(1 - core_ref[0]), given_ref[:, columns])
        d_act = part if h == 0 else d_act + part
    d_normed = d_act * gain_ref[...]
    d_resid = across(cot_ref).astype(F32) + root * (
        d_normed - normed * jnp.mean(d_normed * normed, axis=0, keepdims=True)
    )
    dres_ref[...] = d_resid
    low = d_resid.astype(BF)
    low_ref[:, :width] = jnp.transpose(low)
    if low_ref.shape[1] > width:
        low_ref[:, width:] = jnp.zeros((low_ref.shape[0], low_ref.shape[1] - width), BF)
    wait_attention()
    dattn_ref[...] = jnp.transpose(nn(w_attn[:, :width], low).astype(BF))


def feed_back(core, resid, dy, kept, given, gain, attention_got, pair_got):
    width, tokens = resid.shape
    groups = [attention_got, pair_got]
    counts = [len(pieces) for pieces, _, _ in groups]
    shapes = [shape for _, _, shape in groups]
    outs = (
        jax.ShapeDtypeStruct((width, tokens), F32),
        jax.ShapeDtypeStruct((tokens, rounded_up(width)), BF),
        jax.ShapeDtypeStruct((tokens, width), BF),
    )
    every = [piece for pieces, _, _ in groups for piece in pieces]
    return pl.pallas_call(
        functools.partial(feed_back_kernel, counts),
        name="feed_back",
        in_specs=[IN_SMEM] * 3 + [IN_VMEM] * 5 + [ANYWHERE] * len(every),
        out_specs=(IN_VMEM,) * 3,
        out_shape=outs,
        scratch_shapes=[pltpu.VMEM((width, shapes[0][1]), BF), pltpu.VMEM(shapes[1], BF)]
        + [pltpu.SemaphoreType.DMA(size) for size in ((counts[0],), (counts[1], 2))],
        cost_estimate=cost(
            2 * tokens * width * (2 * shapes[1][1] + width), 0, resid, dy, kept, given, *outs, *every
        ),
        compiler_params=pltpu.CompilerParams(vmem_limit_bytes=VMEM_MOST),
    )(core, *(starts for _, starts, _ in groups), resid, dy, kept, given, gain, *every)


def pick_rows(source, starts_ref, base, rows, count, target):
    for t in range(count):
        start = pl.multiple_of(starts_ref[base + t], 16)
        target[t * rows : (t + 1) * rows, :] = source[pl.ds(start, rows), :]


def down_grad_kernel(shards, cut, info_ref, cot_ref, far_cot_ref, inner_ref, far_inner_ref, low_ref, high_ref, dy):
    micro, width, rows = cot_ref.shape
    tokens, part = micro * rows, low_ref.shape[0] // (shards // 2)
    first = pl.multiple_of(info_ref[0], 16)
    for i, ref in enumerate((cot_ref, far_cot_ref)):
        for m in range(micro):
            at = i * tokens + m * rows
            dy[:, at : at + rows] = ref[m, pl.ds(first, part), :]
    for t in range(shards):
        columns = pl.ds(pl.multiple_of(info_ref[1 + t], 128), cut)
        made = nn(dy[:, :tokens], inner_ref[:, columns]) + nn(dy[:, tokens:], far_inner_ref[:, columns])
        out_ref, at = (low_ref, t) if t < shards // 2 else (high_ref, t - shards // 2)
        out_ref[at * part : (at + 1) * part, :] = made.astype(BF)


def down_grad(cot, far_cot, inner, far_inner, first, starts):
    shards, (micro, width, rows), (tokens, hidden) = len(starts), cot.shape, inner.shape
    part, cut = width // 2, hidden // shards
    outs = (jax.ShapeDtypeStruct((shards // 2 * part, cut), BF),) * 2
    if part % 16 or cut % 128:
        grad = nn(jnp.concatenate(list(cot), axis=1), inner) + nn(jnp.concatenate(list(far_cot), axis=1), far_inner)
        grad = lax.dynamic_slice_in_dim(grad.astype(BF), first, part, 0)
        blocks = [lax.dynamic_slice_in_dim(grad, start, cut, 1) for start in starts]
        return [jnp.concatenate(blocks[: shards // 2]), jnp.concatenate(blocks[shards // 2 :])]
    return pl.pallas_call(
        functools.partial(down_grad_kernel, shards, cut),
        name="down_grad",
        in_specs=[IN_SMEM] + [IN_VMEM] * 4,
        out_specs=(IN_VMEM,) * 2,
        out_shape=outs,
        scratch_shapes=[pltpu.VMEM((part, 2 * tokens), BF)],
        cost_estimate=cost(4 * part * tokens * hidden, 0, cot, cot, inner, inner, *outs),
        compiler_params=pltpu.CompilerParams(vmem_limit_bytes=VMEM_LIMIT),
    )(numbers([first] + starts), cot, far_cot, inner, far_inner)


def wide_grad_kernel(cuts, count, starts_ref, left_ref, far_left_ref, right_ref, far_right_ref, *refs):
    outs, ordered = refs[: 2 * len(cuts)], refs[2 * len(cuts)]
    tokens = left_ref.shape[1]

    @pl.when(pl.program_id(0) == 0)
    def _():
        at = first = 0
        for cut in cuts:
            for t in range(count):
                start = pl.multiple_of(starts_ref[t] + first, 16)
                ordered[at : at + cut, :tokens] = left_ref[pl.ds(start, cut), :]
                ordered[at : at + cut, tokens:] = far_left_ref[pl.ds(start, cut), :]
                at += cut
            first += cut

    made = nn(ordered[:, :tokens], right_ref[...]) + nn(ordered[:, tokens:], far_right_ref[...])
    at = 0
    for i, out_ref in enumerate(outs):
        size = out_ref.shape[0]
        out_ref[...] = made[at : at + size].astype(BF)
        at += size


def wide_grad(left, far_left, right, far_right, rows, cuts, starts):
    count, (tokens, columns) = len(starts), right.shape
    outs = tuple(jax.ShapeDtypeStruct((count // 2 * cut, columns), BF) for cut in cuts for _ in range(2))
    if rows % 16 or any(cut % 16 for cut in cuts):
        grad = (nn(left, right) + nn(far_left, far_right)).astype(BF)
        made, first = [], 0
        for cut in cuts:
            blocks = [lax.dynamic_slice_in_dim(grad, start + first, cut, 0) for start in starts]
            made += [jnp.concatenate(blocks[: count // 2]), jnp.concatenate(blocks[count // 2 :])]
            first += cut
        return made
    tile = 512 if columns % 512 == 0 else columns
    part = pl.BlockSpec((tokens, tile), lambda n, starts: (0, n))
    whole = pl.BlockSpec(left.shape, lambda n, starts: (0, 0))
    return pl.pallas_call(
        functools.partial(wide_grad_kernel, cuts, count),
        grid_spec=pltpu.PrefetchScalarGridSpec(
            num_scalar_prefetch=1,
            grid=(columns // tile,),
            in_specs=[whole, whole, part, part],
            out_specs=tuple(pl.BlockSpec((out.shape[0], tile), lambda n, starts: (0, n)) for out in outs),
            scratch_shapes=[pltpu.VMEM((count * rows, 2 * tokens), BF)],
        ),
        out_shape=outs,
        name="wide_grad",
        cost_estimate=cost(4 * tokens * rows * count * columns, 0, left, left, right, right, *outs),
        compiler_params=pltpu.CompilerParams(vmem_limit_bytes=VMEM_LIMIT),
    )(numbers(starts), left, far_left, right, far_right)


def settle_wide_kernel(cuts, core_ref, gain_ref, *refs):
    sums = refs[: 2 * len(cuts)]
    w_left, w_right, left_ref, right_ref, sum_ref = refs[2 * len(cuts) :]
    even = core_ref[0] == 0
    at = 0
    for c, cut in enumerate(cuts):
        here = slice(at, at + cut)
        mine, theirs = sums[2 * c][...].astype(F32), sums[2 * c + 1][...].astype(F32)
        left, right = jnp.where(even, mine, theirs), jnp.where(even, theirs, mine)
        left_ref[here, :], right_ref[here, :] = left, right
        both = w_left[here, :].astype(F32) * left + w_right[here, :].astype(F32) * right
        sum_ref[here, :] = jnp.sum(both, axis=1, keepdims=True) / gain_ref[here, :]
        at += cut


def settle_wide(core, gain, sums, cuts, w_left, w_right):
    out = jax.ShapeDtypeStruct(w_left.shape, F32)
    column = jax.ShapeDtypeStruct((w_left.shape[0], 1), F32)
    if any(cut % 16 for cut in cuts):
        pairs = [(mine.astype(F32), theirs.astype(F32)) for mine, theirs in sums]
        left = jnp.concatenate([jnp.where(core[0] == 0, a, b) for a, b in pairs])
        right = jnp.concatenate([jnp.where(core[0] == 0, b, a) for a, b in pairs])
        both = w_left.astype(F32) * left + w_right.astype(F32) * right
        return left, right, jnp.sum(both, axis=1, keepdims=True) / gain
    args = [value for pair in sums for value in pair]
    return pl.pallas_call(
        functools.partial(settle_wide_kernel, cuts),
        name="settle",
        in_specs=[IN_SMEM] + [IN_VMEM] * (3 + len(args)),
        out_specs=(IN_VMEM,) * 3,
        out_shape=(out, out, column),
        cost_estimate=cost(4 * w_left.size, 0, out, out, *args),
        compiler_params=pltpu.CompilerParams(vmem_limit_bytes=VMEM_LIMIT),
    )(core, gain, *args, w_left, w_right)


def settle_some_kernel(core_ref, gain_ref, mine_ref, theirs_ref, wq_ref, wk_ref, wv_ref, *refs):
    q_ref, o_ref, k_ref, v_ref, sum_ref, kv = refs
    rows, width = q_ref.shape
    half, wide = mine_ref.shape[0], rounded_up(width)
    even = core_ref[0] == 0
    mine, theirs = mine_ref[...].astype(F32), theirs_ref[...].astype(F32)
    parts = (
        (0, jnp.where(even, mine, theirs)[: rows - half]),
        (rows - half, jnp.where(even, theirs, mine)),
    )
    for at, part in parts:
        here = slice(at, at + part.shape[0])
        q_ref[here, :] = part[:, :width]
        o_ref[here, :] = part[:, wide : wide + width]
        kv[here, :] = part[:, 2 * wide :]
        sum_ref[here, :] = jnp.sum(wq_ref[here, :].astype(F32) * part[:, :width], axis=1, keepdims=True)
    sums = sum_ref[...]
    for out_ref, w_ref, first in ((k_ref, wk_ref, 0), (v_ref, wv_ref, KV_WIDTH)):
        grad = kv[:, first : first + KV_WIDTH]
        out_ref[...] = jnp.transpose(grad)
        weight = jnp.transpose(w_ref[...]).astype(F32)
        sums += jnp.sum(weight * grad, axis=1, keepdims=True)
    sum_ref[...] = sums / gain_ref[...]


def settle_some(core, gain, mine, theirs, w_query, w_key, w_value):
    rows, width = w_query.shape
    half, wide = mine.shape[0], rounded_up(width)
    if (rows - half) % 16:
        low, high = jnp.where(core[0] == 0, mine, theirs), jnp.where(core[0] == 0, theirs, mine)
        grad = jnp.concatenate([low[: rows - half], high]).astype(F32)
        key, value = grad[:, 2 * wide : 2 * wide + KV_WIDTH], grad[:, 2 * wide + KV_WIDTH :]
        pairs = ((w_query, grad[:, :width]), (w_key.T, key), (w_value.T, value))
        sums = sum(jnp.sum(w.astype(F32) * g, axis=1, keepdims=True) for w, g in pairs)
        return grad[:, :width], grad[:, wide : wide + width], key.T, value.T, sums / gain
    outs = (jax.ShapeDtypeStruct((rows, width), F32),) * 2
    outs += (jax.ShapeDtypeStruct((KV_WIDTH, rows), F32),) * 2
    outs += (jax.ShapeDtypeStruct((rows, 1), F32),)
    return pl.pallas_call(
        settle_some_kernel,
        name="settle_some",
        in_specs=[IN_SMEM] + [IN_VMEM] * 6,
        out_specs=(IN_VMEM,) * 5,
        out_shape=outs,
        scratch_shapes=[pltpu.VMEM((rows, 2 * KV_WIDTH), F32)],
        cost_estimate=cost(4 * w_query.size, 0, mine, theirs, *outs),
        compiler_params=pltpu.CompilerParams(vmem_limit_bytes=VMEM_LIMIT),
    )(core, gain, mine, theirs, w_query, w_key, w_value)


def turn_keys(source, target, at, cosine, sine):
    rows = source.shape[0]
    for first in range(0, KV_WIDTH, 128):
        chunk = turn(source[:, first : first + 128].astype(F32), cosine, -sine).astype(BF)
        last = min(first + 128, KV_WIDTH)
        target[at : at + rows, first:last] = chunk[:, : last - first]
    target[at : at + rows, KV_WIDTH:] = source[:, KV_WIDTH:]


def attention_grad_kernel(shards, half, starts_ref, gain_ref, cos_ref, sin_ref, dq_ref, attn_ref, low_ref, *refs):
    xs, halves = refs[:shards], refs[shards : shards + 2]
    dkvs = [ref.at[t] for ref in halves for t in range(shards // 2)]
    outs, (act, dkv, ordered, attn_ordered) = refs[shards + 2 : shards + 4], refs[shards + 4 :]
    micro, width, rows = xs[0].shape
    tokens = micro * rows
    wide = rounded_up(width)
    for t in range(shards):
        here = slice(t * tokens, (t + 1) * tokens)
        turn_keys(dkvs[t], dkv, t * tokens, cos_ref[here, :], sin_ref[here, :])
        for m in range(micro):
            x = xs[t][m].astype(F32)
            root = lax.rsqrt(jnp.mean(x * x, axis=0, keepdims=True) + EPS)
            first = t * tokens + m * rows
            act[:, first : first + rows] = (x * root * gain_ref[...]).astype(BF)
    for i, out_ref in enumerate(outs):
        pick_rows(act, starts_ref, i * shards, half, shards, ordered)
        pick_rows(attn_ref, starts_ref, i * shards, half, shards, attn_ordered)
        out_ref[:, :wide] = nn(ordered[:, :tokens], dq_ref[...]).astype(BF)
        out_ref[:, wide : 2 * wide] = nn(attn_ordered[...], low_ref[...]).astype(BF)
        out_ref[:, 2 * wide :] = nn(ordered[...], dkv[...]).astype(BF)


def attention_grad(x_all, gain, cosine, sine, dq, attn_t, low, dkv_all, half, given, kept):
    shards = len(x_all)
    micro, width, rows = x_all[0].shape
    every = shards * micro * rows
    wide = rounded_up(width)
    out = jax.ShapeDtypeStruct((shards * half, 2 * wide + 2 * KV_WIDTH), BF)
    if half % 16 or width // shards % 16:
        xs = jnp.concatenate([x[m] for x in x_all for m in range(micro)], axis=1).astype(F32)
        act = xs * lax.rsqrt(jnp.mean(xs * xs, axis=0, keepdims=True) + EPS) * gain
        act = act.astype(BF)
        dkv = jnp.concatenate(dkv_all, axis=0).reshape(every, 2 * KV_WIDTH)
        keys = dkv[:, :KV_WIDTH].astype(F32).reshape(every, -1, 2, HALF_HEAD)
        c, s = cosine[:, None, :HALF_HEAD], sine[:, None, HALF_HEAD:HEAD_SIZE]
        first, second = keys[:, :, 0], keys[:, :, 1]
        keys = jnp.stack([first * c + second * s, second * c - first * s], axis=2)
        dkv = jnp.concatenate([keys.reshape(every, KV_WIDTH).astype(BF), dkv[:, KV_WIDTH:]], axis=1)
        parts = [nn(act[:, : micro * rows], dq), nn(attn_t, low), nn(act, dkv)]
        grad = jnp.concatenate(parts, axis=1).astype(BF)
        return [
            jnp.concatenate([lax.dynamic_slice_in_dim(grad, start, half, 0) for start in starts])
            for starts in (given, kept)
        ]
    return pl.pallas_call(
        functools.partial(attention_grad_kernel, shards, half),
        name="attention_grad",
        in_specs=[IN_SMEM] + [IN_VMEM] * (8 + shards),
        out_specs=(IN_VMEM,) * 2,
        out_shape=(out, out),
        scratch_shapes=[
            pltpu.VMEM((width, every), BF),
            pltpu.VMEM((every, 2 * KV_WIDTH), BF),
            pltpu.VMEM((shards * half, every), BF),
            pltpu.VMEM((shards * half, micro * rows), BF),
        ],
        cost_estimate=cost(
            4 * shards * half * (every * 2 * KV_WIDTH + 2 * micro * rows * width),
            0,
            *x_all,
            *dkv_all,
            out,
            out,
        ),
        compiler_params=pltpu.CompilerParams(vmem_limit_bytes=VMEM_MOST),
    )(numbers(given + kept), gain, cosine, sine, dq, attn_t, low, *x_all, *dkv_all)


def finish_kernel(count, starts_ref, x_ref, low_ref, kv_ref, dres_ref, gain_ref, cos_ref, sin_ref, *refs):
    pieces = refs[:count]
    dx_ref, whole, kv_turned, sems = refs[count:]
    wait = load(pieces, starts_ref, whole, sems)
    turn_keys(kv_ref, kv_turned, 0, cos_ref[...], sin_ref[...])
    x = across(x_ref).astype(F32)
    width = x.shape[0]
    root = lax.rsqrt(jnp.mean(x * x, axis=0, keepdims=True) + EPS)
    normed = x * root
    wait()
    d_act = nt(whole[:width, :width], low_ref[:, :width])
    d_act += nt(whole[:width, width:], kv_turned[:, :KV_WIDTH])
    d_act += nt(whole[width:, width:], kv_turned[:, KV_WIDTH:])
    d_normed = d_act * gain_ref[...]
    d_x = dres_ref[...] + root * (d_normed - normed * jnp.mean(d_normed * normed, axis=0, keepdims=True))
    spread_out(d_x.astype(BF), dx_ref)


def finish(x, low, kv, dres, gain, cosine, sine, pieces, starts, shape):
    micro, width, rows = x.shape
    tokens = micro * rows
    table = pl.BlockSpec((tokens, 128), lambda i: (0, 0))
    return pl.pallas_call(
        functools.partial(finish_kernel, len(pieces)),
        grid=(1,),
        name="finish",
        in_specs=[IN_SMEM] + [IN_VMEM] * 5 + [table] * 2 + [ANYWHERE] * len(pieces),
        out_specs=IN_VMEM,
        out_shape=jax.ShapeDtypeStruct(x.shape, BF),
        scratch_shapes=[
            pltpu.VMEM(shape, BF),
            pltpu.VMEM((tokens, 2 * KV_WIDTH), BF),
            pltpu.SemaphoreType.DMA((len(pieces),)),
        ],
        cost_estimate=cost(2 * tokens * width * (width + 2 * KV_WIDTH), 0, x, low, dres, *pieces),
        compiler_params=pltpu.CompilerParams(vmem_limit_bytes=VMEM_LIMIT),
    )(starts, x, low, kv, dres, gain, cosine, sine, *pieces)


def head(ref, h):
    return ref[:, h * HEAD_SIZE : (h + 1) * HEAD_SIZE]


def widen(value, columns):
    n = value.shape[0]
    lane = lax.broadcasted_iota(jnp.int32, (n, HEAD_SIZE), 1)
    tail = jnp.zeros((n, HEAD_SIZE), F32)
    for c, column in enumerate(columns):
        tail = jnp.where(lane == c, column, tail)
    return jnp.concatenate([value, tail.astype(BF)], axis=1)


def split(column):
    high = column.astype(BF).astype(F32)
    middle = (column - high).astype(BF).astype(F32)
    return [high, middle, column - high - middle]


def attend_kernel(shards, seg_rows, q_ref, *refs):
    kv = refs[:shards]
    bias_ref = refs[shards]
    o_ref, lse_ref = refs[-2:]
    rows = q_ref.shape[0]
    i = lax.broadcasted_iota(jnp.int32, (rows, rows), 0)
    j = lax.broadcasted_iota(jnp.int32, (rows, rows), 1)
    same = (i // seg_rows) == (j // seg_rows)
    own = jnp.where(j > i, CLOSED, jnp.where(same, 0.0, bias_ref[0:1, :]))
    one = jnp.ones((rows, 1), F32)
    bias_columns = jnp.transpose(bias_ref[...])
    lse = jnp.zeros((rows, 128), F32)
    lane = lax.broadcasted_iota(jnp.int32, (rows, 128), 1)
    for g in range(KEY_VALUE_HEADS):
        keys, values = [], []
        for t in range(shards):
            keys.append(widen(head(kv[t], g), [bias_columns[:, t : t + 1]] if t else []))
            values.append(widen(head(kv[t], KEY_VALUE_HEADS + g), [one]))
        for h in range(g * GROUP, g * GROUP + GROUP):
            q = widen(head(q_ref, h), [one])
            scores = [nt(q, k) for k in keys]
            scores[0] = scores[0] + own
            peak = functools.reduce(jnp.maximum, scores)
            peak = jnp.max(peak, axis=1, keepdims=True)
            terms = [nn(jnp.exp(s - peak).astype(BF), v) for s, v in zip(scores, values)]
            mixed = sum(terms[1:], terms[0])
            total = mixed[:, HEAD_SIZE : HEAD_SIZE + 1]
            o_ref[:, h * HEAD_SIZE : (h + 1) * HEAD_SIZE] = (mixed[:, :HEAD_SIZE] / total).astype(BF)
            lse = jnp.where(lane == h, peak + jnp.log(total), lse)
    lse_ref[...] = lse


def attend_back_kernel(shards, seg_rows, q_ref, *refs):
    kv = refs[:shards]
    bias_ref, o_ref, do_ref, lse_ref, cos_ref, sin_ref = refs[shards : shards + 6]
    dq_ref, low_ref, high_ref = refs[-3:]
    dkv = [ref.at[t] for ref in (low_ref, high_ref) for t in range(shards // 2)]
    rows = q_ref.shape[0]
    i = lax.broadcasted_iota(jnp.int32, (rows, rows), 1)
    j = lax.broadcasted_iota(jnp.int32, (rows, rows), 0)
    bias_columns = jnp.transpose(bias_ref[...])
    same = (i // seg_rows) == (j // seg_rows)
    own_column = jnp.broadcast_to(bias_columns[:, 0:1], (rows, rows))
    own = jnp.where(j > i, CLOSED, jnp.where(same, 0.0, own_column))
    one, zero = jnp.ones((rows, 1), F32), jnp.zeros((rows, 1), F32)
    cosine, sine = cos_ref[...], sin_ref[...]
    if dq_ref.shape[1] > QUERY_HEADS * HEAD_SIZE:
        dq_ref[:, QUERY_HEADS * HEAD_SIZE :] = jnp.zeros((rows, dq_ref.shape[1] - QUERY_HEADS * HEAD_SIZE), BF)
    for g in range(KEY_VALUE_HEADS):
        keys, values, turned = [], [], []
        for t in range(shards):
            k = head(kv[t], g)
            turned.append(jnp.transpose(k))
            keys.append(widen(k, [bias_columns[:, t : t + 1] if t else zero, one, one, one]))
            values.append(widen(head(kv[t], KEY_VALUE_HEADS + g), [one, one, one]))
        dk, dv = [None] * shards, [None] * shards
        for h in range(g * GROUP, g * GROUP + GROUP):
            q, do = head(q_ref, h), head(do_ref, h)
            centre = jnp.sum(head(o_ref, h).astype(F32) * do.astype(F32), axis=1, keepdims=True)
            q_wide = widen(q, [one] + split(-lse_ref[:, h : h + 1]))
            do_wide = widen(do, split(-centre))
            dq = None
            for t in range(shards):
                scores = nt(keys[t], q_wide)
                if t == 0:
                    scores = scores + own
                probs = jnp.exp(scores)
                ds = (probs * nt(values[t], do_wide)).astype(BF)
                v_term = nn(probs.astype(BF), do)
                k_term = nn(ds, q)
                q_term = nn(turned[t], ds)
                dv[t] = v_term if dv[t] is None else dv[t] + v_term
                dk[t] = k_term if dk[t] is None else dk[t] + k_term
                dq = q_term if dq is None else dq + q_term
            dq = dq * SCALE
            first, second = dq[:HALF_HEAD], dq[HALF_HEAD:]
            back = jnp.concatenate(
                [first * cosine + second * sine, second * cosine - first * sine], axis=0
            )
            dq_ref[:, h * HEAD_SIZE : (h + 1) * HEAD_SIZE] = jnp.transpose(back.astype(BF))
        for t in range(shards):
            dkv[t][:, g * HEAD_SIZE : (g + 1) * HEAD_SIZE] = dk[t].astype(BF)
            g_value = KEY_VALUE_HEADS + g
            dkv[t][:, g_value * HEAD_SIZE : (g_value + 1) * HEAD_SIZE] = dv[t].astype(BF)


def attend(micro, seg_rows, q, kv, bias):
    shards, tokens, width = len(kv), q.shape[0], q.shape[1]
    rows = tokens // micro
    here = lambda w: pl.BlockSpec((rows, w), lambda m: (m, 0))
    outs = (jax.ShapeDtypeStruct((tokens, width), BF), jax.ShapeDtypeStruct((tokens, 128), F32))
    pairs = tokens * rows * shards * QUERY_HEADS
    return pl.pallas_call(
        functools.partial(attend_kernel, shards, seg_rows),
        grid=(micro,),
        name="attend",
        in_specs=[here(width)]
        + [here(2 * KV_WIDTH)] * shards
        + [pl.BlockSpec((None,) + bias.shape[1:], lambda m: (m, 0, 0))],
        out_specs=(here(width), here(128)),
        out_shape=outs,
        cost_estimate=cost(16 * HEAD_SIZE * pairs, pairs, q),
        compiler_params=pltpu.CompilerParams(vmem_limit_bytes=VMEM_LIMIT),
    )(q, *kv, bias)


def attend_back(m, rows, seg_rows, q, kv, bias, o, do, lse, cosine, sine, earlier):
    shards, tokens, width = len(kv), q.shape[0], q.shape[1]
    here = lambda w: pl.BlockSpec((rows, w), lambda i: (m, 0))
    turned = pl.BlockSpec((HALF_HEAD, rows), lambda i: (0, m))
    outs = (jax.ShapeDtypeStruct((tokens, rounded_up(width)), BF),)
    outs += (jax.ShapeDtypeStruct((shards // 2, tokens, 2 * KV_WIDTH), BF),) * 2
    pieces = pl.BlockSpec((shards // 2, rows, 2 * KV_WIDTH), lambda i: (0, m, 0))
    pairs = rows * rows * shards * QUERY_HEADS
    return pl.pallas_call(
        functools.partial(attend_back_kernel, shards, seg_rows),
        grid=(1,),
        name="attend_back",
        in_specs=[here(width)]
        + [here(2 * KV_WIDTH)] * shards
        + [pl.BlockSpec((None,) + bias.shape[1:], lambda i: (m, 0, 0))]
        + [here(width), here(width), here(128), turned, turned]
        + [pl.BlockSpec(memory_space=pl.ANY)] * len(earlier),
        out_specs=(here(rounded_up(width)), pieces, pieces),
        out_shape=outs,
        input_output_aliases={shards + 7 + i: i for i in range(len(earlier))},
        cost_estimate=cost(40 * HEAD_SIZE * pairs, pairs, q),
        compiler_params=pltpu.CompilerParams(vmem_limit_bytes=VMEM_LIMIT),
    )(q, *kv, bias, o, do, lse, cosine, sine, *earlier)


def local(
    block_input,
    parent_ids,
    w_query,
    key_weight,
    value_weight,
    w_output,
    w_gate,
    w_up,
    w_down,
    norm_first,
    norm_second,
    out_cotangent,
):
    micro, rows, width = block_input.shape
    shards = lax.axis_size("shard")
    links = Links(lax.axis_size("rep"), shards)
    tree = rows * shards
    segs = parent_ids.shape[2]
    seg_rows = tree // segs
    tokens = micro * rows
    hidden = w_gate.shape[1]

    inputs = block_input.swapaxes(1, 2)
    cotangent = out_cotangent.swapaxes(1, 2)

    even = links.core == 0
    side = lax.axis_index("rep") // 2 % 2
    left = jnp.concatenate([w_query, key_weight], axis=1)
    right = jnp.concatenate([w_output, value_weight], axis=1)
    attn_mine = jnp.where(even, left, right)
    pair_cut = hidden // 2
    pair_mine = lax.dynamic_slice_in_dim(jnp.where(even, w_gate, w_up), side * pair_cut, pair_cut, 1)
    down_own = w_down.T
    down_cut = width // 2
    down_mine = lax.dynamic_slice_in_dim(down_own, links.core * down_cut, down_cut, 0)
    core = numbers([links.core])

    attn_near = links.near(attn_mine)
    gain_pieces = links.small_pieces(jnp.stack([norm_first, norm_second]))
    attn_mine, attn_near, gain_pieces, pair_mine, down_mine = meet(
        attn_mine, attn_near, gain_pieces, pair_mine, down_mine
    )

    gains = links.in_order(gain_pieces).astype(F32)
    attn_all = links.far(attn_mine, attn_near)
    attn_swapped = {t: links.swap(attn_near[t]) for t in attn_near}
    pair_near = {1: links.step(pair_mine, 0)}
    parents = parent_ids[:, 0]
    seg = jnp.arange(segs)
    after_parent = jnp.concatenate([parents[:, 1:], jnp.full((micro, 1), -1, parents.dtype)], axis=1)
    on_path = (seg % 2 == 0)[None] | (after_parent == seg[None])
    below = (seg[None, :] < seg[:, None])[None]
    depth = jnp.sum(jnp.where(below, on_path.astype(F32)[:, None, :], 0.0), axis=-1)

    def row_numbers(hop):
        return (links.shard ^ hop) * rows + jnp.arange(rows)

    def pick(table, numbers):
        hit = (numbers // seg_rows)[..., None] == seg
        return jnp.sum(jnp.where(hit[None], table.reshape(micro, *(1,) * numbers.ndim, segs), 0), axis=-1)

    key_rows = jnp.stack([row_numbers(hop) for hop in links.hops])
    positions = pick(depth, key_rows) * seg_rows + (key_rows % seg_rows).astype(F32)
    freqs = jnp.exp(-math.log(10000.0) * jnp.arange(HALF_HEAD, dtype=F32) * (2.0 / HEAD_SIZE))
    angles = freqs[:, None] * positions.swapaxes(0, 1).reshape(1, shards * tokens)
    cosine_t, sine_t = jnp.cos(angles), jnp.sin(angles)
    cosine = jnp.tile(cosine_t.T, (1, 4))
    sine = jnp.tile(jnp.concatenate([-sine_t.T, sine_t.T], axis=1), (1, 2))
    open_key = (pick(on_path.astype(F32), key_rows) > 0.5) & (
        (key_rows < links.shard * rows) | (jnp.arange(shards) == 0)[:, None]
    )
    bias = jnp.where(open_key, 0.0, CLOSED)
    bias = jnp.pad(bias, ((0, 0), (0, 8 - shards), (0, 0)))

    gain_one, gain_two = gains[0][:, None], gains[1][:, None]
    tables = (cosine, sine, cosine_t, sine_t, bias, gains, gain_one, gain_two)
    attn_all, attn_swapped, pair_mine, pair_near, down_mine, tables = meet(
        attn_all, attn_swapped, pair_mine, pair_near, down_mine, tables
    )
    cosine, sine, cosine_t, sine_t, bias, gains, gain_one, gain_two = tables

    for t in range(1, shards):
        if t not in attn_swapped:
            attn_swapped[t] = links.swap(attn_all[t])
    shard_rows = width // shards

    def pair_place(weight, hop):
        return weight * width + (links.shard ^ hop) * shard_rows

    pieces, starts = [left, right], [(pair_place(0, 0), 0), (pair_place(1, 0), 0)]
    for t in range(1, shards):
        pieces += [attn_all[t], attn_swapped[t]]
        starts += [
            (pair_place(links.core, links.hops[t]), 0),
            (pair_place(1 - links.core, links.hops[links.twin(t)]), 0),
        ]
    attention_got = joined(pieces, starts, (2 * width, left.shape[1]))
    pair_near |= {1 << i: links.step(pair_mine, i) for i in range(1, links.bits)}
    pair_beside = {1: links.beside(pair_near[1])}
    down_near = {1: links.step(down_mine, 0)}
    queries, kv = project(inputs, gains, cosine, sine, *attention_got)
    queries, kv, pair_mine, pair_near, pair_beside, down_mine, down_near = meet(
        queries, kv, pair_mine, pair_near, pair_beside, down_mine, down_near
    )

    kv_near = links.near(kv)
    pair_beside |= {t: links.beside(pair_near[t]) for t in pair_near if t > 1}
    kv_near, kv, pair_beside, pair_near, pair_mine = meet(kv_near, kv, pair_beside, pair_near, pair_mine)

    kv_all = links.far(kv, kv_near)
    pair_all = links.far(pair_mine, pair_near)
    pair_swapped = {t: links.swap(pair_near[t]) for t in pair_near}
    pair_crossed = {t: links.swap(pair_beside[t]) for t in pair_beside}
    kv_all, pair_all, pair_swapped, pair_crossed, pair_beside, down_mine, down_near = meet(
        kv_all, pair_all, pair_swapped, pair_crossed, pair_beside, down_mine, down_near
    )

    down_near |= {1 << i: links.step(down_mine, i) for i in range(1, links.bits)}
    down_all = links.far(down_mine, down_near)
    pair_beside |= {t: links.beside(pair_all[t]) for t in range(1, shards) if t not in pair_beside}
    attn, lse = attend(micro, seg_rows, queries, kv_all, bias)
    pair_swapped |= {t: links.swap(pair_all[t]) for t in range(1, shards) if t not in pair_swapped}
    attn, lse, down_all, pair_beside, pair_all, pair_swapped = meet(
        attn, lse, down_all, pair_beside, pair_all, pair_swapped
    )

    pair_crossed |= {t: links.swap(pair_beside[t]) for t in range(1, shards) if t not in pair_crossed}
    down_swapped = [None] + [links.swap(down_all[t]) for t in range(1, shards)]
    pieces, starts = [w_gate, w_up], [(pair_place(0, 0), 0), (pair_place(1, 0), 0)]
    for t in range(1, shards):
        pieces += [pair_all[t], pair_beside[t], pair_swapped[t], pair_crossed[t]]
        for row in (
            pair_place(links.core, links.hops[t]),
            pair_place(1 - links.core, links.hops[links.twin(t)]),
        ):
            starts += [(row, side * pair_cut), (row, (1 - side) * pair_cut)]
    pair_got = joined(pieces, starts, (2 * width, hidden))
    own = w_down.shape[0]
    pieces, starts = [down_own], [(0, links.shard * own)]
    for t in range(1, shards):
        pieces += [down_all[t], down_swapped[t]]
        starts += [
            (links.core * down_cut, (links.shard ^ links.hops[t]) * own),
            ((1 - links.core) * down_cut, (links.shard ^ links.hops[links.twin(t)]) * own),
        ]
    down_got = joined(pieces, starts, (width, own * shards))
    attn, pair_pieces, down_pieces = meet(attn, pair_got[0], down_got[0])
    pair_got, down_got = (pair_pieces, *pair_got[1:]), (down_pieces, *down_got[1:])

    plan = Plan()
    have = lambda *names: [plan.have[name] for name in names]
    x_near = links.near(inputs)
    far_cotangent = links.swap(cotangent)
    made = feed(core, inputs, attn, cotangent, gains, attention_got, pair_got, down_got)
    names = ("out", "inner", "kept", "given", "act", "attn_t", "resid")
    plan.have = dict(zip(names, made)) | {"x_near": x_near, "far_dy": far_cotangent, "queries": queries, "kv": kv_all, "lse": lse, "attn": attn}
    plan.close()

    half, mine, theirs = links.half_rows(shard_rows)
    some_kept, some_given = links.order(shard_rows, mine, theirs)
    cuts = (-(-shard_rows // 32) * 16, shard_rows - -(-shard_rows // 32) * 16)

    plan.have["x_all"] = links.far(inputs, plan.have.pop("x_near"))
    for name in ("inner", "act", "given"):
        plan.have["far_" + name] = links.swap(plan.have[name])
    names = ("d_resid", "low", "d_attn")
    resid, kept, given = have("resid", "kept", "given")
    plan.have |= dict(zip(names, feed_back(core, resid, cotangent, kept, given, gain_two, attention_got, pair_got)))
    plan.close()

    names = ("down.low", "down.high")
    far_dy, inner, far_inner = have("far_dy", "inner", "far_inner")
    starts = [(links.shard ^ hop) * own for hop in links.hops]
    plan.have |= dict(zip(names, down_grad(cotangent, far_dy, inner, far_inner, links.core * down_cut, starts)))
    plan.close()

    for name in ("down", "wide0", "wide1", "some"):
        plan.start(name, links.reduce(plan, name, name == "some"))
    plan.advance("down")
    names = ("wide0.low", "wide0.high", "wide1.low", "wide1.high")
    act, far_act, kept, far_kept = have("act", "far_act", "kept", "far_given")
    starts = [(links.shard ^ hop) * shard_rows for hop in links.hops]
    plan.have |= dict(zip(names, wide_grad(act, far_act, kept, far_kept, shard_rows, cuts, starts)))
    plan.close()

    made = ()
    hops = [("down", "wide0"), ("down", "wide0", "wide1")]
    for m in range(micro):
        plan.advance(*hops[min(m, 1)])
        q, kv_now, o, do, lse_now = have("queries", "kv", "attn", "d_attn", "lse")
        made = attend_back(m, rows, seg_rows, q, kv_now, bias, o, do, lse_now, cosine_t, sine_t, made)
        plan.have["attn_grads"] = made = tuple(made)
        plan.close()
        made = plan.have["attn_grads"]

    d_queries, *d_kv = plan.have.pop("attn_grads")
    plan.have["dkv.pieces"] = d_kv
    plan.have["d_queries"] = d_queries
    plan.start("dkv", links.collect(plan, "dkv"))
    plan.advance("dkv", "wide0", "wide1", "down")
    given, kept = attention_grad(
        plan.have["x_all"],
        gain_one,
        cosine,
        sine,
        d_queries,
        *have("attn_t", "low"),
        d_kv,
        half,
        some_given,
        some_kept,
    )
    plan.have["some.given"], plan.have["some.kept"] = given, kept
    plan.close()

    def settle():
        have, done = plan.have, plan.have.setdefault("done", {})
        if "dkv" in have and "d_input" not in done:
            done["d_input"] = finish(
                inputs, have["d_queries"], have["dkv"], have["d_resid"], gain_one, cosine, sine, *attention_got
            )
        if "down" in have and "down" not in done:
            done["down"] = links.finish_rows(*have["down"], width).T
        if "wide0" in have and "wide1" in have and "gate" not in done:
            done["gate"], done["upper"], gain = settle_wide(
                core,
                norm_second.astype(F32)[:, None],
                (have["wide0"], have["wide1"]),
                cuts,
                w_gate,
                w_up,
            )
            done["gain_two"] = gain[:, 0]
        if "some" in have and "query" not in done:
            done["query"], done["output"], key, value, gain = settle_some(
                core,
                norm_first.astype(F32)[:, None],
                *have["some"],
                w_query,
                key_weight.T,
                value_weight.T,
            )
            done["key"], done["value"], done["gain_one"] = key.T, value.T, gain[:, 0]

    order, rounds = [], 0
    while plan.tasks:
        plan.advance(*(order.pop(0) if order else tuple(plan.tasks)))
        plan.advance(*{0: ('some',), 1: ('some',)}.get(rounds, ()))
        settle()
        rounds += 1
        if rounds <= 2 and plan.tasks:
            plan.close()

    done = plan.have["done"]
    return (
        plan.have["out"].swapaxes(1, 2),
        done["d_input"].swapaxes(1, 2),
        *(done[name] for name in ("query", "key", "value", "output", "gate", "upper", "down")),
        done["gain_one"],
        done["gain_two"],
    )


def solution(mesh):
    rows = P(None, AXES, None)
    weight, gain = P("shard", None), P("shard")
    return jax.shard_map(
        local,
        mesh=mesh,
        in_specs=(rows, P(None, "rep", None)) + (weight,) * 7 + (gain, gain, rows),
        out_specs=(rows, rows) + (weight,) * 7 + (gain, gain),
        check_vma=False,
    )
```

```python
import functools
import math

import jax
import jax.numpy as jnp
from jax import lax
from jax.experimental import pallas as pl
from jax.experimental.pallas import tpu as pltpu
from jax.sharding import PartitionSpec as P

QUERY_HEADS = 15
KEY_VALUE_HEADS = 5
HEAD_SIZE = 64
HALF_HEAD = HEAD_SIZE // 2
GROUP = QUERY_HEADS // KEY_VALUE_HEADS
KV_WIDTH = KEY_VALUE_HEADS * HEAD_SIZE
SCALE = HEAD_SIZE ** (-0.5)
EPS = 1e-05
AXES = ("rep", "shard")
BF = jnp.bfloat16
F32 = jnp.float32
CLOSED = -1e30
VMEM_LIMIT = 32 << 20
VMEM_MOST = 60 << 20


def dot(a, b, dims):
    return lax.dot_general(a, b, (dims, ((), ())), preferred_element_type=F32)


def nn(a, b):
    return dot(a, b, ((1,), (0,)))


def nt(a, b):
    return dot(a, b, ((1,), (1,)))


def tn(a, b):
    return dot(a, b, ((0,), (0,)))


def total(parts):
    return sum(part.astype(F32) for part in parts).astype(parts[0].dtype)


def meet(*values):
    return lax.optimization_barrier(values)


def rounded_up(columns):
    return -(-columns // 128) * 128


def rms_inverse(x):
    return lax.rsqrt(jnp.mean(x * x, axis=-1, keepdims=True) + EPS)


def cost(flops, exps, *arrays):
    size = sum(a.size * a.dtype.itemsize for a in arrays)
    return pl.CostEstimate(flops=flops, transcendentals=exps, bytes_accessed=size)


class Links:
    def __init__(self, reps, shards):
        self.reps, self.shards = reps, shards
        self.core = lax.axis_index("rep") % 2
        self.shard = lax.axis_index("shard")
        self.bits = shards.bit_length() - 1
        even = [1 << i for i in range(self.bits)]
        odd = even[:2][::-1] + even[2:]
        self.steps = list(zip(even, odd))
        self.hops = []
        for piece in range(shards):
            sums = [0, 0]
            for i, step in enumerate(self.steps):
                if piece >> i & 1:
                    sums = [sums[0] ^ step[0], sums[1] ^ step[1]]
            self.hops.append(jnp.where(self.core == 0, sums[0], sums[1]))

    def move(self, value, target):
        pairs = []
        for r in range(self.reps):
            for s in range(self.shards):
                goal = target(r, s)
                if goal is not None:
                    pairs.append((r * self.shards + s, goal[0] * self.shards + goal[1]))
        return lax.ppermute(value, AXES, pairs)

    def step(self, value, i):
        return self.move(value, lambda r, s: (r, s ^ self.steps[i][r % 2]))

    def swap(self, value):
        return self.move(value, lambda r, s: (r ^ 1, s))

    def reduce(self, plan, name, quick=False):
        top = self.bits
        if name + ".given" in plan.have:
            got = yield self.swap(plan.have.pop(name + ".given"))
            sums = [plan.have.pop(name + ".kept"), got]
        else:
            got = yield self.step(plan.have.pop(name + ".high"), top - 1)
            sums = [plan.have.pop(name + ".low"), got]
            top -= 1
        for i in reversed(range(top)):
            block = sums[0].shape[0] // 2
            got = yield self.step(total([part[block:] for part in sums]), i)
            sums = [part[:block] for part in sums] + [got]
        value = total(sums)
        chips = self.reps // 2
        place = lax.axis_index("rep") // 2
        span = 1
        if chips % 4 == 0 and quick and value.shape[0] % 4 == 0:
            quarter = value.shape[0] // 4
            across = lambda value, j: self.move(value, lambda r, s: (r ^ (2 * j), s))
            cut = lambda j: lax.dynamic_slice_in_dim(value, (place % 4 ^ j) * quarter, quarter, 0)
            got = yield [across(cut(j), j) for j in range(1, 4)]
            mine = total([cut(0)] + got)
            got = yield [across(mine, j) for j in range(1, 4)]
            parts = jnp.stack([mine] + got).reshape(2, 2, quarter, -1)
            parts = jnp.where(place % 4 >= 2, parts[::-1], parts)
            parts = jnp.where(place % 2 == 1, parts[:, ::-1], parts)
            value = parts.reshape(4 * quarter, -1)
            span = 4
        elif chips % 4 == 0:
            inward, outward, middle = {0: 1, 3: 2}, {1: 0, 2: 3}, {1: 2, 2: 1}

            def along(value, table):
                def target(r, s):
                    chip = r // 2
                    if chip % 4 not in table:
                        return None
                    return ((chip - chip % 4 + table[chip % 4]) * 2 + r % 2, s)

                return self.move(value, target)

            value = total([value, (yield along(value, inward))])
            value = total([value, (yield along(value, middle))])
            back = yield along(value, outward)
            inner = (place % 4 == 1) | (place % 4 == 2)
            value = jnp.where(inner, value, back)
            span = 4
        while span < chips:
            value = total([value, self.move(value, lambda r, s: (r ^ (2 * span), s))])
            span *= 2
        other = yield self.swap(value)
        plan.have[name] = (value, other)

    def collect(self, plan, name):
        low, high = plan.have[name + ".pieces"]
        got = yield self.step(high, self.bits - 1)
        sums = [low, got]
        for i in reversed(range(self.bits - 1)):
            block = sums[0].shape[0] // 2
            got = yield self.step(total([part[block:] for part in sums]), i)
            sums = [part[:block] for part in sums] + [got]
        plan.have[name] = total(sums)[0]

    def beside(self, value):
        return self.move(value, lambda r, s: (r ^ 2, s))

    def near(self, value):
        return {1 << i: self.step(value, i) for i in range(self.bits)}

    def far(self, value, near):
        pieces = [value]
        for t in range(1, self.shards):
            top = t.bit_length() - 1
            pieces.append(near[t] if t in near else self.step(pieces[t - (1 << top)], top))
        return pieces

    def twin(self, piece):
        return piece if self.bits < 2 else piece >> 2 << 2 | (piece & 1) << 1 | (piece >> 1 & 1)

    def small_pieces(self, value):
        return [
            value if hop == 0 else self.move(value, lambda r, s, hop=hop: (r, s ^ hop))
            for hop in range(self.shards)
        ]

    def in_order(self, pieces):
        pieces = jnp.stack(pieces)
        value = pieces
        order = self.shard ^ jnp.arange(self.shards)
        hit = (order[:, None] == jnp.arange(self.shards)[None, :])[:, :, None, None]
        pieces = jnp.sum(jnp.where(hit, pieces[None], 0), axis=1, dtype=value.dtype)
        return jnp.concatenate([pieces[j] for j in range(self.shards)], axis=-1)

    def half_rows(self, rows):
        half = -(-rows // 32) * 16
        return half, self.core * (rows - half), (1 - self.core) * (rows - half)

    def order(self, scale, mine, theirs):
        kept = [(self.shard ^ hop) * scale + mine for hop in self.hops]
        given = [(self.shard ^ self.hops[self.twin(t)]) * scale + theirs for t in range(self.shards)]
        return kept, given

    def finish_rows(self, owned, other, rows):
        low = jnp.where(self.core == 0, owned, other)
        high = jnp.where(self.core == 0, other, owned)
        return jnp.concatenate([low[: rows - owned.shape[0]], high], axis=0).astype(F32)


class Plan:
    def __init__(self):
        self.have, self.tasks, self.made = {}, {}, {}

    def start(self, name, task):
        self.tasks[name] = task
        self.made[name] = None

    def advance(self, *names):
        for name in names:
            if name in self.tasks:
                try:
                    self.made[name] = self.tasks[name].send(self.made[name])
                except StopIteration:
                    del self.tasks[name], self.made[name]

    def close(self):
        self.have, self.made = lax.optimization_barrier((self.have, self.made))


def joined(pieces, starts, shape):
    if any(piece.shape[0] % 16 or piece.shape[1] % 128 and piece.shape[1] < shape[1] for piece in pieces):
        whole = jnp.zeros(shape, pieces[0].dtype)
        for piece, start in zip(pieces, starts):
            whole = lax.dynamic_update_slice(whole, piece, start)
        pieces, starts = (whole,), [(0, 0)]
    return tuple(pieces), numbers([at for start in starts for at in start]), shape


def numbers(values):
    return jnp.stack([jnp.asarray(value, jnp.int32) for value in values])


def load(pieces, starts_ref, whole, sems):
    copies = copies_of(pieces, starts_ref, whole, sems, 0)
    for _, copy in copies:
        copy.start()
    return lambda: [copy.wait() for _, copy in copies]


def copies_of(pieces, starts_ref, whole, sems, row):
    copies = []
    for i, piece in enumerate(pieces):
        rows = pl.ds(pl.multiple_of(starts_ref[2 * i] - row, 16), piece.shape[0])
        if piece.shape[1] == whole.shape[1]:
            place = whole.at[rows, :]
        else:
            columns = pl.ds(pl.multiple_of(starts_ref[2 * i + 1], 128), piece.shape[1])
            place = whole.at[rows, columns]
        copies.append((i, pltpu.make_async_copy(piece, place, sems.at[i])))
    return copies


def load_lower(pieces, starts_ref, whole, sems, row):
    if pieces[0].shape[0] > row:
        copy = pltpu.make_async_copy(pieces[0].at[row:, :], whole, sems.at[0])
        copy.start()
        return copy.wait
    copies = copies_of(pieces, starts_ref, whole, sems, row)

    def each(act):
        for i, copy in copies:
            pl.when(starts_ref[2 * i] >= row)(functools.partial(act, copy))

    each(lambda copy: copy.start())
    return lambda: each(lambda copy: copy.wait())


def load_halves(pieces, starts_ref, whole, sems):
    half = whole.shape[1] // 2
    copies = []
    for i, piece in enumerate(pieces):
        rows = pl.ds(pl.multiple_of(starts_ref[2 * i], 16), piece.shape[0])
        for h in range(2):
            columns = slice(h * half, (h + 1) * half)
            source = piece.at[:, columns] if piece.shape[1] > half else piece
            copy = pltpu.make_async_copy(source, whole.at[rows, columns], sems.at[i, h])
            copies.append((h, None if piece.shape[1] > half else starts_ref[2 * i + 1] == h * half, copy))

    def each(h, act):
        for at, there, copy in copies:
            if at == h and there is None:
                act(copy)
            elif at == h:
                pl.when(there)(functools.partial(act, copy))

    return lambda h: each(h, lambda copy: copy.start()), lambda h: each(h, lambda copy: copy.wait())


IN_VMEM = pl.BlockSpec(memory_space=pltpu.VMEM)
IN_SMEM = pl.BlockSpec(memory_space=pltpu.SMEM)
ANYWHERE = pl.BlockSpec(memory_space=pl.ANY)


def upright(ref):
    return jnp.concatenate([jnp.transpose(ref[m]) for m in range(ref.shape[0])], axis=0)


def turn(chunk, cosine, sine):
    lane = lax.broadcasted_iota(jnp.int32, chunk.shape, 1)
    partner = jnp.where(
        lane % HEAD_SIZE < HALF_HEAD,
        pltpu.roll(chunk, 128 - HALF_HEAD, 1),
        pltpu.roll(chunk, HALF_HEAD, 1),
    )
    return chunk * cosine + partner * sine


def project_kernel(count, starts_ref, x_ref, gains_ref, cos_ref, sin_ref, *refs):
    pieces = refs[:count]
    q_ref, kv_ref, whole, sems = refs[count:]
    wait = load(pieces, starts_ref, whole, sems)
    x = upright(x_ref).astype(F32)
    width = x.shape[1]
    act = (x * rms_inverse(x) * gains_ref[0:1, :]).astype(BF)
    wait()
    cosine, sine = cos_ref[...], sin_ref[...]
    for first in range(0, width + KV_WIDTH, 256):
        linear = nn(act, whole[:width, first : first + 256])
        for at in range(first, first + 256, 128):
            chunk = turn(linear[:, at - first : at - first + 128], cosine, sine)
            if at + 128 <= width:
                q_ref[:, at : at + 128] = (chunk * SCALE).astype(BF)
            elif at < width:
                q_ref[:, at:width] = (chunk[:, : width - at] * SCALE).astype(BF)
                kv_ref[:, : at + 128 - width] = chunk[:, width - at :].astype(BF)
            else:
                kv_ref[:, at - width : at - width + 128] = chunk.astype(BF)
    start = width // 128 * 128
    kv_ref[:, KV_WIDTH:] = nn(act, whole[width:, start:])[:, width - start :].astype(BF)


def project(x, gains, cosine, sine, pieces, starts, shape):
    micro, width, rows = x.shape
    tokens = micro * rows
    outs = (
        jax.ShapeDtypeStruct((tokens, width), BF),
        jax.ShapeDtypeStruct((tokens, 2 * KV_WIDTH), BF),
    )
    table = pl.BlockSpec((tokens, 128), lambda i: (0, 0))
    return pl.pallas_call(
        functools.partial(project_kernel, len(pieces)),
        grid=(1,),
        name="project",
        in_specs=[IN_SMEM] + [IN_VMEM] * 2 + [table] * 2 + [ANYWHERE] * len(pieces),
        out_specs=(IN_VMEM,) * 2,
        out_shape=outs,
        scratch_shapes=[pltpu.VMEM(shape, BF), pltpu.SemaphoreType.DMA((len(pieces),))],
        cost_estimate=cost(2 * tokens * width * (width + 2 * KV_WIDTH), 0, x, *outs, *pieces),
        compiler_params=pltpu.CompilerParams(vmem_limit_bytes=VMEM_LIMIT),
    )(starts, x, gains, cosine, sine, *pieces)


def across(ref):
    return jnp.concatenate([ref[m] for m in range(ref.shape[0])], axis=1)


def spread_out(value, ref):
    rows = ref.shape[2]
    for m in range(ref.shape[0]):
        ref[m] = value[:, m * rows : (m + 1) * rows]


def feed_kernel(counts, core_ref, s0_ref, s1_ref, s2_ref, x_ref, attn_ref, cot_ref, gains_ref, *refs):
    total_count = sum(counts)
    attention_pieces = refs[: counts[0]]
    pair_pieces = refs[counts[0] : counts[0] + counts[1]]
    down_pieces = refs[counts[0] + counts[1] : total_count]
    out_ref, inner_ref, kept_ref, given_ref, act_t_ref, attn_t_ref, resid_ref = refs[total_count : total_count + 7]
    w_attn, w_pair, w_down, sum_ref, sems0, sems1, sems2 = refs[total_count + 7 :]
    width = x_ref.shape[1]
    hidden = w_pair.shape[1]
    tile = hidden // 4
    wait_attention = load_lower(attention_pieces, s0_ref, w_attn, sems0, width)
    start_pair, wait_pair = load_halves(pair_pieces, s1_ref, w_pair, sems1)
    start_pair(0)
    wait_down = load(down_pieces, s2_ref, w_down, sems2)
    start_pair(1)
    even = core_ref[0] == 0
    x = upright(x_ref).astype(F32)
    dy = upright(cot_ref)
    attn_t_ref[...] = jnp.transpose(attn_ref[...])
    wait_attention()
    resid = x + nn(attn_ref[...], w_attn[:, : rounded_up(width)])[:, :width]
    resid_t = jnp.transpose(resid)
    resid_ref[...] = resid_t
    sum_ref[...] = resid_t
    act = (resid * rms_inverse(resid) * gains_ref[1:2, :]).astype(BF)
    act_t_ref[...] = jnp.transpose(act)
    wait_pair(0)
    wait_down()
    for first in range(0, hidden, tile):
        if first == hidden // 2:
            wait_pair(1)
        here = slice(first, first + tile)
        gate = nn(act, w_pair[:width, here])
        upper = nn(act, w_pair[width:, here])
        d_inner = nn(dy, w_down[:, here])
        sigmoid = 1.0 / (1.0 + jnp.exp(-gate))
        silu = gate * sigmoid
        inner = (silu * upper).astype(BF)
        inner_ref[:, here] = inner
        d_gate = d_inner * upper * sigmoid * (1.0 + gate * (1.0 - sigmoid))
        d_upper = d_inner * silu
        kept_ref[:, here] = jnp.where(even, d_gate, d_upper).astype(BF)
        given_ref[:, here] = jnp.where(even, d_upper, d_gate).astype(BF)
        sum_ref[...] += nn(w_down[:, here], jnp.transpose(inner))
    spread_out(sum_ref[...].astype(BF), out_ref)


def feed(core, x, attn, dy, gains, attention_got, pair_got, down_got):
    micro, width, rows = x.shape
    tokens = micro * rows
    groups = [attention_got, pair_got, down_got]
    counts = [len(pieces) for pieces, _, _ in groups]
    shapes = [shape for _, _, shape in groups]
    hidden = shapes[1][1]
    outs = (jax.ShapeDtypeStruct(x.shape, BF),)
    outs += (jax.ShapeDtypeStruct((tokens, hidden), BF),) * 3
    outs += (jax.ShapeDtypeStruct((width, tokens), BF),) * 2
    outs += (jax.ShapeDtypeStruct((width, tokens), F32),)
    every = [piece for pieces, _, _ in groups for piece in pieces]
    return pl.pallas_call(
        functools.partial(feed_kernel, counts),
        name="feed",
        in_specs=[IN_SMEM] * 4 + [IN_VMEM] * 4 + [ANYWHERE] * len(every),
        out_specs=(IN_VMEM,) * 7,
        out_shape=outs,
        scratch_shapes=[pltpu.VMEM((width, shapes[0][1]), BF)]
        + [pltpu.VMEM(shape, BF) for shape in shapes[1:]]
        + [pltpu.VMEM((width, tokens), F32)]
        + [pltpu.SemaphoreType.DMA(size) for size in ((counts[0],), (counts[1], 2), (counts[2],))],
        cost_estimate=cost(
            2 * tokens * width * (4 * hidden + width), tokens * hidden, x, x, x, *outs, *every
        ),
        compiler_params=pltpu.CompilerParams(vmem_limit_bytes=VMEM_MOST),
    )(core, *(starts for _, starts, _ in groups), x, attn, dy, gains, *every)


def feed_back_kernel(counts, core_ref, s0_ref, s1_ref, resid_ref, cot_ref, kept_ref, given_ref, gain_ref, *refs):
    total_count = sum(counts)
    dres_ref, low_ref, dattn_ref, w_attn, w_pair, sems0, sems1 = refs[total_count:]
    width = resid_ref.shape[0]
    start_pair, wait_pair = load_halves(refs[counts[0] : total_count], s1_ref, w_pair, sems1)
    start_pair(0)
    start_pair(1)
    wait_attention = load_lower(refs[: counts[0]], s0_ref, w_attn, sems0, width)
    resid = resid_ref[...]
    root = lax.rsqrt(jnp.mean(resid * resid, axis=0, keepdims=True) + EPS)
    normed = resid * root
    half = w_pair.shape[1] // 2
    for h in range(2):
        columns = slice(h * half, (h + 1) * half)
        weight = lambda i: w_pair[pl.ds(pl.multiple_of(i * width, 16), width), columns]
        wait_pair(h)
        part = nt(weight(core_ref[0]), kept_ref[:, columns]) + nt(weight(1 - core_ref[0]), given_ref[:, columns])
        d_act = part if h == 0 else d_act + part
    d_normed = d_act * gain_ref[...]
    d_resid = across(cot_ref).astype(F32) + root * (
        d_normed - normed * jnp.mean(d_normed * normed, axis=0, keepdims=True)
    )
    dres_ref[...] = d_resid
    low = d_resid.astype(BF)
    low_ref[:, :width] = jnp.transpose(low)
    if low_ref.shape[1] > width:
        low_ref[:, width:] = jnp.zeros((low_ref.shape[0], low_ref.shape[1] - width), BF)
    wait_attention()
    dattn_ref[...] = jnp.transpose(nn(w_attn[:, :width], low).astype(BF))


def feed_back(core, resid, dy, kept, given, gain, attention_got, pair_got):
    width, tokens = resid.shape
    groups = [attention_got, pair_got]
    counts = [len(pieces) for pieces, _, _ in groups]
    shapes = [shape for _, _, shape in groups]
    outs = (
        jax.ShapeDtypeStruct((width, tokens), F32),
        jax.ShapeDtypeStruct((tokens, rounded_up(width)), BF),
        jax.ShapeDtypeStruct((tokens, width), BF),
    )
    every = [piece for pieces, _, _ in groups for piece in pieces]
    return pl.pallas_call(
        functools.partial(feed_back_kernel, counts),
        name="feed_back",
        in_specs=[IN_SMEM] * 3 + [IN_VMEM] * 5 + [ANYWHERE] * len(every),
        out_specs=(IN_VMEM,) * 3,
        out_shape=outs,
        scratch_shapes=[pltpu.VMEM((width, shapes[0][1]), BF), pltpu.VMEM(shapes[1], BF)]
        + [pltpu.SemaphoreType.DMA(size) for size in ((counts[0],), (counts[1], 2))],
        cost_estimate=cost(
            2 * tokens * width * (2 * shapes[1][1] + width), 0, resid, dy, kept, given, *outs, *every
        ),
        compiler_params=pltpu.CompilerParams(vmem_limit_bytes=VMEM_MOST),
    )(core, *(starts for _, starts, _ in groups), resid, dy, kept, given, gain, *every)


def pick_rows(source, starts_ref, base, rows, count, target):
    for t in range(count):
        start = pl.multiple_of(starts_ref[base + t], 16)
        target[t * rows : (t + 1) * rows, :] = source[pl.ds(start, rows), :]


def down_grad_kernel(shards, cut, info_ref, cot_ref, far_cot_ref, inner_ref, far_inner_ref, low_ref, high_ref, dy):
    micro, width, rows = cot_ref.shape
    tokens, part = micro * rows, low_ref.shape[0] // (shards // 2)
    first = pl.multiple_of(info_ref[0], 16)
    for i, ref in enumerate((cot_ref, far_cot_ref)):
        for m in range(micro):
            at = i * tokens + m * rows
            dy[:, at : at + rows] = ref[m, pl.ds(first, part), :]
    for t in range(shards):
        columns = pl.ds(pl.multiple_of(info_ref[1 + t], 128), cut)
        made = nn(dy[:, :tokens], inner_ref[:, columns]) + nn(dy[:, tokens:], far_inner_ref[:, columns])
        out_ref, at = (low_ref, t) if t < shards // 2 else (high_ref, t - shards // 2)
        out_ref[at * part : (at + 1) * part, :] = made.astype(BF)


def down_grad(cot, far_cot, inner, far_inner, first, starts):
    shards, (micro, width, rows), (tokens, hidden) = len(starts), cot.shape, inner.shape
    part, cut = width // 2, hidden // shards
    outs = (jax.ShapeDtypeStruct((shards // 2 * part, cut), BF),) * 2
    if part % 16 or cut % 128:
        grad = nn(jnp.concatenate(list(cot), axis=1), inner) + nn(jnp.concatenate(list(far_cot), axis=1), far_inner)
        grad = lax.dynamic_slice_in_dim(grad.astype(BF), first, part, 0)
        blocks = [lax.dynamic_slice_in_dim(grad, start, cut, 1) for start in starts]
        return [jnp.concatenate(blocks[: shards // 2]), jnp.concatenate(blocks[shards // 2 :])]
    return pl.pallas_call(
        functools.partial(down_grad_kernel, shards, cut),
        name="down_grad",
        in_specs=[IN_SMEM] + [IN_VMEM] * 4,
        out_specs=(IN_VMEM,) * 2,
        out_shape=outs,
        scratch_shapes=[pltpu.VMEM((part, 2 * tokens), BF)],
        cost_estimate=cost(4 * part * tokens * hidden, 0, cot, cot, inner, inner, *outs),
        compiler_params=pltpu.CompilerParams(vmem_limit_bytes=VMEM_LIMIT),
    )(numbers([first] + starts), cot, far_cot, inner, far_inner)


def wide_grad_kernel(cuts, count, starts_ref, left_ref, far_left_ref, right_ref, far_right_ref, *refs):
    outs, ordered = refs[: 2 * len(cuts)], refs[2 * len(cuts)]
    tokens = left_ref.shape[1]

    @pl.when(pl.program_id(0) == 0)
    def _():
        at = first = 0
        for cut in cuts:
            for t in range(count):
                start = pl.multiple_of(starts_ref[t] + first, 16)
                ordered[at : at + cut, :tokens] = left_ref[pl.ds(start, cut), :]
                ordered[at : at + cut, tokens:] = far_left_ref[pl.ds(start, cut), :]
                at += cut
            first += cut

    made = nn(ordered[:, :tokens], right_ref[...]) + nn(ordered[:, tokens:], far_right_ref[...])
    at = 0
    for i, out_ref in enumerate(outs):
        size = out_ref.shape[0]
        out_ref[...] = made[at : at + size].astype(BF)
        at += size


def wide_grad(left, far_left, right, far_right, rows, cuts, starts):
    count, (tokens, columns) = len(starts), right.shape
    outs = tuple(jax.ShapeDtypeStruct((count // 2 * cut, columns), BF) for cut in cuts for _ in range(2))
    if rows % 16 or any(cut % 16 for cut in cuts):
        grad = (nn(left, right) + nn(far_left, far_right)).astype(BF)
        made, first = [], 0
        for cut in cuts:
            blocks = [lax.dynamic_slice_in_dim(grad, start + first, cut, 0) for start in starts]
            made += [jnp.concatenate(blocks[: count // 2]), jnp.concatenate(blocks[count // 2 :])]
            first += cut
        return made
    tile = 512 if columns % 512 == 0 else columns
    part = pl.BlockSpec((tokens, tile), lambda n, starts: (0, n))
    whole = pl.BlockSpec(left.shape, lambda n, starts: (0, 0))
    return pl.pallas_call(
        functools.partial(wide_grad_kernel, cuts, count),
        grid_spec=pltpu.PrefetchScalarGridSpec(
            num_scalar_prefetch=1,
            grid=(columns // tile,),
            in_specs=[whole, whole, part, part],
            out_specs=tuple(pl.BlockSpec((out.shape[0], tile), lambda n, starts: (0, n)) for out in outs),
            scratch_shapes=[pltpu.VMEM((count * rows, 2 * tokens), BF)],
        ),
        out_shape=outs,
        name="wide_grad",
        cost_estimate=cost(4 * tokens * rows * count * columns, 0, left, left, right, right, *outs),
        compiler_params=pltpu.CompilerParams(vmem_limit_bytes=VMEM_LIMIT),
    )(numbers(starts), left, far_left, right, far_right)


def settle_wide_kernel(cuts, core_ref, gain_ref, *refs):
    sums = refs[: 2 * len(cuts)]
    w_left, w_right, left_ref, right_ref, sum_ref = refs[2 * len(cuts) :]
    even = core_ref[0] == 0
    at = 0
    for c, cut in enumerate(cuts):
        here = slice(at, at + cut)
        mine, theirs = sums[2 * c][...].astype(F32), sums[2 * c + 1][...].astype(F32)
        left, right = jnp.where(even, mine, theirs), jnp.where(even, theirs, mine)
        left_ref[here, :], right_ref[here, :] = left, right
        both = w_left[here, :].astype(F32) * left + w_right[here, :].astype(F32) * right
        sum_ref[here, :] = jnp.sum(both, axis=1, keepdims=True) / gain_ref[here, :]
        at += cut


def settle_wide(core, gain, sums, cuts, w_left, w_right):
    out = jax.ShapeDtypeStruct(w_left.shape, F32)
    column = jax.ShapeDtypeStruct((w_left.shape[0], 1), F32)
    if any(cut % 16 for cut in cuts):
        pairs = [(mine.astype(F32), theirs.astype(F32)) for mine, theirs in sums]
        left = jnp.concatenate([jnp.where(core[0] == 0, a, b) for a, b in pairs])
        right = jnp.concatenate([jnp.where(core[0] == 0, b, a) for a, b in pairs])
        both = w_left.astype(F32) * left + w_right.astype(F32) * right
        return left, right, jnp.sum(both, axis=1, keepdims=True) / gain
    args = [value for pair in sums for value in pair]
    return pl.pallas_call(
        functools.partial(settle_wide_kernel, cuts),
        name="settle",
        in_specs=[IN_SMEM] + [IN_VMEM] * (3 + len(args)),
        out_specs=(IN_VMEM,) * 3,
        out_shape=(out, out, column),
        cost_estimate=cost(4 * w_left.size, 0, out, out, *args),
        compiler_params=pltpu.CompilerParams(vmem_limit_bytes=VMEM_LIMIT),
    )(core, gain, *args, w_left, w_right)


def settle_some_kernel(core_ref, gain_ref, mine_ref, theirs_ref, wq_ref, wk_ref, wv_ref, *refs):
    q_ref, o_ref, k_ref, v_ref, sum_ref, kv = refs
    rows, width = q_ref.shape
    half, wide = mine_ref.shape[0], rounded_up(width)
    even = core_ref[0] == 0
    mine, theirs = mine_ref[...].astype(F32), theirs_ref[...].astype(F32)
    parts = (
        (0, jnp.where(even, mine, theirs)[: rows - half]),
        (rows - half, jnp.where(even, theirs, mine)),
    )
    for at, part in parts:
        here = slice(at, at + part.shape[0])
        q_ref[here, :] = part[:, :width]
        o_ref[here, :] = part[:, wide : wide + width]
        kv[here, :] = part[:, 2 * wide :]
        sum_ref[here, :] = jnp.sum(wq_ref[here, :].astype(F32) * part[:, :width], axis=1, keepdims=True)
    sums = sum_ref[...]
    for out_ref, w_ref, first in ((k_ref, wk_ref, 0), (v_ref, wv_ref, KV_WIDTH)):
        grad = kv[:, first : first + KV_WIDTH]
        out_ref[...] = jnp.transpose(grad)
        weight = jnp.transpose(w_ref[...]).astype(F32)
        sums += jnp.sum(weight * grad, axis=1, keepdims=True)
    sum_ref[...] = sums / gain_ref[...]


def settle_some(core, gain, mine, theirs, w_query, w_key, w_value):
    rows, width = w_query.shape
    half, wide = mine.shape[0], rounded_up(width)
    if (rows - half) % 16:
        low, high = jnp.where(core[0] == 0, mine, theirs), jnp.where(core[0] == 0, theirs, mine)
        grad = jnp.concatenate([low[: rows - half], high]).astype(F32)
        key, value = grad[:, 2 * wide : 2 * wide + KV_WIDTH], grad[:, 2 * wide + KV_WIDTH :]
        pairs = ((w_query, grad[:, :width]), (w_key.T, key), (w_value.T, value))
        sums = sum(jnp.sum(w.astype(F32) * g, axis=1, keepdims=True) for w, g in pairs)
        return grad[:, :width], grad[:, wide : wide + width], key.T, value.T, sums / gain
    outs = (jax.ShapeDtypeStruct((rows, width), F32),) * 2
    outs += (jax.ShapeDtypeStruct((KV_WIDTH, rows), F32),) * 2
    outs += (jax.ShapeDtypeStruct((rows, 1), F32),)
    return pl.pallas_call(
        settle_some_kernel,
        name="settle_some",
        in_specs=[IN_SMEM] + [IN_VMEM] * 6,
        out_specs=(IN_VMEM,) * 5,
        out_shape=outs,
        scratch_shapes=[pltpu.VMEM((rows, 2 * KV_WIDTH), F32)],
        cost_estimate=cost(4 * w_query.size, 0, mine, theirs, *outs),
        compiler_params=pltpu.CompilerParams(vmem_limit_bytes=VMEM_LIMIT),
    )(core, gain, mine, theirs, w_query, w_key, w_value)


def turn_keys(source, target, at, cosine, sine):
    rows = source.shape[0]
    for first in range(0, KV_WIDTH, 128):
        chunk = turn(source[:, first : first + 128].astype(F32), cosine, -sine).astype(BF)
        last = min(first + 128, KV_WIDTH)
        target[at : at + rows, first:last] = chunk[:, : last - first]
    target[at : at + rows, KV_WIDTH:] = source[:, KV_WIDTH:]


def attention_grad_kernel(shards, half, starts_ref, gain_ref, cos_ref, sin_ref, dq_ref, attn_ref, low_ref, *refs):
    xs, halves = refs[:shards], refs[shards : shards + 2]
    dkvs = [ref.at[t] for ref in halves for t in range(shards // 2)]
    outs, (act, dkv, ordered, attn_ordered) = refs[shards + 2 : shards + 4], refs[shards + 4 :]
    micro, width, rows = xs[0].shape
    tokens = micro * rows
    wide = rounded_up(width)
    for t in range(shards):
        here = slice(t * tokens, (t + 1) * tokens)
        turn_keys(dkvs[t], dkv, t * tokens, cos_ref[here, :], sin_ref[here, :])
        for m in range(micro):
            x = xs[t][m].astype(F32)
            root = lax.rsqrt(jnp.mean(x * x, axis=0, keepdims=True) + EPS)
            first = t * tokens + m * rows
            act[:, first : first + rows] = (x * root * gain_ref[...]).astype(BF)
    for i, out_ref in enumerate(outs):
        pick_rows(act, starts_ref, i * shards, half, shards, ordered)
        pick_rows(attn_ref, starts_ref, i * shards, half, shards, attn_ordered)
        out_ref[:, :wide] = nn(ordered[:, :tokens], dq_ref[...]).astype(BF)
        out_ref[:, wide : 2 * wide] = nn(attn_ordered[...], low_ref[...]).astype(BF)
        out_ref[:, 2 * wide :] = nn(ordered[...], dkv[...]).astype(BF)


def attention_grad(x_all, gain, cosine, sine, dq, attn_t, low, dkv_all, half, given, kept):
    shards = len(x_all)
    micro, width, rows = x_all[0].shape
    every = shards * micro * rows
    wide = rounded_up(width)
    out = jax.ShapeDtypeStruct((shards * half, 2 * wide + 2 * KV_WIDTH), BF)
    if half % 16 or width // shards % 16:
        xs = jnp.concatenate([x[m] for x in x_all for m in range(micro)], axis=1).astype(F32)
        act = xs * lax.rsqrt(jnp.mean(xs * xs, axis=0, keepdims=True) + EPS) * gain
        act = act.astype(BF)
        dkv = jnp.concatenate(dkv_all, axis=0).reshape(every, 2 * KV_WIDTH)
        keys = dkv[:, :KV_WIDTH].astype(F32).reshape(every, -1, 2, HALF_HEAD)
        c, s = cosine[:, None, :HALF_HEAD], sine[:, None, HALF_HEAD:HEAD_SIZE]
        first, second = keys[:, :, 0], keys[:, :, 1]
        keys = jnp.stack([first * c + second * s, second * c - first * s], axis=2)
        dkv = jnp.concatenate([keys.reshape(every, KV_WIDTH).astype(BF), dkv[:, KV_WIDTH:]], axis=1)
        parts = [nn(act[:, : micro * rows], dq), nn(attn_t, low), nn(act, dkv)]
        grad = jnp.concatenate(parts, axis=1).astype(BF)
        return [
            jnp.concatenate([lax.dynamic_slice_in_dim(grad, start, half, 0) for start in starts])
            for starts in (given, kept)
        ]
    return pl.pallas_call(
        functools.partial(attention_grad_kernel, shards, half),
        name="attention_grad",
        in_specs=[IN_SMEM] + [IN_VMEM] * (8 + shards),
        out_specs=(IN_VMEM,) * 2,
        out_shape=(out, out),
        scratch_shapes=[
            pltpu.VMEM((width, every), BF),
            pltpu.VMEM((every, 2 * KV_WIDTH), BF),
            pltpu.VMEM((shards * half, every), BF),
            pltpu.VMEM((shards * half, micro * rows), BF),
        ],
        cost_estimate=cost(
            4 * shards * half * (every * 2 * KV_WIDTH + 2 * micro * rows * width),
            0,
            *x_all,
            *dkv_all,
            out,
            out,
        ),
        compiler_params=pltpu.CompilerParams(vmem_limit_bytes=VMEM_MOST),
    )(numbers(given + kept), gain, cosine, sine, dq, attn_t, low, *x_all, *dkv_all)


def finish_kernel(count, starts_ref, x_ref, low_ref, kv_ref, dres_ref, gain_ref, cos_ref, sin_ref, *refs):
    pieces = refs[:count]
    dx_ref, whole, kv_turned, sems = refs[count:]
    wait = load(pieces, starts_ref, whole, sems)
    turn_keys(kv_ref, kv_turned, 0, cos_ref[...], sin_ref[...])
    x = across(x_ref).astype(F32)
    width = x.shape[0]
    root = lax.rsqrt(jnp.mean(x * x, axis=0, keepdims=True) + EPS)
    normed = x * root
    wait()
    d_act = nt(whole[:width, :width], low_ref[:, :width])
    d_act += nt(whole[:width, width:], kv_turned[:, :KV_WIDTH])
    d_act += nt(whole[width:, width:], kv_turned[:, KV_WIDTH:])
    d_normed = d_act * gain_ref[...]
    d_x = dres_ref[...] + root * (d_normed - normed * jnp.mean(d_normed * normed, axis=0, keepdims=True))
    spread_out(d_x.astype(BF), dx_ref)


def finish(x, low, kv, dres, gain, cosine, sine, pieces, starts, shape):
    micro, width, rows = x.shape
    tokens = micro * rows
    table = pl.BlockSpec((tokens, 128), lambda i: (0, 0))
    return pl.pallas_call(
        functools.partial(finish_kernel, len(pieces)),
        grid=(1,),
        name="finish",
        in_specs=[IN_SMEM] + [IN_VMEM] * 5 + [table] * 2 + [ANYWHERE] * len(pieces),
        out_specs=IN_VMEM,
        out_shape=jax.ShapeDtypeStruct(x.shape, BF),
        scratch_shapes=[
            pltpu.VMEM(shape, BF),
            pltpu.VMEM((tokens, 2 * KV_WIDTH), BF),
            pltpu.SemaphoreType.DMA((len(pieces),)),
        ],
        cost_estimate=cost(2 * tokens * width * (width + 2 * KV_WIDTH), 0, x, low, dres, *pieces),
        compiler_params=pltpu.CompilerParams(vmem_limit_bytes=VMEM_LIMIT),
    )(starts, x, low, kv, dres, gain, cosine, sine, *pieces)


def head(ref, h):
    return ref[:, h * HEAD_SIZE : (h + 1) * HEAD_SIZE]


def widen(value, columns):
    n = value.shape[0]
    lane = lax.broadcasted_iota(jnp.int32, (n, HEAD_SIZE), 1)
    tail = jnp.zeros((n, HEAD_SIZE), F32)
    for c, column in enumerate(columns):
        tail = jnp.where(lane == c, column, tail)
    return jnp.concatenate([value, tail.astype(BF)], axis=1)


def split(column):
    high = column.astype(BF).astype(F32)
    middle = (column - high).astype(BF).astype(F32)
    return [high, middle, column - high - middle]


def attend_kernel(shards, seg_rows, q_ref, *refs):
    kv = refs[:shards]
    bias_ref = refs[shards]
    o_ref, lse_ref = refs[-2:]
    rows = q_ref.shape[0]
    i = lax.broadcasted_iota(jnp.int32, (rows, rows), 0)
    j = lax.broadcasted_iota(jnp.int32, (rows, rows), 1)
    same = (i // seg_rows) == (j // seg_rows)
    own = jnp.where(j > i, CLOSED, jnp.where(same, 0.0, bias_ref[0:1, :]))
    one = jnp.ones((rows, 1), F32)
    bias_columns = jnp.transpose(bias_ref[...])
    lse = jnp.zeros((rows, 128), F32)
    lane = lax.broadcasted_iota(jnp.int32, (rows, 128), 1)
    for g in range(KEY_VALUE_HEADS):
        keys, values = [], []
        for t in range(shards):
            keys.append(widen(head(kv[t], g), [bias_columns[:, t : t + 1]] if t else []))
            values.append(widen(head(kv[t], KEY_VALUE_HEADS + g), [one]))
        for h in range(g * GROUP, g * GROUP + GROUP):
            q = widen(head(q_ref, h), [one])
            scores = [nt(q, k) for k in keys]
            scores[0] = scores[0] + own
            peak = functools.reduce(jnp.maximum, scores)
            peak = jnp.max(peak, axis=1, keepdims=True)
            terms = [nn(jnp.exp(s - peak).astype(BF), v) for s, v in zip(scores, values)]
            mixed = sum(terms[1:], terms[0])
            total = mixed[:, HEAD_SIZE : HEAD_SIZE + 1]
            o_ref[:, h * HEAD_SIZE : (h + 1) * HEAD_SIZE] = (mixed[:, :HEAD_SIZE] / total).astype(BF)
            lse = jnp.where(lane == h, peak + jnp.log(total), lse)
    lse_ref[...] = lse


def attend_back_kernel(shards, seg_rows, q_ref, *refs):
    kv = refs[:shards]
    bias_ref, o_ref, do_ref, lse_ref, cos_ref, sin_ref = refs[shards : shards + 6]
    dq_ref, low_ref, high_ref = refs[-3:]
    dkv = [ref.at[t] for ref in (low_ref, high_ref) for t in range(shards // 2)]
    rows = q_ref.shape[0]
    i = lax.broadcasted_iota(jnp.int32, (rows, rows), 1)
    j = lax.broadcasted_iota(jnp.int32, (rows, rows), 0)
    bias_columns = jnp.transpose(bias_ref[...])
    same = (i // seg_rows) == (j // seg_rows)
    own_column = jnp.broadcast_to(bias_columns[:, 0:1], (rows, rows))
    own = jnp.where(j > i, CLOSED, jnp.where(same, 0.0, own_column))
    one, zero = jnp.ones((rows, 1), F32), jnp.zeros((rows, 1), F32)
    cosine, sine = cos_ref[...], sin_ref[...]
    if dq_ref.shape[1] > QUERY_HEADS * HEAD_SIZE:
        dq_ref[:, QUERY_HEADS * HEAD_SIZE :] = jnp.zeros((rows, dq_ref.shape[1] - QUERY_HEADS * HEAD_SIZE), BF)
    for g in range(KEY_VALUE_HEADS):
        keys, values, turned = [], [], []
        for t in range(shards):
            k = head(kv[t], g)
            turned.append(jnp.transpose(k))
            keys.append(widen(k, [bias_columns[:, t : t + 1] if t else zero, one, one, one]))
            values.append(widen(head(kv[t], KEY_VALUE_HEADS + g), [one, one, one]))
        dk, dv = [None] * shards, [None] * shards
        for h in range(g * GROUP, g * GROUP + GROUP):
            q, do = head(q_ref, h), head(do_ref, h)
            centre = jnp.sum(head(o_ref, h).astype(F32) * do.astype(F32), axis=1, keepdims=True)
            q_wide = widen(q, [one] + split(-lse_ref[:, h : h + 1]))
            do_wide = widen(do, split(-centre))
            dq = None
            for t in range(shards):
                scores = nt(keys[t], q_wide)
                if t == 0:
                    scores = scores + own
                probs = jnp.exp(scores)
                ds = (probs * nt(values[t], do_wide)).astype(BF)
                v_term = nn(probs.astype(BF), do)
                k_term = nn(ds, q)
                q_term = nn(turned[t], ds)
                dv[t] = v_term if dv[t] is None else dv[t] + v_term
                dk[t] = k_term if dk[t] is None else dk[t] + k_term
                dq = q_term if dq is None else dq + q_term
            dq = dq * SCALE
            first, second = dq[:HALF_HEAD], dq[HALF_HEAD:]
            back = jnp.concatenate(
                [first * cosine + second * sine, second * cosine - first * sine], axis=0
            )
            dq_ref[:, h * HEAD_SIZE : (h + 1) * HEAD_SIZE] = jnp.transpose(back.astype(BF))
        for t in range(shards):
            dkv[t][:, g * HEAD_SIZE : (g + 1) * HEAD_SIZE] = dk[t].astype(BF)
            g_value = KEY_VALUE_HEADS + g
            dkv[t][:, g_value * HEAD_SIZE : (g_value + 1) * HEAD_SIZE] = dv[t].astype(BF)


def attend(micro, seg_rows, q, kv, bias):
    shards, tokens, width = len(kv), q.shape[0], q.shape[1]
    rows = tokens // micro
    here = lambda w: pl.BlockSpec((rows, w), lambda m: (m, 0))
    outs = (jax.ShapeDtypeStruct((tokens, width), BF), jax.ShapeDtypeStruct((tokens, 128), F32))
    pairs = tokens * rows * shards * QUERY_HEADS
    return pl.pallas_call(
        functools.partial(attend_kernel, shards, seg_rows),
        grid=(micro,),
        name="attend",
        in_specs=[here(width)]
        + [here(2 * KV_WIDTH)] * shards
        + [pl.BlockSpec((None,) + bias.shape[1:], lambda m: (m, 0, 0))],
        out_specs=(here(width), here(128)),
        out_shape=outs,
        cost_estimate=cost(16 * HEAD_SIZE * pairs, pairs, q),
        compiler_params=pltpu.CompilerParams(vmem_limit_bytes=VMEM_LIMIT),
    )(q, *kv, bias)


def attend_back(m, rows, seg_rows, q, kv, bias, o, do, lse, cosine, sine, earlier):
    shards, tokens, width = len(kv), q.shape[0], q.shape[1]
    here = lambda w: pl.BlockSpec((rows, w), lambda i: (m, 0))
    turned = pl.BlockSpec((HALF_HEAD, rows), lambda i: (0, m))
    outs = (jax.ShapeDtypeStruct((tokens, rounded_up(width)), BF),)
    outs += (jax.ShapeDtypeStruct((shards // 2, tokens, 2 * KV_WIDTH), BF),) * 2
    pieces = pl.BlockSpec((shards // 2, rows, 2 * KV_WIDTH), lambda i: (0, m, 0))
    pairs = rows * rows * shards * QUERY_HEADS
    return pl.pallas_call(
        functools.partial(attend_back_kernel, shards, seg_rows),
        grid=(1,),
        name="attend_back",
        in_specs=[here(width)]
        + [here(2 * KV_WIDTH)] * shards
        + [pl.BlockSpec((None,) + bias.shape[1:], lambda i: (m, 0, 0))]
        + [here(width), here(width), here(128), turned, turned]
        + [pl.BlockSpec(memory_space=pl.ANY)] * len(earlier),
        out_specs=(here(rounded_up(width)), pieces, pieces),
        out_shape=outs,
        input_output_aliases={shards + 7 + i: i for i in range(len(earlier))},
        cost_estimate=cost(40 * HEAD_SIZE * pairs, pairs, q),
        compiler_params=pltpu.CompilerParams(vmem_limit_bytes=VMEM_LIMIT),
    )(q, *kv, bias, o, do, lse, cosine, sine, *earlier)


def local(
    block_input,
    parent_ids,
    w_query,
    key_weight,
    value_weight,
    w_output,
    w_gate,
    w_up,
    w_down,
    norm_first,
    norm_second,
    out_cotangent,
):
    micro, rows, width = block_input.shape
    shards = lax.axis_size("shard")
    links = Links(lax.axis_size("rep"), shards)
    tree = rows * shards
    segs = parent_ids.shape[2]
    seg_rows = tree // segs
    tokens = micro * rows
    hidden = w_gate.shape[1]

    inputs = block_input.swapaxes(1, 2)
    cotangent = out_cotangent.swapaxes(1, 2)

    even = links.core == 0
    side = lax.axis_index("rep") // 2 % 2
    left = jnp.concatenate([w_query, key_weight], axis=1)
    right = jnp.concatenate([w_output, value_weight], axis=1)
    attn_mine = jnp.where(even, left, right)
    pair_cut = hidden // 2
    pair_mine = lax.dynamic_slice_in_dim(jnp.where(even, w_gate, w_up), side * pair_cut, pair_cut, 1)
    down_own = w_down.T
    down_cut = width // 2
    down_mine = lax.dynamic_slice_in_dim(down_own, links.core * down_cut, down_cut, 0)
    core = numbers([links.core])

    attn_near = links.near(attn_mine)
    gain_pieces = links.small_pieces(jnp.stack([norm_first, norm_second]))
    attn_mine, attn_near, gain_pieces, pair_mine, down_mine = meet(
        attn_mine, attn_near, gain_pieces, pair_mine, down_mine
    )

    gains = links.in_order(gain_pieces).astype(F32)
    attn_all = links.far(attn_mine, attn_near)
    attn_swapped = {t: links.swap(attn_near[t]) for t in attn_near}
    pair_near = {1: links.step(pair_mine, 0)}
    parents = parent_ids[:, 0]
    seg = jnp.arange(segs)
    after_parent = jnp.concatenate([parents[:, 1:], jnp.full((micro, 1), -1, parents.dtype)], axis=1)
    on_path = (seg % 2 == 0)[None] | (after_parent == seg[None])
    below = (seg[None, :] < seg[:, None])[None]
    depth = jnp.sum(jnp.where(below, on_path.astype(F32)[:, None, :], 0.0), axis=-1)

    def row_numbers(hop):
        return (links.shard ^ hop) * rows + jnp.arange(rows)

    def pick(table, numbers):
        hit = (numbers // seg_rows)[..., None] == seg
        return jnp.sum(jnp.where(hit[None], table.reshape(micro, *(1,) * numbers.ndim, segs), 0), axis=-1)

    key_rows = jnp.stack([row_numbers(hop) for hop in links.hops])
    positions = pick(depth, key_rows) * seg_rows + (key_rows % seg_rows).astype(F32)
    freqs = jnp.exp(-math.log(10000.0) * jnp.arange(HALF_HEAD, dtype=F32) * (2.0 / HEAD_SIZE))
    angles = freqs[:, None] * positions.swapaxes(0, 1).reshape(1, shards * tokens)
    cosine_t, sine_t = jnp.cos(angles), jnp.sin(angles)
    cosine = jnp.tile(cosine_t.T, (1, 4))
    sine = jnp.tile(jnp.concatenate([-sine_t.T, sine_t.T], axis=1), (1, 2))
    open_key = (pick(on_path.astype(F32), key_rows) > 0.5) & (
        (key_rows < links.shard * rows) | (jnp.arange(shards) == 0)[:, None]
    )
    bias = jnp.where(open_key, 0.0, CLOSED)
    bias = jnp.pad(bias, ((0, 0), (0, 8 - shards), (0, 0)))

    gain_one, gain_two = gains[0][:, None], gains[1][:, None]
    tables = (cosine, sine, cosine_t, sine_t, bias, gains, gain_one, gain_two)
    attn_all, attn_swapped, pair_mine, pair_near, down_mine, tables = meet(
        attn_all, attn_swapped, pair_mine, pair_near, down_mine, tables
    )
    cosine, sine, cosine_t, sine_t, bias, gains, gain_one, gain_two = tables

    for t in range(1, shards):
        if t not in attn_swapped:
            attn_swapped[t] = links.swap(attn_all[t])
    shard_rows = width // shards

    def pair_place(weight, hop):
        return weight * width + (links.shard ^ hop) * shard_rows

    pieces, starts = [left, right], [(pair_place(0, 0), 0), (pair_place(1, 0), 0)]
    for t in range(1, shards):
        pieces += [attn_all[t], attn_swapped[t]]
        starts += [
            (pair_place(links.core, links.hops[t]), 0),
            (pair_place(1 - links.core, links.hops[links.twin(t)]), 0),
        ]
    attention_got = joined(pieces, starts, (2 * width, left.shape[1]))
    pair_near |= {1 << i: links.step(pair_mine, i) for i in range(1, links.bits)}
    pair_beside = {1: links.beside(pair_near[1])}
    down_near = {1: links.step(down_mine, 0)}
    queries, kv = project(inputs, gains, cosine, sine, *attention_got)
    queries, kv, pair_mine, pair_near, pair_beside, down_mine, down_near = meet(
        queries, kv, pair_mine, pair_near, pair_beside, down_mine, down_near
    )

    kv_near = links.near(kv)
    pair_beside |= {t: links.beside(pair_near[t]) for t in pair_near if t > 1}
    kv_near, kv, pair_beside, pair_near, pair_mine = meet(kv_near, kv, pair_beside, pair_near, pair_mine)

    kv_all = links.far(kv, kv_near)
    pair_all = links.far(pair_mine, pair_near)
    pair_swapped = {t: links.swap(pair_near[t]) for t in pair_near}
    pair_crossed = {t: links.swap(pair_beside[t]) for t in pair_beside}
    kv_all, pair_all, pair_swapped, pair_crossed, pair_beside, down_mine, down_near = meet(
        kv_all, pair_all, pair_swapped, pair_crossed, pair_beside, down_mine, down_near
    )

    down_near |= {1 << i: links.step(down_mine, i) for i in range(1, links.bits)}
    down_all = links.far(down_mine, down_near)
    pair_beside |= {t: links.beside(pair_all[t]) for t in range(1, shards) if t not in pair_beside}
    attn, lse = attend(micro, seg_rows, queries, kv_all, bias)
    pair_swapped |= {t: links.swap(pair_all[t]) for t in range(1, shards) if t not in pair_swapped}
    attn, lse, down_all, pair_beside, pair_all, pair_swapped = meet(
        attn, lse, down_all, pair_beside, pair_all, pair_swapped
    )

    pair_crossed |= {t: links.swap(pair_beside[t]) for t in range(1, shards) if t not in pair_crossed}
    down_swapped = [None] + [links.swap(down_all[t]) for t in range(1, shards)]
    pieces, starts = [w_gate, w_up], [(pair_place(0, 0), 0), (pair_place(1, 0), 0)]
    for t in range(1, shards):
        pieces += [pair_all[t], pair_beside[t], pair_swapped[t], pair_crossed[t]]
        for row in (
            pair_place(links.core, links.hops[t]),
            pair_place(1 - links.core, links.hops[links.twin(t)]),
        ):
            starts += [(row, side * pair_cut), (row, (1 - side) * pair_cut)]
    pair_got = joined(pieces, starts, (2 * width, hidden))
    own = w_down.shape[0]
    pieces, starts = [down_own], [(0, links.shard * own)]
    for t in range(1, shards):
        pieces += [down_all[t], down_swapped[t]]
        starts += [
            (links.core * down_cut, (links.shard ^ links.hops[t]) * own),
            ((1 - links.core) * down_cut, (links.shard ^ links.hops[links.twin(t)]) * own),
        ]
    down_got = joined(pieces, starts, (width, own * shards))
    attn, pair_pieces, down_pieces = meet(attn, pair_got[0], down_got[0])
    pair_got, down_got = (pair_pieces, *pair_got[1:]), (down_pieces, *down_got[1:])

    plan = Plan()
    have = lambda *names: [plan.have[name] for name in names]
    x_near = links.near(inputs)
    far_cotangent = links.swap(cotangent)
    made = feed(core, inputs, attn, cotangent, gains, attention_got, pair_got, down_got)
    names = ("out", "inner", "kept", "given", "act", "attn_t", "resid")
    plan.have = dict(zip(names, made)) | {"x_near": x_near, "far_dy": far_cotangent, "queries": queries, "kv": kv_all, "lse": lse, "attn": attn}
    plan.close()

    half, mine, theirs = links.half_rows(shard_rows)
    some_kept, some_given = links.order(shard_rows, mine, theirs)
    cuts = (-(-shard_rows // 32) * 16, shard_rows - -(-shard_rows // 32) * 16)

    plan.have["x_all"] = links.far(inputs, plan.have.pop("x_near"))
    for name in ("inner", "act", "given"):
        plan.have["far_" + name] = links.swap(plan.have[name])
    names = ("d_resid", "low", "d_attn")
    resid, kept, given = have("resid", "kept", "given")
    plan.have |= dict(zip(names, feed_back(core, resid, cotangent, kept, given, gain_two, attention_got, pair_got)))
    plan.close()

    names = ("down.low", "down.high")
    far_dy, inner, far_inner = have("far_dy", "inner", "far_inner")
    starts = [(links.shard ^ hop) * own for hop in links.hops]
    plan.have |= dict(zip(names, down_grad(cotangent, far_dy, inner, far_inner, links.core * down_cut, starts)))
    plan.close()

    for name in ("down", "wide0", "wide1", "some"):
        plan.start(name, links.reduce(plan, name, name == "some"))
    plan.advance("down")
    names = ("wide0.low", "wide0.high", "wide1.low", "wide1.high")
    act, far_act, kept, far_kept = have("act", "far_act", "kept", "far_given")
    starts = [(links.shard ^ hop) * shard_rows for hop in links.hops]
    plan.have |= dict(zip(names, wide_grad(act, far_act, kept, far_kept, shard_rows, cuts, starts)))
    plan.close()

    made = ()
    hops = [("down", "wide0"), ("down", "wide0", "wide1")]
    for m in range(micro):
        plan.advance(*hops[min(m, 1)])
        q, kv_now, o, do, lse_now = have("queries", "kv", "attn", "d_attn", "lse")
        made = attend_back(m, rows, seg_rows, q, kv_now, bias, o, do, lse_now, cosine_t, sine_t, made)
        plan.have["attn_grads"] = made = tuple(made)
        plan.close()
        made = plan.have["attn_grads"]

    d_queries, *d_kv = plan.have.pop("attn_grads")
    plan.have["dkv.pieces"] = d_kv
    plan.have["d_queries"] = d_queries
    plan.start("dkv", links.collect(plan, "dkv"))
    plan.advance("dkv", "wide0", "wide1", "down")
    given, kept = attention_grad(
        plan.have["x_all"],
        gain_one,
        cosine,
        sine,
        d_queries,
        *have("attn_t", "low"),
        d_kv,
        half,
        some_given,
        some_kept,
    )
    plan.have["some.given"], plan.have["some.kept"] = given, kept
    plan.close()

    def settle():
        have, done = plan.have, plan.have.setdefault("done", {})
        if "dkv" in have and "d_input" not in done:
            done["d_input"] = finish(
                inputs, have["d_queries"], have["dkv"], have["d_resid"], gain_one, cosine, sine, *attention_got
            )
        if "down" in have and "down" not in done:
            done["down"] = links.finish_rows(*have["down"], width).T
        if "wide0" in have and "wide1" in have and "gate" not in done:
            done["gate"], done["upper"], gain = settle_wide(
                core,
                norm_second.astype(F32)[:, None],
                (have["wide0"], have["wide1"]),
                cuts,
                w_gate,
                w_up,
            )
            done["gain_two"] = gain[:, 0]
        if "some" in have and "query" not in done:
            done["query"], done["output"], key, value, gain = settle_some(
                core,
                norm_first.astype(F32)[:, None],
                *have["some"],
                w_query,
                key_weight.T,
                value_weight.T,
            )
            done["key"], done["value"], done["gain_one"] = key.T, value.T, gain[:, 0]

    order, rounds = [], 0
    while plan.tasks:
        plan.advance(*(order.pop(0) if order else tuple(plan.tasks)))
        plan.advance(*{0: ('some',), 1: ('some',)}.get(rounds, ()))
        settle()
        rounds += 1
        if rounds <= 2 and plan.tasks:
            plan.close()

    done = plan.have["done"]
    return (
        plan.have["out"].swapaxes(1, 2),
        done["d_input"].swapaxes(1, 2),
        *(done[name] for name in ("query", "key", "value", "output", "gate", "upper", "down")),
        done["gain_one"],
        done["gain_two"],
    )


def solution(mesh):
    rows = P(None, AXES, None)
    weight, gain = P("shard", None), P("shard")
    return jax.shard_map(
        local,
        mesh=mesh,
        in_specs=(rows, P(None, "rep", None)) + (weight,) * 7 + (gain, gain, rows),
        out_specs=(rows, rows) + (weight,) * 7 + (gain, gain),
        check_vma=False,
    )
```

```python
import functools
import math

import jax
import jax.numpy as jnp
from jax import lax
from jax.experimental import pallas as pl
from jax.experimental.pallas import tpu as pltpu
from jax.sharding import PartitionSpec as P

QUERY_HEADS = 15
KEY_VALUE_HEADS = 5
HEAD_SIZE = 64
HALF_HEAD = HEAD_SIZE // 2
GROUP = QUERY_HEADS // KEY_VALUE_HEADS
KV_WIDTH = KEY_VALUE_HEADS * HEAD_SIZE
SCALE = HEAD_SIZE ** (-0.5)
EPS = 1e-05
AXES = ("rep", "shard")
BF = jnp.bfloat16
F32 = jnp.float32
CLOSED = -1e30
VMEM_LIMIT = 32 << 20
VMEM_MOST = 60 << 20


def dot(a, b, dims):
    return lax.dot_general(a, b, (dims, ((), ())), preferred_element_type=F32)


def nn(a, b):
    return dot(a, b, ((1,), (0,)))


def nt(a, b):
    return dot(a, b, ((1,), (1,)))


def tn(a, b):
    return dot(a, b, ((0,), (0,)))


def total(parts):
    return sum(part.astype(F32) for part in parts).astype(parts[0].dtype)


def meet(*values):
    return lax.optimization_barrier(values)


def rounded_up(columns):
    return -(-columns // 128) * 128


def rms_inverse(x):
    return lax.rsqrt(jnp.mean(x * x, axis=-1, keepdims=True) + EPS)


def cost(flops, exps, *arrays):
    size = sum(a.size * a.dtype.itemsize for a in arrays)
    return pl.CostEstimate(flops=flops, transcendentals=exps, bytes_accessed=size)


class Links:
    def __init__(self, reps, shards):
        self.reps, self.shards = reps, shards
        self.core = lax.axis_index("rep") % 2
        self.shard = lax.axis_index("shard")
        self.bits = shards.bit_length() - 1
        even = [1 << i for i in range(self.bits)]
        odd = even[:2][::-1] + even[2:]
        self.steps = list(zip(even, odd))
        self.hops = []
        for piece in range(shards):
            sums = [0, 0]
            for i, step in enumerate(self.steps):
                if piece >> i & 1:
                    sums = [sums[0] ^ step[0], sums[1] ^ step[1]]
            self.hops.append(jnp.where(self.core == 0, sums[0], sums[1]))

    def move(self, value, target):
        pairs = []
        for r in range(self.reps):
            for s in range(self.shards):
                goal = target(r, s)
                if goal is not None:
                    pairs.append((r * self.shards + s, goal[0] * self.shards + goal[1]))
        return lax.ppermute(value, AXES, pairs)

    def step(self, value, i):
        return self.move(value, lambda r, s: (r, s ^ self.steps[i][r % 2]))

    def swap(self, value):
        return self.move(value, lambda r, s: (r ^ 1, s))

    def reduce(self, plan, name, quick=False):
        top = self.bits
        if name + ".given" in plan.have:
            got = yield self.swap(plan.have.pop(name + ".given"))
            sums = [plan.have.pop(name + ".kept"), got]
        else:
            got = yield self.step(plan.have.pop(name + ".high"), top - 1)
            sums = [plan.have.pop(name + ".low"), got]
            top -= 1
        for i in reversed(range(top)):
            block = sums[0].shape[0] // 2
            got = yield self.step(total([part[block:] for part in sums]), i)
            sums = [part[:block] for part in sums] + [got]
        value = total(sums)
        chips = self.reps // 2
        place = lax.axis_index("rep") // 2
        span = 1
        if chips % 4 == 0 and quick and value.shape[0] % 4 == 0:
            quarter = value.shape[0] // 4
            across = lambda value, j: self.move(value, lambda r, s: (r ^ (2 * j), s))
            cut = lambda j: lax.dynamic_slice_in_dim(value, (place % 4 ^ j) * quarter, quarter, 0)
            got = yield [across(cut(j), j) for j in range(1, 4)]
            mine = total([cut(0)] + got)
            got = yield [across(mine, j) for j in range(1, 4)]
            parts = jnp.stack([mine] + got).reshape(2, 2, quarter, -1)
            parts = jnp.where(place % 4 >= 2, parts[::-1], parts)
            parts = jnp.where(place % 2 == 1, parts[:, ::-1], parts)
            value = parts.reshape(4 * quarter, -1)
            span = 4
        elif chips % 4 == 0:
            inward, outward, middle = {0: 1, 3: 2}, {1: 0, 2: 3}, {1: 2, 2: 1}

            def along(value, table):
                def target(r, s):
                    chip = r // 2
                    if chip % 4 not in table:
                        return None
                    return ((chip - chip % 4 + table[chip % 4]) * 2 + r % 2, s)

                return self.move(value, target)

            value = total([value, (yield along(value, inward))])
            value = total([value, (yield along(value, middle))])
            back = yield along(value, outward)
            inner = (place % 4 == 1) | (place % 4 == 2)
            value = jnp.where(inner, value, back)
            span = 4
        while span < chips:
            value = total([value, self.move(value, lambda r, s: (r ^ (2 * span), s))])
            span *= 2
        other = yield self.swap(value)
        plan.have[name] = (value, other)

    def collect(self, plan, name):
        low, high = plan.have[name + ".pieces"]
        got = yield self.step(high, self.bits - 1)
        sums = [low, got]
        for i in reversed(range(self.bits - 1)):
            block = sums[0].shape[0] // 2
            got = yield self.step(total([part[block:] for part in sums]), i)
            sums = [part[:block] for part in sums] + [got]
        plan.have[name] = total(sums)[0]

    def beside(self, value):
        return self.move(value, lambda r, s: (r ^ 2, s))

    def near(self, value):
        return {1 << i: self.step(value, i) for i in range(self.bits)}

    def far(self, value, near):
        pieces = [value]
        for t in range(1, self.shards):
            top = t.bit_length() - 1
            pieces.append(near[t] if t in near else self.step(pieces[t - (1 << top)], top))
        return pieces

    def twin(self, piece):
        return piece if self.bits < 2 else piece >> 2 << 2 | (piece & 1) << 1 | (piece >> 1 & 1)

    def small_pieces(self, value):
        return [
            value if hop == 0 else self.move(value, lambda r, s, hop=hop: (r, s ^ hop))
            for hop in range(self.shards)
        ]

    def in_order(self, pieces):
        pieces = jnp.stack(pieces)
        value = pieces
        order = self.shard ^ jnp.arange(self.shards)
        hit = (order[:, None] == jnp.arange(self.shards)[None, :])[:, :, None, None]
        pieces = jnp.sum(jnp.where(hit, pieces[None], 0), axis=1, dtype=value.dtype)
        return jnp.concatenate([pieces[j] for j in range(self.shards)], axis=-1)

    def half_rows(self, rows):
        half = -(-rows // 32) * 16
        return half, self.core * (rows - half), (1 - self.core) * (rows - half)

    def order(self, scale, mine, theirs):
        kept = [(self.shard ^ hop) * scale + mine for hop in self.hops]
        given = [(self.shard ^ self.hops[self.twin(t)]) * scale + theirs for t in range(self.shards)]
        return kept, given

    def finish_rows(self, owned, other, rows):
        low = jnp.where(self.core == 0, owned, other)
        high = jnp.where(self.core == 0, other, owned)
        return jnp.concatenate([low[: rows - owned.shape[0]], high], axis=0).astype(F32)


class Plan:
    def __init__(self):
        self.have, self.tasks, self.made = {}, {}, {}

    def start(self, name, task):
        self.tasks[name] = task
        self.made[name] = None

    def advance(self, *names):
        for name in names:
            if name in self.tasks:
                try:
                    self.made[name] = self.tasks[name].send(self.made[name])
                except StopIteration:
                    del self.tasks[name], self.made[name]

    def close(self):
        self.have, self.made = lax.optimization_barrier((self.have, self.made))


def joined(pieces, starts, shape):
    if any(piece.shape[0] % 16 or piece.shape[1] % 128 and piece.shape[1] < shape[1] for piece in pieces):
        whole = jnp.zeros(shape, pieces[0].dtype)
        for piece, start in zip(pieces, starts):
            whole = lax.dynamic_update_slice(whole, piece, start)
        pieces, starts = (whole,), [(0, 0)]
    return tuple(pieces), numbers([at for start in starts for at in start]), shape


def numbers(values):
    return jnp.stack([jnp.asarray(value, jnp.int32) for value in values])


def load(pieces, starts_ref, whole, sems):
    copies = copies_of(pieces, starts_ref, whole, sems, 0)
    for _, copy in copies:
        copy.start()
    return lambda: [copy.wait() for _, copy in copies]


def copies_of(pieces, starts_ref, whole, sems, row):
    copies = []
    for i, piece in enumerate(pieces):
        rows = pl.ds(pl.multiple_of(starts_ref[2 * i] - row, 16), piece.shape[0])
        if piece.shape[1] == whole.shape[1]:
            place = whole.at[rows, :]
        else:
            columns = pl.ds(pl.multiple_of(starts_ref[2 * i + 1], 128), piece.shape[1])
            place = whole.at[rows, columns]
        copies.append((i, pltpu.make_async_copy(piece, place, sems.at[i])))
    return copies


def load_lower(pieces, starts_ref, whole, sems, row):
    if pieces[0].shape[0] > row:
        copy = pltpu.make_async_copy(pieces[0].at[row:, :], whole, sems.at[0])
        copy.start()
        return copy.wait
    copies = copies_of(pieces, starts_ref, whole, sems, row)

    def each(act):
        for i, copy in copies:
            pl.when(starts_ref[2 * i] >= row)(functools.partial(act, copy))

    each(lambda copy: copy.start())
    return lambda: each(lambda copy: copy.wait())


def load_halves(pieces, starts_ref, whole, sems):
    half = whole.shape[1] // 2
    copies = []
    for i, piece in enumerate(pieces):
        rows = pl.ds(pl.multiple_of(starts_ref[2 * i], 16), piece.shape[0])
        for h in range(2):
            columns = slice(h * half, (h + 1) * half)
            source = piece.at[:, columns] if piece.shape[1] > half else piece
            copy = pltpu.make_async_copy(source, whole.at[rows, columns], sems.at[i, h])
            copies.append((h, None if piece.shape[1] > half else starts_ref[2 * i + 1] == h * half, copy))

    def each(h, act):
        for at, there, copy in copies:
            if at == h and there is None:
                act(copy)
            elif at == h:
                pl.when(there)(functools.partial(act, copy))

    return lambda h: each(h, lambda copy: copy.start()), lambda h: each(h, lambda copy: copy.wait())


IN_VMEM = pl.BlockSpec(memory_space=pltpu.VMEM)
IN_SMEM = pl.BlockSpec(memory_space=pltpu.SMEM)
ANYWHERE = pl.BlockSpec(memory_space=pl.ANY)


def upright(ref):
    return jnp.concatenate([jnp.transpose(ref[m]) for m in range(ref.shape[0])], axis=0)


def turn(chunk, cosine, sine):
    lane = lax.broadcasted_iota(jnp.int32, chunk.shape, 1)
    partner = jnp.where(
        lane % HEAD_SIZE < HALF_HEAD,
        pltpu.roll(chunk, 128 - HALF_HEAD, 1),
        pltpu.roll(chunk, HALF_HEAD, 1),
    )
    return chunk * cosine + partner * sine


def project_kernel(count, starts_ref, x_ref, gains_ref, cos_ref, sin_ref, *refs):
    pieces = refs[:count]
    q_ref, kv_ref, whole, sems = refs[count:]
    wait = load(pieces, starts_ref, whole, sems)
    x = upright(x_ref).astype(F32)
    width = x.shape[1]
    act = (x * rms_inverse(x) * gains_ref[0:1, :]).astype(BF)
    wait()
    cosine, sine = cos_ref[...], sin_ref[...]
    for first in range(0, width + KV_WIDTH, 256):
        linear = nn(act, whole[:width, first : first + 256])
        for at in range(first, first + 256, 128):
            chunk = turn(linear[:, at - first : at - first + 128], cosine, sine)
            if at + 128 <= width:
                q_ref[:, at : at + 128] = (chunk * SCALE).astype(BF)
            elif at < width:
                q_ref[:, at:width] = (chunk[:, : width - at] * SCALE).astype(BF)
                kv_ref[:, : at + 128 - width] = chunk[:, width - at :].astype(BF)
            else:
                kv_ref[:, at - width : at - width + 128] = chunk.astype(BF)
    start = width // 128 * 128
    kv_ref[:, KV_WIDTH:] = nn(act, whole[width:, start:])[:, width - start :].astype(BF)


def project(x, gains, cosine, sine, pieces, starts, shape):
    micro, width, rows = x.shape
    tokens = micro * rows
    outs = (
        jax.ShapeDtypeStruct((tokens, width), BF),
        jax.ShapeDtypeStruct((tokens, 2 * KV_WIDTH), BF),
    )
    table = pl.BlockSpec((tokens, 128), lambda i: (0, 0))
    return pl.pallas_call(
        functools.partial(project_kernel, len(pieces)),
        grid=(1,),
        name="project",
        in_specs=[IN_SMEM] + [IN_VMEM] * 2 + [table] * 2 + [ANYWHERE] * len(pieces),
        out_specs=(IN_VMEM,) * 2,
        out_shape=outs,
        scratch_shapes=[pltpu.VMEM(shape, BF), pltpu.SemaphoreType.DMA((len(pieces),))],
        cost_estimate=cost(2 * tokens * width * (width + 2 * KV_WIDTH), 0, x, *outs, *pieces),
        compiler_params=pltpu.CompilerParams(vmem_limit_bytes=VMEM_LIMIT),
    )(starts, x, gains, cosine, sine, *pieces)


def across(ref):
    return jnp.concatenate([ref[m] for m in range(ref.shape[0])], axis=1)


def spread_out(value, ref):
    rows = ref.shape[2]
    for m in range(ref.shape[0]):
        ref[m] = value[:, m * rows : (m + 1) * rows]


def feed_kernel(counts, core_ref, s0_ref, s1_ref, s2_ref, x_ref, attn_ref, cot_ref, gains_ref, *refs):
    total_count = sum(counts)
    attention_pieces = refs[: counts[0]]
    pair_pieces = refs[counts[0] : counts[0] + counts[1]]
    down_pieces = refs[counts[0] + counts[1] : total_count]
    out_ref, inner_ref, kept_ref, given_ref, act_t_ref, attn_t_ref, resid_ref = refs[total_count : total_count + 7]
    w_attn, w_pair, w_down, sum_ref, sems0, sems1, sems2 = refs[total_count + 7 :]
    width = x_ref.shape[1]
    hidden = w_pair.shape[1]
    tile = hidden // 2
    wait_attention = load_lower(attention_pieces, s0_ref, w_attn, sems0, width)
    start_pair, wait_pair = load_halves(pair_pieces, s1_ref, w_pair, sems1)
    start_pair(0)
    wait_down = load(down_pieces, s2_ref, w_down, sems2)
    start_pair(1)
    even = core_ref[0] == 0
    x = upright(x_ref).astype(F32)
    dy = upright(cot_ref)
    attn_t_ref[...] = jnp.transpose(attn_ref[...])
    wait_attention()
    resid = x + nn(attn_ref[...], w_attn[:, : rounded_up(width)])[:, :width]
    resid_t = jnp.transpose(resid)
    resid_ref[...] = resid_t
    sum_ref[...] = resid_t
    act = (resid * rms_inverse(resid) * gains_ref[1:2, :]).astype(BF)
    act_t_ref[...] = jnp.transpose(act)
    wait_pair(0)
    wait_down()
    for first in range(0, hidden, tile):
        if first == hidden // 2:
            wait_pair(1)
        here = slice(first, first + tile)
        gate = nn(act, w_pair[:width, here])
        upper = nn(act, w_pair[width:, here])
        d_inner = nn(dy, w_down[:, here])
        sigmoid = 1.0 / (1.0 + jnp.exp(-gate))
        silu = gate * sigmoid
        inner = (silu * upper).astype(BF)
        inner_ref[:, here] = inner
        d_gate = d_inner * upper * sigmoid * (1.0 + gate * (1.0 - sigmoid))
        d_upper = d_inner * silu
        kept_ref[:, here] = jnp.where(even, d_gate, d_upper).astype(BF)
        given_ref[:, here] = jnp.where(even, d_upper, d_gate).astype(BF)
        sum_ref[...] += nn(w_down[:, here], jnp.transpose(inner))
    spread_out(sum_ref[...].astype(BF), out_ref)


def feed(core, x, attn, dy, gains, attention_got, pair_got, down_got):
    micro, width, rows = x.shape
    tokens = micro * rows
    groups = [attention_got, pair_got, down_got]
    counts = [len(pieces) for pieces, _, _ in groups]
    shapes = [shape for _, _, shape in groups]
    hidden = shapes[1][1]
    outs = (jax.ShapeDtypeStruct(x.shape, BF),)
    outs += (jax.ShapeDtypeStruct((tokens, hidden), BF),) * 3
    outs += (jax.ShapeDtypeStruct((width, tokens), BF),) * 2
    outs += (jax.ShapeDtypeStruct((width, tokens), F32),)
    every = [piece for pieces, _, _ in groups for piece in pieces]
    return pl.pallas_call(
        functools.partial(feed_kernel, counts),
        name="feed",
        in_specs=[IN_SMEM] * 4 + [IN_VMEM] * 4 + [ANYWHERE] * len(every),
        out_specs=(IN_VMEM,) * 7,
        out_shape=outs,
        scratch_shapes=[pltpu.VMEM((width, shapes[0][1]), BF)]
        + [pltpu.VMEM(shape, BF) for shape in shapes[1:]]
        + [pltpu.VMEM((width, tokens), F32)]
        + [pltpu.SemaphoreType.DMA(size) for size in ((counts[0],), (counts[1], 2), (counts[2],))],
        cost_estimate=cost(
            2 * tokens * width * (4 * hidden + width), tokens * hidden, x, x, x, *outs, *every
        ),
        compiler_params=pltpu.CompilerParams(vmem_limit_bytes=VMEM_MOST),
    )(core, *(starts for _, starts, _ in groups), x, attn, dy, gains, *every)


def feed_back_kernel(counts, core_ref, s0_ref, s1_ref, resid_ref, cot_ref, kept_ref, given_ref, gain_ref, *refs):
    total_count = sum(counts)
    dres_ref, low_ref, dattn_ref, w_attn, w_pair, sems0, sems1 = refs[total_count:]
    width = resid_ref.shape[0]
    start_pair, wait_pair = load_halves(refs[counts[0] : total_count], s1_ref, w_pair, sems1)
    start_pair(0)
    start_pair(1)
    wait_attention = load_lower(refs[: counts[0]], s0_ref, w_attn, sems0, width)
    resid = resid_ref[...]
    root = lax.rsqrt(jnp.mean(resid * resid, axis=0, keepdims=True) + EPS)
    normed = resid * root
    half = w_pair.shape[1] // 2
    for h in range(2):
        columns = slice(h * half, (h + 1) * half)
        weight = lambda i: w_pair[pl.ds(pl.multiple_of(i * width, 16), width), columns]
        wait_pair(h)
        part = nt(weight(core_ref[0]), kept_ref[:, columns]) + nt(weight(1 - core_ref[0]), given_ref[:, columns])
        d_act = part if h == 0 else d_act + part
    d_normed = d_act * gain_ref[...]
    d_resid = across(cot_ref).astype(F32) + root * (
        d_normed - normed * jnp.mean(d_normed * normed, axis=0, keepdims=True)
    )
    dres_ref[...] = d_resid
    low = d_resid.astype(BF)
    low_ref[:, :width] = jnp.transpose(low)
    if low_ref.shape[1] > width:
        low_ref[:, width:] = jnp.zeros((low_ref.shape[0], low_ref.shape[1] - width), BF)
    wait_attention()
    dattn_ref[...] = jnp.transpose(nn(w_attn[:, :width], low).astype(BF))


def feed_back(core, resid, dy, kept, given, gain, attention_got, pair_got):
    width, tokens = resid.shape
    groups = [attention_got, pair_got]
    counts = [len(pieces) for pieces, _, _ in groups]
    shapes = [shape for _, _, shape in groups]
    outs = (
        jax.ShapeDtypeStruct((width, tokens), F32),
        jax.ShapeDtypeStruct((tokens, rounded_up(width)), BF),
        jax.ShapeDtypeStruct((tokens, width), BF),
    )
    every = [piece for pieces, _, _ in groups for piece in pieces]
    return pl.pallas_call(
        functools.partial(feed_back_kernel, counts),
        name="feed_back",
        in_specs=[IN_SMEM] * 3 + [IN_VMEM] * 5 + [ANYWHERE] * len(every),
        out_specs=(IN_VMEM,) * 3,
        out_shape=outs,
        scratch_shapes=[pltpu.VMEM((width, shapes[0][1]), BF), pltpu.VMEM(shapes[1], BF)]
        + [pltpu.SemaphoreType.DMA(size) for size in ((counts[0],), (counts[1], 2))],
        cost_estimate=cost(
            2 * tokens * width * (2 * shapes[1][1] + width), 0, resid, dy, kept, given, *outs, *every
        ),
        compiler_params=pltpu.CompilerParams(vmem_limit_bytes=VMEM_MOST),
    )(core, *(starts for _, starts, _ in groups), resid, dy, kept, given, gain, *every)


def pick_rows(source, starts_ref, base, rows, count, target):
    for t in range(count):
        start = pl.multiple_of(starts_ref[base + t], 16)
        target[t * rows : (t + 1) * rows, :] = source[pl.ds(start, rows), :]


def down_grad_kernel(shards, cut, info_ref, cot_ref, far_cot_ref, inner_ref, far_inner_ref, low_ref, high_ref, dy):
    micro, width, rows = cot_ref.shape
    tokens, part = micro * rows, low_ref.shape[0] // (shards // 2)
    first = pl.multiple_of(info_ref[0], 16)
    for i, ref in enumerate((cot_ref, far_cot_ref)):
        for m in range(micro):
            at = i * tokens + m * rows
            dy[:, at : at + rows] = ref[m, pl.ds(first, part), :]
    for t in range(shards):
        columns = pl.ds(pl.multiple_of(info_ref[1 + t], 128), cut)
        made = nn(dy[:, :tokens], inner_ref[:, columns]) + nn(dy[:, tokens:], far_inner_ref[:, columns])
        out_ref, at = (low_ref, t) if t < shards // 2 else (high_ref, t - shards // 2)
        out_ref[at * part : (at + 1) * part, :] = made.astype(BF)


def down_grad(cot, far_cot, inner, far_inner, first, starts):
    shards, (micro, width, rows), (tokens, hidden) = len(starts), cot.shape, inner.shape
    part, cut = width // 2, hidden // shards
    outs = (jax.ShapeDtypeStruct((shards // 2 * part, cut), BF),) * 2
    if part % 16 or cut % 128:
        grad = nn(jnp.concatenate(list(cot), axis=1), inner) + nn(jnp.concatenate(list(far_cot), axis=1), far_inner)
        grad = lax.dynamic_slice_in_dim(grad.astype(BF), first, part, 0)
        blocks = [lax.dynamic_slice_in_dim(grad, start, cut, 1) for start in starts]
        return [jnp.concatenate(blocks[: shards // 2]), jnp.concatenate(blocks[shards // 2 :])]
    return pl.pallas_call(
        functools.partial(down_grad_kernel, shards, cut),
        name="down_grad",
        in_specs=[IN_SMEM] + [IN_VMEM] * 4,
        out_specs=(IN_VMEM,) * 2,
        out_shape=outs,
        scratch_shapes=[pltpu.VMEM((part, 2 * tokens), BF)],
        cost_estimate=cost(4 * part * tokens * hidden, 0, cot, cot, inner, inner, *outs),
        compiler_params=pltpu.CompilerParams(vmem_limit_bytes=VMEM_LIMIT),
    )(numbers([first] + starts), cot, far_cot, inner, far_inner)


def wide_grad_kernel(cuts, count, starts_ref, left_ref, far_left_ref, right_ref, far_right_ref, *refs):
    outs, ordered = refs[: 2 * len(cuts)], refs[2 * len(cuts)]
    tokens = left_ref.shape[1]

    @pl.when(pl.program_id(0) == 0)
    def _():
        at = first = 0
        for cut in cuts:
            for t in range(count):
                start = pl.multiple_of(starts_ref[t] + first, 16)
                ordered[at : at + cut, :tokens] = left_ref[pl.ds(start, cut), :]
                ordered[at : at + cut, tokens:] = far_left_ref[pl.ds(start, cut), :]
                at += cut
            first += cut

    made = nn(ordered[:, :tokens], right_ref[...]) + nn(ordered[:, tokens:], far_right_ref[...])
    at = 0
    for i, out_ref in enumerate(outs):
        size = out_ref.shape[0]
        out_ref[...] = made[at : at + size].astype(BF)
        at += size


def wide_grad(left, far_left, right, far_right, rows, cuts, starts):
    count, (tokens, columns) = len(starts), right.shape
    outs = tuple(jax.ShapeDtypeStruct((count // 2 * cut, columns), BF) for cut in cuts for _ in range(2))
    if rows % 16 or any(cut % 16 for cut in cuts):
        grad = (nn(left, right) + nn(far_left, far_right)).astype(BF)
        made, first = [], 0
        for cut in cuts:
            blocks = [lax.dynamic_slice_in_dim(grad, start + first, cut, 0) for start in starts]
            made += [jnp.concatenate(blocks[: count // 2]), jnp.concatenate(blocks[count // 2 :])]
            first += cut
        return made
    tile = 512 if columns % 512 == 0 else columns
    part = pl.BlockSpec((tokens, tile), lambda n, starts: (0, n))
    whole = pl.BlockSpec(left.shape, lambda n, starts: (0, 0))
    return pl.pallas_call(
        functools.partial(wide_grad_kernel, cuts, count),
        grid_spec=pltpu.PrefetchScalarGridSpec(
            num_scalar_prefetch=1,
            grid=(columns // tile,),
            in_specs=[whole, whole, part, part],
            out_specs=tuple(pl.BlockSpec((out.shape[0], tile), lambda n, starts: (0, n)) for out in outs),
            scratch_shapes=[pltpu.VMEM((count * rows, 2 * tokens), BF)],
        ),
        out_shape=outs,
        name="wide_grad",
        cost_estimate=cost(4 * tokens * rows * count * columns, 0, left, left, right, right, *outs),
        compiler_params=pltpu.CompilerParams(vmem_limit_bytes=VMEM_LIMIT),
    )(numbers(starts), left, far_left, right, far_right)


def settle_wide_kernel(cuts, core_ref, gain_ref, *refs):
    sums = refs[: 2 * len(cuts)]
    w_left, w_right, left_ref, right_ref, sum_ref = refs[2 * len(cuts) :]
    even = core_ref[0] == 0
    at = 0
    for c, cut in enumerate(cuts):
        here = slice(at, at + cut)
        mine, theirs = sums[2 * c][...].astype(F32), sums[2 * c + 1][...].astype(F32)
        left, right = jnp.where(even, mine, theirs), jnp.where(even, theirs, mine)
        left_ref[here, :], right_ref[here, :] = left, right
        both = w_left[here, :].astype(F32) * left + w_right[here, :].astype(F32) * right
        sum_ref[here, :] = jnp.sum(both, axis=1, keepdims=True) / gain_ref[here, :]
        at += cut


def settle_wide(core, gain, sums, cuts, w_left, w_right):
    out = jax.ShapeDtypeStruct(w_left.shape, F32)
    column = jax.ShapeDtypeStruct((w_left.shape[0], 1), F32)
    if any(cut % 16 for cut in cuts):
        pairs = [(mine.astype(F32), theirs.astype(F32)) for mine, theirs in sums]
        left = jnp.concatenate([jnp.where(core[0] == 0, a, b) for a, b in pairs])
        right = jnp.concatenate([jnp.where(core[0] == 0, b, a) for a, b in pairs])
        both = w_left.astype(F32) * left + w_right.astype(F32) * right
        return left, right, jnp.sum(both, axis=1, keepdims=True) / gain
    args = [value for pair in sums for value in pair]
    return pl.pallas_call(
        functools.partial(settle_wide_kernel, cuts),
        name="settle",
        in_specs=[IN_SMEM] + [IN_VMEM] * (3 + len(args)),
        out_specs=(IN_VMEM,) * 3,
        out_shape=(out, out, column),
        cost_estimate=cost(4 * w_left.size, 0, out, out, *args),
        compiler_params=pltpu.CompilerParams(vmem_limit_bytes=VMEM_LIMIT),
    )(core, gain, *args, w_left, w_right)


def settle_some_kernel(core_ref, gain_ref, mine_ref, theirs_ref, wq_ref, wk_ref, wv_ref, *refs):
    q_ref, o_ref, k_ref, v_ref, sum_ref, kv = refs
    rows, width = q_ref.shape
    half, wide = mine_ref.shape[0], rounded_up(width)
    even = core_ref[0] == 0
    mine, theirs = mine_ref[...].astype(F32), theirs_ref[...].astype(F32)
    parts = (
        (0, jnp.where(even, mine, theirs)[: rows - half]),
        (rows - half, jnp.where(even, theirs, mine)),
    )
    for at, part in parts:
        here = slice(at, at + part.shape[0])
        q_ref[here, :] = part[:, :width]
        o_ref[here, :] = part[:, wide : wide + width]
        kv[here, :] = part[:, 2 * wide :]
        sum_ref[here, :] = jnp.sum(wq_ref[here, :].astype(F32) * part[:, :width], axis=1, keepdims=True)
    sums = sum_ref[...]
    for out_ref, w_ref, first in ((k_ref, wk_ref, 0), (v_ref, wv_ref, KV_WIDTH)):
        grad = kv[:, first : first + KV_WIDTH]
        out_ref[...] = jnp.transpose(grad)
        weight = jnp.transpose(w_ref[...]).astype(F32)
        sums += jnp.sum(weight * grad, axis=1, keepdims=True)
    sum_ref[...] = sums / gain_ref[...]


def settle_some(core, gain, mine, theirs, w_query, w_key, w_value):
    rows, width = w_query.shape
    half, wide = mine.shape[0], rounded_up(width)
    if (rows - half) % 16:
        low, high = jnp.where(core[0] == 0, mine, theirs), jnp.where(core[0] == 0, theirs, mine)
        grad = jnp.concatenate([low[: rows - half], high]).astype(F32)
        key, value = grad[:, 2 * wide : 2 * wide + KV_WIDTH], grad[:, 2 * wide + KV_WIDTH :]
        pairs = ((w_query, grad[:, :width]), (w_key.T, key), (w_value.T, value))
        sums = sum(jnp.sum(w.astype(F32) * g, axis=1, keepdims=True) for w, g in pairs)
        return grad[:, :width], grad[:, wide : wide + width], key.T, value.T, sums / gain
    outs = (jax.ShapeDtypeStruct((rows, width), F32),) * 2
    outs += (jax.ShapeDtypeStruct((KV_WIDTH, rows), F32),) * 2
    outs += (jax.ShapeDtypeStruct((rows, 1), F32),)
    return pl.pallas_call(
        settle_some_kernel,
        name="settle_some",
        in_specs=[IN_SMEM] + [IN_VMEM] * 6,
        out_specs=(IN_VMEM,) * 5,
        out_shape=outs,
        scratch_shapes=[pltpu.VMEM((rows, 2 * KV_WIDTH), F32)],
        cost_estimate=cost(4 * w_query.size, 0, mine, theirs, *outs),
        compiler_params=pltpu.CompilerParams(vmem_limit_bytes=VMEM_LIMIT),
    )(core, gain, mine, theirs, w_query, w_key, w_value)


def turn_keys(source, target, at, cosine, sine):
    rows = source.shape[0]
    for first in range(0, KV_WIDTH, 128):
        chunk = turn(source[:, first : first + 128].astype(F32), cosine, -sine).astype(BF)
        last = min(first + 128, KV_WIDTH)
        target[at : at + rows, first:last] = chunk[:, : last - first]
    target[at : at + rows, KV_WIDTH:] = source[:, KV_WIDTH:]


def attention_grad_kernel(shards, half, starts_ref, gain_ref, cos_ref, sin_ref, dq_ref, attn_ref, low_ref, *refs):
    xs, halves = refs[:shards], refs[shards : shards + 2]
    dkvs = [ref.at[t] for ref in halves for t in range(shards // 2)]
    outs, (act, dkv, ordered, attn_ordered) = refs[shards + 2 : shards + 4], refs[shards + 4 :]
    micro, width, rows = xs[0].shape
    tokens = micro * rows
    wide = rounded_up(width)
    for t in range(shards):
        here = slice(t * tokens, (t + 1) * tokens)
        turn_keys(dkvs[t], dkv, t * tokens, cos_ref[here, :], sin_ref[here, :])
        for m in range(micro):
            x = xs[t][m].astype(F32)
            root = lax.rsqrt(jnp.mean(x * x, axis=0, keepdims=True) + EPS)
            first = t * tokens + m * rows
            act[:, first : first + rows] = (x * root * gain_ref[...]).astype(BF)
    for i, out_ref in enumerate(outs):
        pick_rows(act, starts_ref, i * shards, half, shards, ordered)
        pick_rows(attn_ref, starts_ref, i * shards, half, shards, attn_ordered)
        out_ref[:, :wide] = nn(ordered[:, :tokens], dq_ref[...]).astype(BF)
        out_ref[:, wide : 2 * wide] = nn(attn_ordered[...], low_ref[...]).astype(BF)
        out_ref[:, 2 * wide :] = nn(ordered[...], dkv[...]).astype(BF)


def attention_grad(x_all, gain, cosine, sine, dq, attn_t, low, dkv_all, half, given, kept):
    shards = len(x_all)
    micro, width, rows = x_all[0].shape
    every = shards * micro * rows
    wide = rounded_up(width)
    out = jax.ShapeDtypeStruct((shards * half, 2 * wide + 2 * KV_WIDTH), BF)
    if half % 16 or width // shards % 16:
        xs = jnp.concatenate([x[m] for x in x_all for m in range(micro)], axis=1).astype(F32)
        act = xs * lax.rsqrt(jnp.mean(xs * xs, axis=0, keepdims=True) + EPS) * gain
        act = act.astype(BF)
        dkv = jnp.concatenate(dkv_all, axis=0).reshape(every, 2 * KV_WIDTH)
        keys = dkv[:, :KV_WIDTH].astype(F32).reshape(every, -1, 2, HALF_HEAD)
        c, s = cosine[:, None, :HALF_HEAD], sine[:, None, HALF_HEAD:HEAD_SIZE]
        first, second = keys[:, :, 0], keys[:, :, 1]
        keys = jnp.stack([first * c + second * s, second * c - first * s], axis=2)
        dkv = jnp.concatenate([keys.reshape(every, KV_WIDTH).astype(BF), dkv[:, KV_WIDTH:]], axis=1)
        parts = [nn(act[:, : micro * rows], dq), nn(attn_t, low), nn(act, dkv)]
        grad = jnp.concatenate(parts, axis=1).astype(BF)
        return [
            jnp.concatenate([lax.dynamic_slice_in_dim(grad, start, half, 0) for start in starts])
            for starts in (given, kept)
        ]
    return pl.pallas_call(
        functools.partial(attention_grad_kernel, shards, half),
        name="attention_grad",
        in_specs=[IN_SMEM] + [IN_VMEM] * (8 + shards),
        out_specs=(IN_VMEM,) * 2,
        out_shape=(out, out),
        scratch_shapes=[
            pltpu.VMEM((width, every), BF),
            pltpu.VMEM((every, 2 * KV_WIDTH), BF),
            pltpu.VMEM((shards * half, every), BF),
            pltpu.VMEM((shards * half, micro * rows), BF),
        ],
        cost_estimate=cost(
            4 * shards * half * (every * 2 * KV_WIDTH + 2 * micro * rows * width),
            0,
            *x_all,
            *dkv_all,
            out,
            out,
        ),
        compiler_params=pltpu.CompilerParams(vmem_limit_bytes=VMEM_MOST),
    )(numbers(given + kept), gain, cosine, sine, dq, attn_t, low, *x_all, *dkv_all)


def finish_kernel(count, starts_ref, x_ref, low_ref, kv_ref, dres_ref, gain_ref, cos_ref, sin_ref, *refs):
    pieces = refs[:count]
    dx_ref, whole, kv_turned, sems = refs[count:]
    wait = load(pieces, starts_ref, whole, sems)
    turn_keys(kv_ref, kv_turned, 0, cos_ref[...], sin_ref[...])
    x = across(x_ref).astype(F32)
    width = x.shape[0]
    root = lax.rsqrt(jnp.mean(x * x, axis=0, keepdims=True) + EPS)
    normed = x * root
    wait()
    d_act = nt(whole[:width, :width], low_ref[:, :width])
    d_act += nt(whole[:width, width:], kv_turned[:, :KV_WIDTH])
    d_act += nt(whole[width:, width:], kv_turned[:, KV_WIDTH:])
    d_normed = d_act * gain_ref[...]
    d_x = dres_ref[...] + root * (d_normed - normed * jnp.mean(d_normed * normed, axis=0, keepdims=True))
    spread_out(d_x.astype(BF), dx_ref)


def finish(x, low, kv, dres, gain, cosine, sine, pieces, starts, shape):
    micro, width, rows = x.shape
    tokens = micro * rows
    table = pl.BlockSpec((tokens, 128), lambda i: (0, 0))
    return pl.pallas_call(
        functools.partial(finish_kernel, len(pieces)),
        grid=(1,),
        name="finish",
        in_specs=[IN_SMEM] + [IN_VMEM] * 5 + [table] * 2 + [ANYWHERE] * len(pieces),
        out_specs=IN_VMEM,
        out_shape=jax.ShapeDtypeStruct(x.shape, BF),
        scratch_shapes=[
            pltpu.VMEM(shape, BF),
            pltpu.VMEM((tokens, 2 * KV_WIDTH), BF),
            pltpu.SemaphoreType.DMA((len(pieces),)),
        ],
        cost_estimate=cost(2 * tokens * width * (width + 2 * KV_WIDTH), 0, x, low, dres, *pieces),
        compiler_params=pltpu.CompilerParams(vmem_limit_bytes=VMEM_LIMIT),
    )(starts, x, low, kv, dres, gain, cosine, sine, *pieces)


def head(ref, h):
    return ref[:, h * HEAD_SIZE : (h + 1) * HEAD_SIZE]


def widen(value, columns):
    n = value.shape[0]
    lane = lax.broadcasted_iota(jnp.int32, (n, HEAD_SIZE), 1)
    tail = jnp.zeros((n, HEAD_SIZE), F32)
    for c, column in enumerate(columns):
        tail = jnp.where(lane == c, column, tail)
    return jnp.concatenate([value, tail.astype(BF)], axis=1)


def split(column):
    high = column.astype(BF).astype(F32)
    middle = (column - high).astype(BF).astype(F32)
    return [high, middle, column - high - middle]


def attend_kernel(shards, seg_rows, q_ref, *refs):
    kv = refs[:shards]
    bias_ref = refs[shards]
    o_ref, lse_ref = refs[-2:]
    rows = q_ref.shape[0]
    i = lax.broadcasted_iota(jnp.int32, (rows, rows), 0)
    j = lax.broadcasted_iota(jnp.int32, (rows, rows), 1)
    same = (i // seg_rows) == (j // seg_rows)
    own = jnp.where(j > i, CLOSED, jnp.where(same, 0.0, bias_ref[0:1, :]))
    one = jnp.ones((rows, 1), F32)
    bias_columns = jnp.transpose(bias_ref[...])
    lse = jnp.zeros((rows, 128), F32)
    lane = lax.broadcasted_iota(jnp.int32, (rows, 128), 1)
    for g in range(KEY_VALUE_HEADS):
        keys, values = [], []
        for t in range(shards):
            keys.append(widen(head(kv[t], g), [bias_columns[:, t : t + 1]] if t else []))
            values.append(widen(head(kv[t], KEY_VALUE_HEADS + g), [one]))
        for h in range(g * GROUP, g * GROUP + GROUP):
            q = widen(head(q_ref, h), [one])
            scores = [nt(q, k) for k in keys]
            scores[0] = scores[0] + own
            peak = functools.reduce(jnp.maximum, scores)
            peak = jnp.max(peak, axis=1, keepdims=True)
            terms = [nn(jnp.exp(s - peak).astype(BF), v) for s, v in zip(scores, values)]
            mixed = sum(terms[1:], terms[0])
            total = mixed[:, HEAD_SIZE : HEAD_SIZE + 1]
            o_ref[:, h * HEAD_SIZE : (h + 1) * HEAD_SIZE] = (mixed[:, :HEAD_SIZE] / total).astype(BF)
            lse = jnp.where(lane == h, peak + jnp.log(total), lse)
    lse_ref[...] = lse


def attend_back_kernel(shards, seg_rows, q_ref, *refs):
    kv = refs[:shards]
    bias_ref, o_ref, do_ref, lse_ref, cos_ref, sin_ref = refs[shards : shards + 6]
    dq_ref, low_ref, high_ref = refs[-3:]
    dkv = [ref.at[t] for ref in (low_ref, high_ref) for t in range(shards // 2)]
    rows = q_ref.shape[0]
    i = lax.broadcasted_iota(jnp.int32, (rows, rows), 1)
    j = lax.broadcasted_iota(jnp.int32, (rows, rows), 0)
    bias_columns = jnp.transpose(bias_ref[...])
    same = (i // seg_rows) == (j // seg_rows)
    own_column = jnp.broadcast_to(bias_columns[:, 0:1], (rows, rows))
    own = jnp.where(j > i, CLOSED, jnp.where(same, 0.0, own_column))
    one, zero = jnp.ones((rows, 1), F32), jnp.zeros((rows, 1), F32)
    cosine, sine = cos_ref[...], sin_ref[...]
    if dq_ref.shape[1] > QUERY_HEADS * HEAD_SIZE:
        dq_ref[:, QUERY_HEADS * HEAD_SIZE :] = jnp.zeros((rows, dq_ref.shape[1] - QUERY_HEADS * HEAD_SIZE), BF)
    for g in range(KEY_VALUE_HEADS):
        keys, values, turned = [], [], []
        for t in range(shards):
            k = head(kv[t], g)
            turned.append(jnp.transpose(k))
            keys.append(widen(k, [bias_columns[:, t : t + 1] if t else zero, one, one, one]))
            values.append(widen(head(kv[t], KEY_VALUE_HEADS + g), [one, one, one]))
        dk, dv = [None] * shards, [None] * shards
        for h in range(g * GROUP, g * GROUP + GROUP):
            q, do = head(q_ref, h), head(do_ref, h)
            centre = jnp.sum(head(o_ref, h).astype(F32) * do.astype(F32), axis=1, keepdims=True)
            q_wide = widen(q, [one] + split(-lse_ref[:, h : h + 1]))
            do_wide = widen(do, split(-centre))
            dq = None
            for t in range(shards):
                scores = nt(keys[t], q_wide)
                if t == 0:
                    scores = scores + own
                probs = jnp.exp(scores)
                ds = (probs * nt(values[t], do_wide)).astype(BF)
                v_term = nn(probs.astype(BF), do)
                k_term = nn(ds, q)
                q_term = nn(turned[t], ds)
                dv[t] = v_term if dv[t] is None else dv[t] + v_term
                dk[t] = k_term if dk[t] is None else dk[t] + k_term
                dq = q_term if dq is None else dq + q_term
            dq = dq * SCALE
            first, second = dq[:HALF_HEAD], dq[HALF_HEAD:]
            back = jnp.concatenate(
                [first * cosine + second * sine, second * cosine - first * sine], axis=0
            )
            dq_ref[:, h * HEAD_SIZE : (h + 1) * HEAD_SIZE] = jnp.transpose(back.astype(BF))
        for t in range(shards):
            dkv[t][:, g * HEAD_SIZE : (g + 1) * HEAD_SIZE] = dk[t].astype(BF)
            g_value = KEY_VALUE_HEADS + g
            dkv[t][:, g_value * HEAD_SIZE : (g_value + 1) * HEAD_SIZE] = dv[t].astype(BF)


def attend(micro, seg_rows, q, kv, bias):
    shards, tokens, width = len(kv), q.shape[0], q.shape[1]
    rows = tokens // micro
    here = lambda w: pl.BlockSpec((rows, w), lambda m: (m, 0))
    outs = (jax.ShapeDtypeStruct((tokens, width), BF), jax.ShapeDtypeStruct((tokens, 128), F32))
    pairs = tokens * rows * shards * QUERY_HEADS
    return pl.pallas_call(
        functools.partial(attend_kernel, shards, seg_rows),
        grid=(micro,),
        name="attend",
        in_specs=[here(width)]
        + [here(2 * KV_WIDTH)] * shards
        + [pl.BlockSpec((None,) + bias.shape[1:], lambda m: (m, 0, 0))],
        out_specs=(here(width), here(128)),
        out_shape=outs,
        cost_estimate=cost(16 * HEAD_SIZE * pairs, pairs, q),
        compiler_params=pltpu.CompilerParams(vmem_limit_bytes=VMEM_LIMIT),
    )(q, *kv, bias)


def attend_back(m, rows, seg_rows, q, kv, bias, o, do, lse, cosine, sine, earlier):
    shards, tokens, width = len(kv), q.shape[0], q.shape[1]
    here = lambda w: pl.BlockSpec((rows, w), lambda i: (m, 0))
    turned = pl.BlockSpec((HALF_HEAD, rows), lambda i: (0, m))
    outs = (jax.ShapeDtypeStruct((tokens, rounded_up(width)), BF),)
    outs += (jax.ShapeDtypeStruct((shards // 2, tokens, 2 * KV_WIDTH), BF),) * 2
    pieces = pl.BlockSpec((shards // 2, rows, 2 * KV_WIDTH), lambda i: (0, m, 0))
    pairs = rows * rows * shards * QUERY_HEADS
    return pl.pallas_call(
        functools.partial(attend_back_kernel, shards, seg_rows),
        grid=(1,),
        name="attend_back",
        in_specs=[here(width)]
        + [here(2 * KV_WIDTH)] * shards
        + [pl.BlockSpec((None,) + bias.shape[1:], lambda i: (m, 0, 0))]
        + [here(width), here(width), here(128), turned, turned]
        + [pl.BlockSpec(memory_space=pl.ANY)] * len(earlier),
        out_specs=(here(rounded_up(width)), pieces, pieces),
        out_shape=outs,
        input_output_aliases={shards + 7 + i: i for i in range(len(earlier))},
        cost_estimate=cost(40 * HEAD_SIZE * pairs, pairs, q),
        compiler_params=pltpu.CompilerParams(vmem_limit_bytes=VMEM_LIMIT),
    )(q, *kv, bias, o, do, lse, cosine, sine, *earlier)


def local(
    block_input,
    parent_ids,
    w_query,
    key_weight,
    value_weight,
    w_output,
    w_gate,
    w_up,
    w_down,
    norm_first,
    norm_second,
    out_cotangent,
):
    micro, rows, width = block_input.shape
    shards = lax.axis_size("shard")
    links = Links(lax.axis_size("rep"), shards)
    tree = rows * shards
    segs = parent_ids.shape[2]
    seg_rows = tree // segs
    tokens = micro * rows
    hidden = w_gate.shape[1]

    inputs = block_input.swapaxes(1, 2)
    cotangent = out_cotangent.swapaxes(1, 2)

    even = links.core == 0
    side = lax.axis_index("rep") // 2 % 2
    left = jnp.concatenate([w_query, key_weight], axis=1)
    right = jnp.concatenate([w_output, value_weight], axis=1)
    attn_mine = jnp.where(even, left, right)
    pair_cut = hidden // 2
    pair_mine = lax.dynamic_slice_in_dim(jnp.where(even, w_gate, w_up), side * pair_cut, pair_cut, 1)
    down_own = w_down.T
    down_cut = width // 2
    down_mine = lax.dynamic_slice_in_dim(down_own, links.core * down_cut, down_cut, 0)
    core = numbers([links.core])

    attn_near = links.near(attn_mine)
    gain_pieces = links.small_pieces(jnp.stack([norm_first, norm_second]))
    attn_mine, attn_near, gain_pieces, pair_mine, down_mine = meet(
        attn_mine, attn_near, gain_pieces, pair_mine, down_mine
    )

    gains = links.in_order(gain_pieces).astype(F32)
    attn_all = links.far(attn_mine, attn_near)
    attn_swapped = {t: links.swap(attn_near[t]) for t in attn_near}
    pair_near = {1: links.step(pair_mine, 0)}
    parents = parent_ids[:, 0]
    seg = jnp.arange(segs)
    after_parent = jnp.concatenate([parents[:, 1:], jnp.full((micro, 1), -1, parents.dtype)], axis=1)
    on_path = (seg % 2 == 0)[None] | (after_parent == seg[None])
    below = (seg[None, :] < seg[:, None])[None]
    depth = jnp.sum(jnp.where(below, on_path.astype(F32)[:, None, :], 0.0), axis=-1)

    def row_numbers(hop):
        return (links.shard ^ hop) * rows + jnp.arange(rows)

    def pick(table, numbers):
        hit = (numbers // seg_rows)[..., None] == seg
        return jnp.sum(jnp.where(hit[None], table.reshape(micro, *(1,) * numbers.ndim, segs), 0), axis=-1)

    key_rows = jnp.stack([row_numbers(hop) for hop in links.hops])
    positions = pick(depth, key_rows) * seg_rows + (key_rows % seg_rows).astype(F32)
    freqs = jnp.exp(-math.log(10000.0) * jnp.arange(HALF_HEAD, dtype=F32) * (2.0 / HEAD_SIZE))
    angles = freqs[:, None] * positions.swapaxes(0, 1).reshape(1, shards * tokens)
    cosine_t, sine_t = jnp.cos(angles), jnp.sin(angles)
    cosine = jnp.tile(cosine_t.T, (1, 4))
    sine = jnp.tile(jnp.concatenate([-sine_t.T, sine_t.T], axis=1), (1, 2))
    open_key = (pick(on_path.astype(F32), key_rows) > 0.5) & (
        (key_rows < links.shard * rows) | (jnp.arange(shards) == 0)[:, None]
    )
    bias = jnp.where(open_key, 0.0, CLOSED)
    bias = jnp.pad(bias, ((0, 0), (0, 8 - shards), (0, 0)))

    gain_one, gain_two = gains[0][:, None], gains[1][:, None]
    tables = (cosine, sine, cosine_t, sine_t, bias, gains, gain_one, gain_two)
    attn_all, attn_swapped, pair_mine, pair_near, down_mine, tables = meet(
        attn_all, attn_swapped, pair_mine, pair_near, down_mine, tables
    )
    cosine, sine, cosine_t, sine_t, bias, gains, gain_one, gain_two = tables

    for t in range(1, shards):
        if t not in attn_swapped:
            attn_swapped[t] = links.swap(attn_all[t])
    shard_rows = width // shards

    def pair_place(weight, hop):
        return weight * width + (links.shard ^ hop) * shard_rows

    pieces, starts = [left, right], [(pair_place(0, 0), 0), (pair_place(1, 0), 0)]
    for t in range(1, shards):
        pieces += [attn_all[t], attn_swapped[t]]
        starts += [
            (pair_place(links.core, links.hops[t]), 0),
            (pair_place(1 - links.core, links.hops[links.twin(t)]), 0),
        ]
    attention_got = joined(pieces, starts, (2 * width, left.shape[1]))
    pair_near |= {1 << i: links.step(pair_mine, i) for i in range(1, links.bits)}
    pair_beside = {1: links.beside(pair_near[1])}
    down_near = {1: links.step(down_mine, 0)}
    queries, kv = project(inputs, gains, cosine, sine, *attention_got)
    queries, kv, pair_mine, pair_near, pair_beside, down_mine, down_near = meet(
        queries, kv, pair_mine, pair_near, pair_beside, down_mine, down_near
    )

    kv_near = links.near(kv)
    pair_beside |= {t: links.beside(pair_near[t]) for t in pair_near if t > 1}
    kv_near, kv, pair_beside, pair_near, pair_mine = meet(kv_near, kv, pair_beside, pair_near, pair_mine)

    kv_all = links.far(kv, kv_near)
    pair_all = links.far(pair_mine, pair_near)
    pair_swapped = {t: links.swap(pair_near[t]) for t in pair_near}
    pair_crossed = {t: links.swap(pair_beside[t]) for t in pair_beside}
    kv_all, pair_all, pair_swapped, pair_crossed, pair_beside, down_mine, down_near = meet(
        kv_all, pair_all, pair_swapped, pair_crossed, pair_beside, down_mine, down_near
    )

    down_near |= {1 << i: links.step(down_mine, i) for i in range(1, links.bits)}
    down_all = links.far(down_mine, down_near)
    pair_beside |= {t: links.beside(pair_all[t]) for t in range(1, shards) if t not in pair_beside}
    attn, lse = attend(micro, seg_rows, queries, kv_all, bias)
    pair_swapped |= {t: links.swap(pair_all[t]) for t in range(1, shards) if t not in pair_swapped}
    attn, lse, down_all, pair_beside, pair_all, pair_swapped = meet(
        attn, lse, down_all, pair_beside, pair_all, pair_swapped
    )

    pair_crossed |= {t: links.swap(pair_beside[t]) for t in range(1, shards) if t not in pair_crossed}
    down_swapped = [None] + [links.swap(down_all[t]) for t in range(1, shards)]
    pieces, starts = [w_gate, w_up], [(pair_place(0, 0), 0), (pair_place(1, 0), 0)]
    for t in range(1, shards):
        pieces += [pair_all[t], pair_beside[t], pair_swapped[t], pair_crossed[t]]
        for row in (
            pair_place(links.core, links.hops[t]),
            pair_place(1 - links.core, links.hops[links.twin(t)]),
        ):
            starts += [(row, side * pair_cut), (row, (1 - side) * pair_cut)]
    pair_got = joined(pieces, starts, (2 * width, hidden))
    own = w_down.shape[0]
    pieces, starts = [down_own], [(0, links.shard * own)]
    for t in range(1, shards):
        pieces += [down_all[t], down_swapped[t]]
        starts += [
            (links.core * down_cut, (links.shard ^ links.hops[t]) * own),
            ((1 - links.core) * down_cut, (links.shard ^ links.hops[links.twin(t)]) * own),
        ]
    down_got = joined(pieces, starts, (width, own * shards))
    attn, pair_pieces, down_pieces = meet(attn, pair_got[0], down_got[0])
    pair_got, down_got = (pair_pieces, *pair_got[1:]), (down_pieces, *down_got[1:])

    plan = Plan()
    have = lambda *names: [plan.have[name] for name in names]
    x_near = links.near(inputs)
    far_cotangent = links.swap(cotangent)
    made = feed(core, inputs, attn, cotangent, gains, attention_got, pair_got, down_got)
    names = ("out", "inner", "kept", "given", "act", "attn_t", "resid")
    plan.have = dict(zip(names, made)) | {"x_near": x_near, "far_dy": far_cotangent, "queries": queries, "kv": kv_all, "lse": lse, "attn": attn}
    plan.close()

    half, mine, theirs = links.half_rows(shard_rows)
    some_kept, some_given = links.order(shard_rows, mine, theirs)
    cuts = (-(-shard_rows // 32) * 16, shard_rows - -(-shard_rows // 32) * 16)

    plan.have["x_all"] = links.far(inputs, plan.have.pop("x_near"))
    for name in ("inner", "act", "given"):
        plan.have["far_" + name] = links.swap(plan.have[name])
    names = ("d_resid", "low", "d_attn")
    resid, kept, given = have("resid", "kept", "given")
    plan.have |= dict(zip(names, feed_back(core, resid, cotangent, kept, given, gain_two, attention_got, pair_got)))
    plan.close()

    names = ("down.low", "down.high")
    far_dy, inner, far_inner = have("far_dy", "inner", "far_inner")
    starts = [(links.shard ^ hop) * own for hop in links.hops]
    plan.have |= dict(zip(names, down_grad(cotangent, far_dy, inner, far_inner, links.core * down_cut, starts)))
    plan.close()

    for name in ("down", "wide0", "wide1", "some"):
        plan.start(name, links.reduce(plan, name, name == "some"))
    plan.advance("down")
    names = ("wide0.low", "wide0.high", "wide1.low", "wide1.high")
    act, far_act, kept, far_kept = have("act", "far_act", "kept", "far_given")
    starts = [(links.shard ^ hop) * shard_rows for hop in links.hops]
    plan.have |= dict(zip(names, wide_grad(act, far_act, kept, far_kept, shard_rows, cuts, starts)))
    plan.close()

    made = ()
    hops = [("down", "wide0"), ("down", "wide0", "wide1")]
    for m in range(micro):
        plan.advance(*hops[min(m, 1)])
        q, kv_now, o, do, lse_now = have("queries", "kv", "attn", "d_attn", "lse")
        made = attend_back(m, rows, seg_rows, q, kv_now, bias, o, do, lse_now, cosine_t, sine_t, made)
        plan.have["attn_grads"] = made = tuple(made)
        plan.close()
        made = plan.have["attn_grads"]

    d_queries, *d_kv = plan.have.pop("attn_grads")
    plan.have["dkv.pieces"] = d_kv
    plan.have["d_queries"] = d_queries
    plan.start("dkv", links.collect(plan, "dkv"))
    plan.advance("dkv", "wide0", "wide1", "down")
    given, kept = attention_grad(
        plan.have["x_all"],
        gain_one,
        cosine,
        sine,
        d_queries,
        *have("attn_t", "low"),
        d_kv,
        half,
        some_given,
        some_kept,
    )
    plan.have["some.given"], plan.have["some.kept"] = given, kept
    plan.close()

    def settle():
        have, done = plan.have, plan.have.setdefault("done", {})
        if "dkv" in have and "d_input" not in done:
            done["d_input"] = finish(
                inputs, have["d_queries"], have["dkv"], have["d_resid"], gain_one, cosine, sine, *attention_got
            )
        if "down" in have and "down" not in done:
            done["down"] = links.finish_rows(*have["down"], width).T
        if "wide0" in have and "wide1" in have and "gate" not in done:
            done["gate"], done["upper"], gain = settle_wide(
                core,
                norm_second.astype(F32)[:, None],
                (have["wide0"], have["wide1"]),
                cuts,
                w_gate,
                w_up,
            )
            done["gain_two"] = gain[:, 0]
        if "some" in have and "query" not in done:
            done["query"], done["output"], key, value, gain = settle_some(
                core,
                norm_first.astype(F32)[:, None],
                *have["some"],
                w_query,
                key_weight.T,
                value_weight.T,
            )
            done["key"], done["value"], done["gain_one"] = key.T, value.T, gain[:, 0]

    order, rounds = [], 0
    while plan.tasks:
        plan.advance(*(order.pop(0) if order else tuple(plan.tasks)))
        plan.advance(*{0: ('some',), 1: ('some',)}.get(rounds, ()))
        settle()
        rounds += 1
        if rounds <= 2 and plan.tasks:
            plan.close()

    done = plan.have["done"]
    return (
        plan.have["out"].swapaxes(1, 2),
        done["d_input"].swapaxes(1, 2),
        *(done[name] for name in ("query", "key", "value", "output", "gate", "upper", "down")),
        done["gain_one"],
        done["gain_two"],
    )


def solution(mesh):
    rows = P(None, AXES, None)
    weight, gain = P("shard", None), P("shard")
    return jax.shard_map(
        local,
        mesh=mesh,
        in_specs=(rows, P(None, "rep", None)) + (weight,) * 7 + (gain, gain, rows),
        out_specs=(rows, rows) + (weight,) * 7 + (gain, gain),
        check_vma=False,
    )
```
